32 devices in a mesh: dp: 4 (over y, x), seg: 8 (over z, core).
Axes of the slice: x: 2, y: 2, z: 4, core: 2. Of those that a mesh axis runs over, the one named last changes fastest.
Arguments:
- inputs: bfloat16 [4, 4096, 768], P('dp', 'seg'), may hold values from -6 to 6
- doc_ids: int32 [4, 32], P('dp'), may hold values from 0 to 7, never falling along the last dimension, each value on 1 to 16 neighbouring positions
- cotangent: bfloat16 [4, 4096, 768], P('dp', 'seg'), may hold values from -6 to 6
- query_weight: bfloat16 [2, 768, 768], P(None, 'dp'), may hold values from -0.21875 to 0.21875
- query_bias: bfloat16 [2, 768], replicated, may hold values from -3 to 3
- key_weight: bfloat16 [2, 768, 768], P(None, 'dp'), may hold values from -0.21875 to 0.21875
- value_weight: bfloat16 [2, 768, 768], P(None, 'dp'), may hold values from -0.21875 to 0.21875
- value_bias: bfloat16 [2, 768], replicated, may hold values from -3 to 3
- out_weight: bfloat16 [2, 768, 768], P(None, 'dp'), may hold values from -1.75 to 1.75
- out_bias: bfloat16 [2, 768], replicated, may hold values from -3 to 3
- first_gain: bfloat16 [2, 768], replicated, may hold values from 0.5 to 1.5
- first_shift: bfloat16 [2, 768], replicated, may hold values from -2 to 2
- inner_weight: bfloat16 [2, 768, 3072], P(None, 'dp'), may hold values from -0.21875 to 0.21875
- inner_bias: bfloat16 [2, 3072], replicated, may hold values from -3 to 3
- outer_weight: bfloat16 [2, 3072, 768], P(None, 'dp'), may hold values from -0.109375 to 0.109375
- outer_bias: bfloat16 [2, 768], replicated, may hold values from -3 to 3
- second_gain: bfloat16 [2, 768], replicated, may hold values from 0.5 to 1.5
- second_shift: bfloat16 [2, 768], replicated, may hold values from -2 to 2
- segment_embed: bfloat16 [32, 768], replicated, may hold values from -3 to 3
Outputs:
- output: bfloat16 [4, 4096, 768], P('dp', 'seg')
- input_grad: bfloat16 [4, 4096, 768], P('dp', 'seg')
- grad_query_weight: float32 [2, 768, 768], P(None, 'dp')
- grad_query_bias: float32 [2, 768], P(None, 'dp')
- grad_key_weight: float32 [2, 768, 768], P(None, 'dp')
- grad_value_weight: float32 [2, 768, 768], P(None, 'dp')
- grad_value_bias: float32 [2, 768], P(None, 'dp')
- grad_out_weight: float32 [2, 768, 768], P(None, 'dp')
- grad_out_bias: float32 [2, 768], P(None, 'dp')
- grad_first_gain: float32 [2, 768], P(None, 'dp')
- grad_first_shift: float32 [2, 768], P(None, 'dp')
- grad_inner_weight: float32 [2, 768, 3072], P(None, 'dp')
- grad_inner_bias: float32 [2, 3072], P(None, 'dp')
- grad_outer_weight: float32 [2, 3072, 768], P(None, 'dp')
- grad_outer_bias: float32 [2, 768], P(None, 'dp')
- grad_second_gain: float32 [2, 768], P(None, 'dp')
- grad_second_shift: float32 [2, 768], P(None, 'dp')
- grad_segment_embed: float32 [32, 768], P(None, 'dp')
The draws below stay inside these ranges and needn't reach their ends.
Inputs may be any that keep to these rules, and one draw needn't show every extreme that they name: `doc_ids`: along each row document numbers never fall; each document covers one to half of 32 consecutive segments, and some document of each row covers exactly half of 32.
All inputs are finite; a program needn't handle non-finite values.
Results may differ from the reference program's by a relative error of at most 0.02.
Values may be sent and summed in bfloat16 or wider, within the bound.
A program may use at most 256 MiB of HBM per device.

```python
import math
import jax
import jax.numpy as jnp
import numpy as np
from jax import lax

D = 768
HEADS = 12
HEAD_DIM = 64
FF = 3072
SEG_LEN = 128
SEGS = 32
ROWS = 4
ROW_LEN = 4096


def levels(key, shape, cuts, smallest, top_value):
    factor_of, own = 1.0, jax.random.fold_in(key, 6)
    for position, shards_of in cuts:
        draws = jnp.exp(jax.random.uniform(jax.random.fold_in(own, position), (shards_of,), jnp.float32, smallest / len(cuts), top_value / len(cuts)))
        factor_of = factor_of * jnp.repeat(draws, shape[position] // shards_of).reshape([-1 if axis == position else 1 for axis in range(len(shape))])
    return factor_of


def split_up(amount, total, bound, lean):
    weights = [(1 << 20) // math.isqrt(rank ** lean) + 1 for rank in range(2, amount + 1)]
    surplus, given = total - bound - (amount - 1), [1] * (amount - 1)
    while surplus > 0:
        candidates = [i for i in range(amount - 1) if given[i] < bound]
        pool, left = sum([weights[i] for i in candidates]), surplus
        for i in candidates:
            addition = min(bound - given[i], max(1, left * weights[i] // pool), surplus)
            given[i] = given[i] + addition
            surplus = surplus - addition
    return np.array([bound] + given)


def ragged_sizes(stream_key, number_of, total, reach, skew):
    if number_of == 2:
        one = jax.random.randint(stream_key, (), max(1, total - reach), min(reach, total - 1) + 1)
        return jnp.stack([one, total - one])
    lengths = jnp.asarray(split_up(number_of, total, reach, skew), jnp.int32)
    pairs = (number_of - 1) // 2
    donor, taker = lengths[1:1 + 2 * pairs:2], lengths[2:2 + 2 * pairs:2]
    room = jnp.minimum(donor - 1, reach - taker)
    passed = jax.random.randint(jax.random.fold_in(stream_key, 1), (pairs,), 0, 1 << 20) % (room + 1)
    lengths = lengths.at[1:1 + 2 * pairs:2].set(donor - passed).at[2:2 + 2 * pairs:2].set(taker + passed)
    return lengths[jax.random.permutation(jax.random.fold_in(stream_key, 2), number_of)]


def bell_draw(rng, shape, scale, most, shards=(), kind=jnp.bfloat16):
    level = levels(rng, shape, shards, -0.22, 0.18) if shards else 1.0
    result = jax.random.normal(rng, shape, jnp.float32) * scale * level
    return jnp.minimum(jnp.maximum(result, -most), most).astype(kind)


def setup_inputs(seed: int = 0) -> dict:
    key_list = jax.random.split(jax.random.key(seed), 20)
    inputs = bell_draw(key_list[0], (ROWS, ROW_LEN, D), 1.0, 6.0, ((0, 4), (1, 8)))
    doc_ids = jax.vmap(lambda own: jnp.searchsorted(jnp.cumsum(ragged_sizes(own, SEGS // 4, SEGS, SEGS // 2, 1)), jnp.arange(SEGS), side="right"))(jax.random.split(key_list[1], ROWS)).reshape((ROWS, SEGS)).astype(jnp.int32)
    cotangent = bell_draw(key_list[2], (ROWS, ROW_LEN, D), 1.0, 6.0, ((0, 4), (1, 8)))
    query_weight = bell_draw(key_list[3], (2, D, D), D ** -0.5, 0.21875, ((1, 4),))
    query_bias = bell_draw(key_list[4], (2, D), 0.5, 3.0)
    key_weight = bell_draw(key_list[5], (2, D, D), D ** -0.5, 0.21875, ((1, 4),))
    value_weight = bell_draw(key_list[6], (2, D, D), D ** -0.5, 0.21875, ((1, 4),))
    value_bias = bell_draw(key_list[7], (2, D), 0.5, 3.0)
    out_weight = bell_draw(key_list[8], (2, D, D), (max(D // 64, 1)) ** -0.5, 1.75, ((1, 4),))
    out_bias = bell_draw(key_list[9], (2, D), 0.5, 3.0)
    first_gain = jnp.clip(1.0 + 0.1 * jax.random.normal(key_list[10], (2, D), jnp.float32), 0.5, 1.5).astype(jnp.bfloat16)
    first_shift = bell_draw(key_list[11], (2, D), 0.3, 2.0)
    inner_weight = bell_draw(key_list[12], (2, D, FF), D ** -0.5, 0.21875, ((1, 4),))
    inner_bias = bell_draw(key_list[13], (2, FF), 0.5, 3.0)
    outer_weight = bell_draw(key_list[14], (2, FF, D), FF ** -0.5, 0.109375, ((1, 4),))
    outer_bias = bell_draw(key_list[15], (2, D), 0.5, 3.0)
    second_gain = jnp.clip(1.0 + 0.1 * jax.random.normal(key_list[16], (2, D), jnp.float32), 0.5, 1.5).astype(jnp.bfloat16)
    second_shift = bell_draw(key_list[17], (2, D), 0.3, 2.0)
    segment_embed = bell_draw(key_list[18], (SEGS, D), 0.5, 3.0)
    return dict(inputs=inputs, doc_ids=doc_ids, cotangent=cotangent, query_weight=query_weight, query_bias=query_bias, key_weight=key_weight, value_weight=value_weight, value_bias=value_bias, out_weight=out_weight, out_bias=out_bias, first_gain=first_gain, first_shift=first_shift, inner_weight=inner_weight, inner_bias=inner_bias, outer_weight=outer_weight, outer_bias=outer_bias, second_gain=second_gain, second_shift=second_shift, segment_embed=segment_embed)


@jax.custom_vjp
def low(v):
    return lax.optimization_barrier(v.astype(jnp.bfloat16)).astype(jnp.float32)

@jax.custom_vjp
def low_back(v):
    return v

def low_keep(v):
    return (low(v), None)

def low_pass(kept, grad):
    return (grad,)

def back_keep(v):
    return (v, None)

def back_low(kept, grad):
    return (low(grad),)
low.defvjp(low_keep, low_pass)
low_back.defvjp(back_keep, back_low)
epsilon = 1e-05
highest = lax.Precision.HIGHEST

def twice(values):
    return low_back(low(values))

def normalize(values, gain, shift):
    centred = values - lax.optimization_barrier(jnp.mean(values, axis=-1, keepdims=True))
    spread = lax.optimization_barrier(jnp.mean(centred * centred, axis=-1, keepdims=True))
    return centred * lax.rsqrt(spread + epsilon) * gain + shift

def gelu_exact(values):
    return jax.nn.gelu(values, approximate=False)

def apply_layer(params, source, allowed):
    query_weight, query_bias, key_weight, value_weight, value_bias, out_weight, out_bias, first_gain, first_shift, inner_weight, inner_bias, outer_weight, outer_bias, second_gain, second_shift = params
    groups, length, width = source.shape

    def project(values, weight):
        return jnp.einsum('gnd,de->gne', values, weight, precision=highest)
    queries = twice(project(source, query_weight) + query_bias)
    key_rows = twice(project(source, key_weight))
    value_rows = twice(project(source, value_weight) + value_bias)
    query_heads = queries.reshape(groups, length, HEADS, HEAD_DIM)
    key_heads = key_rows.reshape(groups, length, HEADS, HEAD_DIM)
    value_heads = value_rows.reshape(groups, length, HEADS, HEAD_DIM)
    scores = low_back(0.125 * jnp.einsum('gqhe,gkhe->ghqk', query_heads, key_heads, precision=highest))
    if allowed is not None:
        scores = jnp.where(allowed[:, None], scores, -1e+30)
    attend = twice(jax.nn.softmax(scores, axis=-1))
    mixed = twice(jnp.einsum('ghqk,gkhe->gqhe', attend, value_heads, precision=highest).reshape(groups, length, width))
    branch = low_back(project(mixed, out_weight) + out_bias)
    hidden = normalize(source + branch, first_gain, first_shift)
    inner = low_back(jnp.einsum('gnd,df->gnf', low(hidden), inner_weight, precision=highest) + inner_bias)
    active = twice(gelu_exact(inner))
    outer = low_back(jnp.einsum('gnf,fd->gnd', active, outer_weight, precision=highest) + outer_bias)
    return normalize(hidden + outer, second_gain, second_shift)

def row_forward(first, cross, table, row, docs):
    pieces = row.reshape(SEGS, SEG_LEN, D)
    segment_out = apply_layer(first, pieces, None)
    heads_in = twice(segment_out[:, 0, :] + table)
    allowed = (docs[:, None] == docs[None, :])[None]
    cross_out = apply_layer(cross, heads_in[None], allowed)[0]
    joined = jnp.concatenate([cross_out[:, None, :], segment_out[:, 1:, :]], axis=1)
    return low(joined.reshape(SEGS * SEG_LEN, D))

def reference(inputs, doc_ids, cotangent, query_weight, query_bias, key_weight, value_weight, value_bias, out_weight, out_bias, first_gain, first_shift, inner_weight, inner_bias, outer_weight, outer_bias, second_gain, second_shift, segment_embed):
    params = tuple((w.astype(jnp.float32) for w in (query_weight, query_bias, key_weight, value_weight, value_bias, out_weight, out_bias, first_gain, first_shift, inner_weight, inner_bias, outer_weight, outer_bias, second_gain, second_shift, segment_embed)))

    def whole(source, weights):
        first = tuple((w[0] for w in weights[:15]))
        cross = tuple((w[1] for w in weights[:15]))
        table = weights[15]
        row_step = jax.checkpoint(row_forward)

        def step(carry, pair):
            row, docs = pair
            return (carry, row_step(first, cross, table, row, docs))
        _, rows_out = lax.scan(step, None, (source, doc_ids))
        return rows_out
    output, pull = jax.vjp(whole, inputs.astype(jnp.float32), params)
    grad_input, grads = pull(cotangent.astype(jnp.float32))
    return (output.astype(jnp.bfloat16), grad_input.astype(jnp.bfloat16), grads[0], grads[1], grads[2], grads[3], grads[4], grads[5], grads[6], grads[7], grads[8], grads[9], grads[10], grads[11], grads[12], grads[13], grads[14], grads[15])
```

```python
import functools

import jax
import jax.numpy as jnp
from jax import lax
from jax.experimental import pallas as pl
from jax.experimental.pallas import tpu as pltpu
from jax.sharding import PartitionSpec as P

MESH = pl.DeviceIdType.MESH
ANY = pl.BlockSpec(memory_space=pl.ANY)
BF = jnp.bfloat16
F32 = jnp.float32


def place():
    d = lax.axis_index("dp")
    s = lax.axis_index("seg")
    return d, s


def greet(peers):
    barrier = pltpu.get_barrier_semaphore()
    for peer in peers:
        pl.semaphore_signal(barrier, inc=1, device_id=peer, device_id_type=MESH)
    pl.semaphore_wait(barrier, len(peers))


def remote(src, dst, send, recv, peer):
    return pltpu.make_async_remote_copy(
        src_ref=src, dst_ref=dst, send_sem=send, recv_sem=recv, device_id=peer, device_id_type=MESH
    )


def plane_peers(d, s):
    c = s % 2
    x, y = d % 2, d // 2
    dx = 2 * y + 1 - x
    dy = 2 * (1 - y) + x
    first = dx * (1 - c) + dy * c
    second = dy * (1 - c) + dx * c
    return c, first, second, s + 1 - 2 * c


def gather_kernel(pieces, tensors, block, *refs):
    n = tensors
    shards, outs = refs[:n], refs[n : 2 * n]
    bounce = refs[2 * n : 3 * n]
    load_sem, store_sem, own_send, own_recv, fwd_send, fwd_recv, core_send, core_recv = refs[3 * n :]
    d, s = place()
    c, first, second, other = plane_peers(d, s)
    diagonal = 3 - d
    greet([(first, s), (second, s), (d, other)])

    def cols(ref):
        half = ref.shape[-1] // 2
        return pl.ds(pl.multiple_of(c * half, half), half)

    def mine(p):
        i, r0, rn = pieces[p]
        return shards[i].at[block, pl.ds(r0, rn), cols(shards[i])]

    def slot(p, src):
        i, r0, rn = pieces[p]
        return outs[i].at[src, pl.ds(r0, rn), cols(outs[i])]

    count = len(pieces)
    owns = []
    for p in range(count):
        a = remote(mine(p), slot(p, d), own_send.at[0, p], own_recv.at[0, p], (first, s))
        b = remote(mine(p), slot(p, d), own_send.at[1, p], own_recv.at[1, p], (second, s))
        a.start()
        b.start()
        owns.append((a, b))
    loads = []
    for i in range(n):
        cp = pltpu.make_async_copy(shards[i].at[block], bounce[i], load_sem.at[i])
        cp.start()
        loads.append(cp)
    stores = []
    for i in range(n):
        loads[i].wait()
        cp = pltpu.make_async_copy(bounce[i], outs[i].at[d], store_sem.at[i])
        cp.start()
        stores.append(cp)
    fwds, cores = [], []

    def share(p, src, k):
        cp = remote(slot(p, src), slot(p, src), core_send.at[k, p], core_recv.at[k, p], (d, other))
        cp.start()
        cores.append(cp)

    for p in range(count):
        got = remote(slot(p, first), slot(p, first), own_send.at[0, p], own_recv.at[0, p], (first, s))
        got.wait_recv()
        f = remote(slot(p, first), slot(p, first), fwd_send.at[p], fwd_recv.at[p], (second, s))
        f.start()
        fwds.append(f)
        share(p, first, 0)
        got = remote(slot(p, second), slot(p, second), own_send.at[1, p], own_recv.at[1, p], (second, s))
        got.wait_recv()
        share(p, second, 1)
        if p > 0:
            fwd_wait(p - 1, slot, fwd_send, fwd_recv, diagonal, second, s)
            share(p - 1, diagonal, 2)
    fwd_wait(count - 1, slot, fwd_send, fwd_recv, diagonal, second, s)
    share(count - 1, diagonal, 2)
    for a, b in owns:
        a.wait_send()
        b.wait_send()
    for f in fwds:
        f.wait_send()
    for cp in cores:
        cp.wait()
    for cp in stores:
        cp.wait()


def fwd_wait(p, slot, fwd_send, fwd_recv, diagonal, second, s):
    remote(slot(p, diagonal), slot(p, diagonal), fwd_send.at[p], fwd_recv.at[p], (second, s)).wait_recv()


def gather(shards, block, collective_id):
    pieces = []
    for i, w in enumerate(shards):
        rows = w.shape[1]
        parts = max(1, (rows * w.shape[2]) // (192 * 1536))
        for p in range(parts):
            pieces.append((i, p * rows // parts, rows // parts))
    n, count = len(shards), len(pieces)
    return pl.pallas_call(
        functools.partial(gather_kernel, pieces, n, block),
        out_shape=[jax.ShapeDtypeStruct((4,) + w.shape[1:], w.dtype) for w in shards],
        in_specs=[ANY] * n,
        out_specs=[ANY] * n,
        scratch_shapes=[pltpu.VMEM(w.shape[1:], w.dtype) for w in shards]
        + [
            pltpu.SemaphoreType.DMA((n,)),
            pltpu.SemaphoreType.DMA((n,)),
            pltpu.SemaphoreType.DMA((2, count)),
            pltpu.SemaphoreType.DMA((2, count)),
            pltpu.SemaphoreType.DMA((count,)),
            pltpu.SemaphoreType.DMA((count,)),
            pltpu.SemaphoreType.DMA((3, count)),
            pltpu.SemaphoreType.DMA((3, count)),
        ],
        compiler_params=pltpu.CompilerParams(collective_id=collective_id, has_side_effects=True),
        name="gather_weights",
    )(*shards)


def add_into(dst, a, b, rows):
    step = 48

    def body(i, carry):
        r = pl.ds(pl.multiple_of(i * step, 16), step)
        dst[r, :] = (a[r, :].astype(F32) + b[r, :].astype(F32)).astype(dst.dtype)
        return carry

    lax.fori_loop(0, rows // step, body, 0)


def reduce_kernel(nc, r, g, out, own, recv0, recv1, recv2, recv3, recv4, fin, load_sem, out_sem,
                  send0, rcv0, send1, rcv1, send2, rcv2, send3, rcv3, send4, rcv4, send5, rcv5, send6, rcv6, send7, rcv7):
    d, s = place()
    c, first, second, other = plane_peers(d, s)
    x, y = d % 2, d // 2
    a = x * (1 - c) + y * c
    b = y * (1 - c) + x * c
    z = s // 2
    z0, z1 = z % 2, z // 2
    znear = (z + 1 - 2 * z0) * 2 + c
    zfar = (z + 2 - 4 * z1) * 2 + c
    h, q = r // 2, r // 4
    greet([(first, s), (second, s), (d, other), (d, znear), (d, zfar)])

    def quarter(aa, bb):
        return aa * (1 + c) + bb * (2 - c)

    def rows(core, k):
        return pl.ds(pl.multiple_of(core * (nc * r) + k * r, 16), r)

    started = []

    def go(cp):
        cp.start()
        started.append(cp)

    loads = []
    for k in range(nc):
        go(remote(g.at[:, rows(1 - c, k), :], recv0.at[k], send0.at[k], rcv0.at[k], (d, other)))
        cp = pltpu.make_async_copy(g.at[:, rows(c, k), :], own.at[k], load_sem.at[k])
        cp.start()
        loads.append(cp)

    def arrived(ref, sem):
        pltpu.make_async_copy(ref, ref, sem).wait()

    def piece(k, i0, i1):
        return fin.at[c, k, pl.ds(pl.multiple_of(i0 * h + i1 * q, 16), q), :]

    outs = []

    def stage(t, k):
        if t == 1:
            arrived(recv0.at[k], rcv0.at[k])
            loads[k].wait()
            for bb in range(2):
                away = quarter(1 - a, bb)
                add_into(own.at[k, away], own.at[k, away], recv0.at[k, away], r)
                go(remote(own.at[k, away], recv1.at[k, bb], send1.at[k, bb], rcv1.at[k, bb], (first, s)))
            for bb in range(2):
                keep = quarter(a, bb)
                add_into(own.at[k, keep], own.at[k, keep], recv0.at[k, keep], r)
        elif t == 2:
            for bb in range(2):
                arrived(recv1.at[k, bb], rcv1.at[k, bb])
            away, keep = quarter(a, 1 - b), quarter(a, b)
            add_into(own.at[k, away], own.at[k, away], recv1.at[k, 1 - b], r)
            go(remote(own.at[k, away], recv2.at[k], send2.at[k], rcv2.at[k], (second, s)))
            add_into(own.at[k, keep], own.at[k, keep], recv1.at[k, b], r)
        elif t == 3:
            arrived(recv2.at[k], rcv2.at[k])
            keep = quarter(a, b)
            away = pl.ds(pl.multiple_of((1 - z0) * h, 16), h)
            mine = pl.ds(pl.multiple_of(z0 * h, 16), h)
            add_into(own.at[k, keep, away], own.at[k, keep, away], recv2.at[k, away], h)
            go(remote(own.at[k, keep, away], recv3.at[k], send3.at[k], rcv3.at[k], (d, znear)))
            add_into(own.at[k, keep, mine], own.at[k, keep, mine], recv2.at[k, mine], h)
        elif t == 4:
            arrived(recv3.at[k], rcv3.at[k])
            keep = quarter(a, b)
            away = pl.ds(pl.multiple_of(z0 * h + (1 - z1) * q, 16), q)
            mine = pl.ds(pl.multiple_of(z0 * h + z1 * q, 16), q)
            raway = pl.ds(pl.multiple_of((1 - z1) * q, 16), q)
            rmine = pl.ds(pl.multiple_of(z1 * q, 16), q)
            add_into(own.at[k, keep, away], own.at[k, keep, away], recv3.at[k, raway], q)
            go(remote(own.at[k, keep, away], recv4.at[k], send4.at[k], rcv4.at[k], (d, zfar)))
            add_into(own.at[k, keep, mine], own.at[k, keep, mine], recv3.at[k, rmine], q)
        elif t == 5:
            arrived(recv4.at[k], rcv4.at[k])
            keep = quarter(a, b)
            mine = pl.ds(pl.multiple_of(z0 * h + z1 * q, 16), q)
            add_into(piece(k, z0, z1), own.at[k, keep, mine], recv4.at[k], q)
            go(remote(piece(k, z0, z1), piece(k, z0, z1), send5.at[k], rcv5.at[k], (d, zfar)))
        elif t == 6:
            arrived(piece(k, z0, 1 - z1), rcv5.at[k])
            half = fin.at[c, k, pl.ds(pl.multiple_of(z0 * h, 16), h), :]
            go(remote(half, half, send6.at[k], rcv6.at[k], (d, znear)))
        elif t == 7:
            half = fin.at[c, k, pl.ds(pl.multiple_of((1 - z0) * h, 16), h), :]
            arrived(half, rcv6.at[k])
            go(remote(fin.at[c, k], fin.at[c, k], send7.at[k], rcv7.at[k], (d, other)))
            cp = pltpu.make_async_copy(fin.at[c, k], out.at[rows(c, k), :], out_sem.at[0, k])
            cp.start()
            outs.append(cp)
        elif t == 8:
            arrived(fin.at[1 - c, k], rcv7.at[k])
            cp = pltpu.make_async_copy(fin.at[1 - c, k], out.at[rows(1 - c, k), :], out_sem.at[1, k])
            cp.start()
            outs.append(cp)

    for slot in range(nc + 8):
        for t in range(8, 0, -1):
            k = slot - (t - 1)
            if 0 <= k < nc:
                stage(t, k)
    for cp in started:
        cp.wait_send()
    for cp in outs:
        cp.wait()


def reduce(g, nc, collective_id):
    _, total, width = g.shape
    r = total // 2 // nc
    dma = pltpu.SemaphoreType.DMA
    return pl.pallas_call(
        functools.partial(reduce_kernel, nc, r),
        out_shape=jax.ShapeDtypeStruct((total, width), g.dtype),
        in_specs=[ANY],
        out_specs=ANY,
        scratch_shapes=[
            pltpu.VMEM((nc, 4, r, width), g.dtype),
            pltpu.VMEM((nc, 4, r, width), g.dtype),
            pltpu.VMEM((nc, 2, r, width), g.dtype),
            pltpu.VMEM((nc, r, width), g.dtype),
            pltpu.VMEM((nc, r // 2, width), g.dtype),
            pltpu.VMEM((nc, r // 4, width), g.dtype),
            pltpu.VMEM((2, nc, r, width), g.dtype),
            dma((nc,)),
            dma((2, nc)),
            dma((nc,)), dma((nc,)),
            dma((nc, 2)), dma((nc, 2)),
            dma((nc,)), dma((nc,)),
            dma((nc,)), dma((nc,)),
            dma((nc,)), dma((nc,)),
            dma((nc,)), dma((nc,)),
            dma((nc,)), dma((nc,)),
            dma((nc,)), dma((nc,)),
        ],
        compiler_params=pltpu.CompilerParams(collective_id=collective_id, has_side_effects=True, vmem_limit_bytes=60 << 20),
        name="reduce_grads",
    )(g)


HEADS = 12
HEAD_DIM = 64
SEG_LEN = 128


epsilon = 1e-05


def normalize(values, gain, shift):
    centred = values - jnp.mean(values, axis=-1, keepdims=True)
    spread = jnp.mean(centred * centred, axis=-1, keepdims=True)
    return centred * lax.rsqrt(spread + epsilon) * gain + shift


def gelu_exact(values):
    return jax.nn.gelu(values, approximate=False)


def project(values, weight):
    return jnp.einsum("gnd,de->gne", values, weight, preferred_element_type=jnp.float32)


def back_project(values, weight):
    return jnp.einsum("gne,de->gnd", values, weight, preferred_element_type=jnp.float32)


def weight_grad(source, grads):
    return jnp.einsum("gnd,gne->de", source, grads, preferred_element_type=jnp.float32)


def row_total(values):
    return jnp.sum(values.astype(jnp.float32), axis=(0, 1))


def keep_pair(first_part, second_part):
    return (first_part, second_part)


def forward_layer(params, source, allowed, spread_keys):
    (
        query_weight,
        query_bias,
        key_weight,
        value_weight,
        value_bias,
        out_weight,
        out_bias,
        first_gain,
        first_shift,
        inner_weight,
        inner_bias,
        outer_weight,
        outer_bias,
        second_gain,
        second_shift,
    ) = params
    groups, length, width = source.shape
    queries = (project(source, query_weight) + query_bias.astype(jnp.float32)).astype(jnp.bfloat16)
    key_rows = project(source, key_weight).astype(jnp.bfloat16)
    value_rows = (project(source, value_weight) + value_bias.astype(jnp.float32)).astype(
        jnp.bfloat16
    )
    key_all, value_all = spread_keys(key_rows, value_rows)
    key_length = key_all.shape[1]
    query_heads = queries.reshape(groups, length, HEADS, HEAD_DIM)
    key_heads = key_all.reshape(groups, key_length, HEADS, HEAD_DIM)
    value_heads = value_all.reshape(groups, key_length, HEADS, HEAD_DIM)
    scores = (
        jnp.einsum("gqhe,gkhe->ghqk", query_heads, key_heads, preferred_element_type=jnp.float32)
        * 0.125
    )
    if allowed is not None:
        scores = jnp.where(allowed[:, None], scores, -1e30)
    attend = jax.nn.softmax(scores, axis=-1)
    attend_low = attend.astype(jnp.bfloat16)
    mixed = jnp.einsum(
        "ghqk,gkhe->gqhe", attend_low, value_heads, preferred_element_type=jnp.float32
    )
    mixed = mixed.astype(jnp.bfloat16).reshape(groups, length, width)
    branch = project(mixed, out_weight) + out_bias.astype(jnp.float32)
    hidden, first_pull = jax.vjp(
        normalize,
        source.astype(jnp.float32) + branch,
        first_gain.astype(jnp.float32),
        first_shift.astype(jnp.float32),
    )
    hidden_low = hidden.astype(jnp.bfloat16)
    inner = project(hidden_low, inner_weight) + inner_bias.astype(jnp.float32)
    active, gelu_pull = jax.vjp(gelu_exact, inner)
    active_low = active.astype(jnp.bfloat16)
    outer = project(active_low, outer_weight) + outer_bias.astype(jnp.float32)
    result, second_pull = jax.vjp(
        normalize, hidden + outer, second_gain.astype(jnp.float32), second_shift.astype(jnp.float32)
    )
    stored = (
        source,
        query_heads,
        key_heads,
        value_heads,
        attend,
        attend_low,
        mixed,
        first_pull,
        hidden_low,
        gelu_pull,
        active_low,
        second_pull,
    )
    return (result, stored)


def backward_layer(params, stored, grad_result, collect_keys):
    (
        query_weight,
        query_bias,
        key_weight,
        value_weight,
        value_bias,
        out_weight,
        out_bias,
        first_gain,
        first_shift,
        inner_weight,
        inner_bias,
        outer_weight,
        outer_bias,
        second_gain,
        second_shift,
    ) = params
    (
        source,
        query_heads,
        key_heads,
        value_heads,
        attend,
        attend_low,
        mixed,
        first_pull,
        hidden_low,
        gelu_pull,
        active_low,
        second_pull,
    ) = stored
    groups, length, width = source.shape
    key_length = key_heads.shape[1]
    grad_second_sum, grad_second_gain, grad_second_shift = second_pull(grad_result)
    grad_outer = grad_second_sum.astype(jnp.bfloat16)
    grad_outer_bias = row_total(grad_outer)
    grad_outer_weight = weight_grad(active_low, grad_outer)
    grad_active = back_project(grad_outer, outer_weight).astype(jnp.bfloat16)
    (grad_inner,) = gelu_pull(grad_active.astype(jnp.float32))
    grad_inner_low = grad_inner.astype(jnp.bfloat16)
    grad_inner_bias = row_total(grad_inner_low)
    grad_inner_weight = weight_grad(hidden_low, grad_inner_low)
    grad_hidden = grad_second_sum + back_project(grad_inner_low, inner_weight)
    grad_first_sum, grad_first_gain, grad_first_shift = first_pull(grad_hidden)
    grad_branch = grad_first_sum.astype(jnp.bfloat16)
    grad_out_bias = row_total(grad_branch)
    grad_out_weight = weight_grad(mixed, grad_branch)
    grad_mixed = back_project(grad_branch, out_weight).astype(jnp.bfloat16)
    grad_mixed = grad_mixed.reshape(groups, length, HEADS, HEAD_DIM)
    grad_attend = jnp.einsum(
        "gqhe,gkhe->ghqk", grad_mixed, value_heads, preferred_element_type=jnp.float32
    )
    grad_attend = grad_attend.astype(jnp.bfloat16).astype(jnp.float32)
    grad_value = jnp.einsum(
        "ghqk,gqhe->gkhe", attend_low, grad_mixed, preferred_element_type=jnp.float32
    )
    grad_value = grad_value.reshape(groups, key_length, width)
    grad_scores = attend * (grad_attend - jnp.sum(attend * grad_attend, axis=-1, keepdims=True))
    grad_scores = grad_scores.astype(jnp.bfloat16)
    grad_query = (
        jnp.einsum("ghqk,gkhe->gqhe", grad_scores, key_heads, preferred_element_type=jnp.float32)
        * 0.125
    )
    grad_query = grad_query.astype(jnp.bfloat16).reshape(groups, length, width)
    grad_key = (
        jnp.einsum("ghqk,gqhe->gkhe", grad_scores, query_heads, preferred_element_type=jnp.float32)
        * 0.125
    )
    grad_key = grad_key.reshape(groups, key_length, width)
    grad_key, grad_value = collect_keys(grad_key, grad_value)
    grad_key = grad_key.astype(jnp.bfloat16)
    grad_value = grad_value.astype(jnp.bfloat16)
    grad_source = (
        grad_first_sum
        + back_project(grad_query, query_weight)
        + back_project(grad_key, key_weight)
        + back_project(grad_value, value_weight)
    )
    gradients = (
        weight_grad(source, grad_query),
        row_total(grad_query),
        weight_grad(source, grad_key),
        weight_grad(source, grad_value),
        row_total(grad_value),
        grad_out_weight,
        grad_out_bias,
        grad_first_gain,
        grad_first_shift,
        grad_inner_weight,
        grad_inner_bias,
        grad_outer_weight,
        grad_outer_bias,
        grad_second_gain,
        grad_second_shift,
    )
    return (grad_source, gradients)


def shards(
    inputs,
    doc_ids,
    cotangent,
    query_weight,
    query_bias,
    key_weight,
    value_weight,
    value_bias,
    out_weight,
    out_bias,
    first_gain,
    first_shift,
    inner_weight,
    inner_bias,
    outer_weight,
    outer_bias,
    second_gain,
    second_shift,
    segment_embed,
):
    seg_count = lax.axis_size("seg")
    seg_index = lax.axis_index("seg")
    group_rows, local_length, width = inputs.shape
    seg_local = local_length // SEG_LEN
    query_full, key_full, value_full, out_full, inner_full, outer_full = (
        lax.all_gather(query_weight, "dp", axis=1, tiled=True),
        lax.all_gather(key_weight, "dp", axis=1, tiled=True),
        lax.all_gather(value_weight, "dp", axis=1, tiled=True),
        lax.all_gather(out_weight, "dp", axis=1, tiled=True),
        lax.all_gather(inner_weight, "dp", axis=1, tiled=True),
        lax.all_gather(outer_weight, "dp", axis=1, tiled=True),
    )
    stacked = (
        query_full,
        query_bias,
        key_full,
        value_full,
        value_bias,
        out_full,
        out_bias,
        first_gain,
        first_shift,
        inner_full,
        inner_bias,
        outer_full,
        outer_bias,
        second_gain,
        second_shift,
    )
    first_params = tuple((weight[0] for weight in stacked))
    cross_params = tuple((weight[1] for weight in stacked))
    pieces = inputs.reshape(group_rows * seg_local, SEG_LEN, width)
    segment_out, segment_stored = forward_layer(first_params, pieces, None, keep_pair)
    segment_grid = segment_out.reshape(group_rows, seg_local, SEG_LEN, width)
    position = lax.dynamic_slice_in_dim(segment_embed, seg_index * seg_local, seg_local, 0).astype(
        jnp.float32
    )
    heads_in = (segment_grid[:, :, 0, :] + position).astype(jnp.bfloat16)
    row_input = lax.all_gather(heads_in, "seg", axis=1, tiled=True)
    allowed = doc_ids[:, :, None] == doc_ids[:, None, :]
    cross_out, cross_stored = forward_layer(cross_params, row_input, allowed, keep_pair)
    returned = lax.dynamic_slice_in_dim(cross_out, seg_index * seg_local, seg_local, 1).astype(
        jnp.bfloat16
    )
    output = jnp.concatenate(
        [returned[:, :, None, :], segment_grid[:, :, 1:, :].astype(jnp.bfloat16)], axis=2
    )
    output = output.reshape(group_rows, local_length, width)
    cot_grid = cotangent.reshape(group_rows, seg_local, SEG_LEN, width)
    cot_heads = cot_grid[:, :, 0, :]
    grad_cross = lax.all_gather(cot_heads, "seg", axis=1, tiled=True)
    grad_row_input, cross_grads = backward_layer(
        cross_params, cross_stored, grad_cross.astype(jnp.float32), keep_pair
    )
    grad_row_low = grad_row_input.astype(jnp.bfloat16)
    factor = 1.0 / seg_count
    embed_grad = jnp.sum(grad_row_low.astype(jnp.float32), axis=0) * factor
    cross_grads = tuple((part * factor for part in cross_grads))
    grad_heads = lax.dynamic_slice_in_dim(grad_row_low, seg_index * seg_local, seg_local, 1)
    grad_grid = jnp.concatenate(
        [grad_heads[:, :, None, :].astype(jnp.float32), cot_grid[:, :, 1:, :].astype(jnp.float32)],
        axis=2,
    )
    grad_grid = grad_grid.reshape(group_rows * seg_local, SEG_LEN, width)
    grad_pieces, segment_grads = backward_layer(first_params, segment_stored, grad_grid, keep_pair)
    input_grad = grad_pieces.astype(jnp.bfloat16).reshape(group_rows, local_length, width)
    shares = (
        lax.psum_scatter(segment_grads[0], "dp", scatter_dimension=0, tiled=True),
        lax.psum_scatter(segment_grads[1], "dp", scatter_dimension=0, tiled=True),
        lax.psum_scatter(segment_grads[2], "dp", scatter_dimension=0, tiled=True),
        lax.psum_scatter(segment_grads[3], "dp", scatter_dimension=0, tiled=True),
        lax.psum_scatter(segment_grads[4], "dp", scatter_dimension=0, tiled=True),
        lax.psum_scatter(segment_grads[5], "dp", scatter_dimension=0, tiled=True),
        lax.psum_scatter(segment_grads[6], "dp", scatter_dimension=0, tiled=True),
        lax.psum_scatter(segment_grads[7], "dp", scatter_dimension=0, tiled=True),
        lax.psum_scatter(segment_grads[8], "dp", scatter_dimension=0, tiled=True),
        lax.psum_scatter(segment_grads[9], "dp", scatter_dimension=0, tiled=True),
        lax.psum_scatter(segment_grads[10], "dp", scatter_dimension=0, tiled=True),
        lax.psum_scatter(segment_grads[11], "dp", scatter_dimension=0, tiled=True),
        lax.psum_scatter(segment_grads[12], "dp", scatter_dimension=0, tiled=True),
        lax.psum_scatter(segment_grads[13], "dp", scatter_dimension=0, tiled=True),
        lax.psum_scatter(segment_grads[14], "dp", scatter_dimension=0, tiled=True),
        lax.psum_scatter(cross_grads[0], "dp", scatter_dimension=0, tiled=True),
        lax.psum_scatter(cross_grads[1], "dp", scatter_dimension=0, tiled=True),
        lax.psum_scatter(cross_grads[2], "dp", scatter_dimension=0, tiled=True),
        lax.psum_scatter(cross_grads[3], "dp", scatter_dimension=0, tiled=True),
        lax.psum_scatter(cross_grads[4], "dp", scatter_dimension=0, tiled=True),
        lax.psum_scatter(cross_grads[5], "dp", scatter_dimension=0, tiled=True),
        lax.psum_scatter(cross_grads[6], "dp", scatter_dimension=0, tiled=True),
        lax.psum_scatter(cross_grads[7], "dp", scatter_dimension=0, tiled=True),
        lax.psum_scatter(cross_grads[8], "dp", scatter_dimension=0, tiled=True),
        lax.psum_scatter(cross_grads[9], "dp", scatter_dimension=0, tiled=True),
        lax.psum_scatter(cross_grads[10], "dp", scatter_dimension=0, tiled=True),
        lax.psum_scatter(cross_grads[11], "dp", scatter_dimension=0, tiled=True),
        lax.psum_scatter(cross_grads[12], "dp", scatter_dimension=0, tiled=True),
        lax.psum_scatter(cross_grads[13], "dp", scatter_dimension=0, tiled=True),
        lax.psum_scatter(cross_grads[14], "dp", scatter_dimension=0, tiled=True),
        lax.psum_scatter(embed_grad, "dp", scatter_dimension=1, tiled=True),
    )
    summed = lax.psum(
        (
            shares[0],
            shares[1],
            shares[2],
            shares[3],
            shares[4],
            shares[5],
            shares[6],
            shares[7],
            shares[8],
            shares[9],
            shares[10],
            shares[11],
            shares[12],
            shares[13],
            shares[14],
            shares[15],
            shares[16],
            shares[17],
            shares[18],
            shares[19],
            shares[20],
            shares[21],
            shares[22],
            shares[23],
            shares[24],
            shares[25],
            shares[26],
            shares[27],
            shares[28],
            shares[29],
            shares[30],
        ),
        "seg",
    )
    totals = tuple((jnp.stack([summed[index], summed[index + 15]]) for index in range(15)))
    totals = totals + (summed[30],)
    return (output, input_grad) + tuple(totals)


def square_shards(
    inputs,
    doc_ids,
    cotangent,
    query_weight,
    query_bias,
    key_weight,
    value_weight,
    value_bias,
    out_weight,
    out_bias,
    first_gain,
    first_shift,
    inner_weight,
    inner_bias,
    outer_weight,
    outer_bias,
    second_gain,
    second_shift,
    segment_embed,
):
    seg_count = lax.axis_size("seg")
    seg_index = lax.axis_index("seg")
    group_rows, local_length, width = inputs.shape
    seg_local = local_length // SEG_LEN
    weights = (query_weight, key_weight, value_weight, out_weight, inner_weight, outer_weight)
    first_full = gather(weights, 0, 1)
    cross_full = gather(weights, 1, 2)
    query_full, key_full, value_full, out_full, inner_full, outer_full = (
        (one.reshape(-1, one.shape[-1]), two.reshape(-1, two.shape[-1]))
        for one, two in zip(first_full, cross_full)
    )
    stacked = (
        query_full,
        query_bias,
        key_full,
        value_full,
        value_bias,
        out_full,
        out_bias,
        first_gain,
        first_shift,
        inner_full,
        inner_bias,
        outer_full,
        outer_bias,
        second_gain,
        second_shift,
    )
    first_params = tuple((weight[0] for weight in stacked))
    cross_params = tuple((weight[1] for weight in stacked))
    pieces = inputs.reshape(group_rows * seg_local, SEG_LEN, width)
    segment_out, segment_stored = forward_layer(first_params, pieces, None, keep_pair)
    segment_grid = segment_out.reshape(group_rows, seg_local, SEG_LEN, width)
    position = lax.dynamic_slice_in_dim(segment_embed, seg_index * seg_local, seg_local, 0).astype(
        jnp.float32
    )
    heads_in = (segment_grid[:, :, 0, :] + position).astype(jnp.bfloat16)
    row_input = lax.all_gather(heads_in, "seg", axis=1, tiled=True)
    allowed = doc_ids[:, :, None] == doc_ids[:, None, :]
    cross_out, cross_stored = forward_layer(cross_params, row_input, allowed, keep_pair)
    returned = lax.dynamic_slice_in_dim(cross_out, seg_index * seg_local, seg_local, 1).astype(
        jnp.bfloat16
    )
    output = jnp.concatenate(
        [returned[:, :, None, :], segment_grid[:, :, 1:, :].astype(jnp.bfloat16)], axis=2
    )
    output = output.reshape(group_rows, local_length, width)
    cot_grid = cotangent.reshape(group_rows, seg_local, SEG_LEN, width)
    cot_heads = cot_grid[:, :, 0, :]
    grad_cross = lax.all_gather(cot_heads, "seg", axis=1, tiled=True)
    grad_row_input, cross_grads = backward_layer(
        cross_params, cross_stored, grad_cross.astype(jnp.float32), keep_pair
    )
    grad_row_low = grad_row_input.astype(jnp.bfloat16)
    factor = 1.0 / seg_count
    embed_grad = jnp.sum(grad_row_low.astype(jnp.float32), axis=0) * factor
    cross_grads = tuple((part * factor for part in cross_grads))
    grad_heads = lax.dynamic_slice_in_dim(grad_row_low, seg_index * seg_local, seg_local, 1)
    grad_grid = jnp.concatenate(
        [grad_heads[:, :, None, :].astype(jnp.float32), cot_grid[:, :, 1:, :].astype(jnp.float32)],
        axis=2,
    )
    grad_grid = grad_grid.reshape(group_rows * seg_local, SEG_LEN, width)
    grad_pieces, segment_grads = backward_layer(first_params, segment_stored, grad_grid, keep_pair)
    input_grad = grad_pieces.astype(jnp.bfloat16).reshape(group_rows, local_length, width)
    matrices = (0, 2, 3, 5, 9, 11)
    own = lax.axis_index("dp")
    summed = {}
    for block, grads in ((0, segment_grads), (1, cross_grads)):
        packed = []
        for i in matrices:
            part = grads[i].reshape(4, -1, grads[i].shape[-1])
            if part.shape[2] != width:
                part = part.reshape(4, part.shape[1], -1, width).transpose(0, 2, 1, 3)
                part = part.reshape(4, -1, width)
            packed.append(part.astype(jnp.bfloat16))
        total = reduce(jnp.concatenate(packed, axis=1), 6, 3 + block).astype(jnp.float32)
        at = 0
        for i, part in zip(matrices, packed):
            rows = part.shape[1]
            piece = total[at : at + rows]
            at += rows
            if grads[i].shape[1] != width:
                piece = piece.reshape(-1, grads[i].shape[0] // 4, width).transpose(1, 0, 2)
                piece = piece.reshape(grads[i].shape[0] // 4, -1)
            summed[i, block] = piece
    vectors = [i for i in range(15) if i not in matrices]
    flat = jnp.concatenate(
        [grads[i] for grads in (segment_grads, cross_grads) for i in vectors]
        + [embed_grad.reshape(-1)]
    )
    flat = lax.psum(flat, ("dp", "seg"))
    at = 0
    for block in range(2):
        for i in vectors:
            size = segment_grads[i].shape[0]
            share = size // 4
            summed[i, block] = lax.dynamic_slice_in_dim(flat, at + own * share, share, 0)
            at += size
    embed = lax.dynamic_slice_in_dim(flat[at:].reshape(embed_grad.shape), own * (width // 4), width // 4, 1)
    totals = tuple((jnp.stack([summed[index, 0], summed[index, 1]]) for index in range(15)))
    totals = totals + (embed,)
    return (output, input_grad) + tuple(totals)


def solution(mesh):
    placed = (
        P("dp", "seg", None),
        P("dp", None),
        P("dp", "seg", None),
        P(None, "dp", None),
        P(),
        P(None, "dp", None),
        P(None, "dp", None),
        P(),
        P(None, "dp", None),
        P(),
        P(),
        P(),
        P(None, "dp", None),
        P(),
        P(None, "dp", None),
        P(),
        P(),
        P(),
        P(),
    )
    square = mesh.shape["dp"] == 4 and mesh.shape["seg"] == 8
    return jax.shard_map(
        square_shards if square else shards,
        mesh=mesh,
        in_specs=placed,
        out_specs=(
            P("dp", "seg", None),
            P("dp", "seg", None),
            P(None, "dp", None),
            P(None, "dp"),
            P(None, "dp", None),
            P(None, "dp", None),
            P(None, "dp"),
            P(None, "dp", None),
            P(None, "dp"),
            P(None, "dp"),
            P(None, "dp"),
            P(None, "dp", None),
            P(None, "dp"),
            P(None, "dp", None),
            P(None, "dp"),
            P(None, "dp"),
            P(None, "dp"),
            P(None, "dp"),
        ),
        check_vma=False,
    )
```

```python
import functools

import jax
import jax.numpy as jnp
from jax import lax
from jax.experimental import pallas as pl
from jax.experimental.pallas import tpu as pltpu
from jax.sharding import PartitionSpec as P

HEADS = 12
HEAD_DIM = 64
SEG_LEN = 128


epsilon = 1e-05


def normalize(values, gain, shift):
    centred = values - jnp.mean(values, axis=-1, keepdims=True)
    spread = jnp.mean(centred * centred, axis=-1, keepdims=True)
    return centred * lax.rsqrt(spread + epsilon) * gain + shift


def gelu_exact(values):
    return jax.nn.gelu(values, approximate=False)


def project(values, weight):
    return jnp.einsum("gnd,de->gne", values, weight, preferred_element_type=jnp.float32)


def back_project(values, weight):
    return jnp.einsum("gne,de->gnd", values, weight, preferred_element_type=jnp.float32)


def weight_grad(source, grads):
    return jnp.einsum("gnd,gne->de", source, grads, preferred_element_type=jnp.float32)


def row_total(values):
    return jnp.sum(values.astype(jnp.float32), axis=(0, 1))


def keep_pair(first_part, second_part):
    return (first_part, second_part)


def forward_layer(params, source, allowed, spread_keys):
    (
        query_weight,
        query_bias,
        key_weight,
        value_weight,
        value_bias,
        out_weight,
        out_bias,
        first_gain,
        first_shift,
        inner_weight,
        inner_bias,
        outer_weight,
        outer_bias,
        second_gain,
        second_shift,
    ) = params
    groups, length, width = source.shape
    queries = (project(source, query_weight) + query_bias.astype(jnp.float32)).astype(jnp.bfloat16)
    key_rows = project(source, key_weight).astype(jnp.bfloat16)
    value_rows = (project(source, value_weight) + value_bias.astype(jnp.float32)).astype(
        jnp.bfloat16
    )
    key_all, value_all = spread_keys(key_rows, value_rows)
    key_length = key_all.shape[1]
    query_heads = queries.reshape(groups, length, HEADS, HEAD_DIM)
    key_heads = key_all.reshape(groups, key_length, HEADS, HEAD_DIM)
    value_heads = value_all.reshape(groups, key_length, HEADS, HEAD_DIM)
    scores = (
        jnp.einsum("gqhe,gkhe->ghqk", query_heads, key_heads, preferred_element_type=jnp.float32)
        * 0.125
    )
    if allowed is not None:
        scores = jnp.where(allowed[:, None], scores, -1e30)
    attend = jax.nn.softmax(scores, axis=-1)
    attend_low = attend.astype(jnp.bfloat16)
    mixed = jnp.einsum(
        "ghqk,gkhe->gqhe", attend_low, value_heads, preferred_element_type=jnp.float32
    )
    mixed = mixed.astype(jnp.bfloat16).reshape(groups, length, width)
    branch = project(mixed, out_weight) + out_bias.astype(jnp.float32)
    hidden, first_pull = jax.vjp(
        normalize,
        source.astype(jnp.float32) + branch,
        first_gain.astype(jnp.float32),
        first_shift.astype(jnp.float32),
    )
    hidden_low = hidden.astype(jnp.bfloat16)
    inner = project(hidden_low, inner_weight) + inner_bias.astype(jnp.float32)
    active, gelu_pull = jax.vjp(gelu_exact, inner)
    active_low = active.astype(jnp.bfloat16)
    outer = project(active_low, outer_weight) + outer_bias.astype(jnp.float32)
    result, second_pull = jax.vjp(
        normalize, hidden + outer, second_gain.astype(jnp.float32), second_shift.astype(jnp.float32)
    )
    stored = (
        source,
        query_heads,
        key_heads,
        value_heads,
        attend,
        attend_low,
        mixed,
        first_pull,
        hidden_low,
        gelu_pull,
        active_low,
        second_pull,
    )
    return (result, stored)


def backward_layer(params, stored, grad_result, collect_keys):
    (
        query_weight,
        query_bias,
        key_weight,
        value_weight,
        value_bias,
        out_weight,
        out_bias,
        first_gain,
        first_shift,
        inner_weight,
        inner_bias,
        outer_weight,
        outer_bias,
        second_gain,
        second_shift,
    ) = params
    (
        source,
        query_heads,
        key_heads,
        value_heads,
        attend,
        attend_low,
        mixed,
        first_pull,
        hidden_low,
        gelu_pull,
        active_low,
        second_pull,
    ) = stored
    groups, length, width = source.shape
    key_length = key_heads.shape[1]
    grad_second_sum, grad_second_gain, grad_second_shift = second_pull(grad_result)
    grad_outer = grad_second_sum.astype(jnp.bfloat16)
    grad_outer_bias = row_total(grad_outer)
    grad_outer_weight = weight_grad(active_low, grad_outer)
    grad_active = back_project(grad_outer, outer_weight).astype(jnp.bfloat16)
    (grad_inner,) = gelu_pull(grad_active.astype(jnp.float32))
    grad_inner_low = grad_inner.astype(jnp.bfloat16)
    grad_inner_bias = row_total(grad_inner_low)
    grad_inner_weight = weight_grad(hidden_low, grad_inner_low)
    grad_hidden = grad_second_sum + back_project(grad_inner_low, inner_weight)
    grad_first_sum, grad_first_gain, grad_first_shift = first_pull(grad_hidden)
    grad_branch = grad_first_sum.astype(jnp.bfloat16)
    grad_out_bias = row_total(grad_branch)
    grad_out_weight = weight_grad(mixed, grad_branch)
    grad_mixed = back_project(grad_branch, out_weight).astype(jnp.bfloat16)
    grad_mixed = grad_mixed.reshape(groups, length, HEADS, HEAD_DIM)
    grad_attend = jnp.einsum(
        "gqhe,gkhe->ghqk", grad_mixed, value_heads, preferred_element_type=jnp.float32
    )
    grad_attend = grad_attend.astype(jnp.bfloat16).astype(jnp.float32)
    grad_value = jnp.einsum(
        "ghqk,gqhe->gkhe", attend_low, grad_mixed, preferred_element_type=jnp.float32
    )
    grad_value = grad_value.reshape(groups, key_length, width)
    grad_scores = attend * (grad_attend - jnp.sum(attend * grad_attend, axis=-1, keepdims=True))
    grad_scores = grad_scores.astype(jnp.bfloat16)
    grad_query = (
        jnp.einsum("ghqk,gkhe->gqhe", grad_scores, key_heads, preferred_element_type=jnp.float32)
        * 0.125
    )
    grad_query = grad_query.astype(jnp.bfloat16).reshape(groups, length, width)
    grad_key = (
        jnp.einsum("ghqk,gqhe->gkhe", grad_scores, query_heads, preferred_element_type=jnp.float32)
        * 0.125
    )
    grad_key = grad_key.reshape(groups, key_length, width)
    grad_key, grad_value = collect_keys(grad_key, grad_value)
    grad_key = grad_key.astype(jnp.bfloat16)
    grad_value = grad_value.astype(jnp.bfloat16)
    grad_source = (
        grad_first_sum
        + back_project(grad_query, query_weight)
        + back_project(grad_key, key_weight)
        + back_project(grad_value, value_weight)
    )
    gradients = (
        weight_grad(source, grad_query),
        row_total(grad_query),
        weight_grad(source, grad_key),
        weight_grad(source, grad_value),
        row_total(grad_value),
        grad_out_weight,
        grad_out_bias,
        grad_first_gain,
        grad_first_shift,
        grad_inner_weight,
        grad_inner_bias,
        grad_outer_weight,
        grad_outer_bias,
        grad_second_gain,
        grad_second_shift,
    )
    return (grad_source, gradients)


def shards(
    inputs,
    doc_ids,
    cotangent,
    query_weight,
    query_bias,
    key_weight,
    value_weight,
    value_bias,
    out_weight,
    out_bias,
    first_gain,
    first_shift,
    inner_weight,
    inner_bias,
    outer_weight,
    outer_bias,
    second_gain,
    second_shift,
    segment_embed,
):
    seg_count = lax.axis_size("seg")
    seg_index = lax.axis_index("seg")
    group_rows, local_length, width = inputs.shape
    seg_local = local_length // SEG_LEN
    query_full, key_full, value_full, out_full, inner_full, outer_full = (
        lax.all_gather(query_weight, "dp", axis=1, tiled=True),
        lax.all_gather(key_weight, "dp", axis=1, tiled=True),
        lax.all_gather(value_weight, "dp", axis=1, tiled=True),
        lax.all_gather(out_weight, "dp", axis=1, tiled=True),
        lax.all_gather(inner_weight, "dp", axis=1, tiled=True),
        lax.all_gather(outer_weight, "dp", axis=1, tiled=True),
    )
    stacked = (
        query_full,
        query_bias,
        key_full,
        value_full,
        value_bias,
        out_full,
        out_bias,
        first_gain,
        first_shift,
        inner_full,
        inner_bias,
        outer_full,
        outer_bias,
        second_gain,
        second_shift,
    )
    first_params = tuple((weight[0] for weight in stacked))
    cross_params = tuple((weight[1] for weight in stacked))
    pieces = inputs.reshape(group_rows * seg_local, SEG_LEN, width)
    segment_out, segment_stored = forward_layer(first_params, pieces, None, keep_pair)
    segment_grid = segment_out.reshape(group_rows, seg_local, SEG_LEN, width)
    position = lax.dynamic_slice_in_dim(segment_embed, seg_index * seg_local, seg_local, 0).astype(
        jnp.float32
    )
    heads_in = (segment_grid[:, :, 0, :] + position).astype(jnp.bfloat16)
    row_input = lax.all_gather(heads_in, "seg", axis=1, tiled=True)
    allowed = doc_ids[:, :, None] == doc_ids[:, None, :]
    cross_out, cross_stored = forward_layer(cross_params, row_input, allowed, keep_pair)
    returned = lax.dynamic_slice_in_dim(cross_out, seg_index * seg_local, seg_local, 1).astype(
        jnp.bfloat16
    )
    output = jnp.concatenate(
        [returned[:, :, None, :], segment_grid[:, :, 1:, :].astype(jnp.bfloat16)], axis=2
    )
    output = output.reshape(group_rows, local_length, width)
    cot_grid = cotangent.reshape(group_rows, seg_local, SEG_LEN, width)
    cot_heads = cot_grid[:, :, 0, :]
    grad_cross = lax.all_gather(cot_heads, "seg", axis=1, tiled=True)
    grad_row_input, cross_grads = backward_layer(
        cross_params, cross_stored, grad_cross.astype(jnp.float32), keep_pair
    )
    grad_row_low = grad_row_input.astype(jnp.bfloat16)
    factor = 1.0 / seg_count
    embed_grad = jnp.sum(grad_row_low.astype(jnp.float32), axis=0) * factor
    cross_grads = tuple((part * factor for part in cross_grads))
    grad_heads = lax.dynamic_slice_in_dim(grad_row_low, seg_index * seg_local, seg_local, 1)
    grad_grid = jnp.concatenate(
        [grad_heads[:, :, None, :].astype(jnp.float32), cot_grid[:, :, 1:, :].astype(jnp.float32)],
        axis=2,
    )
    grad_grid = grad_grid.reshape(group_rows * seg_local, SEG_LEN, width)
    grad_pieces, segment_grads = backward_layer(first_params, segment_stored, grad_grid, keep_pair)
    input_grad = grad_pieces.astype(jnp.bfloat16).reshape(group_rows, local_length, width)
    shares = (
        lax.psum_scatter(segment_grads[0], "dp", scatter_dimension=0, tiled=True),
        lax.psum_scatter(segment_grads[1], "dp", scatter_dimension=0, tiled=True),
        lax.psum_scatter(segment_grads[2], "dp", scatter_dimension=0, tiled=True),
        lax.psum_scatter(segment_grads[3], "dp", scatter_dimension=0, tiled=True),
        lax.psum_scatter(segment_grads[4], "dp", scatter_dimension=0, tiled=True),
        lax.psum_scatter(segment_grads[5], "dp", scatter_dimension=0, tiled=True),
        lax.psum_scatter(segment_grads[6], "dp", scatter_dimension=0, tiled=True),
        lax.psum_scatter(segment_grads[7], "dp", scatter_dimension=0, tiled=True),
        lax.psum_scatter(segment_grads[8], "dp", scatter_dimension=0, tiled=True),
        lax.psum_scatter(segment_grads[9], "dp", scatter_dimension=0, tiled=True),
        lax.psum_scatter(segment_grads[10], "dp", scatter_dimension=0, tiled=True),
        lax.psum_scatter(segment_grads[11], "dp", scatter_dimension=0, tiled=True),
        lax.psum_scatter(segment_grads[12], "dp", scatter_dimension=0, tiled=True),
        lax.psum_scatter(segment_grads[13], "dp", scatter_dimension=0, tiled=True),
        lax.psum_scatter(segment_grads[14], "dp", scatter_dimension=0, tiled=True),
        lax.psum_scatter(cross_grads[0], "dp", scatter_dimension=0, tiled=True),
        lax.psum_scatter(cross_grads[1], "dp", scatter_dimension=0, tiled=True),
        lax.psum_scatter(cross_grads[2], "dp", scatter_dimension=0, tiled=True),
        lax.psum_scatter(cross_grads[3], "dp", scatter_dimension=0, tiled=True),
        lax.psum_scatter(cross_grads[4], "dp", scatter_dimension=0, tiled=True),
        lax.psum_scatter(cross_grads[5], "dp", scatter_dimension=0, tiled=True),
        lax.psum_scatter(cross_grads[6], "dp", scatter_dimension=0, tiled=True),
        lax.psum_scatter(cross_grads[7], "dp", scatter_dimension=0, tiled=True),
        lax.psum_scatter(cross_grads[8], "dp", scatter_dimension=0, tiled=True),
        lax.psum_scatter(cross_grads[9], "dp", scatter_dimension=0, tiled=True),
        lax.psum_scatter(cross_grads[10], "dp", scatter_dimension=0, tiled=True),
        lax.psum_scatter(cross_grads[11], "dp", scatter_dimension=0, tiled=True),
        lax.psum_scatter(cross_grads[12], "dp", scatter_dimension=0, tiled=True),
        lax.psum_scatter(cross_grads[13], "dp", scatter_dimension=0, tiled=True),
        lax.psum_scatter(cross_grads[14], "dp", scatter_dimension=0, tiled=True),
        lax.psum_scatter(embed_grad, "dp", scatter_dimension=1, tiled=True),
    )
    summed = lax.psum(
        (
            shares[0],
            shares[1],
            shares[2],
            shares[3],
            shares[4],
            shares[5],
            shares[6],
            shares[7],
            shares[8],
            shares[9],
            shares[10],
            shares[11],
            shares[12],
            shares[13],
            shares[14],
            shares[15],
            shares[16],
            shares[17],
            shares[18],
            shares[19],
            shares[20],
            shares[21],
            shares[22],
            shares[23],
            shares[24],
            shares[25],
            shares[26],
            shares[27],
            shares[28],
            shares[29],
            shares[30],
        ),
        "seg",
    )
    totals = tuple((jnp.stack([summed[index], summed[index + 15]]) for index in range(15)))
    totals = totals + (summed[30],)
    return (output, input_grad) + tuple(totals)


MESH = pl.DeviceIdType.MESH
ANY = pl.BlockSpec(memory_space=pl.ANY)
BF = jnp.bfloat16
F32 = jnp.float32


def place():
    d = lax.axis_index("dp")
    s = lax.axis_index("seg")
    return d, s


def greet(peers):
    barrier = pltpu.get_barrier_semaphore()
    for peer in peers:
        pl.semaphore_signal(barrier, inc=1, device_id=peer, device_id_type=MESH)
    pl.semaphore_wait(barrier, len(peers))


def remote(src, dst, send, recv, peer):
    return pltpu.make_async_remote_copy(
        src_ref=src, dst_ref=dst, send_sem=send, recv_sem=recv, device_id=peer, device_id_type=MESH
    )


def plane_peers(d, s):
    c = s % 2
    x, y = d % 2, d // 2
    dx = 2 * y + 1 - x
    dy = 2 * (1 - y) + x
    first = dx * (1 - c) + dy * c
    second = dy * (1 - c) + dx * c
    return c, first, second, s + 1 - 2 * c


def window(d):
    return pl.multiple_of((3 * d) // 2 * 128, 128), d % 2 * 64


def everyone(d, s):
    me = d * 8 + s
    ahead = [lax.rem(me + j, 32) for j in range(1, 32)]
    behind = [lax.rem(me + 32 - j, 32) for j in range(1, 32)]
    return me, ahead, behind


def gather_kernel(pieces, tensors, block, *refs):
    n = tensors
    shards, (cot, docs), refs = refs[:n], refs[n : n + 2], refs[n + 2 :]
    outs, wins, (cot_all, docs_all), refs = refs[:n], refs[n : n + 4], refs[n + 4 : n + 6], refs[n + 6 :]
    bounce, wbounce, (first_rows, heads, ids), refs = refs[:n], refs[n : n + 4], refs[n + 4 : n + 7], refs[n + 7 :]
    load_sem, store_sem, own_send, own_recv, fwd_send, fwd_recv, core_send, core_recv = refs[:8]
    wload_sem, wstore_sem, win_send, win_recv, wcore_send, wcore_recv, row_sem, all_send, all_recv, ids_send, ids_recv = refs[8:]
    d, s = place()
    c, first, second, other = plane_peers(d, s)
    diagonal = 3 - d
    me, ahead, behind = everyone(d, s)
    segs = first_rows.shape[0]
    row_loads = [pltpu.make_async_copy(cot.at[0, pl.ds(i * 128, 8)], first_rows.at[i], row_sem.at[i]) for i in range(segs)]
    row_loads.append(pltpu.make_async_copy(docs, ids, row_sem.at[segs]))
    for cp in row_loads:
        cp.start()
    for cp in row_loads:
        cp.wait()
    heads[...] = jnp.concatenate([first_rows[i].astype(F32)[0:1] for i in range(segs)], axis=0).astype(BF)
    greet([(i // 8, i % 8) for i in ahead])

    def cols(ref):
        half = ref.shape[-1] // 2
        return pl.ds(pl.multiple_of(c * half, half), half)

    def mine(p):
        i, r0, rn = pieces[p]
        return shards[i].at[block, pl.ds(r0, rn), cols(shards[i])]

    def slot(p, src):
        i, r0, rn = pieces[p]
        return outs[i].at[src, pl.ds(r0, rn), cols(outs[i])]

    count = len(pieces)
    owns = []
    for p in range(count):
        a = remote(mine(p), slot(p, d), own_send.at[0, p], own_recv.at[0, p], (first, s))
        b = remote(mine(p), slot(p, d), own_send.at[1, p], own_recv.at[1, p], (second, s))
        a.start()
        b.start()
        owns.append((a, b))
    loads = []
    for i in range(n):
        cp = pltpu.make_async_copy(shards[i].at[block], bounce[i], load_sem.at[i])
        cp.start()
        loads.append(cp)
    stores = []
    for i in range(n):
        loads[i].wait()
        cp = pltpu.make_async_copy(bounce[i], outs[i].at[d], store_sem.at[i])
        cp.start()
        stores.append(cp)
    far = (diagonal, first, second)

    def columns(w, dev, core):
        width = wins[w].shape[-1]
        at = window(dev)[0] if w < 3 else dev * width
        return pl.ds(pl.multiple_of(at + core * (width // 2), 128), width // 2)

    origins = (shards[0], shards[1], shards[2], shards[4])
    small = []
    for k, peer in enumerate(far):
        cp = remote(ids, docs_all.at[d], ids_send.at[k], ids_recv.at[k], (peer, s))
        cp.start()
        small.append(cp)
        for w in range(4):
            cp = remote(
                origins[w].at[1, :, columns(w, peer, c)], wins[w].at[d, :, cols(wins[w])],
                win_send.at[k, w], win_recv.at[k, w], (peer, s),
            )
            cp.start()
            small.append(cp)
    for j, i in enumerate(ahead):
        cp = remote(heads, cot_all.at[me], all_send.at[j], all_recv.at[j], (i // 8, i % 8))
        cp.start()
        small.append(cp)
    wloads = []
    for w in range(4):
        width = wins[w].shape[-1]
        at = window(d)[0] if w < 3 else d * width
        cp = pltpu.make_async_copy(origins[w].at[1, :, pl.ds(pl.multiple_of(at, 128), width)], wbounce[w], wload_sem.at[w])
        cp.start()
        wloads.append(cp)
    for w in range(4):
        wloads[w].wait()
        cp = pltpu.make_async_copy(wbounce[w], wins[w].at[d], wstore_sem.at[w])
        cp.start()
        stores.append(cp)
    for src, dst, i in ((heads, cot_all.at[me], 4), (ids, docs_all.at[d], 5)):
        cp = pltpu.make_async_copy(src, dst, wstore_sem.at[i])
        cp.start()
        stores.append(cp)
    fwds, cores = [], []

    def share(p, src, k):
        cp = remote(slot(p, src), slot(p, src), core_send.at[k, p], core_recv.at[k, p], (d, other))
        cp.start()
        cores.append(cp)

    for p in range(count):
        got = remote(slot(p, first), slot(p, first), own_send.at[0, p], own_recv.at[0, p], (first, s))
        got.wait_recv()
        f = remote(slot(p, first), slot(p, first), fwd_send.at[p], fwd_recv.at[p], (second, s))
        f.start()
        fwds.append(f)
        share(p, first, 0)
        got = remote(slot(p, second), slot(p, second), own_send.at[1, p], own_recv.at[1, p], (second, s))
        got.wait_recv()
        share(p, second, 1)
        if p > 0:
            fwd_wait(p - 1, slot, fwd_send, fwd_recv, diagonal, second, s)
            share(p - 1, diagonal, 2)
    fwd_wait(count - 1, slot, fwd_send, fwd_recv, diagonal, second, s)
    share(count - 1, diagonal, 2)
    for k, peer in enumerate(far):
        for w in range(4):
            got = wins[w].at[peer, :, cols(wins[w])]
            remote(got, got, win_send.at[k, w], win_recv.at[k, w], (peer, s)).wait_recv()
            cp = remote(got, got, wcore_send.at[k, w], wcore_recv.at[k, w], (d, other))
            cp.start()
            cores.append(cp)
        remote(ids, docs_all.at[peer], ids_send.at[k], ids_recv.at[k], (peer, s)).wait_recv()
    for j, i in enumerate(behind):
        remote(heads, cot_all.at[i], all_send.at[j], all_recv.at[j], (i // 8, i % 8)).wait_recv()
    for cp in small:
        cp.wait_send()
    for a, b in owns:
        a.wait_send()
        b.wait_send()
    for f in fwds:
        f.wait_send()
    for cp in cores:
        cp.wait()
    for cp in stores:
        cp.wait()


def fwd_wait(p, slot, fwd_send, fwd_recv, diagonal, second, s):
    remote(slot(p, diagonal), slot(p, diagonal), fwd_send.at[p], fwd_recv.at[p], (second, s)).wait_recv()


def gather(shards, cot, docs, collective_id):
    pieces = []
    for i, w in enumerate(shards):
        rows = w.shape[1]
        parts = max(1, (rows * w.shape[2]) // (192 * 1536))
        for p in range(parts):
            pieces.append((i, p * rows // parts, rows // parts))
    n, count = len(shards), len(pieces)
    S, VM, dma = jax.ShapeDtypeStruct, pltpu.VMEM, pltpu.SemaphoreType.DMA
    rows, width = shards[0].shape[1:]
    segs = cot.shape[1] // 128
    wins = [(rows, 256)] * 3 + [(rows, shards[4].shape[2] // 4)]
    return pl.pallas_call(
        functools.partial(gather_kernel, pieces, n, 0),
        out_shape=[S((4,) + w.shape[1:], w.dtype) for w in shards]
        + [S((4,) + w, BF) for w in wins]
        + [S((32, segs, width), BF), S((4,) + docs.shape, docs.dtype)],
        in_specs=[ANY] * (n + 2),
        out_specs=[ANY] * (n + 6),
        scratch_shapes=[VM(w.shape[1:], w.dtype) for w in shards]
        + [VM(w, BF) for w in wins]
        + [VM((segs, 8, width), BF), VM((segs, width), BF), VM(docs.shape, docs.dtype)]
        + [dma((n,)), dma((n,)), dma((2, count)), dma((2, count)), dma((count,)), dma((count,)), dma((3, count)), dma((3, count))]
        + [dma((4,)), dma((6,)), dma((3, 4)), dma((3, 4)), dma((3, 4)), dma((3, 4)), dma((segs + 1,)), dma((31,)), dma((31,)), dma((3,)), dma((3,))],
        compiler_params=pltpu.CompilerParams(collective_id=collective_id, has_side_effects=True),
        name="gather_weights",
    )(*shards, cot, docs)


def add_into(dst, a, b, rows):
    step = 48

    def body(i, carry):
        r = pl.ds(pl.multiple_of(i * step, 16), step)
        dst[r, :] = (a[r, :].astype(F32) + b[r, :].astype(F32)).astype(dst.dtype)
        return carry

    lax.fori_loop(0, rows // step, body, 0)


def reduce_kernel(nc, r, g, vec, out, vec_out, own, recv0, recv1, recv2, recv3, recv4, fin, load_sem, out_sem,
                  send0, rcv0, send1, rcv1, send2, rcv2, send3, rcv3, send4, rcv4, send5, rcv5, send6, rcv6, send7, rcv7, vsum, vgot, vsend, vrcv):
    d, s = place()
    c, first, second, other = plane_peers(d, s)
    x, y = d % 2, d // 2
    a = x * (1 - c) + y * c
    b = y * (1 - c) + x * c
    z = s // 2
    z0, z1 = z % 2, z // 2
    znear = (z + 1 - 2 * z0) * 2 + c
    zfar = (z + 2 - 4 * z1) * 2 + c
    h, q = r // 2, r // 4
    greet([(first, s), (second, s), (d, other), (d, znear), (d, zfar)])

    def quarter(aa, bb):
        return aa * (1 + c) + bb * (2 - c)

    def rows(core, k):
        return pl.ds(pl.multiple_of(core * (nc * r) + k * r, 16), r)

    started = []

    def go(cp):
        cp.start()
        started.append(cp)

    loads = []
    for k in range(nc):
        go(remote(g.at[:, rows(1 - c, k), :], recv0.at[k], send0.at[k], rcv0.at[k], (d, other)))
        cp = pltpu.make_async_copy(g.at[:, rows(c, k), :], own.at[k], load_sem.at[k])
        cp.start()
        loads.append(cp)

    def arrived(ref, sem):
        pltpu.make_async_copy(ref, ref, sem).wait()

    def piece(k, i0, i1):
        return fin.at[c, k, pl.ds(pl.multiple_of(i0 * h + i1 * q, 16), q), :]

    outs = []

    def stage(t, k):
        if t == 1:
            arrived(recv0.at[k], rcv0.at[k])
            loads[k].wait()
            for bb in range(2):
                away = quarter(1 - a, bb)
                add_into(own.at[k, away], own.at[k, away], recv0.at[k, away], r)
                go(remote(own.at[k, away], recv1.at[k, bb], send1.at[k, bb], rcv1.at[k, bb], (first, s)))
            for bb in range(2):
                keep = quarter(a, bb)
                add_into(own.at[k, keep], own.at[k, keep], recv0.at[k, keep], r)
        elif t == 2:
            for bb in range(2):
                arrived(recv1.at[k, bb], rcv1.at[k, bb])
            away, keep = quarter(a, 1 - b), quarter(a, b)
            add_into(own.at[k, away], own.at[k, away], recv1.at[k, 1 - b], r)
            go(remote(own.at[k, away], recv2.at[k], send2.at[k], rcv2.at[k], (second, s)))
            add_into(own.at[k, keep], own.at[k, keep], recv1.at[k, b], r)
        elif t == 3:
            arrived(recv2.at[k], rcv2.at[k])
            keep = quarter(a, b)
            away = pl.ds(pl.multiple_of((1 - z0) * h, 16), h)
            mine = pl.ds(pl.multiple_of(z0 * h, 16), h)
            add_into(own.at[k, keep, away], own.at[k, keep, away], recv2.at[k, away], h)
            go(remote(own.at[k, keep, away], recv3.at[k], send3.at[k], rcv3.at[k], (d, znear)))
            add_into(own.at[k, keep, mine], own.at[k, keep, mine], recv2.at[k, mine], h)
        elif t == 4:
            arrived(recv3.at[k], rcv3.at[k])
            keep = quarter(a, b)
            away = pl.ds(pl.multiple_of(z0 * h + (1 - z1) * q, 16), q)
            mine = pl.ds(pl.multiple_of(z0 * h + z1 * q, 16), q)
            raway = pl.ds(pl.multiple_of((1 - z1) * q, 16), q)
            rmine = pl.ds(pl.multiple_of(z1 * q, 16), q)
            add_into(own.at[k, keep, away], own.at[k, keep, away], recv3.at[k, raway], q)
            go(remote(own.at[k, keep, away], recv4.at[k], send4.at[k], rcv4.at[k], (d, zfar)))
            add_into(own.at[k, keep, mine], own.at[k, keep, mine], recv3.at[k, rmine], q)
        elif t == 5:
            arrived(recv4.at[k], rcv4.at[k])
            keep = quarter(a, b)
            mine = pl.ds(pl.multiple_of(z0 * h + z1 * q, 16), q)
            add_into(piece(k, z0, z1), own.at[k, keep, mine], recv4.at[k], q)
            go(remote(piece(k, z0, z1), piece(k, z0, z1), send5.at[k], rcv5.at[k], (d, zfar)))
        elif t == 6:
            arrived(piece(k, z0, 1 - z1), rcv5.at[k])
            half = fin.at[c, k, pl.ds(pl.multiple_of(z0 * h, 16), h), :]
            go(remote(half, half, send6.at[k], rcv6.at[k], (d, znear)))
        elif t == 7:
            half = fin.at[c, k, pl.ds(pl.multiple_of((1 - z0) * h, 16), h), :]
            arrived(half, rcv6.at[k])
            go(remote(fin.at[c, k], fin.at[c, k], send7.at[k], rcv7.at[k], (d, other)))
            cp = pltpu.make_async_copy(fin.at[c, k], out.at[rows(c, k), :], out_sem.at[0, k])
            cp.start()
            outs.append(cp)
        elif t == 8:
            arrived(fin.at[1 - c, k], rcv7.at[k])
            cp = pltpu.make_async_copy(fin.at[1 - c, k], out.at[rows(1 - c, k), :], out_sem.at[1, k])
            cp.start()
            outs.append(cp)

    hops = [(d, other), (first, s), (second, s), (d, znear), (d, zfar)]
    vsum[0] = vec[...]

    def vector_hop(j):
        if j > 0:
            arrived(vgot.at[j - 1], vrcv.at[j - 1])
            vsum[j] = vsum[j - 1] + vgot[j - 1]
        if j < 5:
            go(remote(vsum.at[j], vgot.at[j], vsend.at[j], vrcv.at[j], hops[j]))

    for slot in range(nc + 8):
        for t in range(8, 0, -1):
            k = slot - (t - 1)
            if 0 <= k < nc:
                stage(t, k)
        if slot < 6:
            vector_hop(slot)
    vec_out[...] = vsum[5]
    for cp in started:
        cp.wait_send()
    for cp in outs:
        cp.wait()


def reduce(g, vec, nc, collective_id):
    _, total, width = g.shape
    r = total // 2 // nc
    dma = pltpu.SemaphoreType.DMA
    return pl.pallas_call(
        functools.partial(reduce_kernel, nc, r),
        out_shape=[jax.ShapeDtypeStruct((total, width), g.dtype), jax.ShapeDtypeStruct(vec.shape, vec.dtype)],
        in_specs=[ANY, pl.BlockSpec(memory_space=pltpu.VMEM)],
        out_specs=[ANY, pl.BlockSpec(memory_space=pltpu.VMEM)],
        scratch_shapes=[
            pltpu.VMEM((nc, 4, r, width), g.dtype),
            pltpu.VMEM((nc, 4, r, width), g.dtype),
            pltpu.VMEM((nc, 2, r, width), g.dtype),
            pltpu.VMEM((nc, r, width), g.dtype),
            pltpu.VMEM((nc, r // 2, width), g.dtype),
            pltpu.VMEM((nc, r // 4, width), g.dtype),
            pltpu.VMEM((2, nc, r, width), g.dtype),
            dma((nc,)),
            dma((2, nc)),
            dma((nc,)), dma((nc,)),
            dma((nc, 2)), dma((nc, 2)),
            dma((nc,)), dma((nc,)),
            dma((nc,)), dma((nc,)),
            dma((nc,)), dma((nc,)),
            dma((nc,)), dma((nc,)),
            dma((nc,)), dma((nc,)),
            dma((nc,)), dma((nc,)),
            pltpu.VMEM((6,) + vec.shape, vec.dtype),
            pltpu.VMEM((5,) + vec.shape, vec.dtype),
            dma((5,)), dma((5,)),
        ],
        compiler_params=pltpu.CompilerParams(collective_id=collective_id, has_side_effects=True, vmem_limit_bytes=60 << 20),
        name="reduce_grads",
    )(g, vec)


TILE = 256


def dot(a, b):
    return lax.dot_general(a, b, (((1,), (0,)), ((), ())), preferred_element_type=F32)


def dot_nt(a, b):
    return lax.dot_general(a, b, (((1,), (1,)), ((), ())), preferred_element_type=F32)


def dot_tn(a, b):
    return lax.dot_general(a, b, (((0,), (0,)), ((), ())), preferred_element_type=F32)


def tiles(i, size=TILE):
    return pl.ds(pl.multiple_of(i * size, size), size)


def standard(r):
    centred = r - jnp.mean(r, axis=-1, keepdims=True)
    rstd = lax.rsqrt(jnp.mean(centred * centred, axis=-1, keepdims=True) + epsilon)
    return centred * rstd, rstd


def standard_back(grad, xhat, rstd):
    return rstd * (
        grad
        - jnp.mean(grad, axis=-1, keepdims=True)
        - xhat * jnp.mean(grad * xhat, axis=-1, keepdims=True)
    )


def gelu_parts(u):
    phi = 0.5 * (1.0 + lax.erf(u * 0.7071067811865476))
    return u * phi, phi + u * (0.3989422804014327 * jnp.exp(-0.5 * u * u))


def head_masks():
    lane = lax.broadcasted_iota(jnp.int32, (1, 128), 1)
    low = (lane < 64).astype(F32)
    return (low.astype(BF), (1.0 - low).astype(BF))


def row_sum(v):
    return jnp.sum(v, axis=0, keepdims=True)


def forward_kernel(x, wq, wk, wv, wo, wi, w2, qb, vb, ob, g1, c1, ib, b2, g2, c2,
                   q_o, k_o, v_o, p_o, o_o, hb_o, e_o, gp_o, x1_o, r1_o, x2_o, r2_o, y_o, cls_o,
                   vq, vk, vv, vo, vi, v2, x1, x2, in_sem, p_s, e_s, gp_s, out_sem):
    loads = [
        pltpu.make_async_copy(src, dst, in_sem.at[i])
        for i, (src, dst) in enumerate(((wq, vq), (wk, vk), (wv, vv), (wo, vo), (wi, vi), (w2, v2)))
    ]
    for cp in loads:
        cp.start()
    rows, width = x.shape
    segs = rows // 128
    nt = width // TILE
    loads[0].wait()
    loads[1].wait()
    loads[2].wait()

    def qkv(t, carry):
        lanes = tiles(t)
        q_o[:, lanes] = (dot(x[...], vq[:, lanes]) + qb[0:1, lanes].astype(F32)).astype(BF)
        k_o[:, lanes] = dot(x[...], vk[:, lanes]).astype(BF)
        v_o[:, lanes] = (dot(x[...], vv[:, lanes]) + vb[0:1, lanes].astype(F32)).astype(BF)
        return carry

    lax.fori_loop(0, nt, qkv, 0)
    masks = head_masks()

    def attend(hp, carry):
        lanes = tiles(hp, 128)
        for s in range(segs):
            here = slice(s * 128, s * 128 + 128)
            qs, ks, vs = q_o[here, lanes], k_o[here, lanes], v_o[here, lanes]
            mixed = None
            for h in range(2):
                scores = dot_nt(qs * masks[h], ks)
                top = jnp.max(scores, axis=-1, keepdims=True)
                weight = jnp.exp((scores - top) * 0.125)
                share = (weight * (1.0 / jnp.sum(weight, axis=-1, keepdims=True))).astype(BF)
                p_s[hp, s, h] = share
                part = dot(share, vs * masks[h])
                mixed = part if mixed is None else mixed + part
            o_o[here, lanes] = mixed.astype(BF)
        return carry

    lax.fori_loop(0, width // 128, attend, 0)
    p_copy = pltpu.make_async_copy(p_s, p_o, out_sem.at[0])
    p_copy.start()
    loads[3].wait()

    def out(t, carry):
        lanes = tiles(t)
        x1[:, lanes] = dot(o_o[...], vo[:, lanes]) + ob[0:1, lanes].astype(F32) + x[:, lanes].astype(F32)
        return carry

    lax.fori_loop(0, nt, out, 0)

    def first(i, carry):
        r = tiles(i, 64)
        xhat, rstd = standard(x1[r, :])
        x1_o[r, :] = xhat
        r1_o[r, :] = jnp.broadcast_to(rstd, (64, 128))
        hidden = xhat * g1[0:1, :].astype(F32) + c1[0:1, :].astype(F32)
        hb_o[r, :] = hidden.astype(BF)
        x2[r, :] = hidden + b2[0:1, :].astype(F32)
        return carry

    lax.fori_loop(0, rows // 64, first, 0)
    loads[4].wait()
    loads[5].wait()

    def ffn(t, carry):
        lanes = tiles(t)
        u = dot(hb_o[...], vi[:, lanes]) + ib[0:1, lanes].astype(F32)
        e, gp = gelu_parts(u)
        e_s[:, lanes] = e.astype(BF)
        gp_s[:, lanes] = gp.astype(BF)
        return carry

    lax.fori_loop(0, vi.shape[1] // TILE, ffn, 0)
    e_copy = pltpu.make_async_copy(e_s, e_o, out_sem.at[1])
    gp_copy = pltpu.make_async_copy(gp_s, gp_o, out_sem.at[2])
    e_copy.start()
    gp_copy.start()

    def outer(t, carry):
        lanes = tiles(t)
        x2[:, lanes] += dot(e_s[...], v2[:, lanes])
        return carry

    lax.fori_loop(0, nt, outer, 0)

    def second(i, carry):
        r = tiles(i, 64)
        xhat, rstd = standard(x2[r, :])
        x2_o[r, :] = xhat
        r2_o[r, :] = jnp.broadcast_to(rstd, (64, 128))
        y_o[r, :] = (xhat * g2[0:1, :].astype(F32) + c2[0:1, :].astype(F32)).astype(BF)
        return carry

    lax.fori_loop(0, rows // 64, second, 0)
    for s in range(segs):
        cls_o[s : s + 1, :] = x2_o[s * 128 : s * 128 + 1, :] * g2[0:1, :].astype(F32) + c2[0:1, :].astype(F32)
    p_copy.wait()
    e_copy.wait()
    gp_copy.wait()


def forward(x, weights, vectors):
    rows, width = x.shape
    ff = weights[4].shape[1]
    segs, pairs = rows // 128, width // 128
    S = jax.ShapeDtypeStruct
    V = pl.BlockSpec(memory_space=pltpu.VMEM)
    low, full = S((rows, width), BF), S((rows, width), F32)
    wide = S((rows, ff), BF)
    probs = S((pairs, segs, 2, 128, 128), BF)
    col = S((rows, 128), F32)
    return pl.pallas_call(
        forward_kernel,
        out_shape=[low, low, low, probs, low, low, wide, wide, full, col, full, col, low, S((segs, width), F32)],
        in_specs=[V] + [ANY] * 6 + [V] * 9,
        out_specs=[V, V, V, ANY, V, V, ANY, ANY, V, V, V, V, V, V],
        scratch_shapes=[pltpu.VMEM(w.shape, BF) for w in weights]
        + [pltpu.VMEM((rows, width), F32)] * 2
        + [
            pltpu.SemaphoreType.DMA((6,)),
            pltpu.VMEM(probs.shape, BF),
            pltpu.VMEM(wide.shape, BF),
            pltpu.VMEM(wide.shape, BF),
            pltpu.SemaphoreType.DMA((3,)),
        ],
        compiler_params=pltpu.CompilerParams(vmem_limit_bytes=60 << 20),
        name="segment_forward",
    )(x, *weights, *vectors)


def backward_kernel(x, cot, dcl, q, k, v, p, o, hb, e, gp, x1, r1, x2, r2, y, z, wq, wk, wv, wo, wi, w2, g1, g2,
                    dx_o, y_o, g_o, vec_o,
                    vq, vk, vv, vo, vi, v2, e_s, gp_s, p_s, gs, dr2, acc, df, ht, da, do, dq, dk, dv, in_sem, out_sem):
    loads = [
        pltpu.make_async_copy(src, dst, in_sem.at[i])
        for i, (src, dst) in enumerate(
            ((w2, v2), (e, e_s), (gp, gp_s), (wi, vi), (wo, vo), (p, p_s), (wq, vq), (wk, vk), (wv, vv))
        )
    ]
    for cp in loads:
        cp.start()
    rows, width = x.shape
    segs, nt = rows // 128, width // TILE
    ff = vi.shape[1]
    share = width // 4
    vec_o[...] = jnp.zeros_like(vec_o)

    def second(i, carry):
        gain_sum, shift_sum, bias_sum = carry
        r = tiles(i, 64)
        dy, out = cot[r, :].astype(F32), y[r, :].astype(F32)
        at = lax.broadcasted_iota(jnp.int32, (64, 1), 0) + i * 64
        for s in range(segs):
            dy = jnp.where(at == s * 128, dcl[s : s + 1, :], dy)
            out = jnp.where(at == s * 128, z[s : s + 1, :], out)
        y_o[r, :] = out.astype(BF)
        xhat = x2[r, :]
        back = standard_back(dy * g2[0:1, :].astype(F32), xhat, r2[r, 0:1])
        dr2[r, :] = back
        low = back.astype(BF)
        df[r, :] = low
        return (gain_sum + row_sum(dy * xhat), shift_sum + row_sum(dy), bias_sum + row_sum(low.astype(F32)))

    zero = jnp.zeros((1, width), F32)
    sums = lax.fori_loop(0, rows // 64, second, (zero, zero, zero))
    vec_o[6:7, :], vec_o[7:8, :], vec_o[5:6, :] = sums
    ht[...] = hb[...].T
    acc[...] = dr2[...]
    for i in range(4):
        loads[i].wait()

    def ffn(t, carry):
        wide = tiles(t)
        block, lanes = t // nt, tiles(t % nt)
        de = dot_nt(df[...], v2[wide, :]).astype(BF).astype(F32)
        du = (de * gp_s[:, wide].astype(F32)).astype(BF)
        vec_o[pl.ds(8 + block, 1), lanes] = row_sum(du.astype(F32))
        back = dot_tn(e_s[:, wide], df[...])
        gs[block, pl.ds(pl.multiple_of(8 * share + (t % nt) * TILE, TILE), TILE), :] = back.astype(BF)
        inner = dot(ht[...], du).astype(BF)
        for d in range(4):
            gs[d, pl.ds(pl.multiple_of(4 * share + block * share, 64), share), lanes] = inner[d * share : d * share + share]
        acc[...] += dot_nt(du, vi[:, wide])
        return carry

    lax.fori_loop(0, ff // TILE, ffn, 0)
    half = 4 * share
    copies = [pltpu.make_async_copy(gs.at[:, half:, :], g_o.at[:, half:, :], out_sem.at[0])]
    copies[0].start()

    def first(i, carry):
        gain_sum, shift_sum, bias_sum = carry
        r = tiles(i, 64)
        dh = acc[r, :]
        xhat = x1[r, :]
        back = standard_back(dh * g1[0:1, :].astype(F32), xhat, r1[r, 0:1])
        dr2[r, :] = back
        low = back.astype(BF)
        da[r, :] = low
        return (gain_sum + row_sum(dh * xhat), shift_sum + row_sum(dh), bias_sum + row_sum(low.astype(F32)))

    sums = lax.fori_loop(0, rows // 64, first, (zero, zero, zero))
    vec_o[3:4, :], vec_o[4:5, :], vec_o[2:3, :] = sums
    loads[4].wait()
    do[...] = dot_nt(da[...], vo[...]).astype(BF)

    def spread(at, lhs, rhs):
        back = dot_tn(lhs, rhs).astype(BF)
        for d in range(4):
            gs[d, at * share : at * share + share, :] = back[d * share : d * share + share]

    spread(3, o[...], da[...])
    loads[5].wait()
    masks = head_masks()

    def attend(hp, carry):
        lanes = tiles(hp, 128)
        for s in range(segs):
            here = slice(s * 128, s * 128 + 128)
            qs, ks, vs, dos = q[here, lanes], k[here, lanes], v[here, lanes], do[here, lanes]
            dqs = dks = dvs = 0.0
            for h in range(2):
                pl_ = p_s[hp, s, h]
                pf = pl_.astype(F32)
                dom = dos * masks[h]
                dp = dot_nt(dom, vs).astype(BF).astype(F32)
                ds = (pf * (dp - jnp.sum(pf * dp, axis=-1, keepdims=True))).astype(BF)
                dqs += dot(ds, ks * masks[h])
                dks += dot_tn(ds, qs * masks[h])
                dvs += dot_tn(pl_, dom)
            dq[here, lanes] = (dqs * 0.125).astype(BF)
            dk[here, lanes] = (dks * 0.125).astype(BF)
            dv[here, lanes] = dvs.astype(BF)
        return carry

    lax.fori_loop(0, width // 128, attend, 0)
    vec_o[0:1, :] = row_sum(dq[...].astype(F32))
    vec_o[1:2, :] = row_sum(dv[...].astype(F32))
    ht[...] = x[...].T
    for i in range(6, 9):
        loads[i].wait()

    def weights(at, rhs):
        back = dot(ht[...], rhs[...]).astype(BF)
        for d in range(4):
            gs[d, at * share : at * share + share, :] = back[d * share : d * share + share]

    weights(0, dq)
    weights(1, dk)
    weights(2, dv)
    copies.append(pltpu.make_async_copy(gs.at[:, :half, :], g_o.at[:, :half, :], out_sem.at[1]))
    copies[1].start()

    def source(t, carry):
        r = tiles(t)
        dx = dr2[:, r] + dot_nt(dq[...], vq[r, :]) + dot_nt(dk[...], vk[r, :]) + dot_nt(dv[...], vv[r, :])
        dx_o[:, r] = dx.astype(BF)
        return carry

    lax.fori_loop(0, nt, source, 0)
    for cp in copies:
        cp.wait()


def backward(x, cot, dcl, saved, y, z, weights, g1, g2):
    q, k, v, p, o, hb, e, gp, x1, r1, x2, r2 = saved
    rows, width = x.shape
    ff = weights[4].shape[1]
    S = jax.ShapeDtypeStruct
    V = pl.BlockSpec(memory_space=pltpu.VMEM)
    packed = S((4, width // 4 * 4 + 2 * ff // 4, width), BF)
    VM = pltpu.VMEM
    low, full = VM((rows, width), BF), VM((rows, width), F32)
    return pl.pallas_call(
        backward_kernel,
        out_shape=[S((rows, width), BF), S((rows, width), BF), packed, S((16, width), F32)],
        in_specs=[V, V, V, V, V, V, ANY, V, V, ANY, ANY, V, V, V, V, V, V] + [ANY] * 6 + [V] * 2,
        out_specs=[V, V, ANY, V],
        scratch_shapes=[VM(w.shape, BF) for w in weights]
        + [
            VM((rows, ff), BF),
            VM((rows, ff), BF),
            VM(p.shape, BF),
            VM(packed.shape, BF),
            full, full, low,
            VM((width, rows), BF),
            low, low, low, low, low,
            pltpu.SemaphoreType.DMA((9,)),
            pltpu.SemaphoreType.DMA((2,)),
        ],
        compiler_params=pltpu.CompilerParams(vmem_limit_bytes=63 << 20),
        name="segment_backward",
    )(x, cot, dcl, q, k, v, p, o, hb, e, gp, x1, r1, x2, r2, y, z, *weights, g1, g2)


def cross_kernel(cls, emb, cot_all, docs, wq, wk, wv, wi, out_w, outer_w,
                 qb, vb, ob, g1, c1, ib, b2, g2, c2,
                 z_o, dcl_o, xw_o, hw_o, ow_o, e_o, dqkv_o, du_o, da_o, df_o, vec_o, emb_o,
                 vq, vk, vv, vi, vo, v2, heads, xall, rows_s, p_s, dqkv_s, du_s, send1, got1, send2, got2,
                 in_sem, all_send, all_recv, s1, r1, s2, r2, qs_send, qs_recv, us_send, us_recv, o_sem):
    d, s = place()
    c, first, second, other = plane_peers(d, s)
    start, off = window(d)
    me, ahead, behind = everyone(d, s)
    far = [3 - d, first, second]
    lane_w = pl.ds(start, 256)
    loads = [
        pltpu.make_async_copy(src, dst, in_sem.at[i])
        for i, (src, dst) in enumerate(
            (
                (wq, vq), (wk, vk), (wv, vv),
                (out_w.at[1], vo.at[pl.ds(pl.multiple_of(off, 64), 192)]),
                (wi, vi), (outer_w.at[1], v2),
            )
        )
    ]
    for cp in loads:
        cp.start()
    vo[pl.ds(pl.multiple_of(192 * (1 - d % 2), 64), 64), :] = jnp.zeros((64, 768), BF)
    pick = lax.broadcasted_iota(jnp.int32, (8, 32), 0) + 4 * s == lax.broadcasted_iota(jnp.int32, (8, 32), 1)
    position = dot(pick.astype(BF), emb[...])
    heads[...] = (cls[...] + position[0:4]).astype(BF)
    greet([(i // 8, i % 8) for i in ahead])
    sent = []
    for j, i in enumerate(ahead):
        cp = remote(heads, xall.at[me], all_send.at[j], all_recv.at[j], (i // 8, i % 8))
        cp.start()
        sent.append(cp)
    xall[me] = heads[...]
    dys = []
    for i in range(32):
        rows_s[4 * i : 4 * i + 4, :] = cot_all[i].astype(F32)
    dy = rows_s[...]
    ids = lax.broadcasted_iota(jnp.int32, (8, 128), 1) // 32 * 1024
    ids = ids.astype(F32)
    lane = lax.broadcasted_iota(jnp.int32, (32, 128), 1)
    key = lax.broadcasted_iota(jnp.int32, (32, 128), 0)
    for r in range(4):
        numbers = jnp.broadcast_to(docs[r], (8, 32)).astype(F32).astype(BF)
        ids = ids + dot(numbers, (lane == key + 32 * r).astype(BF))
    across = jnp.broadcast_to(ids[0:1], (128, 128))
    allowed = across == across.T
    for j, i in enumerate(behind):
        remote(heads, xall.at[i], all_send.at[j], all_recv.at[j], (i // 8, i % 8)).wait_recv()
    for i in range(32):
        rows_s[4 * i : 4 * i + 4, :] = xall[i].astype(F32)
    xf = rows_s[...]
    x = xf.astype(BF)

    def total(n, partial):
        send1[n] = partial.astype(BF)
        one = remote(send1.at[n], got1.at[n], s1.at[n], r1.at[n], (first, s))
        one.start()
        one.wait_recv()
        both = send1[n].astype(F32) + got1[n].astype(F32)
        send2[n] = both.astype(BF)
        two = remote(send2.at[n], got2.at[n], s2.at[n], r2.at[n], (second, s))
        two.start()
        two.wait_recv()
        sent.append(one)
        sent.append(two)
        return send2[n].astype(F32) + got2[n].astype(F32)

    def vector(ref, lanes=slice(None)):
        return ref[1:2, lanes].astype(F32)

    for i in range(3):
        loads[i].wait()
    q = (dot(x, vq[...]) + vector(qb, lane_w)).astype(BF)
    k = dot(x, vk[...]).astype(BF)
    v = (dot(x, vv[...]) + vector(vb, lane_w)).astype(BF)
    masks = head_masks()
    mixed = []
    for pair in range(2):
        l = slice(pair * 128, pair * 128 + 128)
        both = None
        for h in range(2):
            scores = jnp.where(allowed, dot_nt(q[:, l] * masks[h], k[:, l]) * 0.125, -1e30)
            weight = jnp.exp(scores - jnp.max(scores, axis=-1, keepdims=True))
            share = (weight * (1.0 / jnp.sum(weight, axis=-1, keepdims=True))).astype(BF)
            p_s[2 * pair + h] = share
            part = dot(share, v[:, l] * masks[h])
            both = part if both is None else both + part
        mixed.append(both.astype(BF))
    loads[3].wait()
    ow = jnp.concatenate(mixed, axis=1)
    ow_o[...] = ow
    branch = total(0, dot(ow, vo[...]))
    xhat1, rstd1 = standard(xf + branch + vector(ob))
    hidden = xhat1 * vector(g1) + vector(c1)
    hb = hidden.astype(BF)
    rows_s[...] = hidden
    hw_o[...] = rows_s[:, lane_w].astype(BF)
    rows_s[...] = xf
    xw_o[...] = rows_s[:, lane_w].astype(BF)
    loads[4].wait()
    loads[5].wait()
    wide = pl.ds(pl.multiple_of(d * 768, 768), 768)
    e, gp = gelu_parts(dot(hb, vi[...]) + vector(ib, wide))
    e = e.astype(BF)
    e_o[...] = e
    outer = total(1, dot(e, v2[...]))
    xhat2, rstd2 = standard(hidden + outer + vector(b2))
    z = (xhat2 * vector(g2) + vector(c2)).astype(BF)
    own = lax.broadcasted_iota(jnp.int32, (8, 128), 0) + 4 * me == lax.broadcasted_iota(jnp.int32, (8, 128), 1)
    own = own.astype(BF)
    z_o[...] = dot(own, z)
    vec_o[6:7, :] = row_sum(dy * xhat2)
    vec_o[7:8, :] = row_sum(dy)
    dr2 = standard_back(dy * vector(g2), xhat2, rstd2)
    df = dr2.astype(BF)
    df_o[...] = df
    vec_o[5:6, :] = row_sum(df.astype(F32))
    du = (dot_nt(df, v2[...]).astype(BF).astype(F32) * gp).astype(BF)
    du_s[d] = du
    dh = dr2 + total(2, dot_nt(du, vi[...]))
    for n, peer in enumerate(far):
        cp = remote(du_s.at[d], du_s.at[d], us_send.at[n], us_recv.at[n], (peer, s))
        cp.start()
        sent.append(cp)
    vec_o[3:4, :] = row_sum(dh * xhat1)
    vec_o[4:5, :] = row_sum(dh)
    dr1 = standard_back(dh * vector(g1), xhat1, rstd1)
    da = dr1.astype(BF)
    da_o[...] = da
    vec_o[2:3, :] = row_sum(da.astype(F32))
    do = dot_nt(da, vo[...]).astype(BF)
    dqs, dks, dvs = [], [], []
    for pair in range(2):
        l = slice(pair * 128, pair * 128 + 128)
        dqp = dkp = dvp = 0.0
        for h in range(2):
            share = p_s[2 * pair + h]
            pf = share.astype(F32)
            dom = do[:, l] * masks[h]
            dp = dot_nt(dom, v[:, l]).astype(BF).astype(F32)
            ds = (pf * (dp - jnp.sum(pf * dp, axis=-1, keepdims=True))).astype(BF)
            dqp += dot(ds, k[:, l] * masks[h])
            dkp += dot_tn(ds, q[:, l] * masks[h])
            dvp += dot_tn(share, dom)
        dqs.append((dqp * 0.125).astype(BF))
        dks.append((dkp * 0.125).astype(BF))
        dvs.append(dvp.astype(BF))
    dq, dk, dv = (jnp.concatenate(t, axis=1) for t in (dqs, dks, dvs))
    dqkv_s[d, :, 0:256] = dq
    dqkv_s[d, :, 256:512] = dk
    dqkv_s[d, :, 512:768] = dv
    dx = dr1 + total(3, dot_nt(dq, vq[...]) + dot_nt(dk, vk[...]) + dot_nt(dv, vv[...]))
    for n, peer in enumerate(far):
        cp = remote(dqkv_s.at[d], dqkv_s.at[d], qs_send.at[n], qs_recv.at[n], (peer, s))
        cp.start()
        sent.append(cp)
    dcl = dx.astype(BF)
    dcl_o[...] = dot(own, dcl)
    back = dcl.astype(F32)
    emb_o[...] = back[0:32] + back[32:64] + back[64:96] + back[96:128]
    for n, peer in enumerate(far):
        remote(du_s.at[peer], du_s.at[peer], us_send.at[n], us_recv.at[n], (peer, s)).wait_recv()
        remote(dqkv_s.at[peer], dqkv_s.at[peer], qs_send.at[n], qs_recv.at[n], (peer, s)).wait_recv()
    outs = [pltpu.make_async_copy(du_s, du_o, o_sem.at[0]), pltpu.make_async_copy(dqkv_s, dqkv_o, o_sem.at[1])]
    for cp in outs:
        cp.start()
    for cp in sent:
        cp.wait_send()
    for cp in outs:
        cp.wait()


def cross(cls, emb, cot_all, docs, wq, wk, wv, wi, out_w, outer_w, vectors, collective_id):
    S = jax.ShapeDtypeStruct
    V = pl.BlockSpec(memory_space=pltpu.VMEM)
    VM, dma = pltpu.VMEM, pltpu.SemaphoreType.DMA
    low, win, four = S((128, 768), BF), S((128, 256), BF), S((4, 128, 768), BF)
    return pl.pallas_call(
        cross_kernel,
        out_shape=[
            S((8, 768), F32), S((8, 768), F32), win, win, win, low, four, four, low, low,
            S((8, 768), F32), S((32, 768), F32),
        ],
        in_specs=[V] * 4 + [ANY] * 6 + [V] * 9,
        out_specs=[V] * 6 + [ANY] * 2 + [V] * 4,
        scratch_shapes=[
            VM((768, 256), BF), VM((768, 256), BF), VM((768, 256), BF), VM((768, 768), BF), VM((256, 768), BF), VM((768, 768), BF),
            VM((4, 768), BF), VM((32, 4, 768), BF), VM((128, 768), F32), VM((4, 128, 128), BF),
            VM((4, 128, 768), BF), VM((4, 128, 768), BF),
            VM((4, 128, 768), BF), VM((4, 128, 768), BF), VM((4, 128, 768), BF), VM((4, 128, 768), BF),
            dma((6,)), dma((31,)), dma((31,)),
            dma((4,)), dma((4,)), dma((4,)), dma((4,)), dma((3,)), dma((3,)), dma((3,)), dma((3,)), dma((2,)),
        ],
        compiler_params=pltpu.CompilerParams(collective_id=collective_id, has_side_effects=True, vmem_limit_bytes=48 << 20),
        name="cross_block",
    )(cls, emb, cot_all, docs, wq, wk, wv, wi, out_w, outer_w, *vectors)


def finish_kernel(red, vec, emb, xw, hw, ow, e, dqkv, du, da, df, vec1,
                  gq, gqb, gk, gv, gvb, go, gob, gg1, gc1, gi, gib, g2_, gb2, gg2, gc2, gemb, vec_s):
    d = lax.axis_index("dp")
    odd = d % 2 == 1
    start, _ = window(d)

    def own(w):
        return jnp.where(odd, w[:, 64:256], w[:, 0:192])

    def whole(at):
        parts = [dqkv[i, :, at * 256 : at * 256 + 256] for i in range(4)]
        return jnp.concatenate(
            [
                parts[0][:, :128], parts[0][:, 128:] + parts[1][:, :128], parts[1][:, 128:],
                parts[2][:, :128], parts[2][:, 128:] + parts[3][:, :128], parts[3][:, 128:],
            ],
            axis=1,
        )

    x, h, o = own(xw[...].astype(F32)).astype(BF), own(hw[...].astype(F32)).astype(BF), own(ow[...].astype(F32)).astype(BF)
    dq, dk, dv = whole(0), whole(1), whole(2)
    for at, (out, left, right) in enumerate(((gq, x, dq), (gk, x, dk), (gv, x, dv), (go, o, da[...]))):
        out[0] = red[at * 192 : at * 192 + 192, :].astype(F32)
        out[1] = dot_tn(left, right)
    for j in range(4):
        l = slice(j * 768, j * 768 + 768)
        gi[0, :, l] = red[768 + j * 192 : 960 + j * 192, :].astype(F32)
        gi[1, :, l] = dot_tn(h, du[j])
    g2_[0] = red[1536:2304, :].astype(F32)
    g2_[1] = dot_tn(e[...], df[...])
    lanes = pl.ds(start, 256)
    mine = own(vec[:, lanes])
    vec_s[...] = vec1[...]
    vec_s[0:1, :] = row_sum(dq.astype(F32))
    vec_s[1:2, :] = row_sum(dv.astype(F32))
    cross = own(vec_s[:, lanes])
    for r, out in enumerate((gqb, gvb, gob, gg1, gc1, gb2, gg2, gc2)):
        out[0:1, :] = mine[r : r + 1]
        out[1:2, :] = cross[r : r + 1]
    gib[0:1, :] = vec[pl.ds(8 + d, 1), :]
    gib[1:2, :] = row_sum(du[d].astype(F32))
    gemb[...] = own(emb[:, lanes])


def finish(red, vec, crossed):
    (_, _, xw, hw, ow, e, dqkv, du, da, df, vec1, emb) = crossed
    S = jax.ShapeDtypeStruct
    V = pl.BlockSpec(memory_space=pltpu.VMEM)
    square, line = S((2, 192, 768), F32), S((2, 192), F32)
    return pl.pallas_call(
        finish_kernel,
        out_shape=[
            square, line, square, square, line, square, line, line, line,
            S((2, 192, 3072), F32), S((2, 768), F32), S((2, 768, 768), F32), line, line, line, S((32, 192), F32),
        ],
        in_specs=[V] * 12,
        out_specs=[V] * 16,
        scratch_shapes=[pltpu.VMEM((8, 768), F32)],
        compiler_params=pltpu.CompilerParams(vmem_limit_bytes=48 << 20),
        name="finish_grads",
    )(red, vec, emb, xw, hw, ow, e, dqkv, du, da, df, vec1)


def fast_shards(
    inputs,
    doc_ids,
    cotangent,
    query_weight,
    query_bias,
    key_weight,
    value_weight,
    value_bias,
    out_weight,
    out_bias,
    first_gain,
    first_shift,
    inner_weight,
    inner_bias,
    outer_weight,
    outer_bias,
    second_gain,
    second_shift,
    segment_embed,
):
    weights = (query_weight, key_weight, value_weight, out_weight, inner_weight, outer_weight)
    vectors = (query_bias, value_bias, out_bias, first_gain, first_shift, inner_bias, outer_bias, second_gain, second_shift)
    gathered = gather(weights, cotangent, doc_ids, 1)
    full = [w.reshape(-1, w.shape[-1]) for w in gathered[:6]]
    windows = [w.reshape(-1, w.shape[-1]) for w in gathered[6:10]]
    cot_all, docs = gathered[10:]
    *saved, y, cls = forward(inputs[0], full, vectors)
    crossed = cross(cls, segment_embed, cot_all, docs, *windows, out_weight, outer_weight, vectors, 2)
    grad, output, packed, vec = backward(
        inputs[0], cotangent[0], crossed[1], saved, y, crossed[0], full, first_gain, second_gain
    )
    total, vec = reduce(packed, vec, 6, 3)
    return (output[None], grad[None], *finish(total, vec, crossed))


def solution(mesh):
    placed = (
        P("dp", "seg", None),
        P("dp", None),
        P("dp", "seg", None),
        P(None, "dp", None),
        P(),
        P(None, "dp", None),
        P(None, "dp", None),
        P(),
        P(None, "dp", None),
        P(),
        P(),
        P(),
        P(None, "dp", None),
        P(),
        P(None, "dp", None),
        P(),
        P(),
        P(),
        P(),
    )
    square = mesh.shape["dp"] == 4 and mesh.shape["seg"] == 8
    return jax.shard_map(
        fast_shards if square else shards,
        mesh=mesh,
        in_specs=placed,
        out_specs=(
            P("dp", "seg", None),
            P("dp", "seg", None),
            P(None, "dp", None),
            P(None, "dp"),
            P(None, "dp", None),
            P(None, "dp", None),
            P(None, "dp"),
            P(None, "dp", None),
            P(None, "dp"),
            P(None, "dp"),
            P(None, "dp"),
            P(None, "dp", None),
            P(None, "dp"),
            P(None, "dp", None),
            P(None, "dp"),
            P(None, "dp"),
            P(None, "dp"),
            P(None, "dp"),
        ),
        check_vma=False,
    )
```

```python
import functools

import jax
import jax.numpy as jnp
from jax import lax
from jax.experimental import pallas as pl
from jax.experimental.pallas import tpu as pltpu
from jax.sharding import PartitionSpec as P

HEADS = 12
HEAD_DIM = 64
SEG_LEN = 128


epsilon = 1e-05


def normalize(values, gain, shift):
    centred = values - jnp.mean(values, axis=-1, keepdims=True)
    spread = jnp.mean(centred * centred, axis=-1, keepdims=True)
    return centred * lax.rsqrt(spread + epsilon) * gain + shift


def gelu_exact(values):
    return jax.nn.gelu(values, approximate=False)


def project(values, weight):
    return jnp.einsum("gnd,de->gne", values, weight, preferred_element_type=jnp.float32)


def back_project(values, weight):
    return jnp.einsum("gne,de->gnd", values, weight, preferred_element_type=jnp.float32)


def weight_grad(source, grads):
    return jnp.einsum("gnd,gne->de", source, grads, preferred_element_type=jnp.float32)


def row_total(values):
    return jnp.sum(values.astype(jnp.float32), axis=(0, 1))


def keep_pair(first_part, second_part):
    return (first_part, second_part)


def forward_layer(params, source, allowed, spread_keys):
    (
        query_weight,
        query_bias,
        key_weight,
        value_weight,
        value_bias,
        out_weight,
        out_bias,
        first_gain,
        first_shift,
        inner_weight,
        inner_bias,
        outer_weight,
        outer_bias,
        second_gain,
        second_shift,
    ) = params
    groups, length, width = source.shape
    queries = (project(source, query_weight) + query_bias.astype(jnp.float32)).astype(jnp.bfloat16)
    key_rows = project(source, key_weight).astype(jnp.bfloat16)
    value_rows = (project(source, value_weight) + value_bias.astype(jnp.float32)).astype(
        jnp.bfloat16
    )
    key_all, value_all = spread_keys(key_rows, value_rows)
    key_length = key_all.shape[1]
    query_heads = queries.reshape(groups, length, HEADS, HEAD_DIM)
    key_heads = key_all.reshape(groups, key_length, HEADS, HEAD_DIM)
    value_heads = value_all.reshape(groups, key_length, HEADS, HEAD_DIM)
    scores = (
        jnp.einsum("gqhe,gkhe->ghqk", query_heads, key_heads, preferred_element_type=jnp.float32)
        * 0.125
    )
    if allowed is not None:
        scores = jnp.where(allowed[:, None], scores, -1e30)
    attend = jax.nn.softmax(scores, axis=-1)
    attend_low = attend.astype(jnp.bfloat16)
    mixed = jnp.einsum(
        "ghqk,gkhe->gqhe", attend_low, value_heads, preferred_element_type=jnp.float32
    )
    mixed = mixed.astype(jnp.bfloat16).reshape(groups, length, width)
    branch = project(mixed, out_weight) + out_bias.astype(jnp.float32)
    hidden, first_pull = jax.vjp(
        normalize,
        source.astype(jnp.float32) + branch,
        first_gain.astype(jnp.float32),
        first_shift.astype(jnp.float32),
    )
    hidden_low = hidden.astype(jnp.bfloat16)
    inner = project(hidden_low, inner_weight) + inner_bias.astype(jnp.float32)
    active, gelu_pull = jax.vjp(gelu_exact, inner)
    active_low = active.astype(jnp.bfloat16)
    outer = project(active_low, outer_weight) + outer_bias.astype(jnp.float32)
    result, second_pull = jax.vjp(
        normalize, hidden + outer, second_gain.astype(jnp.float32), second_shift.astype(jnp.float32)
    )
    stored = (
        source,
        query_heads,
        key_heads,
        value_heads,
        attend,
        attend_low,
        mixed,
        first_pull,
        hidden_low,
        gelu_pull,
        active_low,
        second_pull,
    )
    return (result, stored)


def backward_layer(params, stored, grad_result, collect_keys):
    (
        query_weight,
        query_bias,
        key_weight,
        value_weight,
        value_bias,
        out_weight,
        out_bias,
        first_gain,
        first_shift,
        inner_weight,
        inner_bias,
        outer_weight,
        outer_bias,
        second_gain,
        second_shift,
    ) = params
    (
        source,
        query_heads,
        key_heads,
        value_heads,
        attend,
        attend_low,
        mixed,
        first_pull,
        hidden_low,
        gelu_pull,
        active_low,
        second_pull,
    ) = stored
    groups, length, width = source.shape
    key_length = key_heads.shape[1]
    grad_second_sum, grad_second_gain, grad_second_shift = second_pull(grad_result)
    grad_outer = grad_second_sum.astype(jnp.bfloat16)
    grad_outer_bias = row_total(grad_outer)
    grad_outer_weight = weight_grad(active_low, grad_outer)
    grad_active = back_project(grad_outer, outer_weight).astype(jnp.bfloat16)
    (grad_inner,) = gelu_pull(grad_active.astype(jnp.float32))
    grad_inner_low = grad_inner.astype(jnp.bfloat16)
    grad_inner_bias = row_total(grad_inner_low)
    grad_inner_weight = weight_grad(hidden_low, grad_inner_low)
    grad_hidden = grad_second_sum + back_project(grad_inner_low, inner_weight)
    grad_first_sum, grad_first_gain, grad_first_shift = first_pull(grad_hidden)
    grad_branch = grad_first_sum.astype(jnp.bfloat16)
    grad_out_bias = row_total(grad_branch)
    grad_out_weight = weight_grad(mixed, grad_branch)
    grad_mixed = back_project(grad_branch, out_weight).astype(jnp.bfloat16)
    grad_mixed = grad_mixed.reshape(groups, length, HEADS, HEAD_DIM)
    grad_attend = jnp.einsum(
        "gqhe,gkhe->ghqk", grad_mixed, value_heads, preferred_element_type=jnp.float32
    )
    grad_attend = grad_attend.astype(jnp.bfloat16).astype(jnp.float32)
    grad_value = jnp.einsum(
        "ghqk,gqhe->gkhe", attend_low, grad_mixed, preferred_element_type=jnp.float32
    )
    grad_value = grad_value.reshape(groups, key_length, width)
    grad_scores = attend * (grad_attend - jnp.sum(attend * grad_attend, axis=-1, keepdims=True))
    grad_scores = grad_scores.astype(jnp.bfloat16)
    grad_query = (
        jnp.einsum("ghqk,gkhe->gqhe", grad_scores, key_heads, preferred_element_type=jnp.float32)
        * 0.125
    )
    grad_query = grad_query.astype(jnp.bfloat16).reshape(groups, length, width)
    grad_key = (
        jnp.einsum("ghqk,gqhe->gkhe", grad_scores, query_heads, preferred_element_type=jnp.float32)
        * 0.125
    )
    grad_key = grad_key.reshape(groups, key_length, width)
    grad_key, grad_value = collect_keys(grad_key, grad_value)
    grad_key = grad_key.astype(jnp.bfloat16)
    grad_value = grad_value.astype(jnp.bfloat16)
    grad_source = (
        grad_first_sum
        + back_project(grad_query, query_weight)
        + back_project(grad_key, key_weight)
        + back_project(grad_value, value_weight)
    )
    gradients = (
        weight_grad(source, grad_query),
        row_total(grad_query),
        weight_grad(source, grad_key),
        weight_grad(source, grad_value),
        row_total(grad_value),
        grad_out_weight,
        grad_out_bias,
        grad_first_gain,
        grad_first_shift,
        grad_inner_weight,
        grad_inner_bias,
        grad_outer_weight,
        grad_outer_bias,
        grad_second_gain,
        grad_second_shift,
    )
    return (grad_source, gradients)


def shards(
    inputs,
    doc_ids,
    cotangent,
    query_weight,
    query_bias,
    key_weight,
    value_weight,
    value_bias,
    out_weight,
    out_bias,
    first_gain,
    first_shift,
    inner_weight,
    inner_bias,
    outer_weight,
    outer_bias,
    second_gain,
    second_shift,
    segment_embed,
):
    seg_count = lax.axis_size("seg")
    seg_index = lax.axis_index("seg")
    group_rows, local_length, width = inputs.shape
    seg_local = local_length // SEG_LEN
    query_full, key_full, value_full, out_full, inner_full, outer_full = (
        lax.all_gather(query_weight, "dp", axis=1, tiled=True),
        lax.all_gather(key_weight, "dp", axis=1, tiled=True),
        lax.all_gather(value_weight, "dp", axis=1, tiled=True),
        lax.all_gather(out_weight, "dp", axis=1, tiled=True),
        lax.all_gather(inner_weight, "dp", axis=1, tiled=True),
        lax.all_gather(outer_weight, "dp", axis=1, tiled=True),
    )
    stacked = (
        query_full,
        query_bias,
        key_full,
        value_full,
        value_bias,
        out_full,
        out_bias,
        first_gain,
        first_shift,
        inner_full,
        inner_bias,
        outer_full,
        outer_bias,
        second_gain,
        second_shift,
    )
    first_params = tuple((weight[0] for weight in stacked))
    cross_params = tuple((weight[1] for weight in stacked))
    pieces = inputs.reshape(group_rows * seg_local, SEG_LEN, width)
    segment_out, segment_stored = forward_layer(first_params, pieces, None, keep_pair)
    segment_grid = segment_out.reshape(group_rows, seg_local, SEG_LEN, width)
    position = lax.dynamic_slice_in_dim(segment_embed, seg_index * seg_local, seg_local, 0).astype(
        jnp.float32
    )
    heads_in = (segment_grid[:, :, 0, :] + position).astype(jnp.bfloat16)
    row_input = lax.all_gather(heads_in, "seg", axis=1, tiled=True)
    allowed = doc_ids[:, :, None] == doc_ids[:, None, :]
    cross_out, cross_stored = forward_layer(cross_params, row_input, allowed, keep_pair)
    returned = lax.dynamic_slice_in_dim(cross_out, seg_index * seg_local, seg_local, 1).astype(
        jnp.bfloat16
    )
    output = jnp.concatenate(
        [returned[:, :, None, :], segment_grid[:, :, 1:, :].astype(jnp.bfloat16)], axis=2
    )
    output = output.reshape(group_rows, local_length, width)
    cot_grid = cotangent.reshape(group_rows, seg_local, SEG_LEN, width)
    cot_heads = cot_grid[:, :, 0, :]
    grad_cross = lax.all_gather(cot_heads, "seg", axis=1, tiled=True)
    grad_row_input, cross_grads = backward_layer(
        cross_params, cross_stored, grad_cross.astype(jnp.float32), keep_pair
    )
    grad_row_low = grad_row_input.astype(jnp.bfloat16)
    factor = 1.0 / seg_count
    embed_grad = jnp.sum(grad_row_low.astype(jnp.float32), axis=0) * factor
    cross_grads = tuple((part * factor for part in cross_grads))
    grad_heads = lax.dynamic_slice_in_dim(grad_row_low, seg_index * seg_local, seg_local, 1)
    grad_grid = jnp.concatenate(
        [grad_heads[:, :, None, :].astype(jnp.float32), cot_grid[:, :, 1:, :].astype(jnp.float32)],
        axis=2,
    )
    grad_grid = grad_grid.reshape(group_rows * seg_local, SEG_LEN, width)
    grad_pieces, segment_grads = backward_layer(first_params, segment_stored, grad_grid, keep_pair)
    input_grad = grad_pieces.astype(jnp.bfloat16).reshape(group_rows, local_length, width)
    shares = (
        lax.psum_scatter(segment_grads[0], "dp", scatter_dimension=0, tiled=True),
        lax.psum_scatter(segment_grads[1], "dp", scatter_dimension=0, tiled=True),
        lax.psum_scatter(segment_grads[2], "dp", scatter_dimension=0, tiled=True),
        lax.psum_scatter(segment_grads[3], "dp", scatter_dimension=0, tiled=True),
        lax.psum_scatter(segment_grads[4], "dp", scatter_dimension=0, tiled=True),
        lax.psum_scatter(segment_grads[5], "dp", scatter_dimension=0, tiled=True),
        lax.psum_scatter(segment_grads[6], "dp", scatter_dimension=0, tiled=True),
        lax.psum_scatter(segment_grads[7], "dp", scatter_dimension=0, tiled=True),
        lax.psum_scatter(segment_grads[8], "dp", scatter_dimension=0, tiled=True),
        lax.psum_scatter(segment_grads[9], "dp", scatter_dimension=0, tiled=True),
        lax.psum_scatter(segment_grads[10], "dp", scatter_dimension=0, tiled=True),
        lax.psum_scatter(segment_grads[11], "dp", scatter_dimension=0, tiled=True),
        lax.psum_scatter(segment_grads[12], "dp", scatter_dimension=0, tiled=True),
        lax.psum_scatter(segment_grads[13], "dp", scatter_dimension=0, tiled=True),
        lax.psum_scatter(segment_grads[14], "dp", scatter_dimension=0, tiled=True),
        lax.psum_scatter(cross_grads[0], "dp", scatter_dimension=0, tiled=True),
        lax.psum_scatter(cross_grads[1], "dp", scatter_dimension=0, tiled=True),
        lax.psum_scatter(cross_grads[2], "dp", scatter_dimension=0, tiled=True),
        lax.psum_scatter(cross_grads[3], "dp", scatter_dimension=0, tiled=True),
        lax.psum_scatter(cross_grads[4], "dp", scatter_dimension=0, tiled=True),
        lax.psum_scatter(cross_grads[5], "dp", scatter_dimension=0, tiled=True),
        lax.psum_scatter(cross_grads[6], "dp", scatter_dimension=0, tiled=True),
        lax.psum_scatter(cross_grads[7], "dp", scatter_dimension=0, tiled=True),
        lax.psum_scatter(cross_grads[8], "dp", scatter_dimension=0, tiled=True),
        lax.psum_scatter(cross_grads[9], "dp", scatter_dimension=0, tiled=True),
        lax.psum_scatter(cross_grads[10], "dp", scatter_dimension=0, tiled=True),
        lax.psum_scatter(cross_grads[11], "dp", scatter_dimension=0, tiled=True),
        lax.psum_scatter(cross_grads[12], "dp", scatter_dimension=0, tiled=True),
        lax.psum_scatter(cross_grads[13], "dp", scatter_dimension=0, tiled=True),
        lax.psum_scatter(cross_grads[14], "dp", scatter_dimension=0, tiled=True),
        lax.psum_scatter(embed_grad, "dp", scatter_dimension=1, tiled=True),
    )
    summed = lax.psum(
        (
            shares[0],
            shares[1],
            shares[2],
            shares[3],
            shares[4],
            shares[5],
            shares[6],
            shares[7],
            shares[8],
            shares[9],
            shares[10],
            shares[11],
            shares[12],
            shares[13],
            shares[14],
            shares[15],
            shares[16],
            shares[17],
            shares[18],
            shares[19],
            shares[20],
            shares[21],
            shares[22],
            shares[23],
            shares[24],
            shares[25],
            shares[26],
            shares[27],
            shares[28],
            shares[29],
            shares[30],
        ),
        "seg",
    )
    totals = tuple((jnp.stack([summed[index], summed[index + 15]]) for index in range(15)))
    totals = totals + (summed[30],)
    return (output, input_grad) + tuple(totals)


MESH = pl.DeviceIdType.MESH
ANY = pl.BlockSpec(memory_space=pl.ANY)
BF = jnp.bfloat16
F32 = jnp.float32


def place():
    d = lax.axis_index("dp")
    s = lax.axis_index("seg")
    return d, s


def greet(peers):
    barrier = pltpu.get_barrier_semaphore()
    for peer in peers:
        pl.semaphore_signal(barrier, inc=1, device_id=peer, device_id_type=MESH)
    pl.semaphore_wait(barrier, len(peers))


def remote(src, dst, send, recv, peer):
    return pltpu.make_async_remote_copy(
        src_ref=src, dst_ref=dst, send_sem=send, recv_sem=recv, device_id=peer, device_id_type=MESH
    )


def plane_peers(d, s):
    c = s % 2
    x, y = d % 2, d // 2
    dx = 2 * y + 1 - x
    dy = 2 * (1 - y) + x
    first = dx * (1 - c) + dy * c
    second = dy * (1 - c) + dx * c
    return c, first, second, s + 1 - 2 * c


def window(d):
    return pl.multiple_of((3 * d) // 2 * 128, 128), d % 2 * 64


def everyone(d, s):
    me = d * 8 + s
    ahead = [lax.rem(me + j, 32) for j in range(1, 32)]
    behind = [lax.rem(me + 32 - j, 32) for j in range(1, 32)]
    return me, ahead, behind


def start_kernel(pieces, *refs):
    x, (qb, vb, ob, g1, c1, ib, b2, g2, c2), refs = refs[0], refs[1:10], refs[10:]
    shards, (cot, docs), refs = refs[:6], refs[6:8], refs[8:]
    fulls, wins, (cot_all, docs_all), refs = refs[:6], refs[6:10], refs[10:12], refs[12:]
    saved_o, y_o, cls_o, refs = refs[:12], refs[12], refs[13], refs[14:]
    full, wbounce, (first_rows, heads, ids), refs = refs[:6], refs[6:10], refs[10:13], refs[13:]
    (q_s, k_s, v_s, p_s, o_s, h_s, e_s, gp_s, x1, r1, x2, r2), y_s, refs = refs[:12], refs[12], refs[13:]
    load_sem, link_send, link_recv, core_send, core_recv, wload_sem, store_sem, refs = *refs[:7], refs[7:]
    win_send, win_recv, wcore_send, wcore_recv, row_sem, all_send, all_recv, ids_send, ids_recv, full_sem, out_sem = refs
    vq, vk, vv, vo, vi, v2 = full
    d, s = place()
    c = s % 2
    z = s // 2
    xx, yy = d % 2, d // 2
    dx, dy, dd = 2 * yy + 1 - xx, 2 * (1 - yy) + xx, 3 - d
    other = s + 1 - 2 * c
    even = 1 - z % 2
    xpeer, ypeer, zpeer = (dx, s), (dy, s), (d, s + 4 * even - 2)

    def either(a, b):
        return a * even + b * (1 - even)

    me, ahead, behind = everyone(d, s)
    segs = first_rows.shape[0]
    count = len(pieces)
    loads = [
        pltpu.make_async_copy(shards[i].at[0], full[i].at[pl.ds(pl.multiple_of(d * shards[i].shape[1], 64), shards[i].shape[1])], load_sem.at[i])
        for i in range(6)
    ]
    for cp in loads:
        cp.start()
    row_loads = [pltpu.make_async_copy(cot.at[0, pl.ds(i * 128, 8)], first_rows.at[i], row_sem.at[i]) for i in range(segs)]
    row_loads.append(pltpu.make_async_copy(docs, ids, row_sem.at[segs]))
    for cp in row_loads:
        cp.start()
    origins = (shards[0], shards[1], shards[2], shards[4])
    wloads = []
    for w in range(4):
        width = wins[w].shape[-1]
        at = window(d)[0] if w < 3 else d * width
        cp = pltpu.make_async_copy(origins[w].at[1, :, pl.ds(pl.multiple_of(at, 128), width)], wbounce[w], wload_sem.at[w])
        cp.start()
        wloads.append(cp)
    greet([(i // 8, i % 8) for i in ahead])

    def cols(ref):
        half = ref.shape[-1] // 2
        return pl.ds(pl.multiple_of(c * half, half), half)

    def mine(p, h):
        i, r0, rn = pieces[p]
        return shards[i].at[0, pl.ds(r0 + h * (rn // 2), rn // 2), cols(shards[i])]

    def slot(p, src, h):
        i, r0, rn = pieces[p]
        at = src * shards[i].shape[1] + r0 + h * (rn // 2)
        return full[i].at[pl.ds(pl.multiple_of(at, 16), rn // 2), cols(full[i])]

    started, shared, stores = [], [], []

    def link(kind, p, src, dst, peer):
        return remote(src, dst, link_send.at[kind, p], link_recv.at[kind, p], peer)

    def go(cp):
        cp.start()
        started.append(cp)

    def arrived(kind, p, ref):
        link(kind, p, ref, ref, zpeer).wait_recv()
        cp = remote(ref, ref, core_send.at[kind, p], core_recv.at[kind, p], (d, other))
        cp.start()
        shared.append((pieces[p][0], cp))
        started.append(cp)

    def own(p):
        if p < count:
            go(link(0, p, mine(p, 1), slot(p, d, 1), xpeer))
            go(link(1, p, mine(p, 0), slot(p, d, 0), ypeer))

    loaded = set()

    def step(p):
        own(p + 3)
        if p < count:
            i = pieces[p][0]
            if i not in loaded:
                loads[i].wait()
                loaded.add(i)
            arrived(0, p, slot(p, dx, 1))
            arrived(1, p, slot(p, dy, 0))
            ref = slot(p, either(d, dy), 0)
            go(link(2, p, ref, ref, xpeer))
            ref = slot(p, either(d, dx), 1)
            go(link(3, p, ref, ref, ypeer))
        if 0 <= p - 1 < count:
            for kind, src, h in ((2, either(dx, dd), 0), (3, either(dy, dd), 1)):
                ref = slot(p - 1, src, h)
                arrived(kind, p - 1, ref)
                go(link(kind + 2, p - 1, ref, ref, zpeer))
        if 0 <= p - 2 < count:
            arrived(4, p - 2, slot(p - 2, either(dd, dx), 0))
            arrived(5, p - 2, slot(p - 2, either(dd, dy), 1))

    ready = set()

    def whole(i):
        for j, cp in shared:
            if j == i:
                cp.wait_recv()
        assert i not in ready
        ready.add(i)
        cp = pltpu.make_async_copy(full[i], fulls[i], full_sem.at[i])
        cp.start()
        stores.append(cp)

    def save(n, ref):
        cp = pltpu.make_async_copy(ref, y_o if n == 12 else saved_o[n], out_sem.at[n])
        cp.start()
        stores.append(cp)

    rows, width = x.shape
    nt = width // TILE
    for p in range(3):
        own(p)
    at = 0

    def advance(upto):
        nonlocal at
        while at < min(upto, count + 2):
            step(at)
            at += 1

    last = {i: max(p for p in range(count) if pieces[p][0] == i) for i in range(6)}
    advance(last[2] + 3)
    for i in range(3):
        whole(i)

    for t in range(nt):
        lanes = slice(t * TILE, t * TILE + TILE)
        q_s[:, lanes] = (dot(x[...], vq[:, lanes]) + qb[0:1, lanes].astype(F32)).astype(BF)
        k_s[:, lanes] = dot(x[...], vk[:, lanes]).astype(BF)
        v_s[:, lanes] = (dot(x[...], vv[:, lanes]) + vb[0:1, lanes].astype(F32)).astype(BF)
    for n, ref in enumerate((q_s, k_s, v_s)):
        save(n, ref)
    advance(last[2] + 4)
    masks = head_masks()

    def attend(hp, carry):
        lanes = tiles(hp, 128)
        for s in range(segs):
            here = slice(s * 128, s * 128 + 128)
            qs, ks, vs = q_s[here, lanes], k_s[here, lanes], v_s[here, lanes]
            mixed = None
            for h in range(2):
                scores = dot_nt(qs * masks[h], ks)
                top = jnp.max(scores, axis=-1, keepdims=True)
                weight = jnp.exp((scores - top) * 0.125)
                share = (weight * (1.0 / jnp.sum(weight, axis=-1, keepdims=True))).astype(BF)
                p_s[hp, s, h] = share
                part = dot(share, vs * masks[h])
                mixed = part if mixed is None else mixed + part
            o_s[here, lanes] = mixed.astype(BF)
        return carry

    pairs = width // 128
    for g in range(pairs // 2):
        lax.fori_loop(2 * g, 2 * g + 2, attend, 0)
        advance(last[3] + 4 + g)
    save(3, p_s)
    save(4, o_s)
    whole(3)

    def out(t, carry):
        lanes = tiles(t)
        x1[:, lanes] = dot(o_s[...], vo[:, lanes]) + ob[0:1, lanes].astype(F32) + x[:, lanes].astype(F32)
        return carry

    lax.fori_loop(0, nt, out, 0)

    def first(i, carry):
        r = tiles(i, 64)
        xhat, rstd = standard(x1[r, :])
        x1[r, :] = xhat
        r1[r, :] = jnp.broadcast_to(rstd, (64, 128))
        hidden = xhat * g1[0:1, :].astype(F32) + c1[0:1, :].astype(F32)
        h_s[r, :] = hidden.astype(BF)
        x2[r, :] = hidden + b2[0:1, :].astype(F32)
        return carry

    lax.fori_loop(0, rows // 64, first, 0)
    for n, ref in ((5, h_s), (8, x1), (9, r1)):
        save(n, ref)
    advance(last[4] + 3)
    whole(4)

    def ffn(t, carry):
        lanes = tiles(t)
        u = dot(h_s[...], vi[:, lanes]) + ib[0:1, lanes].astype(F32)
        e, gp = gelu_parts(u)
        e_s[:, lanes] = e.astype(BF)
        gp_s[:, lanes] = gp.astype(BF)
        return carry

    groups = vi.shape[1] // TILE // 2
    far = (dd, dx, dy)
    for g in range(groups):
        lax.fori_loop(2 * g, 2 * g + 2, ffn, 0)
        advance(last[4] + 4 + g)
    advance(count + 2)
    heads_small(row_loads, first_rows, heads, segs)

    def columns(w, dev, core):
        wide = wins[w].shape[-1]
        begin = window(dev)[0] if w < 3 else dev * wide
        return pl.ds(pl.multiple_of(begin + core * (wide // 2), 128), wide // 2)

    for k, peer in enumerate(far):
        for w in range(4):
            go(remote(
                origins[w].at[1, :, columns(w, peer, c)], wins[w].at[d, :, cols(wins[w])],
                win_send.at[k, w], win_recv.at[k, w], (peer, s),
            ))
        go(remote(ids, docs_all.at[d], ids_send.at[k], ids_recv.at[k], (peer, s)))
    for j, i in enumerate(ahead):
        go(remote(heads, cot_all.at[me], all_send.at[j], all_recv.at[j], (i // 8, i % 8)))
    for w in range(4):
        wloads[w].wait()
        cp = pltpu.make_async_copy(wbounce[w], wins[w].at[d], store_sem.at[w])
        cp.start()
        stores.append(cp)
    for src, dst, i in ((heads, cot_all.at[me], 4), (ids, docs_all.at[d], 5)):
        cp = pltpu.make_async_copy(src, dst, store_sem.at[i])
        cp.start()
        stores.append(cp)
    save(6, e_s)
    save(7, gp_s)
    whole(5)

    def outer(t, carry):
        lanes = tiles(t)
        x2[:, lanes] += dot(e_s[...], v2[:, lanes])
        return carry

    lax.fori_loop(0, nt, outer, 0)

    def second(i, carry):
        r = tiles(i, 64)
        xhat, rstd = standard(x2[r, :])
        x2[r, :] = xhat
        r2[r, :] = jnp.broadcast_to(rstd, (64, 128))
        y_s[r, :] = (xhat * g2[0:1, :].astype(F32) + c2[0:1, :].astype(F32)).astype(BF)
        return carry

    lax.fori_loop(0, rows // 64, second, 0)
    for n, ref in ((10, x2), (11, r2), (12, y_s)):
        save(n, ref)
    for s_ in range(segs):
        cls_o[s_ : s_ + 1, :] = x2[s_ * 128 : s_ * 128 + 1, :] * g2[0:1, :].astype(F32) + c2[0:1, :].astype(F32)
    wcores = []
    for k, peer in enumerate(far):
        for w in range(4):
            got = wins[w].at[peer, :, cols(wins[w])]
            remote(got, got, win_send.at[k, w], win_recv.at[k, w], (peer, s)).wait_recv()
            cp = remote(got, got, wcore_send.at[k, w], wcore_recv.at[k, w], (d, other))
            cp.start()
            wcores.append(cp)
        remote(ids, docs_all.at[peer], ids_send.at[k], ids_recv.at[k], (peer, s)).wait_recv()
    for j, i in enumerate(behind):
        remote(heads, cot_all.at[i], all_send.at[j], all_recv.at[j], (i // 8, i % 8)).wait_recv()
    for cp in started:
        cp.wait_send()
    for cp in wcores:
        cp.wait()
    for cp in stores:
        cp.wait()


def heads_small(row_loads, first_rows, heads, segs):
    for cp in row_loads:
        cp.wait()
    heads[...] = jnp.concatenate([first_rows[i].astype(F32)[0:1] for i in range(segs)], axis=0).astype(BF)


def start(x, shards, cot, docs, vectors, collective_id):
    cuts = (2, 2, 2, 1, 3, 4)
    pieces = []
    for i, w in enumerate(shards):
        n = w.shape[1] // cuts[i]
        pieces += [(i, p * n, n) for p in range(cuts[i])]
    count = len(pieces)
    S, VM, dma = jax.ShapeDtypeStruct, pltpu.VMEM, pltpu.SemaphoreType.DMA
    V = pl.BlockSpec(memory_space=pltpu.VMEM)
    part, width = shards[0].shape[1:]
    rows = x.shape[0]
    ff = shards[4].shape[2]
    segs = rows // 128
    wins = [(part, 256)] * 3 + [(part, ff // 4)]
    low, full, wide, col = ((rows, width), BF), ((rows, width), F32), ((rows, ff), BF), ((rows, 128), F32)
    saved = [low, low, low, ((width // 128, segs, 2, 128, 128), BF), low, low, wide, wide, full, col, full, col, low]
    outs = pl.pallas_call(
        functools.partial(start_kernel, pieces),
        out_shape=[S((4 * w.shape[1], w.shape[2]), w.dtype) for w in shards]
        + [S((4,) + w, BF) for w in wins]
        + [S((32, segs, width), BF), S((4,) + docs.shape, docs.dtype)]
        + [S(*t) for t in saved]
        + [S((segs, width), F32)],
        in_specs=[V] * 10 + [ANY] * 8,
        out_specs=[ANY] * 25 + [V],
        scratch_shapes=[VM((4 * w.shape[1], w.shape[2]), w.dtype) for w in shards]
        + [VM(w, BF) for w in wins]
        + [VM((segs, 8, width), BF), VM((segs, width), BF), VM(docs.shape, docs.dtype)]
        + [VM(*t) for t in saved]
        + [dma((6,)), dma((6, count)), dma((6, count)), dma((6, count)), dma((6, count)), dma((4,)), dma((6,))]
        + [dma((3, 4)), dma((3, 4)), dma((3, 4)), dma((3, 4)), dma((segs + 1,)), dma((31,)), dma((31,)), dma((3,)), dma((3,)), dma((6,)), dma((13,))],
        compiler_params=pltpu.CompilerParams(collective_id=collective_id, has_side_effects=True, vmem_limit_bytes=67043328),
        name="gather_forward",
    )(x, *vectors, *shards, cot, docs)
    return outs[:6], outs[6:10], outs[10], outs[11], outs[12:24], outs[24], outs[25]


def add_into(dst, a, b, rows):
    step = 48

    def body(i, carry):
        r = pl.ds(pl.multiple_of(i * step, 16), step)
        dst[r, :] = (a[r, :].astype(F32) + b[r, :].astype(F32)).astype(dst.dtype)
        return carry

    lax.fori_loop(0, rows // step, body, 0)


def reduce_kernel(nc, r, g, vec, out, vec_out, own, recv0, recv1, recv2, recv3, recv4, fin, load_sem, out_sem,
                  send0, rcv0, send1, rcv1, send2, rcv2, send3, rcv3, send4, rcv4, send5, rcv5, send6, rcv6, send7, rcv7, vsum, vgot, vsend, vrcv):
    d, s = place()
    c, first, second, other = plane_peers(d, s)
    x, y = d % 2, d // 2
    a = x * (1 - c) + y * c
    b = y * (1 - c) + x * c
    z = s // 2
    z0, z1 = z % 2, z // 2
    znear = (z + 1 - 2 * z0) * 2 + c
    zfar = (z + 2 - 4 * z1) * 2 + c
    h, q = r // 2, r // 4
    greet([(first, s), (second, s), (d, other), (d, znear), (d, zfar)])

    def quarter(aa, bb):
        return aa * (1 + c) + bb * (2 - c)

    def rows(core, k):
        return pl.ds(pl.multiple_of(core * (nc * r) + k * r, 16), r)

    started = []

    def go(cp):
        cp.start()
        started.append(cp)

    loads = []
    for k in range(nc):
        go(remote(g.at[:, rows(1 - c, k), :], recv0.at[k], send0.at[k], rcv0.at[k], (d, other)))
        cp = pltpu.make_async_copy(g.at[:, rows(c, k), :], own.at[k], load_sem.at[k])
        cp.start()
        loads.append(cp)

    def arrived(ref, sem):
        pltpu.make_async_copy(ref, ref, sem).wait()

    def piece(k, i0, i1):
        return fin.at[c, k, pl.ds(pl.multiple_of(i0 * h + i1 * q, 16), q), :]

    outs = []

    def stage(t, k):
        if t == 1:
            arrived(recv0.at[k], rcv0.at[k])
            loads[k].wait()
            for bb in range(2):
                away = quarter(1 - a, bb)
                add_into(own.at[k, away], own.at[k, away], recv0.at[k, away], r)
                go(remote(own.at[k, away], recv1.at[k, bb], send1.at[k, bb], rcv1.at[k, bb], (first, s)))
            for bb in range(2):
                keep = quarter(a, bb)
                add_into(own.at[k, keep], own.at[k, keep], recv0.at[k, keep], r)
        elif t == 2:
            for bb in range(2):
                arrived(recv1.at[k, bb], rcv1.at[k, bb])
            away, keep = quarter(a, 1 - b), quarter(a, b)
            add_into(own.at[k, away], own.at[k, away], recv1.at[k, 1 - b], r)
            go(remote(own.at[k, away], recv2.at[k], send2.at[k], rcv2.at[k], (second, s)))
            add_into(own.at[k, keep], own.at[k, keep], recv1.at[k, b], r)
        elif t == 3:
            arrived(recv2.at[k], rcv2.at[k])
            keep = quarter(a, b)
            away = pl.ds(pl.multiple_of((1 - z0) * h, 16), h)
            mine = pl.ds(pl.multiple_of(z0 * h, 16), h)
            add_into(own.at[k, keep, away], own.at[k, keep, away], recv2.at[k, away], h)
            go(remote(own.at[k, keep, away], recv3.at[k], send3.at[k], rcv3.at[k], (d, znear)))
            add_into(own.at[k, keep, mine], own.at[k, keep, mine], recv2.at[k, mine], h)
        elif t == 4:
            arrived(recv3.at[k], rcv3.at[k])
            keep = quarter(a, b)
            away = pl.ds(pl.multiple_of(z0 * h + (1 - z1) * q, 16), q)
            mine = pl.ds(pl.multiple_of(z0 * h + z1 * q, 16), q)
            raway = pl.ds(pl.multiple_of((1 - z1) * q, 16), q)
            rmine = pl.ds(pl.multiple_of(z1 * q, 16), q)
            add_into(own.at[k, keep, away], own.at[k, keep, away], recv3.at[k, raway], q)
            go(remote(own.at[k, keep, away], recv4.at[k], send4.at[k], rcv4.at[k], (d, zfar)))
            add_into(own.at[k, keep, mine], own.at[k, keep, mine], recv3.at[k, rmine], q)
        elif t == 5:
            arrived(recv4.at[k], rcv4.at[k])
            keep = quarter(a, b)
            mine = pl.ds(pl.multiple_of(z0 * h + z1 * q, 16), q)
            add_into(piece(k, z0, z1), own.at[k, keep, mine], recv4.at[k], q)
            go(remote(piece(k, z0, z1), piece(k, z0, z1), send5.at[k], rcv5.at[k], (d, zfar)))
        elif t == 6:
            arrived(piece(k, z0, 1 - z1), rcv5.at[k])
            half = fin.at[c, k, pl.ds(pl.multiple_of(z0 * h, 16), h), :]
            go(remote(half, half, send6.at[k], rcv6.at[k], (d, znear)))
        elif t == 7:
            half = fin.at[c, k, pl.ds(pl.multiple_of((1 - z0) * h, 16), h), :]
            arrived(half, rcv6.at[k])
            go(remote(fin.at[c, k], fin.at[c, k], send7.at[k], rcv7.at[k], (d, other)))
            cp = pltpu.make_async_copy(fin.at[c, k], out.at[rows(c, k), :], out_sem.at[0, k])
            cp.start()
            outs.append(cp)
        elif t == 8:
            arrived(fin.at[1 - c, k], rcv7.at[k])
            cp = pltpu.make_async_copy(fin.at[1 - c, k], out.at[rows(1 - c, k), :], out_sem.at[1, k])
            cp.start()
            outs.append(cp)

    hops = [(d, other), (first, s), (second, s), (d, znear), (d, zfar)]
    vsum[0] = vec[...]

    def vector_hop(j):
        if j > 0:
            arrived(vgot.at[j - 1], vrcv.at[j - 1])
            vsum[j] = vsum[j - 1] + vgot[j - 1]
        if j < 5:
            go(remote(vsum.at[j], vgot.at[j], vsend.at[j], vrcv.at[j], hops[j]))

    for slot in range(nc + 8):
        for t in range(8, 0, -1):
            k = slot - (t - 1)
            if 0 <= k < nc:
                stage(t, k)
        if slot < 6:
            vector_hop(slot)
    vec_out[...] = vsum[5]
    for cp in started:
        cp.wait_send()
    for cp in outs:
        cp.wait()


def reduce(g, vec, nc, collective_id):
    _, total, width = g.shape
    r = total // 2 // nc
    dma = pltpu.SemaphoreType.DMA
    return pl.pallas_call(
        functools.partial(reduce_kernel, nc, r),
        out_shape=[jax.ShapeDtypeStruct((total, width), g.dtype), jax.ShapeDtypeStruct(vec.shape, vec.dtype)],
        in_specs=[ANY, pl.BlockSpec(memory_space=pltpu.VMEM)],
        out_specs=[ANY, pl.BlockSpec(memory_space=pltpu.VMEM)],
        scratch_shapes=[
            pltpu.VMEM((nc, 4, r, width), g.dtype),
            pltpu.VMEM((nc, 4, r, width), g.dtype),
            pltpu.VMEM((nc, 2, r, width), g.dtype),
            pltpu.VMEM((nc, r, width), g.dtype),
            pltpu.VMEM((nc, r // 2, width), g.dtype),
            pltpu.VMEM((nc, r // 4, width), g.dtype),
            pltpu.VMEM((2, nc, r, width), g.dtype),
            dma((nc,)),
            dma((2, nc)),
            dma((nc,)), dma((nc,)),
            dma((nc, 2)), dma((nc, 2)),
            dma((nc,)), dma((nc,)),
            dma((nc,)), dma((nc,)),
            dma((nc,)), dma((nc,)),
            dma((nc,)), dma((nc,)),
            dma((nc,)), dma((nc,)),
            dma((nc,)), dma((nc,)),
            pltpu.VMEM((6,) + vec.shape, vec.dtype),
            pltpu.VMEM((5,) + vec.shape, vec.dtype),
            dma((5,)), dma((5,)),
        ],
        compiler_params=pltpu.CompilerParams(collective_id=collective_id, has_side_effects=True, vmem_limit_bytes=67043328),
        name="reduce_grads",
    )(g, vec)


TILE = 256


def dot(a, b):
    return lax.dot_general(a, b, (((1,), (0,)), ((), ())), preferred_element_type=F32)


def dot_nt(a, b):
    return lax.dot_general(a, b, (((1,), (1,)), ((), ())), preferred_element_type=F32)


def dot_tn(a, b):
    return lax.dot_general(a, b, (((0,), (0,)), ((), ())), preferred_element_type=F32)


def tiles(i, size=TILE):
    return pl.ds(pl.multiple_of(i * size, size), size)


def standard(r):
    centred = r - jnp.mean(r, axis=-1, keepdims=True)
    rstd = lax.rsqrt(jnp.mean(centred * centred, axis=-1, keepdims=True) + epsilon)
    return centred * rstd, rstd


def standard_back(grad, xhat, rstd):
    return rstd * (
        grad
        - jnp.mean(grad, axis=-1, keepdims=True)
        - xhat * jnp.mean(grad * xhat, axis=-1, keepdims=True)
    )


def gelu_parts(u):
    phi = 0.5 * (1.0 + lax.erf(u * 0.7071067811865476))
    return u * phi, phi + u * (0.3989422804014327 * jnp.exp(-0.5 * u * u))


def head_masks():
    lane = lax.broadcasted_iota(jnp.int32, (1, 128), 1)
    low = (lane < 64).astype(F32)
    return (low.astype(BF), (1.0 - low).astype(BF))


def row_sum(v):
    return jnp.sum(v, axis=0, keepdims=True)


def backward_kernel(x, cot, dcl, q, k, v, p, o, hb, e, gp, x1, r1, x2, r2, y, z, wq, wk, wv, wo, wi, w2, g1, g2,
                    dx_o, y_o, g_o, vec_o,
                    vq, vk, vv, vo, vi, v2, e_s, gp_s, p_s, gs, dr2, acc, df, ht, da, do, dq, dk, dv, in_sem, out_sem):
    loads = [
        pltpu.make_async_copy(src, dst, in_sem.at[i])
        for i, (src, dst) in enumerate(
            ((w2, v2), (e, e_s), (gp, gp_s), (wi, vi), (wo, vo), (p, p_s), (wq, vq), (wk, vk), (wv, vv))
        )
    ]
    for cp in loads:
        cp.start()
    rows, width = x.shape
    segs, nt = rows // 128, width // TILE
    ff = vi.shape[1]
    share = width // 4
    vec_o[...] = jnp.zeros_like(vec_o)

    def second(i, carry):
        gain_sum, shift_sum, bias_sum = carry
        r = tiles(i, 64)
        dy, out = cot[r, :].astype(F32), y[r, :].astype(F32)
        at = lax.broadcasted_iota(jnp.int32, (64, 1), 0) + i * 64
        for s in range(segs):
            dy = jnp.where(at == s * 128, dcl[s : s + 1, :], dy)
            out = jnp.where(at == s * 128, z[s : s + 1, :], out)
        y_o[r, :] = out.astype(BF)
        xhat = x2[r, :]
        back = standard_back(dy * g2[0:1, :].astype(F32), xhat, r2[r, 0:1])
        dr2[r, :] = back
        low = back.astype(BF)
        df[r, :] = low
        return (gain_sum + row_sum(dy * xhat), shift_sum + row_sum(dy), bias_sum + row_sum(low.astype(F32)))

    zero = jnp.zeros((1, width), F32)
    sums = lax.fori_loop(0, rows // 64, second, (zero, zero, zero))
    vec_o[6:7, :], vec_o[7:8, :], vec_o[5:6, :] = sums
    ht[...] = hb[...].T
    acc[...] = dr2[...]
    for i in range(4):
        loads[i].wait()

    def ffn(t, carry):
        wide = tiles(t)
        block, lanes = t // nt, tiles(t % nt)
        de = dot_nt(df[...], v2[wide, :]).astype(BF).astype(F32)
        du = (de * gp_s[:, wide].astype(F32)).astype(BF)
        vec_o[pl.ds(8 + block, 1), lanes] = row_sum(du.astype(F32))
        back = dot_tn(e_s[:, wide], df[...])
        gs[block, pl.ds(pl.multiple_of(8 * share + (t % nt) * TILE, TILE), TILE), :] = back.astype(BF)
        inner = dot(ht[...], du).astype(BF)
        for d in range(4):
            gs[d, pl.ds(pl.multiple_of(4 * share + block * share, 64), share), lanes] = inner[d * share : d * share + share]
        acc[...] += dot_nt(du, vi[:, wide])
        return carry

    lax.fori_loop(0, ff // TILE, ffn, 0)
    half = 4 * share
    copies = [pltpu.make_async_copy(gs.at[:, half:, :], g_o.at[:, half:, :], out_sem.at[0])]
    copies[0].start()

    def first(i, carry):
        gain_sum, shift_sum, bias_sum = carry
        r = tiles(i, 64)
        dh = acc[r, :]
        xhat = x1[r, :]
        back = standard_back(dh * g1[0:1, :].astype(F32), xhat, r1[r, 0:1])
        dr2[r, :] = back
        low = back.astype(BF)
        da[r, :] = low
        return (gain_sum + row_sum(dh * xhat), shift_sum + row_sum(dh), bias_sum + row_sum(low.astype(F32)))

    sums = lax.fori_loop(0, rows // 64, first, (zero, zero, zero))
    vec_o[3:4, :], vec_o[4:5, :], vec_o[2:3, :] = sums
    loads[4].wait()
    do[...] = dot_nt(da[...], vo[...]).astype(BF)

    def spread(at, lhs, rhs):
        back = dot_tn(lhs, rhs).astype(BF)
        for d in range(4):
            gs[d, at * share : at * share + share, :] = back[d * share : d * share + share]

    spread(3, o[...], da[...])
    loads[5].wait()
    masks = head_masks()

    def attend(hp, carry):
        lanes = tiles(hp, 128)
        for s in range(segs):
            here = slice(s * 128, s * 128 + 128)
            qs, ks, vs, dos = q[here, lanes], k[here, lanes], v[here, lanes], do[here, lanes]
            dqs = dks = dvs = 0.0
            for h in range(2):
                pl_ = p_s[hp, s, h]
                pf = pl_.astype(F32)
                dom = dos * masks[h]
                dp = dot_nt(dom, vs).astype(BF).astype(F32)
                ds = (pf * (dp - jnp.sum(pf * dp, axis=-1, keepdims=True))).astype(BF)
                dqs += dot(ds, ks * masks[h])
                dks += dot_tn(ds, qs * masks[h])
                dvs += dot_tn(pl_, dom)
            dq[here, lanes] = (dqs * 0.125).astype(BF)
            dk[here, lanes] = (dks * 0.125).astype(BF)
            dv[here, lanes] = dvs.astype(BF)
        return carry

    lax.fori_loop(0, width // 128, attend, 0)
    vec_o[0:1, :] = row_sum(dq[...].astype(F32))
    vec_o[1:2, :] = row_sum(dv[...].astype(F32))
    ht[...] = x[...].T
    for i in range(6, 9):
        loads[i].wait()

    def weights(at, rhs):
        back = dot(ht[...], rhs[...]).astype(BF)
        for d in range(4):
            gs[d, at * share : at * share + share, :] = back[d * share : d * share + share]

    weights(0, dq)
    weights(1, dk)
    weights(2, dv)
    copies.append(pltpu.make_async_copy(gs.at[:, :half, :], g_o.at[:, :half, :], out_sem.at[1]))
    copies[1].start()

    def source(t, carry):
        r = tiles(t)
        dx = dr2[:, r] + dot_nt(dq[...], vq[r, :]) + dot_nt(dk[...], vk[r, :]) + dot_nt(dv[...], vv[r, :])
        dx_o[:, r] = dx.astype(BF)
        return carry

    lax.fori_loop(0, nt, source, 0)
    for cp in copies:
        cp.wait()


def backward(x, cot, dcl, saved, y, z, weights, g1, g2):
    q, k, v, p, o, hb, e, gp, x1, r1, x2, r2 = saved
    rows, width = x.shape
    ff = weights[4].shape[1]
    S = jax.ShapeDtypeStruct
    V = pl.BlockSpec(memory_space=pltpu.VMEM)
    packed = S((4, width // 4 * 4 + 2 * ff // 4, width), BF)
    VM = pltpu.VMEM
    low, full = VM((rows, width), BF), VM((rows, width), F32)
    return pl.pallas_call(
        backward_kernel,
        out_shape=[S((rows, width), BF), S((rows, width), BF), packed, S((16, width), F32)],
        in_specs=[V, V, V, V, V, V, ANY, V, V, ANY, ANY, V, V, V, V, V, V] + [ANY] * 6 + [V] * 2,
        out_specs=[V, V, ANY, V],
        scratch_shapes=[VM(w.shape, BF) for w in weights]
        + [
            VM((rows, ff), BF),
            VM((rows, ff), BF),
            VM(p.shape, BF),
            VM(packed.shape, BF),
            full, full, low,
            VM((width, rows), BF),
            low, low, low, low, low,
            pltpu.SemaphoreType.DMA((9,)),
            pltpu.SemaphoreType.DMA((2,)),
        ],
        compiler_params=pltpu.CompilerParams(vmem_limit_bytes=67043328),
        name="segment_backward",
    )(x, cot, dcl, q, k, v, p, o, hb, e, gp, x1, r1, x2, r2, y, z, *weights, g1, g2)


def cross_kernel(cls, emb, cot_all, docs, wq, wk, wv, wi, out_w, outer_w,
                 qb, vb, ob, g1, c1, ib, b2, g2, c2,
                 z_o, dcl_o, xw_o, hw_o, ow_o, e_o, dqkv_o, du_o, da_o, df_o, vec_o, emb_o,
                 vq, vk, vv, vi, vo, v2, heads, xall, rows_s, p_s, dqkv_s, du_s, send1, got1, send2, got2,
                 in_sem, all_send, all_recv, s1, r1, s2, r2, qs_send, qs_recv, us_send, us_recv, o_sem):
    d, s = place()
    c, first, second, other = plane_peers(d, s)
    start, off = window(d)
    me, ahead, behind = everyone(d, s)
    far = [3 - d, first, second]
    lane_w = pl.ds(start, 256)
    loads = [
        pltpu.make_async_copy(src, dst, in_sem.at[i])
        for i, (src, dst) in enumerate(
            (
                (wq, vq), (wk, vk), (wv, vv),
                (out_w.at[1], vo.at[pl.ds(pl.multiple_of(off, 64), 192)]),
                (wi, vi), (outer_w.at[1], v2),
            )
        )
    ]
    for cp in loads:
        cp.start()
    vo[pl.ds(pl.multiple_of(192 * (1 - d % 2), 64), 64), :] = jnp.zeros((64, 768), BF)
    pick = lax.broadcasted_iota(jnp.int32, (8, 32), 0) + 4 * s == lax.broadcasted_iota(jnp.int32, (8, 32), 1)
    position = dot(pick.astype(BF), emb[...])
    heads[...] = (cls[...] + position[0:4]).astype(BF)
    greet([(i // 8, i % 8) for i in ahead])
    sent = []
    for j, i in enumerate(ahead):
        cp = remote(heads, xall.at[me], all_send.at[j], all_recv.at[j], (i // 8, i % 8))
        cp.start()
        sent.append(cp)
    xall[me] = heads[...]
    dys = []
    for i in range(32):
        rows_s[4 * i : 4 * i + 4, :] = cot_all[i].astype(F32)
    dy = rows_s[...]
    ids = lax.broadcasted_iota(jnp.int32, (8, 128), 1) // 32 * 1024
    ids = ids.astype(F32)
    lane = lax.broadcasted_iota(jnp.int32, (32, 128), 1)
    key = lax.broadcasted_iota(jnp.int32, (32, 128), 0)
    for r in range(4):
        numbers = jnp.broadcast_to(docs[r], (8, 32)).astype(F32).astype(BF)
        ids = ids + dot(numbers, (lane == key + 32 * r).astype(BF))
    across = jnp.broadcast_to(ids[0:1], (128, 128))
    allowed = across == across.T
    for j, i in enumerate(behind):
        remote(heads, xall.at[i], all_send.at[j], all_recv.at[j], (i // 8, i % 8)).wait_recv()
    for i in range(32):
        rows_s[4 * i : 4 * i + 4, :] = xall[i].astype(F32)
    xf = rows_s[...]
    x = xf.astype(BF)

    def total(n, partial):
        send1[n] = partial.astype(BF)
        one = remote(send1.at[n], got1.at[n], s1.at[n], r1.at[n], (first, s))
        one.start()
        one.wait_recv()
        both = send1[n].astype(F32) + got1[n].astype(F32)
        send2[n] = both.astype(BF)
        two = remote(send2.at[n], got2.at[n], s2.at[n], r2.at[n], (second, s))
        two.start()
        two.wait_recv()
        sent.append(one)
        sent.append(two)
        return send2[n].astype(F32) + got2[n].astype(F32)

    def vector(ref, lanes=slice(None)):
        return ref[1:2, lanes].astype(F32)

    for i in range(3):
        loads[i].wait()
    q = (dot(x, vq[...]) + vector(qb, lane_w)).astype(BF)
    k = dot(x, vk[...]).astype(BF)
    v = (dot(x, vv[...]) + vector(vb, lane_w)).astype(BF)
    masks = head_masks()
    mixed = []
    for pair in range(2):
        l = slice(pair * 128, pair * 128 + 128)
        both = None
        for h in range(2):
            scores = jnp.where(allowed, dot_nt(q[:, l] * masks[h], k[:, l]) * 0.125, -1e30)
            weight = jnp.exp(scores - jnp.max(scores, axis=-1, keepdims=True))
            share = (weight * (1.0 / jnp.sum(weight, axis=-1, keepdims=True))).astype(BF)
            p_s[2 * pair + h] = share
            part = dot(share, v[:, l] * masks[h])
            both = part if both is None else both + part
        mixed.append(both.astype(BF))
    loads[3].wait()
    ow = jnp.concatenate(mixed, axis=1)
    ow_o[...] = ow
    branch = total(0, dot(ow, vo[...]))
    xhat1, rstd1 = standard(xf + branch + vector(ob))
    hidden = xhat1 * vector(g1) + vector(c1)
    hb = hidden.astype(BF)
    rows_s[...] = hidden
    hw_o[...] = rows_s[:, lane_w].astype(BF)
    rows_s[...] = xf
    xw_o[...] = rows_s[:, lane_w].astype(BF)
    loads[4].wait()
    loads[5].wait()
    wide = pl.ds(pl.multiple_of(d * 768, 768), 768)
    e, gp = gelu_parts(dot(hb, vi[...]) + vector(ib, wide))
    e = e.astype(BF)
    e_o[...] = e
    outer = total(1, dot(e, v2[...]))
    xhat2, rstd2 = standard(hidden + outer + vector(b2))
    z = (xhat2 * vector(g2) + vector(c2)).astype(BF)
    own = lax.broadcasted_iota(jnp.int32, (8, 128), 0) + 4 * me == lax.broadcasted_iota(jnp.int32, (8, 128), 1)
    own = own.astype(BF)
    z_o[...] = dot(own, z)
    vec_o[6:7, :] = row_sum(dy * xhat2)
    vec_o[7:8, :] = row_sum(dy)
    dr2 = standard_back(dy * vector(g2), xhat2, rstd2)
    df = dr2.astype(BF)
    df_o[...] = df
    vec_o[5:6, :] = row_sum(df.astype(F32))
    du = (dot_nt(df, v2[...]).astype(BF).astype(F32) * gp).astype(BF)
    du_s[d] = du
    dh = dr2 + total(2, dot_nt(du, vi[...]))
    for n, peer in enumerate(far):
        cp = remote(du_s.at[d], du_s.at[d], us_send.at[n], us_recv.at[n], (peer, s))
        cp.start()
        sent.append(cp)
    vec_o[3:4, :] = row_sum(dh * xhat1)
    vec_o[4:5, :] = row_sum(dh)
    dr1 = standard_back(dh * vector(g1), xhat1, rstd1)
    da = dr1.astype(BF)
    da_o[...] = da
    vec_o[2:3, :] = row_sum(da.astype(F32))
    do = dot_nt(da, vo[...]).astype(BF)
    dqs, dks, dvs = [], [], []
    for pair in range(2):
        l = slice(pair * 128, pair * 128 + 128)
        dqp = dkp = dvp = 0.0
        for h in range(2):
            share = p_s[2 * pair + h]
            pf = share.astype(F32)
            dom = do[:, l] * masks[h]
            dp = dot_nt(dom, v[:, l]).astype(BF).astype(F32)
            ds = (pf * (dp - jnp.sum(pf * dp, axis=-1, keepdims=True))).astype(BF)
            dqp += dot(ds, k[:, l] * masks[h])
            dkp += dot_tn(ds, q[:, l] * masks[h])
            dvp += dot_tn(share, dom)
        dqs.append((dqp * 0.125).astype(BF))
        dks.append((dkp * 0.125).astype(BF))
        dvs.append(dvp.astype(BF))
    dq, dk, dv = (jnp.concatenate(t, axis=1) for t in (dqs, dks, dvs))
    dqkv_s[d, :, 0:256] = dq
    dqkv_s[d, :, 256:512] = dk
    dqkv_s[d, :, 512:768] = dv
    dx = dr1 + total(3, dot_nt(dq, vq[...]) + dot_nt(dk, vk[...]) + dot_nt(dv, vv[...]))
    for n, peer in enumerate(far):
        cp = remote(dqkv_s.at[d], dqkv_s.at[d], qs_send.at[n], qs_recv.at[n], (peer, s))
        cp.start()
        sent.append(cp)
    dcl = dx.astype(BF)
    dcl_o[...] = dot(own, dcl)
    back = dcl.astype(F32)
    emb_o[...] = back[0:32] + back[32:64] + back[64:96] + back[96:128]
    for n, peer in enumerate(far):
        remote(du_s.at[peer], du_s.at[peer], us_send.at[n], us_recv.at[n], (peer, s)).wait_recv()
        remote(dqkv_s.at[peer], dqkv_s.at[peer], qs_send.at[n], qs_recv.at[n], (peer, s)).wait_recv()
    outs = [pltpu.make_async_copy(du_s, du_o, o_sem.at[0]), pltpu.make_async_copy(dqkv_s, dqkv_o, o_sem.at[1])]
    for cp in outs:
        cp.start()
    for cp in sent:
        cp.wait_send()
    for cp in outs:
        cp.wait()


def cross(cls, emb, cot_all, docs, wq, wk, wv, wi, out_w, outer_w, vectors, collective_id):
    S = jax.ShapeDtypeStruct
    V = pl.BlockSpec(memory_space=pltpu.VMEM)
    VM, dma = pltpu.VMEM, pltpu.SemaphoreType.DMA
    low, win, four = S((128, 768), BF), S((128, 256), BF), S((4, 128, 768), BF)
    return pl.pallas_call(
        cross_kernel,
        out_shape=[
            S((8, 768), F32), S((8, 768), F32), win, win, win, low, four, four, low, low,
            S((8, 768), F32), S((32, 768), F32),
        ],
        in_specs=[V] * 4 + [ANY] * 6 + [V] * 9,
        out_specs=[V] * 6 + [ANY] * 2 + [V] * 4,
        scratch_shapes=[
            VM((768, 256), BF), VM((768, 256), BF), VM((768, 256), BF), VM((768, 768), BF), VM((256, 768), BF), VM((768, 768), BF),
            VM((4, 768), BF), VM((32, 4, 768), BF), VM((128, 768), F32), VM((4, 128, 128), BF),
            VM((4, 128, 768), BF), VM((4, 128, 768), BF),
            VM((4, 128, 768), BF), VM((4, 128, 768), BF), VM((4, 128, 768), BF), VM((4, 128, 768), BF),
            dma((6,)), dma((31,)), dma((31,)),
            dma((4,)), dma((4,)), dma((4,)), dma((4,)), dma((3,)), dma((3,)), dma((3,)), dma((3,)), dma((2,)),
        ],
        compiler_params=pltpu.CompilerParams(collective_id=collective_id, has_side_effects=True, vmem_limit_bytes=67043328),
        name="cross_block",
    )(cls, emb, cot_all, docs, wq, wk, wv, wi, out_w, outer_w, *vectors)


def finish_kernel(red, vec, emb, xw, hw, ow, e, dqkv, du, da, df, vec1,
                  gq, gqb, gk, gv, gvb, go, gob, gg1, gc1, gi, gib, g2_, gb2, gg2, gc2, gemb, vec_s):
    d = lax.axis_index("dp")
    odd = d % 2 == 1
    start, _ = window(d)

    def own(w):
        return jnp.where(odd, w[:, 64:256], w[:, 0:192])

    def whole(at):
        parts = [dqkv[i, :, at * 256 : at * 256 + 256] for i in range(4)]
        return jnp.concatenate(
            [
                parts[0][:, :128], parts[0][:, 128:] + parts[1][:, :128], parts[1][:, 128:],
                parts[2][:, :128], parts[2][:, 128:] + parts[3][:, :128], parts[3][:, 128:],
            ],
            axis=1,
        )

    x, h, o = own(xw[...].astype(F32)).astype(BF), own(hw[...].astype(F32)).astype(BF), own(ow[...].astype(F32)).astype(BF)
    dq, dk, dv = whole(0), whole(1), whole(2)
    for at, (out, left, right) in enumerate(((gq, x, dq), (gk, x, dk), (gv, x, dv), (go, o, da[...]))):
        out[0] = red[at * 192 : at * 192 + 192, :].astype(F32)
        out[1] = dot_tn(left, right)
    for j in range(4):
        l = slice(j * 768, j * 768 + 768)
        gi[0, :, l] = red[768 + j * 192 : 960 + j * 192, :].astype(F32)
        gi[1, :, l] = dot_tn(h, du[j])
    g2_[0] = red[1536:2304, :].astype(F32)
    g2_[1] = dot_tn(e[...], df[...])
    lanes = pl.ds(start, 256)
    mine = own(vec[:, lanes])
    vec_s[...] = vec1[...]
    vec_s[0:1, :] = row_sum(dq.astype(F32))
    vec_s[1:2, :] = row_sum(dv.astype(F32))
    cross = own(vec_s[:, lanes])
    for r, out in enumerate((gqb, gvb, gob, gg1, gc1, gb2, gg2, gc2)):
        out[0:1, :] = mine[r : r + 1]
        out[1:2, :] = cross[r : r + 1]
    gib[0:1, :] = vec[pl.ds(8 + d, 1), :]
    gib[1:2, :] = row_sum(du[d].astype(F32))
    gemb[...] = own(emb[:, lanes])


def finish(red, vec, crossed):
    (_, _, xw, hw, ow, e, dqkv, du, da, df, vec1, emb) = crossed
    S = jax.ShapeDtypeStruct
    V = pl.BlockSpec(memory_space=pltpu.VMEM)
    square, line = S((2, 192, 768), F32), S((2, 192), F32)
    return pl.pallas_call(
        finish_kernel,
        out_shape=[
            square, line, square, square, line, square, line, line, line,
            S((2, 192, 3072), F32), S((2, 768), F32), S((2, 768, 768), F32), line, line, line, S((32, 192), F32),
        ],
        in_specs=[V] * 12,
        out_specs=[V] * 16,
        scratch_shapes=[pltpu.VMEM((8, 768), F32)],
        compiler_params=pltpu.CompilerParams(vmem_limit_bytes=67043328),
        name="finish_grads",
    )(red, vec, emb, xw, hw, ow, e, dqkv, du, da, df, vec1)


def fast_shards(
    inputs,
    doc_ids,
    cotangent,
    query_weight,
    query_bias,
    key_weight,
    value_weight,
    value_bias,
    out_weight,
    out_bias,
    first_gain,
    first_shift,
    inner_weight,
    inner_bias,
    outer_weight,
    outer_bias,
    second_gain,
    second_shift,
    segment_embed,
):
    weights = (query_weight, key_weight, value_weight, out_weight, inner_weight, outer_weight)
    vectors = (query_bias, value_bias, out_bias, first_gain, first_shift, inner_bias, outer_bias, second_gain, second_shift)
    full, windows, cot_all, docs, saved, y, cls = start(inputs[0], weights, cotangent, doc_ids, vectors, 1)
    windows = [w.reshape(-1, w.shape[-1]) for w in windows]
    crossed = cross(cls, segment_embed, cot_all, docs, *windows, out_weight, outer_weight, vectors, 2)
    grad, output, packed, vec = backward(
        inputs[0], cotangent[0], crossed[1], saved, y, crossed[0], full, first_gain, second_gain
    )
    total, vec = reduce(packed, vec, 6, 3)
    return (output[None], grad[None], *finish(total, vec, crossed))


def solution(mesh):
    placed = (
        P("dp", "seg", None),
        P("dp", None),
        P("dp", "seg", None),
        P(None, "dp", None),
        P(),
        P(None, "dp", None),
        P(None, "dp", None),
        P(),
        P(None, "dp", None),
        P(),
        P(),
        P(),
        P(None, "dp", None),
        P(),
        P(None, "dp", None),
        P(),
        P(),
        P(),
        P(),
    )
    square = mesh.shape["dp"] == 4 and mesh.shape["seg"] == 8
    return jax.shard_map(
        fast_shards if square else shards,
        mesh=mesh,
        in_specs=placed,
        out_specs=(
            P("dp", "seg", None),
            P("dp", "seg", None),
            P(None, "dp", None),
            P(None, "dp"),
            P(None, "dp", None),
            P(None, "dp", None),
            P(None, "dp"),
            P(None, "dp", None),
            P(None, "dp"),
            P(None, "dp"),
            P(None, "dp"),
            P(None, "dp", None),
            P(None, "dp"),
            P(None, "dp", None),
            P(None, "dp"),
            P(None, "dp"),
            P(None, "dp"),
            P(None, "dp"),
        ),
        check_vma=False,
    )
```

```python
import functools

import jax
import jax.numpy as jnp
from jax import lax
from jax.experimental import pallas as pl
from jax.experimental.pallas import tpu as pltpu
from jax.sharding import PartitionSpec as P

HEADS = 12
HEAD_DIM = 64
SEG_LEN = 128


epsilon = 1e-05


def normalize(values, gain, shift):
    centred = values - jnp.mean(values, axis=-1, keepdims=True)
    spread = jnp.mean(centred * centred, axis=-1, keepdims=True)
    return centred * lax.rsqrt(spread + epsilon) * gain + shift


def gelu_exact(values):
    return jax.nn.gelu(values, approximate=False)


def project(values, weight):
    return jnp.einsum("gnd,de->gne", values, weight, preferred_element_type=jnp.float32)


def back_project(values, weight):
    return jnp.einsum("gne,de->gnd", values, weight, preferred_element_type=jnp.float32)


def weight_grad(source, grads):
    return jnp.einsum("gnd,gne->de", source, grads, preferred_element_type=jnp.float32)


def row_total(values):
    return jnp.sum(values.astype(jnp.float32), axis=(0, 1))


def keep_pair(first_part, second_part):
    return (first_part, second_part)


def forward_layer(params, source, allowed, spread_keys):
    (
        query_weight,
        query_bias,
        key_weight,
        value_weight,
        value_bias,
        out_weight,
        out_bias,
        first_gain,
        first_shift,
        inner_weight,
        inner_bias,
        outer_weight,
        outer_bias,
        second_gain,
        second_shift,
    ) = params
    groups, length, width = source.shape
    queries = (project(source, query_weight) + query_bias.astype(jnp.float32)).astype(jnp.bfloat16)
    key_rows = project(source, key_weight).astype(jnp.bfloat16)
    value_rows = (project(source, value_weight) + value_bias.astype(jnp.float32)).astype(
        jnp.bfloat16
    )
    key_all, value_all = spread_keys(key_rows, value_rows)
    key_length = key_all.shape[1]
    query_heads = queries.reshape(groups, length, HEADS, HEAD_DIM)
    key_heads = key_all.reshape(groups, key_length, HEADS, HEAD_DIM)
    value_heads = value_all.reshape(groups, key_length, HEADS, HEAD_DIM)
    scores = (
        jnp.einsum("gqhe,gkhe->ghqk", query_heads, key_heads, preferred_element_type=jnp.float32)
        * 0.125
    )
    if allowed is not None:
        scores = jnp.where(allowed[:, None], scores, -1e30)
    attend = jax.nn.softmax(scores, axis=-1)
    attend_low = attend.astype(jnp.bfloat16)
    mixed = jnp.einsum(
        "ghqk,gkhe->gqhe", attend_low, value_heads, preferred_element_type=jnp.float32
    )
    mixed = mixed.astype(jnp.bfloat16).reshape(groups, length, width)
    branch = project(mixed, out_weight) + out_bias.astype(jnp.float32)
    hidden, first_pull = jax.vjp(
        normalize,
        source.astype(jnp.float32) + branch,
        first_gain.astype(jnp.float32),
        first_shift.astype(jnp.float32),
    )
    hidden_low = hidden.astype(jnp.bfloat16)
    inner = project(hidden_low, inner_weight) + inner_bias.astype(jnp.float32)
    active, gelu_pull = jax.vjp(gelu_exact, inner)
    active_low = active.astype(jnp.bfloat16)
    outer = project(active_low, outer_weight) + outer_bias.astype(jnp.float32)
    result, second_pull = jax.vjp(
        normalize, hidden + outer, second_gain.astype(jnp.float32), second_shift.astype(jnp.float32)
    )
    stored = (
        source,
        query_heads,
        key_heads,
        value_heads,
        attend,
        attend_low,
        mixed,
        first_pull,
        hidden_low,
        gelu_pull,
        active_low,
        second_pull,
    )
    return (result, stored)


def backward_layer(params, stored, grad_result, collect_keys):
    (
        query_weight,
        query_bias,
        key_weight,
        value_weight,
        value_bias,
        out_weight,
        out_bias,
        first_gain,
        first_shift,
        inner_weight,
        inner_bias,
        outer_weight,
        outer_bias,
        second_gain,
        second_shift,
    ) = params
    (
        source,
        query_heads,
        key_heads,
        value_heads,
        attend,
        attend_low,
        mixed,
        first_pull,
        hidden_low,
        gelu_pull,
        active_low,
        second_pull,
    ) = stored
    groups, length, width = source.shape
    key_length = key_heads.shape[1]
    grad_second_sum, grad_second_gain, grad_second_shift = second_pull(grad_result)
    grad_outer = grad_second_sum.astype(jnp.bfloat16)
    grad_outer_bias = row_total(grad_outer)
    grad_outer_weight = weight_grad(active_low, grad_outer)
    grad_active = back_project(grad_outer, outer_weight).astype(jnp.bfloat16)
    (grad_inner,) = gelu_pull(grad_active.astype(jnp.float32))
    grad_inner_low = grad_inner.astype(jnp.bfloat16)
    grad_inner_bias = row_total(grad_inner_low)
    grad_inner_weight = weight_grad(hidden_low, grad_inner_low)
    grad_hidden = grad_second_sum + back_project(grad_inner_low, inner_weight)
    grad_first_sum, grad_first_gain, grad_first_shift = first_pull(grad_hidden)
    grad_branch = grad_first_sum.astype(jnp.bfloat16)
    grad_out_bias = row_total(grad_branch)
    grad_out_weight = weight_grad(mixed, grad_branch)
    grad_mixed = back_project(grad_branch, out_weight).astype(jnp.bfloat16)
    grad_mixed = grad_mixed.reshape(groups, length, HEADS, HEAD_DIM)
    grad_attend = jnp.einsum(
        "gqhe,gkhe->ghqk", grad_mixed, value_heads, preferred_element_type=jnp.float32
    )
    grad_attend = grad_attend.astype(jnp.bfloat16).astype(jnp.float32)
    grad_value = jnp.einsum(
        "ghqk,gqhe->gkhe", attend_low, grad_mixed, preferred_element_type=jnp.float32
    )
    grad_value = grad_value.reshape(groups, key_length, width)
    grad_scores = attend * (grad_attend - jnp.sum(attend * grad_attend, axis=-1, keepdims=True))
    grad_scores = grad_scores.astype(jnp.bfloat16)
    grad_query = (
        jnp.einsum("ghqk,gkhe->gqhe", grad_scores, key_heads, preferred_element_type=jnp.float32)
        * 0.125
    )
    grad_query = grad_query.astype(jnp.bfloat16).reshape(groups, length, width)
    grad_key = (
        jnp.einsum("ghqk,gqhe->gkhe", grad_scores, query_heads, preferred_element_type=jnp.float32)
        * 0.125
    )
    grad_key = grad_key.reshape(groups, key_length, width)
    grad_key, grad_value = collect_keys(grad_key, grad_value)
    grad_key = grad_key.astype(jnp.bfloat16)
    grad_value = grad_value.astype(jnp.bfloat16)
    grad_source = (
        grad_first_sum
        + back_project(grad_query, query_weight)
        + back_project(grad_key, key_weight)
        + back_project(grad_value, value_weight)
    )
    gradients = (
        weight_grad(source, grad_query),
        row_total(grad_query),
        weight_grad(source, grad_key),
        weight_grad(source, grad_value),
        row_total(grad_value),
        grad_out_weight,
        grad_out_bias,
        grad_first_gain,
        grad_first_shift,
        grad_inner_weight,
        grad_inner_bias,
        grad_outer_weight,
        grad_outer_bias,
        grad_second_gain,
        grad_second_shift,
    )
    return (grad_source, gradients)


def shards(
    inputs,
    doc_ids,
    cotangent,
    query_weight,
    query_bias,
    key_weight,
    value_weight,
    value_bias,
    out_weight,
    out_bias,
    first_gain,
    first_shift,
    inner_weight,
    inner_bias,
    outer_weight,
    outer_bias,
    second_gain,
    second_shift,
    segment_embed,
):
    seg_count = lax.axis_size("seg")
    seg_index = lax.axis_index("seg")
    group_rows, local_length, width = inputs.shape
    seg_local = local_length // SEG_LEN
    query_full, key_full, value_full, out_full, inner_full, outer_full = (
        lax.all_gather(query_weight, "dp", axis=1, tiled=True),
        lax.all_gather(key_weight, "dp", axis=1, tiled=True),
        lax.all_gather(value_weight, "dp", axis=1, tiled=True),
        lax.all_gather(out_weight, "dp", axis=1, tiled=True),
        lax.all_gather(inner_weight, "dp", axis=1, tiled=True),
        lax.all_gather(outer_weight, "dp", axis=1, tiled=True),
    )
    stacked = (
        query_full,
        query_bias,
        key_full,
        value_full,
        value_bias,
        out_full,
        out_bias,
        first_gain,
        first_shift,
        inner_full,
        inner_bias,
        outer_full,
        outer_bias,
        second_gain,
        second_shift,
    )
    first_params = tuple((weight[0] for weight in stacked))
    cross_params = tuple((weight[1] for weight in stacked))
    pieces = inputs.reshape(group_rows * seg_local, SEG_LEN, width)
    segment_out, segment_stored = forward_layer(first_params, pieces, None, keep_pair)
    segment_grid = segment_out.reshape(group_rows, seg_local, SEG_LEN, width)
    position = lax.dynamic_slice_in_dim(segment_embed, seg_index * seg_local, seg_local, 0).astype(
        jnp.float32
    )
    heads_in = (segment_grid[:, :, 0, :] + position).astype(jnp.bfloat16)
    row_input = lax.all_gather(heads_in, "seg", axis=1, tiled=True)
    allowed = doc_ids[:, :, None] == doc_ids[:, None, :]
    cross_out, cross_stored = forward_layer(cross_params, row_input, allowed, keep_pair)
    returned = lax.dynamic_slice_in_dim(cross_out, seg_index * seg_local, seg_local, 1).astype(
        jnp.bfloat16
    )
    output = jnp.concatenate(
        [returned[:, :, None, :], segment_grid[:, :, 1:, :].astype(jnp.bfloat16)], axis=2
    )
    output = output.reshape(group_rows, local_length, width)
    cot_grid = cotangent.reshape(group_rows, seg_local, SEG_LEN, width)
    cot_heads = cot_grid[:, :, 0, :]
    grad_cross = lax.all_gather(cot_heads, "seg", axis=1, tiled=True)
    grad_row_input, cross_grads = backward_layer(
        cross_params, cross_stored, grad_cross.astype(jnp.float32), keep_pair
    )
    grad_row_low = grad_row_input.astype(jnp.bfloat16)
    factor = 1.0 / seg_count
    embed_grad = jnp.sum(grad_row_low.astype(jnp.float32), axis=0) * factor
    cross_grads = tuple((part * factor for part in cross_grads))
    grad_heads = lax.dynamic_slice_in_dim(grad_row_low, seg_index * seg_local, seg_local, 1)
    grad_grid = jnp.concatenate(
        [grad_heads[:, :, None, :].astype(jnp.float32), cot_grid[:, :, 1:, :].astype(jnp.float32)],
        axis=2,
    )
    grad_grid = grad_grid.reshape(group_rows * seg_local, SEG_LEN, width)
    grad_pieces, segment_grads = backward_layer(first_params, segment_stored, grad_grid, keep_pair)
    input_grad = grad_pieces.astype(jnp.bfloat16).reshape(group_rows, local_length, width)
    shares = (
        lax.psum_scatter(segment_grads[0], "dp", scatter_dimension=0, tiled=True),
        lax.psum_scatter(segment_grads[1], "dp", scatter_dimension=0, tiled=True),
        lax.psum_scatter(segment_grads[2], "dp", scatter_dimension=0, tiled=True),
        lax.psum_scatter(segment_grads[3], "dp", scatter_dimension=0, tiled=True),
        lax.psum_scatter(segment_grads[4], "dp", scatter_dimension=0, tiled=True),
        lax.psum_scatter(segment_grads[5], "dp", scatter_dimension=0, tiled=True),
        lax.psum_scatter(segment_grads[6], "dp", scatter_dimension=0, tiled=True),
        lax.psum_scatter(segment_grads[7], "dp", scatter_dimension=0, tiled=True),
        lax.psum_scatter(segment_grads[8], "dp", scatter_dimension=0, tiled=True),
        lax.psum_scatter(segment_grads[9], "dp", scatter_dimension=0, tiled=True),
        lax.psum_scatter(segment_grads[10], "dp", scatter_dimension=0, tiled=True),
        lax.psum_scatter(segment_grads[11], "dp", scatter_dimension=0, tiled=True),
        lax.psum_scatter(segment_grads[12], "dp", scatter_dimension=0, tiled=True),
        lax.psum_scatter(segment_grads[13], "dp", scatter_dimension=0, tiled=True),
        lax.psum_scatter(segment_grads[14], "dp", scatter_dimension=0, tiled=True),
        lax.psum_scatter(cross_grads[0], "dp", scatter_dimension=0, tiled=True),
        lax.psum_scatter(cross_grads[1], "dp", scatter_dimension=0, tiled=True),
        lax.psum_scatter(cross_grads[2], "dp", scatter_dimension=0, tiled=True),
        lax.psum_scatter(cross_grads[3], "dp", scatter_dimension=0, tiled=True),
        lax.psum_scatter(cross_grads[4], "dp", scatter_dimension=0, tiled=True),
        lax.psum_scatter(cross_grads[5], "dp", scatter_dimension=0, tiled=True),
        lax.psum_scatter(cross_grads[6], "dp", scatter_dimension=0, tiled=True),
        lax.psum_scatter(cross_grads[7], "dp", scatter_dimension=0, tiled=True),
        lax.psum_scatter(cross_grads[8], "dp", scatter_dimension=0, tiled=True),
        lax.psum_scatter(cross_grads[9], "dp", scatter_dimension=0, tiled=True),
        lax.psum_scatter(cross_grads[10], "dp", scatter_dimension=0, tiled=True),
        lax.psum_scatter(cross_grads[11], "dp", scatter_dimension=0, tiled=True),
        lax.psum_scatter(cross_grads[12], "dp", scatter_dimension=0, tiled=True),
        lax.psum_scatter(cross_grads[13], "dp", scatter_dimension=0, tiled=True),
        lax.psum_scatter(cross_grads[14], "dp", scatter_dimension=0, tiled=True),
        lax.psum_scatter(embed_grad, "dp", scatter_dimension=1, tiled=True),
    )
    summed = lax.psum(
        (
            shares[0],
            shares[1],
            shares[2],
            shares[3],
            shares[4],
            shares[5],
            shares[6],
            shares[7],
            shares[8],
            shares[9],
            shares[10],
            shares[11],
            shares[12],
            shares[13],
            shares[14],
            shares[15],
            shares[16],
            shares[17],
            shares[18],
            shares[19],
            shares[20],
            shares[21],
            shares[22],
            shares[23],
            shares[24],
            shares[25],
            shares[26],
            shares[27],
            shares[28],
            shares[29],
            shares[30],
        ),
        "seg",
    )
    totals = tuple((jnp.stack([summed[index], summed[index + 15]]) for index in range(15)))
    totals = totals + (summed[30],)
    return (output, input_grad) + tuple(totals)


MESH = pl.DeviceIdType.MESH
ANY = pl.BlockSpec(memory_space=pl.ANY)
BF = jnp.bfloat16
F32 = jnp.float32


def place():
    d = lax.axis_index("dp")
    s = lax.axis_index("seg")
    return d, s


def greet(peers):
    barrier = pltpu.get_barrier_semaphore()
    for peer in peers:
        pl.semaphore_signal(barrier, inc=1, device_id=peer, device_id_type=MESH)
    pl.semaphore_wait(barrier, len(peers))


def remote(src, dst, send, recv, peer):
    return pltpu.make_async_remote_copy(
        src_ref=src, dst_ref=dst, send_sem=send, recv_sem=recv, device_id=peer, device_id_type=MESH
    )


def plane_peers(d, s):
    c = s % 2
    x, y = d % 2, d // 2
    dx = 2 * y + 1 - x
    dy = 2 * (1 - y) + x
    first = dx * (1 - c) + dy * c
    second = dy * (1 - c) + dx * c
    return c, first, second, s + 1 - 2 * c


def window(d):
    return pl.multiple_of((3 * d) // 2 * 128, 128), d % 2 * 64


def everyone(d, s):
    me = d * 8 + s
    ahead = [lax.rem(me + j, 32) for j in range(1, 32)]
    behind = [lax.rem(me + 32 - j, 32) for j in range(1, 32)]
    return me, ahead, behind


AHEAD, LAG2, LAG4 = 3, 2, 4


def start_kernel(pieces, *refs):
    x, (qb, vb, ob, g1, c1, ib, b2, g2, c2), refs = refs[0], refs[1:10], refs[10:]
    shards, docs, refs = refs[:6], refs[6], refs[7:]
    fulls, wins, docs_all, refs = refs[:6], refs[6:10], refs[10], refs[11:]
    saved_o, y_o, cls_o, refs = refs[:12], refs[12], refs[13], refs[14:]
    full, wbounce, ids, refs = refs[:6], refs[6:10], refs[10], refs[11:]
    (q_s, k_s, v_s, p_s, o_s, h_s, e_s, gp_s, x1, r1, x2, r2), y_s, refs = refs[:12], refs[12], refs[13:]
    load_sem, link_send, link_recv, core_send, core_recv, wload_sem, store_sem, refs = *refs[:7], refs[7:]
    win_send, win_recv, wcore_send, wcore_recv, ids_send, ids_recv, full_sem, out_sem = refs
    vq, vk, vv, vo, vi, v2 = full
    d, s = place()
    c = s % 2
    z = s // 2
    xx, yy = d % 2, d // 2
    dx, dy, dd = 2 * yy + 1 - xx, 2 * (1 - yy) + xx, 3 - d
    other = s + 1 - 2 * c
    even = 1 - z % 2
    xpeer, ypeer, zpeer = (dx, s), (dy, s), (d, s + 4 * even - 2)

    def either(a, b):
        return a * even + b * (1 - even)

    segs = x.shape[0] // 128
    count = len(pieces)
    loads = [
        pltpu.make_async_copy(shards[i].at[0], full[i].at[pl.ds(pl.multiple_of(d * shards[i].shape[1], 64), shards[i].shape[1])], load_sem.at[i])
        for i in range(6)
    ]
    for cp in loads:
        cp.start()
    ids_load = pltpu.make_async_copy(docs, ids, load_sem.at[6])
    ids_load.start()
    origins = (shards[0], shards[1], shards[2], shards[4])
    wloads = []
    for w in range(4):
        width = wins[w].shape[-1]
        at = window(d)[0] if w < 3 else d * width
        cp = pltpu.make_async_copy(origins[w].at[1, :, pl.ds(pl.multiple_of(at, 128), width)], wbounce[w], wload_sem.at[w])
        cp.start()
        wloads.append(cp)
    greet([xpeer, ypeer, (dd, s), zpeer, (d, other)])

    def cols(ref):
        half = ref.shape[-1] // 2
        return pl.ds(pl.multiple_of(c * half, half), half)

    def mine(p, h):
        i, r0, rn = pieces[p]
        n = rn // 4
        return shards[i].at[0, pl.ds(pl.multiple_of(r0 + (2 * h + c) * n, 16), n)]

    def slot(p, src, h):
        i, r0, rn = pieces[p]
        n = rn // 4
        return full[i].at[pl.ds(pl.multiple_of(src * shards[i].shape[1] + r0 + (2 * h + c) * n, 16), n)]

    started, shared, stores = [], [], []

    def link(kind, p, src, dst, peer):
        return remote(src, dst, link_send.at[kind, p], link_recv.at[kind, p], peer)

    def go(cp):
        cp.start()
        started.append(cp)

    def arrived(kind, p, ref):
        link(kind, p, ref, ref, zpeer).wait_recv()
        cp = remote(ref, ref, core_send.at[kind, p], core_recv.at[kind, p], (d, other))
        cp.start()
        shared.append((pieces[p][0], cp))
        started.append(cp)

    def own(p):
        if p < count:
            go(link(0, p, mine(p, 1), slot(p, d, 1), xpeer))
            go(link(1, p, mine(p, 0), slot(p, d, 0), ypeer))

    loaded = set()

    far = (dd, dx, dy)

    def columns(w, dev, core):
        wide = wins[w].shape[-1]
        begin = window(dev)[0] if w < 3 else dev * wide
        return pl.ds(pl.multiple_of(begin + core * (wide // 2), 128), wide // 2)

    def cross_needs():
        ids_load.wait()
        for k, peer in enumerate(far):
            for w in range(4):
                go(remote(
                    origins[w].at[1, :, columns(w, peer, c)], wins[w].at[d, :, cols(wins[w])],
                    win_send.at[k, w], win_recv.at[k, w], (peer, s),
                ))
            go(remote(ids, docs_all.at[d], ids_send.at[k], ids_recv.at[k], (peer, s)))

    def step(p):
        own(p + AHEAD)
        if p < count:
            i = pieces[p][0]
            if i not in loaded:
                loads[i].wait()
                loaded.add(i)
            arrived(0, p, slot(p, dx, 1))
            arrived(1, p, slot(p, dy, 0))
            ref = slot(p, either(d, dy), 0)
            go(link(2, p, ref, ref, xpeer))
            ref = slot(p, either(d, dx), 1)
            go(link(3, p, ref, ref, ypeer))
            if p == count - 1:
                cross_needs()
        n = p - LAG2
        if 0 <= n < count:
            for kind, src, h in ((2, either(dx, dd), 0), (3, either(dy, dd), 1)):
                ref = slot(n, src, h)
                arrived(kind, n, ref)
                go(link(kind + 2, n, ref, ref, zpeer))
        n = p - LAG4
        if 0 <= n < count:
            arrived(4, n, slot(n, either(dd, dx), 0))
            arrived(5, n, slot(n, either(dd, dy), 1))

    ready = set()

    def whole(i):
        for j, cp in shared:
            if j == i:
                cp.wait_recv()
        assert i not in ready
        ready.add(i)
        cp = pltpu.make_async_copy(full[i], fulls[i], full_sem.at[i])
        cp.start()
        stores.append(cp)

    def save(n, ref):
        cp = pltpu.make_async_copy(ref, y_o if n == 12 else saved_o[n], out_sem.at[n])
        cp.start()
        stores.append(cp)

    rows, width = x.shape
    nt = width // TILE
    for p in range(AHEAD):
        own(p)
    at = 0

    def advance(upto):
        nonlocal at
        while at < min(upto, count + LAG4):
            step(at)
            at += 1

    last = {i: max(p for p in range(count) if pieces[p][0] == i) for i in range(6)}
    advance(last[2] + LAG4 + 1)
    for i in range(3):
        whole(i)

    for t in range(nt):
        lanes = slice(t * TILE, t * TILE + TILE)
        q_s[:, lanes] = (dot(x[...], vq[:, lanes]) + qb[0:1, lanes].astype(F32)).astype(BF)
        k_s[:, lanes] = dot(x[...], vk[:, lanes]).astype(BF)
        v_s[:, lanes] = (dot(x[...], vv[:, lanes]) + vb[0:1, lanes].astype(F32)).astype(BF)
    for n, ref in enumerate((q_s, k_s, v_s)):
        save(n, ref)
    advance(last[2] + LAG4 + 2)
    masks = head_masks()

    def attend(hp, carry):
        lanes = tiles(hp, 128)
        for s in range(segs):
            here = slice(s * 128, s * 128 + 128)
            qs, ks, vs = q_s[here, lanes], k_s[here, lanes], v_s[here, lanes]
            mixed = None
            for h in range(2):
                scores = dot_nt(qs * masks[h], ks)
                top = jnp.max(scores, axis=-1, keepdims=True)
                weight = jnp.exp((scores - top) * 0.125)
                share = (weight * (1.0 / jnp.sum(weight, axis=-1, keepdims=True))).astype(BF)
                p_s[hp, s, h] = share
                part = dot(share, vs * masks[h])
                mixed = part if mixed is None else mixed + part
            o_s[here, lanes] = mixed.astype(BF)
        return carry

    pairs = width // 128
    for g in range(pairs // 2):
        lax.fori_loop(2 * g, 2 * g + 2, attend, 0)
        advance(last[2] + LAG4 + 3 + g)
    save(3, p_s)
    save(4, o_s)
    advance(last[3] + LAG4 + 1)
    whole(3)

    def out(t, carry):
        lanes = tiles(t)
        x1[:, lanes] = dot(o_s[...], vo[:, lanes]) + ob[0:1, lanes].astype(F32) + x[:, lanes].astype(F32)
        return carry

    lax.fori_loop(0, nt, out, 0)

    def first(i, carry):
        r = tiles(i, 64)
        xhat, rstd = standard(x1[r, :])
        x1[r, :] = xhat
        r1[r, :] = jnp.broadcast_to(rstd, (64, 128))
        hidden = xhat * g1[0:1, :].astype(F32) + c1[0:1, :].astype(F32)
        h_s[r, :] = hidden.astype(BF)
        x2[r, :] = hidden + b2[0:1, :].astype(F32)
        return carry

    lax.fori_loop(0, rows // 64, first, 0)
    for n, ref in ((5, h_s), (8, x1), (9, r1)):
        save(n, ref)
    advance(last[4] + LAG4 + 1)
    whole(4)

    def ffn(t, carry):
        lanes = tiles(t)
        u = dot(h_s[...], vi[:, lanes]) + ib[0:1, lanes].astype(F32)
        e, gp = gelu_parts(u)
        e_s[:, lanes] = e.astype(BF)
        gp_s[:, lanes] = gp.astype(BF)
        return carry

    groups = vi.shape[1] // TILE // 2
    for g in range(groups):
        lax.fori_loop(2 * g, 2 * g + 2, ffn, 0)
        advance(last[4] + LAG4 + 2 + g)
    advance(count + LAG4)
    for w in range(4):
        wloads[w].wait()
        cp = pltpu.make_async_copy(wbounce[w], wins[w].at[d], store_sem.at[w])
        cp.start()
        stores.append(cp)
    for src, dst, i in ((ids, docs_all.at[d], 4),):
        cp = pltpu.make_async_copy(src, dst, store_sem.at[i])
        cp.start()
        stores.append(cp)
    save(6, e_s)
    save(7, gp_s)
    whole(5)

    def outer(t, carry):
        lanes = tiles(t)
        x2[:, lanes] += dot(e_s[...], v2[:, lanes])
        return carry

    lax.fori_loop(0, nt, outer, 0)

    def second(i, carry):
        r = tiles(i, 64)
        xhat, rstd = standard(x2[r, :])
        x2[r, :] = xhat
        r2[r, :] = jnp.broadcast_to(rstd, (64, 128))
        y_s[r, :] = (xhat * g2[0:1, :].astype(F32) + c2[0:1, :].astype(F32)).astype(BF)
        return carry

    lax.fori_loop(0, rows // 64, second, 0)
    for n, ref in ((10, x2), (11, r2), (12, y_s)):
        save(n, ref)
    for s_ in range(segs):
        cls_o[s_ : s_ + 1, :] = x2[s_ * 128 : s_ * 128 + 1, :] * g2[0:1, :].astype(F32) + c2[0:1, :].astype(F32)
    wcores = []
    for k, peer in enumerate(far):
        for w in range(4):
            got = wins[w].at[peer, :, cols(wins[w])]
            remote(got, got, win_send.at[k, w], win_recv.at[k, w], (peer, s)).wait_recv()
            cp = remote(got, got, wcore_send.at[k, w], wcore_recv.at[k, w], (d, other))
            cp.start()
            wcores.append(cp)
        remote(ids, docs_all.at[peer], ids_send.at[k], ids_recv.at[k], (peer, s)).wait_recv()
    for cp in started:
        cp.wait_send()
    for cp in wcores:
        cp.wait()
    for cp in stores:
        cp.wait()


def start(x, shards, docs, vectors, collective_id):
    cuts = (1, 1, 1, 1, 3, 4)
    pieces = []
    for i, w in enumerate(shards):
        n = w.shape[1] // cuts[i]
        pieces += [(i, p * n, n) for p in range(cuts[i])]
    count = len(pieces)
    S, VM, dma = jax.ShapeDtypeStruct, pltpu.VMEM, pltpu.SemaphoreType.DMA
    V = pl.BlockSpec(memory_space=pltpu.VMEM)
    part, width = shards[0].shape[1:]
    rows = x.shape[0]
    ff = shards[4].shape[2]
    segs = rows // 128
    wins = [(part, 256)] * 3 + [(part, ff // 4)]
    low, full, wide, col = ((rows, width), BF), ((rows, width), F32), ((rows, ff), BF), ((rows, 128), F32)
    saved = [low, low, low, ((width // 128, segs, 2, 128, 128), BF), low, low, wide, wide, full, col, full, col, low]
    outs = pl.pallas_call(
        functools.partial(start_kernel, pieces),
        out_shape=[S((4 * w.shape[1], w.shape[2]), w.dtype) for w in shards]
        + [S((4,) + w, BF) for w in wins]
        + [S((4,) + docs.shape, docs.dtype)]
        + [S(*t) for t in saved]
        + [S((segs, width), F32)],
        in_specs=[V] * 10 + [ANY] * 7,
        out_specs=[ANY] * 24 + [V],
        scratch_shapes=[VM((4 * w.shape[1], w.shape[2]), w.dtype) for w in shards]
        + [VM(w, BF) for w in wins]
        + [VM(docs.shape, docs.dtype)]
        + [VM(*t) for t in saved]
        + [dma((7,)), dma((6, count)), dma((6, count)), dma((6, count)), dma((6, count)), dma((4,)), dma((5,))]
        + [dma((3, 4)), dma((3, 4)), dma((3, 4)), dma((3, 4)), dma((3,)), dma((3,)), dma((6,)), dma((13,))],
        compiler_params=pltpu.CompilerParams(collective_id=collective_id, has_side_effects=True, vmem_limit_bytes=67043328),
        name="gather_forward",
    )(x, *vectors, *shards, docs)
    return outs[:6], outs[6:10], outs[10], outs[11:23], outs[23], outs[24]


def add_into(dst, a, b, rows):
    step = 48

    def body(i, carry):
        r = pl.ds(pl.multiple_of(i * step, 16), step)
        dst[r, :] = (a[r, :].astype(F32) + b[r, :].astype(F32)).astype(dst.dtype)
        return carry

    lax.fori_loop(0, rows // step, body, 0)


def reduce_kernel(nc, r, g, vec, out, vec_out, own, recv0, recv1, recv2, recv3, recv4, fin, load_sem, out_sem,
                  send0, rcv0, send1, rcv1, send2, rcv2, send3, rcv3, send4, rcv4, send5, rcv5, send6, rcv6, send7, rcv7, vsum, vgot, vsend, vrcv):
    d, s = place()
    c, first, second, other = plane_peers(d, s)
    x, y = d % 2, d // 2
    a = x * (1 - c) + y * c
    b = y * (1 - c) + x * c
    z = s // 2
    z0, z1 = z % 2, z // 2
    znear = (z + 1 - 2 * z0) * 2 + c
    zfar = (z + 2 - 4 * z1) * 2 + c
    h, q = r // 2, r // 4
    greet([(first, s), (second, s), (d, other), (d, znear), (d, zfar)])

    def quarter(aa, bb):
        return aa * (1 + c) + bb * (2 - c)

    def rows(core, k):
        return pl.ds(pl.multiple_of(core * (nc * r) + k * r, 16), r)

    started = []

    def go(cp):
        cp.start()
        started.append(cp)

    loads = []
    for k in range(nc):
        go(remote(g.at[:, rows(1 - c, k), :], recv0.at[k], send0.at[k], rcv0.at[k], (d, other)))
        cp = pltpu.make_async_copy(g.at[:, rows(c, k), :], own.at[k], load_sem.at[k])
        cp.start()
        loads.append(cp)

    def arrived(ref, sem):
        pltpu.make_async_copy(ref, ref, sem).wait()

    def piece(k, i0, i1):
        return fin.at[c, k, pl.ds(pl.multiple_of(i0 * h + i1 * q, 16), q), :]

    outs = []

    def stage(t, k):
        if t == 1:
            arrived(recv0.at[k], rcv0.at[k])
            loads[k].wait()
            for bb in range(2):
                away = quarter(1 - a, bb)
                add_into(own.at[k, away], own.at[k, away], recv0.at[k, away], r)
                go(remote(own.at[k, away], recv1.at[k, bb], send1.at[k, bb], rcv1.at[k, bb], (first, s)))
            for bb in range(2):
                keep = quarter(a, bb)
                add_into(own.at[k, keep], own.at[k, keep], recv0.at[k, keep], r)
        elif t == 2:
            for bb in range(2):
                arrived(recv1.at[k, bb], rcv1.at[k, bb])
            away, keep = quarter(a, 1 - b), quarter(a, b)
            add_into(own.at[k, away], own.at[k, away], recv1.at[k, 1 - b], r)
            go(remote(own.at[k, away], recv2.at[k], send2.at[k], rcv2.at[k], (second, s)))
            add_into(own.at[k, keep], own.at[k, keep], recv1.at[k, b], r)
        elif t == 3:
            arrived(recv2.at[k], rcv2.at[k])
            keep = quarter(a, b)
            away = pl.ds(pl.multiple_of((1 - z0) * h, 16), h)
            mine = pl.ds(pl.multiple_of(z0 * h, 16), h)
            add_into(own.at[k, keep, away], own.at[k, keep, away], recv2.at[k, away], h)
            go(remote(own.at[k, keep, away], recv3.at[k], send3.at[k], rcv3.at[k], (d, znear)))
            add_into(own.at[k, keep, mine], own.at[k, keep, mine], recv2.at[k, mine], h)
        elif t == 4:
            arrived(recv3.at[k], rcv3.at[k])
            keep = quarter(a, b)
            away = pl.ds(pl.multiple_of(z0 * h + (1 - z1) * q, 16), q)
            mine = pl.ds(pl.multiple_of(z0 * h + z1 * q, 16), q)
            raway = pl.ds(pl.multiple_of((1 - z1) * q, 16), q)
            rmine = pl.ds(pl.multiple_of(z1 * q, 16), q)
            add_into(own.at[k, keep, away], own.at[k, keep, away], recv3.at[k, raway], q)
            go(remote(own.at[k, keep, away], recv4.at[k], send4.at[k], rcv4.at[k], (d, zfar)))
            add_into(own.at[k, keep, mine], own.at[k, keep, mine], recv3.at[k, rmine], q)
        elif t == 5:
            arrived(recv4.at[k], rcv4.at[k])
            keep = quarter(a, b)
            mine = pl.ds(pl.multiple_of(z0 * h + z1 * q, 16), q)
            add_into(piece(k, z0, z1), own.at[k, keep, mine], recv4.at[k], q)
            go(remote(piece(k, z0, z1), piece(k, z0, z1), send5.at[k], rcv5.at[k], (d, zfar)))
        elif t == 6:
            arrived(piece(k, z0, 1 - z1), rcv5.at[k])
            half = fin.at[c, k, pl.ds(pl.multiple_of(z0 * h, 16), h), :]
            go(remote(half, half, send6.at[k], rcv6.at[k], (d, znear)))
        elif t == 7:
            half = fin.at[c, k, pl.ds(pl.multiple_of((1 - z0) * h, 16), h), :]
            arrived(half, rcv6.at[k])
            go(remote(fin.at[c, k], fin.at[c, k], send7.at[k], rcv7.at[k], (d, other)))
            cp = pltpu.make_async_copy(fin.at[c, k], out.at[rows(c, k), :], out_sem.at[0, k])
            cp.start()
            outs.append(cp)
        elif t == 8:
            arrived(fin.at[1 - c, k], rcv7.at[k])
            cp = pltpu.make_async_copy(fin.at[1 - c, k], out.at[rows(1 - c, k), :], out_sem.at[1, k])
            cp.start()
            outs.append(cp)

    hops = [(d, other), (first, s), (second, s), (d, znear), (d, zfar)]
    vsum[0] = vec[...]

    def vector_hop(j):
        if j > 0:
            arrived(vgot.at[j - 1], vrcv.at[j - 1])
            vsum[j] = vsum[j - 1] + vgot[j - 1]
        if j < 5:
            go(remote(vsum.at[j], vgot.at[j], vsend.at[j], vrcv.at[j], hops[j]))

    for slot in range(nc + 8):
        for t in range(8, 0, -1):
            k = slot - (t - 1)
            if 0 <= k < nc:
                stage(t, k)
        if slot < 6:
            vector_hop(slot)
    vec_out[...] = vsum[5]
    for cp in started:
        cp.wait_send()
    for cp in outs:
        cp.wait()


def reduce(g, vec, nc, collective_id):
    _, total, width = g.shape
    r = total // 2 // nc
    dma = pltpu.SemaphoreType.DMA
    return pl.pallas_call(
        functools.partial(reduce_kernel, nc, r),
        out_shape=[jax.ShapeDtypeStruct((total, width), g.dtype), jax.ShapeDtypeStruct(vec.shape, vec.dtype)],
        in_specs=[ANY, pl.BlockSpec(memory_space=pltpu.VMEM)],
        out_specs=[ANY, pl.BlockSpec(memory_space=pltpu.VMEM)],
        scratch_shapes=[
            pltpu.VMEM((nc, 4, r, width), g.dtype),
            pltpu.VMEM((nc, 4, r, width), g.dtype),
            pltpu.VMEM((nc, 2, r, width), g.dtype),
            pltpu.VMEM((nc, r, width), g.dtype),
            pltpu.VMEM((nc, r // 2, width), g.dtype),
            pltpu.VMEM((nc, r // 4, width), g.dtype),
            pltpu.VMEM((2, nc, r, width), g.dtype),
            dma((nc,)),
            dma((2, nc)),
            dma((nc,)), dma((nc,)),
            dma((nc, 2)), dma((nc, 2)),
            dma((nc,)), dma((nc,)),
            dma((nc,)), dma((nc,)),
            dma((nc,)), dma((nc,)),
            dma((nc,)), dma((nc,)),
            dma((nc,)), dma((nc,)),
            dma((nc,)), dma((nc,)),
            pltpu.VMEM((6,) + vec.shape, vec.dtype),
            pltpu.VMEM((5,) + vec.shape, vec.dtype),
            dma((5,)), dma((5,)),
        ],
        compiler_params=pltpu.CompilerParams(collective_id=collective_id, has_side_effects=True, vmem_limit_bytes=67043328),
        name="reduce_grads",
    )(g, vec)


TILE = 256


def dot(a, b):
    return lax.dot_general(a, b, (((1,), (0,)), ((), ())), preferred_element_type=F32)


def dot_nt(a, b):
    return lax.dot_general(a, b, (((1,), (1,)), ((), ())), preferred_element_type=F32)


def dot_tn(a, b):
    return lax.dot_general(a, b, (((0,), (0,)), ((), ())), preferred_element_type=F32)


def tiles(i, size=TILE):
    return pl.ds(pl.multiple_of(i * size, size), size)


def standard(r):
    centred = r - jnp.mean(r, axis=-1, keepdims=True)
    rstd = lax.rsqrt(jnp.mean(centred * centred, axis=-1, keepdims=True) + epsilon)
    return centred * rstd, rstd


def standard_back(grad, xhat, rstd):
    return rstd * (
        grad
        - jnp.mean(grad, axis=-1, keepdims=True)
        - xhat * jnp.mean(grad * xhat, axis=-1, keepdims=True)
    )


def gelu_parts(u):
    phi = 0.5 * (1.0 + lax.erf(u * 0.7071067811865476))
    return u * phi, phi + u * (0.3989422804014327 * jnp.exp(-0.5 * u * u))


def head_masks():
    lane = lax.broadcasted_iota(jnp.int32, (1, 128), 1)
    low = (lane < 64).astype(F32)
    return (low.astype(BF), (1.0 - low).astype(BF))


def row_sum(v):
    return jnp.sum(v, axis=0, keepdims=True)


def backward_kernel(x, cot, dcl, q, k, v, p, o, hb, e, gp, x1, r1, x2, r2, y, z, wq, wk, wv, wo, wi, w2, g1, g2,
                    dx_o, y_o, g_o, vec_o,
                    vq, vk, vv, vo, vi, v2, e_s, gp_s, p_s, gs, dr2, acc, df, ht, da, do, dq, dk, dv, in_sem, out_sem):
    loads = [
        pltpu.make_async_copy(src, dst, in_sem.at[i])
        for i, (src, dst) in enumerate(
            ((w2, v2), (e, e_s), (gp, gp_s), (wi, vi), (wo, vo), (p, p_s), (wq, vq), (wk, vk), (wv, vv))
        )
    ]
    for cp in loads:
        cp.start()
    rows, width = x.shape
    segs, nt = rows // 128, width // TILE
    ff = vi.shape[1]
    share = width // 4
    vec_o[...] = jnp.zeros_like(vec_o)

    def second(i, carry):
        gain_sum, shift_sum, bias_sum = carry
        r = tiles(i, 64)
        dy, out = cot[r, :].astype(F32), y[r, :].astype(F32)
        at = lax.broadcasted_iota(jnp.int32, (64, 1), 0) + i * 64
        for s in range(segs):
            dy = jnp.where(at == s * 128, dcl[s : s + 1, :], dy)
            out = jnp.where(at == s * 128, z[s : s + 1, :], out)
        y_o[r, :] = out.astype(BF)
        xhat = x2[r, :]
        back = standard_back(dy * g2[0:1, :].astype(F32), xhat, r2[r, 0:1])
        dr2[r, :] = back
        low = back.astype(BF)
        df[r, :] = low
        return (gain_sum + row_sum(dy * xhat), shift_sum + row_sum(dy), bias_sum + row_sum(low.astype(F32)))

    zero = jnp.zeros((1, width), F32)
    sums = lax.fori_loop(0, rows // 64, second, (zero, zero, zero))
    vec_o[6:7, :], vec_o[7:8, :], vec_o[5:6, :] = sums
    ht[...] = hb[...].T
    acc[...] = dr2[...]
    for i in range(4):
        loads[i].wait()

    def ffn(t, carry):
        wide = tiles(t)
        block, lanes = t // nt, tiles(t % nt)
        de = dot_nt(df[...], v2[wide, :]).astype(BF).astype(F32)
        du = (de * gp_s[:, wide].astype(F32)).astype(BF)
        vec_o[pl.ds(8 + block, 1), lanes] = row_sum(du.astype(F32))
        back = dot_tn(e_s[:, wide], df[...])
        gs[block, pl.ds(pl.multiple_of(8 * share + (t % nt) * TILE, TILE), TILE), :] = back.astype(BF)
        inner = dot(ht[...], du).astype(BF)
        for d in range(4):
            gs[d, pl.ds(pl.multiple_of(4 * share + block * share, 64), share), lanes] = inner[d * share : d * share + share]
        acc[...] += dot_nt(du, vi[:, wide])
        return carry

    lax.fori_loop(0, ff // TILE, ffn, 0)
    half = 4 * share
    copies = [pltpu.make_async_copy(gs.at[:, half:, :], g_o.at[:, half:, :], out_sem.at[0])]
    copies[0].start()

    def first(i, carry):
        gain_sum, shift_sum, bias_sum = carry
        r = tiles(i, 64)
        dh = acc[r, :]
        xhat = x1[r, :]
        back = standard_back(dh * g1[0:1, :].astype(F32), xhat, r1[r, 0:1])
        dr2[r, :] = back
        low = back.astype(BF)
        da[r, :] = low
        return (gain_sum + row_sum(dh * xhat), shift_sum + row_sum(dh), bias_sum + row_sum(low.astype(F32)))

    sums = lax.fori_loop(0, rows // 64, first, (zero, zero, zero))
    vec_o[3:4, :], vec_o[4:5, :], vec_o[2:3, :] = sums
    loads[4].wait()
    do[...] = dot_nt(da[...], vo[...]).astype(BF)

    def spread(at, lhs, rhs):
        back = dot_tn(lhs, rhs).astype(BF)
        for d in range(4):
            gs[d, at * share : at * share + share, :] = back[d * share : d * share + share]

    spread(3, o[...], da[...])
    loads[5].wait()
    masks = head_masks()

    def attend(hp, carry):
        lanes = tiles(hp, 128)
        for s in range(segs):
            here = slice(s * 128, s * 128 + 128)
            qs, ks, vs, dos = q[here, lanes], k[here, lanes], v[here, lanes], do[here, lanes]
            dqs = dks = dvs = 0.0
            for h in range(2):
                pl_ = p_s[hp, s, h]
                pf = pl_.astype(F32)
                dom = dos * masks[h]
                dp = dot_nt(dom, vs).astype(BF).astype(F32)
                ds = (pf * (dp - jnp.sum(pf * dp, axis=-1, keepdims=True))).astype(BF)
                dqs += dot(ds, ks * masks[h])
                dks += dot_tn(ds, qs * masks[h])
                dvs += dot_tn(pl_, dom)
            dq[here, lanes] = (dqs * 0.125).astype(BF)
            dk[here, lanes] = (dks * 0.125).astype(BF)
            dv[here, lanes] = dvs.astype(BF)
        return carry

    lax.fori_loop(0, width // 128, attend, 0)
    vec_o[0:1, :] = row_sum(dq[...].astype(F32))
    vec_o[1:2, :] = row_sum(dv[...].astype(F32))
    ht[...] = x[...].T
    for i in range(6, 9):
        loads[i].wait()

    def weights(at, rhs):
        back = dot(ht[...], rhs[...]).astype(BF)
        for d in range(4):
            gs[d, at * share : at * share + share, :] = back[d * share : d * share + share]

    weights(0, dq)
    weights(1, dk)
    weights(2, dv)
    copies.append(pltpu.make_async_copy(gs.at[:, :half, :], g_o.at[:, :half, :], out_sem.at[1]))
    copies[1].start()

    def source(t, carry):
        r = tiles(t)
        dx = dr2[:, r] + dot_nt(dq[...], vq[r, :]) + dot_nt(dk[...], vk[r, :]) + dot_nt(dv[...], vv[r, :])
        dx_o[:, r] = dx.astype(BF)
        return carry

    lax.fori_loop(0, nt, source, 0)
    for cp in copies:
        cp.wait()


def backward(x, cot, dcl, saved, y, z, weights, g1, g2):
    q, k, v, p, o, hb, e, gp, x1, r1, x2, r2 = saved
    rows, width = x.shape
    ff = weights[4].shape[1]
    S = jax.ShapeDtypeStruct
    V = pl.BlockSpec(memory_space=pltpu.VMEM)
    packed = S((4, width // 4 * 4 + 2 * ff // 4, width), BF)
    VM = pltpu.VMEM
    low, full = VM((rows, width), BF), VM((rows, width), F32)
    return pl.pallas_call(
        backward_kernel,
        out_shape=[S((rows, width), BF), S((rows, width), BF), packed, S((16, width), F32)],
        in_specs=[V, V, V, V, V, V, ANY, V, V, ANY, ANY, V, V, V, V, V, V] + [ANY] * 6 + [V] * 2,
        out_specs=[V, V, ANY, V],
        scratch_shapes=[VM(w.shape, BF) for w in weights]
        + [
            VM((rows, ff), BF),
            VM((rows, ff), BF),
            VM(p.shape, BF),
            VM(packed.shape, BF),
            full, full, low,
            VM((width, rows), BF),
            low, low, low, low, low,
            pltpu.SemaphoreType.DMA((9,)),
            pltpu.SemaphoreType.DMA((2,)),
        ],
        compiler_params=pltpu.CompilerParams(vmem_limit_bytes=67043328),
        name="segment_backward",
    )(x, cot, dcl, q, k, v, p, o, hb, e, gp, x1, r1, x2, r2, y, z, *weights, g1, g2)


def cross_kernel(cls, emb, docs, cot, wq, wk, wv, wi, out_w, outer_w,
                 qb, vb, ob, g1, c1, ib, b2, g2, c2,
                 z_o, dcl_o, xw_o, hw_o, ow_o, e_o, dqkv_o, du_o, da_o, df_o, vec_o, emb_o,
                 vq, vk, vv, vi, vo, v2, heads, xall, rows_s, p_s, dqkv_s, du_s, send1, got1, send2, got2,
                 in_sem, all_send, all_recv, first_rows, cots, cot_all, row_sem, cot_send, cot_recv, s1, r1, s2, r2, qs_send, qs_recv, us_send, us_recv, o_sem):
    d, s = place()
    c, first, second, other = plane_peers(d, s)
    start, off = window(d)
    me, ahead, behind = everyone(d, s)
    far = [3 - d, first, second]
    lane_w = pl.ds(start, 256)
    loads = [
        pltpu.make_async_copy(src, dst, in_sem.at[i])
        for i, (src, dst) in enumerate(
            (
                (wq, vq), (wk, vk), (wv, vv),
                (out_w.at[1], vo.at[pl.ds(pl.multiple_of(off, 64), 192)]),
                (wi, vi), (outer_w.at[1], v2),
            )
        )
    ]
    for cp in loads:
        cp.start()
    row_loads = [pltpu.make_async_copy(cot.at[0, pl.ds(i * 128, 8)], first_rows.at[i], row_sem.at[i]) for i in range(4)]
    for cp in row_loads:
        cp.start()
    vo[pl.ds(pl.multiple_of(192 * (1 - d % 2), 64), 64), :] = jnp.zeros((64, 768), BF)
    pick = lax.broadcasted_iota(jnp.int32, (8, 32), 0) + 4 * s == lax.broadcasted_iota(jnp.int32, (8, 32), 1)
    position = dot(pick.astype(BF), emb[...])
    heads[...] = (cls[...] + position[0:4]).astype(BF)
    greet([(i // 8, i % 8) for i in ahead])
    sent = []
    for j, i in enumerate(ahead):
        cp = remote(heads, xall.at[me], all_send.at[j], all_recv.at[j], (i // 8, i % 8))
        cp.start()
        sent.append(cp)
    xall[me] = heads[...]
    for cp in row_loads:
        cp.wait()
    cots[...] = jnp.concatenate([first_rows[i].astype(F32)[0:1] for i in range(4)], axis=0).astype(BF)
    for j, i in enumerate(ahead):
        cp = remote(cots, cot_all.at[me], cot_send.at[j], cot_recv.at[j], (i // 8, i % 8))
        cp.start()
        sent.append(cp)
    cot_all[me] = cots[...]
    ids = lax.broadcasted_iota(jnp.int32, (8, 128), 1) // 32 * 1024
    ids = ids.astype(F32)
    lane = lax.broadcasted_iota(jnp.int32, (32, 128), 1)
    key = lax.broadcasted_iota(jnp.int32, (32, 128), 0)
    for r in range(4):
        numbers = jnp.broadcast_to(docs[r], (8, 32)).astype(F32).astype(BF)
        ids = ids + dot(numbers, (lane == key + 32 * r).astype(BF))
    across = jnp.broadcast_to(ids[0:1], (128, 128))
    allowed = across == across.T
    for j, i in enumerate(behind):
        remote(heads, xall.at[i], all_send.at[j], all_recv.at[j], (i // 8, i % 8)).wait_recv()
    for i in range(32):
        rows_s[4 * i : 4 * i + 4, :] = xall[i].astype(F32)
    xf = rows_s[...]
    x = xf.astype(BF)

    def total(n, partial):
        send1[n] = partial.astype(BF)
        one = remote(send1.at[n], got1.at[n], s1.at[n], r1.at[n], (first, s))
        one.start()
        one.wait_recv()
        both = send1[n].astype(F32) + got1[n].astype(F32)
        send2[n] = both.astype(BF)
        two = remote(send2.at[n], got2.at[n], s2.at[n], r2.at[n], (second, s))
        two.start()
        two.wait_recv()
        sent.append(one)
        sent.append(two)
        return send2[n].astype(F32) + got2[n].astype(F32)

    def vector(ref, lanes=slice(None)):
        return ref[1:2, lanes].astype(F32)

    for i in range(3):
        loads[i].wait()
    q = (dot(x, vq[...]) + vector(qb, lane_w)).astype(BF)
    k = dot(x, vk[...]).astype(BF)
    v = (dot(x, vv[...]) + vector(vb, lane_w)).astype(BF)
    masks = head_masks()
    mixed = []
    for pair in range(2):
        l = slice(pair * 128, pair * 128 + 128)
        both = None
        for h in range(2):
            scores = jnp.where(allowed, dot_nt(q[:, l] * masks[h], k[:, l]) * 0.125, -1e30)
            weight = jnp.exp(scores - jnp.max(scores, axis=-1, keepdims=True))
            share = (weight * (1.0 / jnp.sum(weight, axis=-1, keepdims=True))).astype(BF)
            p_s[2 * pair + h] = share
            part = dot(share, v[:, l] * masks[h])
            both = part if both is None else both + part
        mixed.append(both.astype(BF))
    loads[3].wait()
    ow = jnp.concatenate(mixed, axis=1)
    ow_o[...] = ow
    branch = total(0, dot(ow, vo[...]))
    xhat1, rstd1 = standard(xf + branch + vector(ob))
    hidden = xhat1 * vector(g1) + vector(c1)
    hb = hidden.astype(BF)
    rows_s[...] = hidden
    hw_o[...] = rows_s[:, lane_w].astype(BF)
    rows_s[...] = xf
    xw_o[...] = rows_s[:, lane_w].astype(BF)
    loads[4].wait()
    loads[5].wait()
    wide = pl.ds(pl.multiple_of(d * 768, 768), 768)
    e, gp = gelu_parts(dot(hb, vi[...]) + vector(ib, wide))
    e = e.astype(BF)
    e_o[...] = e
    outer = total(1, dot(e, v2[...]))
    xhat2, rstd2 = standard(hidden + outer + vector(b2))
    z = (xhat2 * vector(g2) + vector(c2)).astype(BF)
    own = lax.broadcasted_iota(jnp.int32, (8, 128), 0) + 4 * me == lax.broadcasted_iota(jnp.int32, (8, 128), 1)
    own = own.astype(BF)
    z_o[...] = dot(own, z)
    for j, i in enumerate(behind):
        remote(cots, cot_all.at[i], cot_send.at[j], cot_recv.at[j], (i // 8, i % 8)).wait_recv()
    for i in range(32):
        rows_s[4 * i : 4 * i + 4, :] = cot_all[i].astype(F32)
    dy = rows_s[...]
    vec_o[6:7, :] = row_sum(dy * xhat2)
    vec_o[7:8, :] = row_sum(dy)
    dr2 = standard_back(dy * vector(g2), xhat2, rstd2)
    df = dr2.astype(BF)
    df_o[...] = df
    vec_o[5:6, :] = row_sum(df.astype(F32))
    du = (dot_nt(df, v2[...]).astype(BF).astype(F32) * gp).astype(BF)
    du_s[d] = du
    dh = dr2 + total(2, dot_nt(du, vi[...]))
    for n, peer in enumerate(far):
        cp = remote(du_s.at[d], du_s.at[d], us_send.at[n], us_recv.at[n], (peer, s))
        cp.start()
        sent.append(cp)
    vec_o[3:4, :] = row_sum(dh * xhat1)
    vec_o[4:5, :] = row_sum(dh)
    dr1 = standard_back(dh * vector(g1), xhat1, rstd1)
    da = dr1.astype(BF)
    da_o[...] = da
    vec_o[2:3, :] = row_sum(da.astype(F32))
    do = dot_nt(da, vo[...]).astype(BF)
    dqs, dks, dvs = [], [], []
    for pair in range(2):
        l = slice(pair * 128, pair * 128 + 128)
        dqp = dkp = dvp = 0.0
        for h in range(2):
            share = p_s[2 * pair + h]
            pf = share.astype(F32)
            dom = do[:, l] * masks[h]
            dp = dot_nt(dom, v[:, l]).astype(BF).astype(F32)
            ds = (pf * (dp - jnp.sum(pf * dp, axis=-1, keepdims=True))).astype(BF)
            dqp += dot(ds, k[:, l] * masks[h])
            dkp += dot_tn(ds, q[:, l] * masks[h])
            dvp += dot_tn(share, dom)
        dqs.append((dqp * 0.125).astype(BF))
        dks.append((dkp * 0.125).astype(BF))
        dvs.append(dvp.astype(BF))
    dq, dk, dv = (jnp.concatenate(t, axis=1) for t in (dqs, dks, dvs))
    dqkv_s[d, :, 0:256] = dq
    dqkv_s[d, :, 256:512] = dk
    dqkv_s[d, :, 512:768] = dv
    dx = dr1 + total(3, dot_nt(dq, vq[...]) + dot_nt(dk, vk[...]) + dot_nt(dv, vv[...]))
    for n, peer in enumerate(far):
        cp = remote(dqkv_s.at[d], dqkv_s.at[d], qs_send.at[n], qs_recv.at[n], (peer, s))
        cp.start()
        sent.append(cp)
    dcl = dx.astype(BF)
    dcl_o[...] = dot(own, dcl)
    back = dcl.astype(F32)
    emb_o[...] = back[0:32] + back[32:64] + back[64:96] + back[96:128]
    for n, peer in enumerate(far):
        remote(du_s.at[peer], du_s.at[peer], us_send.at[n], us_recv.at[n], (peer, s)).wait_recv()
        remote(dqkv_s.at[peer], dqkv_s.at[peer], qs_send.at[n], qs_recv.at[n], (peer, s)).wait_recv()
    outs = [pltpu.make_async_copy(du_s, du_o, o_sem.at[0]), pltpu.make_async_copy(dqkv_s, dqkv_o, o_sem.at[1])]
    for cp in outs:
        cp.start()
    for cp in sent:
        cp.wait_send()
    for cp in outs:
        cp.wait()


def cross(cls, emb, cot, docs, wq, wk, wv, wi, out_w, outer_w, vectors, collective_id):
    S = jax.ShapeDtypeStruct
    V = pl.BlockSpec(memory_space=pltpu.VMEM)
    VM, dma = pltpu.VMEM, pltpu.SemaphoreType.DMA
    low, win, four = S((128, 768), BF), S((128, 256), BF), S((4, 128, 768), BF)
    return pl.pallas_call(
        cross_kernel,
        out_shape=[
            S((8, 768), F32), S((8, 768), F32), win, win, win, low, four, four, low, low,
            S((8, 768), F32), S((32, 768), F32),
        ],
        in_specs=[V] * 3 + [ANY] * 7 + [V] * 9,
        out_specs=[V] * 6 + [ANY] * 2 + [V] * 4,
        scratch_shapes=[
            VM((768, 256), BF), VM((768, 256), BF), VM((768, 256), BF), VM((768, 768), BF), VM((256, 768), BF), VM((768, 768), BF),
            VM((4, 768), BF), VM((32, 4, 768), BF), VM((128, 768), F32), VM((4, 128, 128), BF),
            VM((4, 128, 768), BF), VM((4, 128, 768), BF),
            VM((4, 128, 768), BF), VM((4, 128, 768), BF), VM((4, 128, 768), BF), VM((4, 128, 768), BF),
            dma((6,)), dma((31,)), dma((31,)),
            VM((4, 8, 768), BF), VM((4, 768), BF), VM((32, 4, 768), BF), dma((4,)), dma((31,)), dma((31,)),
            dma((4,)), dma((4,)), dma((4,)), dma((4,)), dma((3,)), dma((3,)), dma((3,)), dma((3,)), dma((2,)),
        ],
        compiler_params=pltpu.CompilerParams(collective_id=collective_id, has_side_effects=True, vmem_limit_bytes=67043328),
        name="cross_block",
    )(cls, emb, docs, cot, wq, wk, wv, wi, out_w, outer_w, *vectors)


def finish_kernel(red, vec, emb, xw, hw, ow, e, dqkv, du, da, df, vec1,
                  gq, gqb, gk, gv, gvb, go, gob, gg1, gc1, gi, gib, g2_, gb2, gg2, gc2, gemb, vec_s):
    d = lax.axis_index("dp")
    odd = d % 2 == 1
    start, _ = window(d)

    def own(w):
        return jnp.where(odd, w[:, 64:256], w[:, 0:192])

    def whole(at):
        parts = [dqkv[i, :, at * 256 : at * 256 + 256] for i in range(4)]
        return jnp.concatenate(
            [
                parts[0][:, :128], parts[0][:, 128:] + parts[1][:, :128], parts[1][:, 128:],
                parts[2][:, :128], parts[2][:, 128:] + parts[3][:, :128], parts[3][:, 128:],
            ],
            axis=1,
        )

    x, h, o = own(xw[...].astype(F32)).astype(BF), own(hw[...].astype(F32)).astype(BF), own(ow[...].astype(F32)).astype(BF)
    dq, dk, dv = whole(0), whole(1), whole(2)
    for at, (out, left, right) in enumerate(((gq, x, dq), (gk, x, dk), (gv, x, dv), (go, o, da[...]))):
        out[0] = red[at * 192 : at * 192 + 192, :].astype(F32)
        out[1] = dot_tn(left, right)
    for j in range(4):
        l = slice(j * 768, j * 768 + 768)
        gi[0, :, l] = red[768 + j * 192 : 960 + j * 192, :].astype(F32)
        gi[1, :, l] = dot_tn(h, du[j])
    g2_[0] = red[1536:2304, :].astype(F32)
    g2_[1] = dot_tn(e[...], df[...])
    lanes = pl.ds(start, 256)
    mine = own(vec[:, lanes])
    vec_s[...] = vec1[...]
    vec_s[0:1, :] = row_sum(dq.astype(F32))
    vec_s[1:2, :] = row_sum(dv.astype(F32))
    cross = own(vec_s[:, lanes])
    for r, out in enumerate((gqb, gvb, gob, gg1, gc1, gb2, gg2, gc2)):
        out[0:1, :] = mine[r : r + 1]
        out[1:2, :] = cross[r : r + 1]
    gib[0:1, :] = vec[pl.ds(8 + d, 1), :]
    gib[1:2, :] = row_sum(du[d].astype(F32))
    gemb[...] = own(emb[:, lanes])


def finish(red, vec, crossed):
    (_, _, xw, hw, ow, e, dqkv, du, da, df, vec1, emb) = crossed
    S = jax.ShapeDtypeStruct
    V = pl.BlockSpec(memory_space=pltpu.VMEM)
    square, line = S((2, 192, 768), F32), S((2, 192), F32)
    return pl.pallas_call(
        finish_kernel,
        out_shape=[
            square, line, square, square, line, square, line, line, line,
            S((2, 192, 3072), F32), S((2, 768), F32), S((2, 768, 768), F32), line, line, line, S((32, 192), F32),
        ],
        in_specs=[V] * 12,
        out_specs=[V] * 16,
        scratch_shapes=[pltpu.VMEM((8, 768), F32)],
        compiler_params=pltpu.CompilerParams(vmem_limit_bytes=67043328),
        name="finish_grads",
    )(red, vec, emb, xw, hw, ow, e, dqkv, du, da, df, vec1)


def fast_shards(
    inputs,
    doc_ids,
    cotangent,
    query_weight,
    query_bias,
    key_weight,
    value_weight,
    value_bias,
    out_weight,
    out_bias,
    first_gain,
    first_shift,
    inner_weight,
    inner_bias,
    outer_weight,
    outer_bias,
    second_gain,
    second_shift,
    segment_embed,
):
    weights = (query_weight, key_weight, value_weight, out_weight, inner_weight, outer_weight)
    vectors = (query_bias, value_bias, out_bias, first_gain, first_shift, inner_bias, outer_bias, second_gain, second_shift)
    full, windows, docs, saved, y, cls = start(inputs[0], weights, doc_ids, vectors, 1)
    windows = [w.reshape(-1, w.shape[-1]) for w in windows]
    crossed = cross(cls, segment_embed, cotangent, docs, *windows, out_weight, outer_weight, vectors, 2)
    grad, output, packed, vec = backward(
        inputs[0], cotangent[0], crossed[1], saved, y, crossed[0], full, first_gain, second_gain
    )
    total, vec = reduce(packed, vec, 6, 3)
    return (output[None], grad[None], *finish(total, vec, crossed))


def solution(mesh):
    placed = (
        P("dp", "seg", None),
        P("dp", None),
        P("dp", "seg", None),
        P(None, "dp", None),
        P(),
        P(None, "dp", None),
        P(None, "dp", None),
        P(),
        P(None, "dp", None),
        P(),
        P(),
        P(),
        P(None, "dp", None),
        P(),
        P(None, "dp", None),
        P(),
        P(),
        P(),
        P(),
    )
    square = mesh.shape["dp"] == 4 and mesh.shape["seg"] == 8
    return jax.shard_map(
        fast_shards if square else shards,
        mesh=mesh,
        in_specs=placed,
        out_specs=(
            P("dp", "seg", None),
            P("dp", "seg", None),
            P(None, "dp", None),
            P(None, "dp"),
            P(None, "dp", None),
            P(None, "dp", None),
            P(None, "dp"),
            P(None, "dp", None),
            P(None, "dp"),
            P(None, "dp"),
            P(None, "dp"),
            P(None, "dp", None),
            P(None, "dp"),
            P(None, "dp", None),
            P(None, "dp"),
            P(None, "dp"),
            P(None, "dp"),
            P(None, "dp"),
        ),
        check_vma=False,
    )
```

```python
import functools

import jax
import jax.numpy as jnp
from jax import lax
from jax.experimental import pallas as pl
from jax.experimental.pallas import tpu as pltpu
from jax.sharding import PartitionSpec as P

HEADS = 12
HEAD_DIM = 64
SEG_LEN = 128


epsilon = 1e-05


def normalize(values, gain, shift):
    centred = values - jnp.mean(values, axis=-1, keepdims=True)
    spread = jnp.mean(centred * centred, axis=-1, keepdims=True)
    return centred * lax.rsqrt(spread + epsilon) * gain + shift


def gelu_exact(values):
    return jax.nn.gelu(values, approximate=False)


def project(values, weight):
    return jnp.einsum("gnd,de->gne", values, weight, preferred_element_type=jnp.float32)


def back_project(values, weight):
    return jnp.einsum("gne,de->gnd", values, weight, preferred_element_type=jnp.float32)


def weight_grad(source, grads):
    return jnp.einsum("gnd,gne->de", source, grads, preferred_element_type=jnp.float32)


def row_total(values):
    return jnp.sum(values.astype(jnp.float32), axis=(0, 1))


def keep_pair(first_part, second_part):
    return (first_part, second_part)


def forward_layer(params, source, allowed, spread_keys):
    (
        query_weight,
        query_bias,
        key_weight,
        value_weight,
        value_bias,
        out_weight,
        out_bias,
        first_gain,
        first_shift,
        inner_weight,
        inner_bias,
        outer_weight,
        outer_bias,
        second_gain,
        second_shift,
    ) = params
    groups, length, width = source.shape
    queries = (project(source, query_weight) + query_bias.astype(jnp.float32)).astype(jnp.bfloat16)
    key_rows = project(source, key_weight).astype(jnp.bfloat16)
    value_rows = (project(source, value_weight) + value_bias.astype(jnp.float32)).astype(
        jnp.bfloat16
    )
    key_all, value_all = spread_keys(key_rows, value_rows)
    key_length = key_all.shape[1]
    query_heads = queries.reshape(groups, length, HEADS, HEAD_DIM)
    key_heads = key_all.reshape(groups, key_length, HEADS, HEAD_DIM)
    value_heads = value_all.reshape(groups, key_length, HEADS, HEAD_DIM)
    scores = (
        jnp.einsum("gqhe,gkhe->ghqk", query_heads, key_heads, preferred_element_type=jnp.float32)
        * 0.125
    )
    if allowed is not None:
        scores = jnp.where(allowed[:, None], scores, -1e30)
    attend = jax.nn.softmax(scores, axis=-1)
    attend_low = attend.astype(jnp.bfloat16)
    mixed = jnp.einsum(
        "ghqk,gkhe->gqhe", attend_low, value_heads, preferred_element_type=jnp.float32
    )
    mixed = mixed.astype(jnp.bfloat16).reshape(groups, length, width)
    branch = project(mixed, out_weight) + out_bias.astype(jnp.float32)
    hidden, first_pull = jax.vjp(
        normalize,
        source.astype(jnp.float32) + branch,
        first_gain.astype(jnp.float32),
        first_shift.astype(jnp.float32),
    )
    hidden_low = hidden.astype(jnp.bfloat16)
    inner = project(hidden_low, inner_weight) + inner_bias.astype(jnp.float32)
    active, gelu_pull = jax.vjp(gelu_exact, inner)
    active_low = active.astype(jnp.bfloat16)
    outer = project(active_low, outer_weight) + outer_bias.astype(jnp.float32)
    result, second_pull = jax.vjp(
        normalize, hidden + outer, second_gain.astype(jnp.float32), second_shift.astype(jnp.float32)
    )
    stored = (
        source,
        query_heads,
        key_heads,
        value_heads,
        attend,
        attend_low,
        mixed,
        first_pull,
        hidden_low,
        gelu_pull,
        active_low,
        second_pull,
    )
    return (result, stored)


def backward_layer(params, stored, grad_result, collect_keys):
    (
        query_weight,
        query_bias,
        key_weight,
        value_weight,
        value_bias,
        out_weight,
        out_bias,
        first_gain,
        first_shift,
        inner_weight,
        inner_bias,
        outer_weight,
        outer_bias,
        second_gain,
        second_shift,
    ) = params
    (
        source,
        query_heads,
        key_heads,
        value_heads,
        attend,
        attend_low,
        mixed,
        first_pull,
        hidden_low,
        gelu_pull,
        active_low,
        second_pull,
    ) = stored
    groups, length, width = source.shape
    key_length = key_heads.shape[1]
    grad_second_sum, grad_second_gain, grad_second_shift = second_pull(grad_result)
    grad_outer = grad_second_sum.astype(jnp.bfloat16)
    grad_outer_bias = row_total(grad_outer)
    grad_outer_weight = weight_grad(active_low, grad_outer)
    grad_active = back_project(grad_outer, outer_weight).astype(jnp.bfloat16)
    (grad_inner,) = gelu_pull(grad_active.astype(jnp.float32))
    grad_inner_low = grad_inner.astype(jnp.bfloat16)
    grad_inner_bias = row_total(grad_inner_low)
    grad_inner_weight = weight_grad(hidden_low, grad_inner_low)
    grad_hidden = grad_second_sum + back_project(grad_inner_low, inner_weight)
    grad_first_sum, grad_first_gain, grad_first_shift = first_pull(grad_hidden)
    grad_branch = grad_first_sum.astype(jnp.bfloat16)
    grad_out_bias = row_total(grad_branch)
    grad_out_weight = weight_grad(mixed, grad_branch)
    grad_mixed = back_project(grad_branch, out_weight).astype(jnp.bfloat16)
    grad_mixed = grad_mixed.reshape(groups, length, HEADS, HEAD_DIM)
    grad_attend = jnp.einsum(
        "gqhe,gkhe->ghqk", grad_mixed, value_heads, preferred_element_type=jnp.float32
    )
    grad_attend = grad_attend.astype(jnp.bfloat16).astype(jnp.float32)
    grad_value = jnp.einsum(
        "ghqk,gqhe->gkhe", attend_low, grad_mixed, preferred_element_type=jnp.float32
    )
    grad_value = grad_value.reshape(groups, key_length, width)
    grad_scores = attend * (grad_attend - jnp.sum(attend * grad_attend, axis=-1, keepdims=True))
    grad_scores = grad_scores.astype(jnp.bfloat16)
    grad_query = (
        jnp.einsum("ghqk,gkhe->gqhe", grad_scores, key_heads, preferred_element_type=jnp.float32)
        * 0.125
    )
    grad_query = grad_query.astype(jnp.bfloat16).reshape(groups, length, width)
    grad_key = (
        jnp.einsum("ghqk,gqhe->gkhe", grad_scores, query_heads, preferred_element_type=jnp.float32)
        * 0.125
    )
    grad_key = grad_key.reshape(groups, key_length, width)
    grad_key, grad_value = collect_keys(grad_key, grad_value)
    grad_key = grad_key.astype(jnp.bfloat16)
    grad_value = grad_value.astype(jnp.bfloat16)
    grad_source = (
        grad_first_sum
        + back_project(grad_query, query_weight)
        + back_project(grad_key, key_weight)
        + back_project(grad_value, value_weight)
    )
    gradients = (
        weight_grad(source, grad_query),
        row_total(grad_query),
        weight_grad(source, grad_key),
        weight_grad(source, grad_value),
        row_total(grad_value),
        grad_out_weight,
        grad_out_bias,
        grad_first_gain,
        grad_first_shift,
        grad_inner_weight,
        grad_inner_bias,
        grad_outer_weight,
        grad_outer_bias,
        grad_second_gain,
        grad_second_shift,
    )
    return (grad_source, gradients)


def shards(
    inputs,
    doc_ids,
    cotangent,
    query_weight,
    query_bias,
    key_weight,
    value_weight,
    value_bias,
    out_weight,
    out_bias,
    first_gain,
    first_shift,
    inner_weight,
    inner_bias,
    outer_weight,
    outer_bias,
    second_gain,
    second_shift,
    segment_embed,
):
    seg_count = lax.axis_size("seg")
    seg_index = lax.axis_index("seg")
    group_rows, local_length, width = inputs.shape
    seg_local = local_length // SEG_LEN
    query_full, key_full, value_full, out_full, inner_full, outer_full = (
        lax.all_gather(query_weight, "dp", axis=1, tiled=True),
        lax.all_gather(key_weight, "dp", axis=1, tiled=True),
        lax.all_gather(value_weight, "dp", axis=1, tiled=True),
        lax.all_gather(out_weight, "dp", axis=1, tiled=True),
        lax.all_gather(inner_weight, "dp", axis=1, tiled=True),
        lax.all_gather(outer_weight, "dp", axis=1, tiled=True),
    )
    stacked = (
        query_full,
        query_bias,
        key_full,
        value_full,
        value_bias,
        out_full,
        out_bias,
        first_gain,
        first_shift,
        inner_full,
        inner_bias,
        outer_full,
        outer_bias,
        second_gain,
        second_shift,
    )
    first_params = tuple((weight[0] for weight in stacked))
    cross_params = tuple((weight[1] for weight in stacked))
    pieces = inputs.reshape(group_rows * seg_local, SEG_LEN, width)
    segment_out, segment_stored = forward_layer(first_params, pieces, None, keep_pair)
    segment_grid = segment_out.reshape(group_rows, seg_local, SEG_LEN, width)
    position = lax.dynamic_slice_in_dim(segment_embed, seg_index * seg_local, seg_local, 0).astype(
        jnp.float32
    )
    heads_in = (segment_grid[:, :, 0, :] + position).astype(jnp.bfloat16)
    row_input = lax.all_gather(heads_in, "seg", axis=1, tiled=True)
    allowed = doc_ids[:, :, None] == doc_ids[:, None, :]
    cross_out, cross_stored = forward_layer(cross_params, row_input, allowed, keep_pair)
    returned = lax.dynamic_slice_in_dim(cross_out, seg_index * seg_local, seg_local, 1).astype(
        jnp.bfloat16
    )
    output = jnp.concatenate(
        [returned[:, :, None, :], segment_grid[:, :, 1:, :].astype(jnp.bfloat16)], axis=2
    )
    output = output.reshape(group_rows, local_length, width)
    cot_grid = cotangent.reshape(group_rows, seg_local, SEG_LEN, width)
    cot_heads = cot_grid[:, :, 0, :]
    grad_cross = lax.all_gather(cot_heads, "seg", axis=1, tiled=True)
    grad_row_input, cross_grads = backward_layer(
        cross_params, cross_stored, grad_cross.astype(jnp.float32), keep_pair
    )
    grad_row_low = grad_row_input.astype(jnp.bfloat16)
    factor = 1.0 / seg_count
    embed_grad = jnp.sum(grad_row_low.astype(jnp.float32), axis=0) * factor
    cross_grads = tuple((part * factor for part in cross_grads))
    grad_heads = lax.dynamic_slice_in_dim(grad_row_low, seg_index * seg_local, seg_local, 1)
    grad_grid = jnp.concatenate(
        [grad_heads[:, :, None, :].astype(jnp.float32), cot_grid[:, :, 1:, :].astype(jnp.float32)],
        axis=2,
    )
    grad_grid = grad_grid.reshape(group_rows * seg_local, SEG_LEN, width)
    grad_pieces, segment_grads = backward_layer(first_params, segment_stored, grad_grid, keep_pair)
    input_grad = grad_pieces.astype(jnp.bfloat16).reshape(group_rows, local_length, width)
    shares = (
        lax.psum_scatter(segment_grads[0], "dp", scatter_dimension=0, tiled=True),
        lax.psum_scatter(segment_grads[1], "dp", scatter_dimension=0, tiled=True),
        lax.psum_scatter(segment_grads[2], "dp", scatter_dimension=0, tiled=True),
        lax.psum_scatter(segment_grads[3], "dp", scatter_dimension=0, tiled=True),
        lax.psum_scatter(segment_grads[4], "dp", scatter_dimension=0, tiled=True),
        lax.psum_scatter(segment_grads[5], "dp", scatter_dimension=0, tiled=True),
        lax.psum_scatter(segment_grads[6], "dp", scatter_dimension=0, tiled=True),
        lax.psum_scatter(segment_grads[7], "dp", scatter_dimension=0, tiled=True),
        lax.psum_scatter(segment_grads[8], "dp", scatter_dimension=0, tiled=True),
        lax.psum_scatter(segment_grads[9], "dp", scatter_dimension=0, tiled=True),
        lax.psum_scatter(segment_grads[10], "dp", scatter_dimension=0, tiled=True),
        lax.psum_scatter(segment_grads[11], "dp", scatter_dimension=0, tiled=True),
        lax.psum_scatter(segment_grads[12], "dp", scatter_dimension=0, tiled=True),
        lax.psum_scatter(segment_grads[13], "dp", scatter_dimension=0, tiled=True),
        lax.psum_scatter(segment_grads[14], "dp", scatter_dimension=0, tiled=True),
        lax.psum_scatter(cross_grads[0], "dp", scatter_dimension=0, tiled=True),
        lax.psum_scatter(cross_grads[1], "dp", scatter_dimension=0, tiled=True),
        lax.psum_scatter(cross_grads[2], "dp", scatter_dimension=0, tiled=True),
        lax.psum_scatter(cross_grads[3], "dp", scatter_dimension=0, tiled=True),
        lax.psum_scatter(cross_grads[4], "dp", scatter_dimension=0, tiled=True),
        lax.psum_scatter(cross_grads[5], "dp", scatter_dimension=0, tiled=True),
        lax.psum_scatter(cross_grads[6], "dp", scatter_dimension=0, tiled=True),
        lax.psum_scatter(cross_grads[7], "dp", scatter_dimension=0, tiled=True),
        lax.psum_scatter(cross_grads[8], "dp", scatter_dimension=0, tiled=True),
        lax.psum_scatter(cross_grads[9], "dp", scatter_dimension=0, tiled=True),
        lax.psum_scatter(cross_grads[10], "dp", scatter_dimension=0, tiled=True),
        lax.psum_scatter(cross_grads[11], "dp", scatter_dimension=0, tiled=True),
        lax.psum_scatter(cross_grads[12], "dp", scatter_dimension=0, tiled=True),
        lax.psum_scatter(cross_grads[13], "dp", scatter_dimension=0, tiled=True),
        lax.psum_scatter(cross_grads[14], "dp", scatter_dimension=0, tiled=True),
        lax.psum_scatter(embed_grad, "dp", scatter_dimension=1, tiled=True),
    )
    summed = lax.psum(
        (
            shares[0],
            shares[1],
            shares[2],
            shares[3],
            shares[4],
            shares[5],
            shares[6],
            shares[7],
            shares[8],
            shares[9],
            shares[10],
            shares[11],
            shares[12],
            shares[13],
            shares[14],
            shares[15],
            shares[16],
            shares[17],
            shares[18],
            shares[19],
            shares[20],
            shares[21],
            shares[22],
            shares[23],
            shares[24],
            shares[25],
            shares[26],
            shares[27],
            shares[28],
            shares[29],
            shares[30],
        ),
        "seg",
    )
    totals = tuple((jnp.stack([summed[index], summed[index + 15]]) for index in range(15)))
    totals = totals + (summed[30],)
    return (output, input_grad) + tuple(totals)


MESH = pl.DeviceIdType.MESH
ANY = pl.BlockSpec(memory_space=pl.ANY)
BF = jnp.bfloat16
F32 = jnp.float32


def place():
    d = lax.axis_index("dp")
    s = lax.axis_index("seg")
    return d, s


def greet(peers):
    barrier = pltpu.get_barrier_semaphore()
    for peer in peers:
        pl.semaphore_signal(barrier, inc=1, device_id=peer, device_id_type=MESH)
    pl.semaphore_wait(barrier, len(peers))


def remote(src, dst, send, recv, peer):
    return pltpu.make_async_remote_copy(
        src_ref=src, dst_ref=dst, send_sem=send, recv_sem=recv, device_id=peer, device_id_type=MESH
    )


def plane_peers(d, s):
    c = s % 2
    x, y = d % 2, d // 2
    dx = 2 * y + 1 - x
    dy = 2 * (1 - y) + x
    first = dx * (1 - c) + dy * c
    second = dy * (1 - c) + dx * c
    return c, first, second, s + 1 - 2 * c


def window(d):
    return pl.multiple_of((3 * d) // 2 * 128, 128), d % 2 * 64


def everyone(d, s):
    me = d * 8 + s
    ahead = [lax.rem(me + j, 32) for j in range(1, 32)]
    behind = [lax.rem(me + 32 - j, 32) for j in range(1, 32)]
    return me, ahead, behind


AHEAD, LAG2, LAG4 = 3, 2, 4


def start_kernel(pieces, *refs):
    x, (qb, vb, ob, g1, c1, ib, b2, g2, c2), refs = refs[0], refs[1:10], refs[10:]
    shards, docs, refs = refs[:6], refs[6], refs[7:]
    fulls, wins, docs_all, refs = refs[:6], refs[6:10], refs[10], refs[11:]
    saved_o, y_o, cls_o, refs = refs[:12], refs[12], refs[13], refs[14:]
    full, wbounce, ids, refs = refs[:6], refs[6:10], refs[10], refs[11:]
    (q_s, k_s, v_s, p_s, o_s, h_s, e_s, gp_s, x1, r1, x2, r2), y_s, refs = refs[:12], refs[12], refs[13:]
    load_sem, link_send, link_recv, core_send, core_recv, wload_sem, store_sem, refs = *refs[:7], refs[7:]
    win_send, win_recv, wcore_send, wcore_recv, ids_send, ids_recv, full_sem, out_sem = refs
    vq, vk, vv, vo, vi, v2 = full
    d, s = place()
    c = s % 2
    z = s // 2
    xx, yy = d % 2, d // 2
    dx, dy, dd = 2 * yy + 1 - xx, 2 * (1 - yy) + xx, 3 - d
    other = s + 1 - 2 * c
    even = 1 - z % 2
    xpeer, ypeer, zpeer = (dx, s), (dy, s), (d, s + 4 * even - 2)

    def either(a, b):
        return a * even + b * (1 - even)

    segs = x.shape[0] // 128
    count = len(pieces)
    loads = [
        pltpu.make_async_copy(shards[i].at[0], full[i].at[pl.ds(pl.multiple_of(d * shards[i].shape[1], 64), shards[i].shape[1])], load_sem.at[i])
        for i in range(6)
    ]
    for cp in loads:
        cp.start()
    ids_load = pltpu.make_async_copy(docs, ids, load_sem.at[6])
    ids_load.start()
    origins = (shards[0], shards[1], shards[2], shards[4])
    wloads = []
    for w in range(4):
        width = wins[w].shape[-1]
        at = window(d)[0] if w < 3 else d * width
        cp = pltpu.make_async_copy(origins[w].at[1, :, pl.ds(pl.multiple_of(at, 128), width)], wbounce[w], wload_sem.at[w])
        cp.start()
        wloads.append(cp)
    greet([xpeer, ypeer, (dd, s), zpeer, (d, other)])

    def cols(ref):
        half = ref.shape[-1] // 2
        return pl.ds(pl.multiple_of(c * half, half), half)

    def mine(p, h):
        i, r0, rn = pieces[p]
        n = rn // 4
        return shards[i].at[0, pl.ds(pl.multiple_of(r0 + (2 * h + c) * n, 16), n)]

    def slot(p, src, h):
        i, r0, rn = pieces[p]
        n = rn // 4
        return full[i].at[pl.ds(pl.multiple_of(src * shards[i].shape[1] + r0 + (2 * h + c) * n, 16), n)]

    started, shared, stores = [], [], []

    def link(kind, p, src, dst, peer):
        return remote(src, dst, link_send.at[kind, p], link_recv.at[kind, p], peer)

    def go(cp):
        cp.start()
        started.append(cp)

    def arrived(kind, p, ref):
        link(kind, p, ref, ref, zpeer).wait_recv()
        cp = remote(ref, ref, core_send.at[kind, p], core_recv.at[kind, p], (d, other))
        cp.start()
        shared.append((pieces[p][0], cp))
        started.append(cp)

    def own(p):
        if p < count:
            go(link(0, p, mine(p, 1), slot(p, d, 1), xpeer))
            go(link(1, p, mine(p, 0), slot(p, d, 0), ypeer))

    loaded = set()

    far = (dd, dx, dy)

    def columns(w, dev, core):
        wide = wins[w].shape[-1]
        begin = window(dev)[0] if w < 3 else dev * wide
        return pl.ds(pl.multiple_of(begin + core * (wide // 2), 128), wide // 2)

    def cross_needs():
        ids_load.wait()
        for k, peer in enumerate(far):
            for w in range(4):
                go(remote(
                    origins[w].at[1, :, columns(w, peer, c)], wins[w].at[d, :, cols(wins[w])],
                    win_send.at[k, w], win_recv.at[k, w], (peer, s),
                ))
            go(remote(ids, docs_all.at[d], ids_send.at[k], ids_recv.at[k], (peer, s)))

    def step(p):
        own(p + AHEAD)
        if p < count:
            i = pieces[p][0]
            if i not in loaded:
                loads[i].wait()
                loaded.add(i)
            arrived(0, p, slot(p, dx, 1))
            arrived(1, p, slot(p, dy, 0))
            ref = slot(p, either(d, dy), 0)
            go(link(2, p, ref, ref, xpeer))
            ref = slot(p, either(d, dx), 1)
            go(link(3, p, ref, ref, ypeer))
            if p == count - 1:
                cross_needs()
        n = p - LAG2
        if 0 <= n < count:
            for kind, src, h in ((2, either(dx, dd), 0), (3, either(dy, dd), 1)):
                ref = slot(n, src, h)
                arrived(kind, n, ref)
                go(link(kind + 2, n, ref, ref, zpeer))
        n = p - LAG4
        if 0 <= n < count:
            arrived(4, n, slot(n, either(dd, dx), 0))
            arrived(5, n, slot(n, either(dd, dy), 1))

    ready = set()

    def whole(i):
        for j, cp in shared:
            if j == i:
                cp.wait_recv()
        assert i not in ready
        ready.add(i)
        cp = pltpu.make_async_copy(full[i], fulls[i], full_sem.at[i])
        cp.start()
        stores.append(cp)

    def save(n, ref):
        cp = pltpu.make_async_copy(ref, y_o if n == 12 else saved_o[n], out_sem.at[n])
        cp.start()
        stores.append(cp)

    rows, width = x.shape
    nt = width // TILE
    for p in range(AHEAD):
        own(p)
    at = 0

    def advance(upto):
        nonlocal at
        while at < min(upto, count + LAG4):
            step(at)
            at += 1

    last = {i: max(p for p in range(count) if pieces[p][0] == i) for i in range(6)}
    advance(last[2] + LAG4 + 1)
    for i in range(3):
        whole(i)

    for t in range(nt):
        lanes = slice(t * TILE, t * TILE + TILE)
        q_s[:, lanes] = (dot(x[...], vq[:, lanes]) + qb[0:1, lanes].astype(F32)).astype(BF)
        k_s[:, lanes] = dot(x[...], vk[:, lanes]).astype(BF)
        v_s[:, lanes] = (dot(x[...], vv[:, lanes]) + vb[0:1, lanes].astype(F32)).astype(BF)
    for n, ref in enumerate((q_s, k_s, v_s)):
        save(n, ref)
    advance(last[2] + LAG4 + 2)
    masks = head_masks()

    def attend(hp, carry):
        lanes = tiles(hp, 128)
        for s in range(segs):
            here = slice(s * 128, s * 128 + 128)
            qs, ks, vs = q_s[here, lanes], k_s[here, lanes], v_s[here, lanes]
            mixed = None
            for h in range(2):
                scores = dot_nt(qs * masks[h], ks)
                top = jnp.max(scores, axis=-1, keepdims=True)
                weight = jnp.exp((scores - top) * 0.125)
                share = (weight * (1.0 / jnp.sum(weight, axis=-1, keepdims=True))).astype(BF)
                p_s[hp, s, h] = share
                part = dot(share, vs * masks[h])
                mixed = part if mixed is None else mixed + part
            o_s[here, lanes] = mixed.astype(BF)
        return carry

    pairs = width // 128
    for g in range(pairs // 2):
        lax.fori_loop(2 * g, 2 * g + 2, attend, 0)
        advance(last[2] + LAG4 + 3 + g)
    save(3, p_s)
    save(4, o_s)
    advance(last[3] + LAG4 + 1)
    whole(3)

    def out(t, carry):
        lanes = tiles(t)
        x1[:, lanes] = dot(o_s[...], vo[:, lanes]) + ob[0:1, lanes].astype(F32) + x[:, lanes].astype(F32)
        return carry

    lax.fori_loop(0, nt, out, 0)

    def first(i, carry):
        r = tiles(i, 64)
        xhat, rstd = standard(x1[r, :])
        x1[r, :] = xhat
        r1[r, :] = jnp.broadcast_to(rstd, (64, 128))
        hidden = xhat * g1[0:1, :].astype(F32) + c1[0:1, :].astype(F32)
        h_s[r, :] = hidden.astype(BF)
        x2[r, :] = hidden + b2[0:1, :].astype(F32)
        return carry

    lax.fori_loop(0, rows // 64, first, 0)
    for n, ref in ((5, h_s), (8, x1), (9, r1)):
        save(n, ref)
    advance(last[4] + LAG4 + 1)
    whole(4)

    def ffn(t, carry):
        lanes = tiles(t)
        u = dot(h_s[...], vi[:, lanes]) + ib[0:1, lanes].astype(F32)
        e, gp = gelu_parts(u)
        e_s[:, lanes] = e.astype(BF)
        gp_s[:, lanes] = gp.astype(BF)
        return carry

    groups = vi.shape[1] // TILE // 2
    for g in range(groups):
        lax.fori_loop(2 * g, 2 * g + 2, ffn, 0)
        advance(last[4] + LAG4 + 2 + g)
    advance(count + LAG4)
    for w in range(4):
        wloads[w].wait()
        cp = pltpu.make_async_copy(wbounce[w], wins[w].at[d], store_sem.at[w])
        cp.start()
        stores.append(cp)
    for src, dst, i in ((ids, docs_all.at[d], 4),):
        cp = pltpu.make_async_copy(src, dst, store_sem.at[i])
        cp.start()
        stores.append(cp)
    save(6, e_s)
    save(7, gp_s)
    whole(5)

    def outer(t, carry):
        lanes = tiles(t)
        x2[:, lanes] += dot(e_s[...], v2[:, lanes])
        return carry

    lax.fori_loop(0, nt, outer, 0)

    def second(i, carry):
        r = tiles(i, 64)
        xhat, rstd = standard(x2[r, :])
        x2[r, :] = xhat
        r2[r, :] = jnp.broadcast_to(rstd, (64, 128))
        y_s[r, :] = (xhat * g2[0:1, :].astype(F32) + c2[0:1, :].astype(F32)).astype(BF)
        return carry

    lax.fori_loop(0, rows // 64, second, 0)
    for n, ref in ((10, x2), (11, r2), (12, y_s)):
        save(n, ref)
    for s_ in range(segs):
        cls_o[s_ : s_ + 1, :] = x2[s_ * 128 : s_ * 128 + 1, :] * g2[0:1, :].astype(F32) + c2[0:1, :].astype(F32)
    wcores = []
    for k, peer in enumerate(far):
        for w in range(4):
            got = wins[w].at[peer, :, cols(wins[w])]
            remote(got, got, win_send.at[k, w], win_recv.at[k, w], (peer, s)).wait_recv()
            cp = remote(got, got, wcore_send.at[k, w], wcore_recv.at[k, w], (d, other))
            cp.start()
            wcores.append(cp)
        remote(ids, docs_all.at[peer], ids_send.at[k], ids_recv.at[k], (peer, s)).wait_recv()
    for cp in started:
        cp.wait_send()
    for cp in wcores:
        cp.wait()
    for cp in stores:
        cp.wait()


def start(x, shards, docs, vectors, collective_id):
    cuts = (1, 1, 1, 1, 3, 4)
    pieces = []
    for i, w in enumerate(shards):
        n = w.shape[1] // cuts[i]
        pieces += [(i, p * n, n) for p in range(cuts[i])]
    count = len(pieces)
    S, VM, dma = jax.ShapeDtypeStruct, pltpu.VMEM, pltpu.SemaphoreType.DMA
    V = pl.BlockSpec(memory_space=pltpu.VMEM)
    part, width = shards[0].shape[1:]
    rows = x.shape[0]
    ff = shards[4].shape[2]
    segs = rows // 128
    wins = [(part, 256)] * 3 + [(part, ff // 4)]
    low, full, wide, col = ((rows, width), BF), ((rows, width), F32), ((rows, ff), BF), ((rows, 128), F32)
    saved = [low, low, low, ((width // 128, segs, 2, 128, 128), BF), low, low, wide, wide, full, col, full, col, low]
    outs = pl.pallas_call(
        functools.partial(start_kernel, pieces),
        out_shape=[S((4 * w.shape[1], w.shape[2]), w.dtype) for w in shards]
        + [S((4,) + w, BF) for w in wins]
        + [S((4,) + docs.shape, docs.dtype)]
        + [S(*t) for t in saved]
        + [S((segs, width), F32)],
        in_specs=[V] * 10 + [ANY] * 7,
        out_specs=[ANY] * 24 + [V],
        scratch_shapes=[VM((4 * w.shape[1], w.shape[2]), w.dtype) for w in shards]
        + [VM(w, BF) for w in wins]
        + [VM(docs.shape, docs.dtype)]
        + [VM(*t) for t in saved]
        + [dma((7,)), dma((6, count)), dma((6, count)), dma((6, count)), dma((6, count)), dma((4,)), dma((5,))]
        + [dma((3, 4)), dma((3, 4)), dma((3, 4)), dma((3, 4)), dma((3,)), dma((3,)), dma((6,)), dma((13,))],
        compiler_params=pltpu.CompilerParams(collective_id=collective_id, has_side_effects=True, vmem_limit_bytes=67043328),
        name="gather_forward",
    )(x, *vectors, *shards, docs)
    return outs[:6], outs[6:10], outs[10], outs[11:23], outs[23], outs[24]


def add_into(dst, a, b, rows):
    step = 48 if rows % 48 == 0 else 32

    def body(i, carry):
        r = pl.ds(pl.multiple_of(i * step, 16), step)
        dst[r, :] = (a[r, :].astype(F32) + b[r, :].astype(F32)).astype(dst.dtype)
        return carry

    lax.fori_loop(0, rows // step, body, 0)


TILE = 256


def dot(a, b):
    return lax.dot_general(a, b, (((1,), (0,)), ((), ())), preferred_element_type=F32)


def dot_nt(a, b):
    return lax.dot_general(a, b, (((1,), (1,)), ((), ())), preferred_element_type=F32)


def dot_tn(a, b):
    return lax.dot_general(a, b, (((0,), (0,)), ((), ())), preferred_element_type=F32)


def tiles(i, size=TILE):
    return pl.ds(pl.multiple_of(i * size, size), size)


def standard(r):
    centred = r - jnp.mean(r, axis=-1, keepdims=True)
    rstd = lax.rsqrt(jnp.mean(centred * centred, axis=-1, keepdims=True) + epsilon)
    return centred * rstd, rstd


def standard_back(grad, xhat, rstd):
    return rstd * (
        grad
        - jnp.mean(grad, axis=-1, keepdims=True)
        - xhat * jnp.mean(grad * xhat, axis=-1, keepdims=True)
    )


def gelu_parts(u):
    phi = 0.5 * (1.0 + lax.erf(u * 0.7071067811865476))
    return u * phi, phi + u * (0.3989422804014327 * jnp.exp(-0.5 * u * u))


def head_masks():
    lane = lax.broadcasted_iota(jnp.int32, (1, 128), 1)
    low = (lane < 64).astype(F32)
    return (low.astype(BF), (1.0 - low).astype(BF))


def row_sum(v):
    return jnp.sum(v, axis=0, keepdims=True)


CHUNKS = [("rows", 0), ("cols", 0), ("rows", 1), ("cols", 1), ("rows", 2), ("cols", 2), ("mats", 3), ("mats", 0), ("mats", 1), ("mats", 2)]


def backward_kernel(dcl, z, g1, g2, x, cot, q, k, v, p, o, hb, e, gp, x1, r1, x2, r2, y, wq, wk, wv, wo, wi, w2, *refs):
    (dx_o, y_o, outer_o, inner_o, mats_o, vec_o), refs = refs[:6], refs[6:]
    (xs, ds_, qs_, ks_, vs_, p_s, os_, hs, e_s, gp_s, x1s, r1s, acc, r2s, ys), refs = refs[:15], refs[15:]
    (vi, v2, df, ht, vecs, g_rows, g_cols, g_mats), refs = refs[:8], refs[8:]
    bufs, refs = refs[:18], refs[18:]
    in_sem, w_sem, res_sem, out_sem, vsum, vgot, vsend, vrcv, send, recv = refs
    dev, s = place()
    c, first, second, other = plane_peers(dev, s)
    px, py = dev % 2, dev // 2
    a = px * (1 - c) + py * c
    b = py * (1 - c) + px * c
    z_at = s // 2
    z0, z1 = z_at % 2, z_at // 2
    znear = (z_at + 1 - 2 * z0) * 2 + c
    zfar = (z_at + 2 - 4 * z1) * 2 + c
    order = [(cot, ds_), (y, ys), (x2, acc), (r2, r2s), (hb, hs), (w2, v2), (e, e_s), (gp, gp_s), (wi, vi),
             (x1, x1s), (r1, r1s), (o, os_), (p, p_s), (q, qs_), (k, ks_), (v, vs_), (x, xs)]
    loads = [pltpu.make_async_copy(src, dst, in_sem.at[i]) for i, (src, dst) in enumerate(order)]
    for cp in loads:
        cp.start()
    greet([(first, s), (second, s), (dev, other), (dev, znear), (dev, zfar)])
    rows, width = xs.shape
    segs, nt = rows // 128, width // TILE
    share = width // 4
    started, outs, results = [], [], []

    def go(cp):
        cp.start()
        started.append(cp)

    def arrived(ref, sem):
        pltpu.make_async_copy(ref, ref, sem).wait()

    families = {"rows": 0, "cols": 1, "mats": 2}

    def part(n, core, quarters):
        kind, i = CHUNKS[n]
        if kind == "rows":
            return g_rows.at[quarters, pl.ds(pl.multiple_of(i * 256 + core * 128, 128), 128), :]
        ref = g_cols if kind == "cols" else g_mats
        half = ref.shape[-1] // 2
        return ref.at[i, quarters, :, pl.ds(pl.multiple_of(core * half, 128), half)]

    def buf(n, j):
        kind, i = CHUNKS[n]
        ref = bufs[families[kind] * 6 + j]
        return ref.at[i] if j < 5 else ref.at[:, i]

    def size(n):
        return 128 if CHUNKS[n][0] == "rows" else 192

    def own(n, quarter):
        return part(n, c, quarter)

    def fin(n, core, at=0, count=None):
        kind, i = CHUNKS[n]
        count = size(n) if count is None else count
        return bufs[families[kind] * 6 + 5].at[core, i, pl.ds(pl.multiple_of(at, 16), count), :]

    def quarter(aa, bb):
        return aa * (1 + c) + bb * (2 - c)

    def offer(n):
        go(remote(part(n, 1 - c, slice(None)), buf(n, 0), send.at[0, n], recv.at[0, n], (dev, other)))

    def write(n, core, i):
        kind, at = CHUNKS[n]
        src = bufs[families[kind] * 6 + 5].at[core, at]
        if kind == "rows":
            pairs_ = [(src, outer_o.at[pl.ds(pl.multiple_of(at * 256 + core * 128, 128), 128), :])]
        elif kind == "mats":
            pairs_ = [(src, mats_o.at[at, :, pl.ds(pl.multiple_of(core * 384, 128), 384)])]
        else:
            pairs_ = [
                (src.at[:, j * 256 : j * 256 + 256], inner_o.at[:, pl.ds(pl.multiple_of((2 * core + j) * 768 + at * 256, 128), 256)])
                for j in range(2)
            ]
        for j, (left, right) in enumerate(pairs_):
            cp = pltpu.make_async_copy(left, right, out_sem.at[i, j, n])
            cp.start()
            outs.append(cp)

    def stage(t, n):
        r = size(n)
        h, f = r // 2, r // 4
        if t == 1:
            got = buf(n, 0)
            arrived(got, recv.at[0, n])
            for bb in range(2):
                away = quarter(1 - a, bb)
                add_into(own(n, away), own(n, away), got.at[away], r)
                go(remote(own(n, away), buf(n, 1).at[bb], send.at[1 + bb, n], recv.at[1 + bb, n], (first, s)))
            for bb in range(2):
                keep = quarter(a, bb)
                add_into(own(n, keep), own(n, keep), got.at[keep], r)
        elif t == 2:
            got = buf(n, 1)
            for bb in range(2):
                arrived(got.at[bb], recv.at[1 + bb, n])
            away, keep = quarter(a, 1 - b), quarter(a, b)
            add_into(own(n, away), own(n, away), got.at[1 - b], r)
            go(remote(own(n, away), buf(n, 2), send.at[3, n], recv.at[3, n], (second, s)))
            add_into(own(n, keep), own(n, keep), got.at[b], r)
        elif t == 3:
            got = buf(n, 2)
            arrived(got, recv.at[3, n])
            keep = own(n, quarter(a, b))
            away = pl.ds(pl.multiple_of((1 - z0) * h, 16), h)
            mine = pl.ds(pl.multiple_of(z0 * h, 16), h)
            add_into(keep.at[away], keep.at[away], got.at[away], h)
            go(remote(keep.at[away], buf(n, 3), send.at[4, n], recv.at[4, n], (dev, znear)))
            add_into(keep.at[mine], keep.at[mine], got.at[mine], h)
        elif t == 4:
            got = buf(n, 3)
            arrived(got, recv.at[4, n])
            keep = own(n, quarter(a, b))
            away = pl.ds(pl.multiple_of(z0 * h + (1 - z1) * f, 16), f)
            mine = pl.ds(pl.multiple_of(z0 * h + z1 * f, 16), f)
            add_into(keep.at[away], keep.at[away], got.at[pl.ds(pl.multiple_of((1 - z1) * f, 16), f)], f)
            go(remote(keep.at[away], buf(n, 4), send.at[5, n], recv.at[5, n], (dev, zfar)))
            add_into(keep.at[mine], keep.at[mine], got.at[pl.ds(pl.multiple_of(z1 * f, 16), f)], f)
        elif t == 5:
            got = buf(n, 4)
            arrived(got, recv.at[5, n])
            mine = own(n, quarter(a, b)).at[pl.ds(pl.multiple_of(z0 * h + z1 * f, 16), f)]
            done = fin(n, c, z0 * h + z1 * f, f)
            add_into(done, mine, got, f)
            go(remote(done, done, send.at[6, n], recv.at[6, n], (dev, zfar)))
        elif t == 6:
            arrived(fin(n, c, z0 * h + (1 - z1) * f, f), recv.at[6, n])
            half = fin(n, c, z0 * h, h)
            go(remote(half, half, send.at[7, n], recv.at[7, n], (dev, znear)))
        elif t == 7:
            arrived(fin(n, c, (1 - z0) * h, h), recv.at[7, n])
            go(remote(fin(n, c), fin(n, c), send.at[8, n], recv.at[8, n], (dev, other)))
            write(n, c, 0)
        elif t == 8:
            arrived(fin(n, 1 - c), recv.at[8, n])
            write(n, 1 - c, 1)

    nc = len(CHUNKS)

    def slot(i):
        for t in range(8, 0, -1):
            n = i - (t - 1)
            if 0 <= n < nc:
                stage(t, n)

    vecs[...] = jnp.zeros_like(vecs)
    for i in range(4):
        loads[i].wait()

    def norm2(i, carry):
        gain_sum, shift_sum, bias_sum = carry
        r = tiles(i, 64)
        dy, out = ds_[r, :].astype(F32), ys[r, :].astype(F32)
        at = lax.broadcasted_iota(jnp.int32, (64, 1), 0) + i * 64
        for j in range(segs):
            dy = jnp.where(at == j * 128, dcl[j : j + 1, :], dy)
            out = jnp.where(at == j * 128, z[j : j + 1, :], out)
        ys[r, :] = out.astype(BF)
        xhat = acc[r, :]
        back = standard_back(dy * g2[0:1, :].astype(F32), xhat, r2s[r, 0:1])
        acc[r, :] = back
        low = back.astype(BF)
        df[r, :] = low
        return (gain_sum + row_sum(dy * xhat), shift_sum + row_sum(dy), bias_sum + row_sum(low.astype(F32)))

    zero = jnp.zeros((1, width), F32)
    sums = lax.fori_loop(0, rows // 64, norm2, (zero, zero, zero))
    vecs[6:7, :], vecs[7:8, :], vecs[5:6, :] = sums
    results.append(pltpu.make_async_copy(ys, y_o, res_sem.at[0]))
    results[0].start()
    loads[4].wait()
    ht[...] = hs[...].T
    for i in range(5, 9):
        loads[i].wait()

    def ffn(j):
        def body(block, carry):
            wide = tiles(block * nt + j)
            lanes = slice(j * TILE, j * TILE + TILE)
            de = dot_nt(df[...], v2[wide, :]).astype(BF).astype(F32)
            du = (de * gp_s[:, wide].astype(F32)).astype(BF)
            vecs[pl.ds(8 + block, 1), lanes] = row_sum(du.astype(F32))
            g_rows[block, lanes, :] = dot_tn(e_s[:, wide], df[...]).astype(BF)
            inner = dot(ht[...], du).astype(BF)
            for i in range(4):
                g_cols[j, i, :, tiles(block)] = inner[i * share : i * share + share]
            acc[...] += dot_nt(du, vi[:, wide])
            return carry

        return body

    lax.fori_loop(0, 4, ffn(0), 0)
    offer(0)
    offer(1)
    lax.fori_loop(0, 2, ffn(1), 0)
    slot(0)
    lax.fori_loop(2, 4, ffn(1), 0)
    offer(2)
    offer(3)
    slot(1)
    lax.fori_loop(0, 2, ffn(2), 0)
    slot(2)
    lax.fori_loop(2, 4, ffn(2), 0)
    offer(4)
    offer(5)
    wloads = [
        pltpu.make_async_copy(src, v2.at[i * width : i * width + width], w_sem.at[i])
        for i, src in enumerate((wo, wq, wk, wv))
    ]
    for cp in wloads:
        cp.start()
    slot(3)
    for i in range(9, 17):
        loads[i].wait()

    def norm1(i, carry):
        gain_sum, shift_sum, bias_sum = carry
        r = tiles(i, 64)
        dh = acc[r, :]
        xhat = x1s[r, :]
        back = standard_back(dh * g1[0:1, :].astype(F32), xhat, r1s[r, 0:1])
        acc[r, :] = back
        low = back.astype(BF)
        df[r, :] = low
        return (gain_sum + row_sum(dh * xhat), shift_sum + row_sum(dh), bias_sum + row_sum(low.astype(F32)))

    sums = lax.fori_loop(0, rows // 64, norm1, (zero, zero, zero))
    vecs[3:4, :], vecs[4:5, :], vecs[2:3, :] = sums
    ht[...] = os_[...].T

    def weights(at, rhs):
        def body(t, carry):
            lanes = tiles(t)
            back = dot(ht[...], rhs[:, lanes]).astype(BF)
            for i in range(4):
                g_mats[at, i, :, lanes] = back[i * share : i * share + share]
            return carry

        lax.fori_loop(0, nt, body, 0)

    weights(3, df)
    offer(6)
    slot(4)
    wloads[0].wait()

    def mixed(t, carry):
        lanes = tiles(t)
        ds_[:, lanes] = dot_nt(df[...], v2[lanes, :]).astype(BF)
        return carry

    lax.fori_loop(0, nt, mixed, 0)
    masks = head_masks()

    def attend(hp, carry):
        lanes = tiles(hp, 128)
        for j in range(segs):
            here = slice(j * 128, j * 128 + 128)
            qs, ks, vs, dos = qs_[here, lanes], ks_[here, lanes], vs_[here, lanes], ds_[here, lanes]
            dqs = dks = dvs = 0.0
            for h in range(2):
                pl_ = p_s[hp, j, h]
                pf = pl_.astype(F32)
                dom = dos * masks[h]
                dp = dot_nt(dom, vs).astype(BF).astype(F32)
                ds = (pf * (dp - jnp.sum(pf * dp, axis=-1, keepdims=True))).astype(BF)
                dqs += dot(ds, ks * masks[h])
                dks += dot_tn(ds, qs * masks[h])
                dvs += dot_tn(pl_, dom)
            qs_[here, lanes] = (dqs * 0.125).astype(BF)
            ks_[here, lanes] = (dks * 0.125).astype(BF)
            vs_[here, lanes] = dvs.astype(BF)
        return carry

    lax.fori_loop(0, 3, attend, 0)
    slot(5)
    lax.fori_loop(3, width // 128, attend, 0)
    vecs[0:1, :] = row_sum(qs_[...].astype(F32))
    vecs[1:2, :] = row_sum(vs_[...].astype(F32))
    ht[...] = xs[...].T
    weights(0, qs_)
    offer(7)
    slot(6)
    weights(1, ks_)
    offer(8)
    weights(2, vs_)
    offer(9)
    hops = [(dev, other), (first, s), (second, s), (dev, znear), (dev, zfar)]
    vsum[0] = vecs[...]

    def vector_hop(j):
        if j > 0:
            arrived(vgot.at[j - 1], vrcv.at[j - 1])
            vsum[j] = vsum[j - 1] + vgot[j - 1]
        if j < 5:
            go(remote(vsum.at[j], vgot.at[j], vsend.at[j], vrcv.at[j], hops[j]))

    slot(7)
    vector_hop(0)
    for i in range(1, 4):
        wloads[i].wait()

    def source(t, carry):
        r = tiles(t)
        dx = acc[:, r]
        for i, g in enumerate((qs_, ks_, vs_)):
            dx += dot_nt(g[...], v2[pl.ds(pl.multiple_of((i + 1) * width + t * TILE, TILE), TILE), :])
        xs[:, r] = dx.astype(BF)
        return carry

    lax.fori_loop(0, nt, source, 0)
    results.append(pltpu.make_async_copy(xs, dx_o, res_sem.at[1]))
    results[1].start()
    for i in range(8, nc + 8):
        slot(i)
        if i < 13:
            vector_hop(i - 7)
    vec_o[...] = vsum[5]
    for cp in started:
        cp.wait_send()
    for cp in outs + results:
        cp.wait()


def backward(x, cot, dcl, saved, y, z, weights, g1, g2, collective_id):
    q, k, v, p, o, hb, e, gp, x1, r1, x2, r2 = saved
    rows, width = x.shape
    ff = weights[4].shape[1]
    share, nc = width // 4, len(CHUNKS)
    S, VM, dma = jax.ShapeDtypeStruct, pltpu.VMEM, pltpu.SemaphoreType.DMA
    V = pl.BlockSpec(memory_space=pltpu.VMEM)
    arrays = (x, cot, q, k, v, p, o, hb, e, gp, x1, r1, x2, r2, y)

    def chunk(n, r, w):
        return [VM(t, BF) for t in ((n, 4, r, w), (n, 2, r, w), (n, r, w), (n, r // 2, w), (n, r // 4, w), (2, n, r, w))]

    return pl.pallas_call(
        backward_kernel,
        out_shape=[
            S((rows, width), BF), S((rows, width), BF), S((ff // 4, width), BF), S((share, ff), BF), S((4, share, width), BF),
            S((16, width), F32),
        ],
        in_specs=[V] * 4 + [ANY] * 21,
        out_specs=[ANY] * 5 + [V],
        scratch_shapes=[VM(t.shape, t.dtype) for t in arrays]
        + [
            VM((width, ff), BF), VM((ff, width), BF), VM((rows, width), BF), VM((width, rows), BF), VM((16, width), F32),
            VM((4, ff // 4, width), BF), VM((3, 4, share, ff // 3), BF), VM((4, 4, share, width), BF),
        ]
        + chunk(3, 128, width) + chunk(3, share, ff // 6) + chunk(4, share, width // 2)
        + [
            dma((17,)), dma((4,)), dma((2,)), dma((2, 2, nc)),
            VM((6, 16, width), F32), VM((5, 16, width), F32), dma((5,)), dma((5,)), dma((9, nc)), dma((9, nc)),
        ],
        compiler_params=pltpu.CompilerParams(collective_id=collective_id, has_side_effects=True, vmem_limit_bytes=67043328),
        name="backward_reduce",
    )(dcl, z, g1, g2, *arrays, *weights)


def cross_kernel(cls, emb, docs, cot, wq, wk, wv, wi, out_w, outer_w,
                 qb, vb, ob, g1, c1, ib, b2, g2, c2,
                 z_o, dcl_o, xw_o, hw_o, ow_o, e_o, dqkv_o, du_o, da_o, df_o, vec_o, emb_o,
                 vq, vk, vv, vi, vo, v2, heads, xall, rows_s, p_s, dqkv_s, du_s, send1, got1, send2, got2,
                 in_sem, all_send, all_recv, first_rows, cots, cot_all, row_sem, cot_send, cot_recv, s1, r1, s2, r2, qs_send, qs_recv, us_send, us_recv, o_sem):
    d, s = place()
    c, first, second, other = plane_peers(d, s)
    start, off = window(d)
    me, ahead, behind = everyone(d, s)
    far = [3 - d, first, second]
    lane_w = pl.ds(start, 256)
    loads = [
        pltpu.make_async_copy(src, dst, in_sem.at[i])
        for i, (src, dst) in enumerate(
            (
                (wq, vq), (wk, vk), (wv, vv),
                (out_w.at[1], vo.at[pl.ds(pl.multiple_of(off, 64), 192)]),
                (wi, vi), (outer_w.at[1], v2),
            )
        )
    ]
    for cp in loads:
        cp.start()
    row_loads = [pltpu.make_async_copy(cot.at[0, pl.ds(i * 128, 8)], first_rows.at[i], row_sem.at[i]) for i in range(4)]
    for cp in row_loads:
        cp.start()
    vo[pl.ds(pl.multiple_of(192 * (1 - d % 2), 64), 64), :] = jnp.zeros((64, 768), BF)
    pick = lax.broadcasted_iota(jnp.int32, (8, 32), 0) + 4 * s == lax.broadcasted_iota(jnp.int32, (8, 32), 1)
    position = dot(pick.astype(BF), emb[...])
    heads[...] = (cls[...] + position[0:4]).astype(BF)
    greet([(i // 8, i % 8) for i in ahead])
    sent = []
    for j, i in enumerate(ahead):
        cp = remote(heads, xall.at[me], all_send.at[j], all_recv.at[j], (i // 8, i % 8))
        cp.start()
        sent.append(cp)
    xall[me] = heads[...]
    for cp in row_loads:
        cp.wait()
    cots[...] = jnp.concatenate([first_rows[i].astype(F32)[0:1] for i in range(4)], axis=0).astype(BF)
    for j, i in enumerate(ahead):
        cp = remote(cots, cot_all.at[me], cot_send.at[j], cot_recv.at[j], (i // 8, i % 8))
        cp.start()
        sent.append(cp)
    cot_all[me] = cots[...]
    ids = lax.broadcasted_iota(jnp.int32, (8, 128), 1) // 32 * 1024
    ids = ids.astype(F32)
    lane = lax.broadcasted_iota(jnp.int32, (32, 128), 1)
    key = lax.broadcasted_iota(jnp.int32, (32, 128), 0)
    for r in range(4):
        numbers = jnp.broadcast_to(docs[r], (8, 32)).astype(F32).astype(BF)
        ids = ids + dot(numbers, (lane == key + 32 * r).astype(BF))
    across = jnp.broadcast_to(ids[0:1], (128, 128))
    allowed = across == across.T
    for j, i in enumerate(behind):
        remote(heads, xall.at[i], all_send.at[j], all_recv.at[j], (i // 8, i % 8)).wait_recv()
    for i in range(32):
        rows_s[4 * i : 4 * i + 4, :] = xall[i].astype(F32)
    xf = rows_s[...]
    x = xf.astype(BF)

    def total(n, partial):
        send1[n] = partial.astype(BF)
        one = remote(send1.at[n], got1.at[n], s1.at[n], r1.at[n], (first, s))
        one.start()
        one.wait_recv()
        both = send1[n].astype(F32) + got1[n].astype(F32)
        send2[n] = both.astype(BF)
        two = remote(send2.at[n], got2.at[n], s2.at[n], r2.at[n], (second, s))
        two.start()
        two.wait_recv()
        sent.append(one)
        sent.append(two)
        return send2[n].astype(F32) + got2[n].astype(F32)

    def vector(ref, lanes=slice(None)):
        return ref[1:2, lanes].astype(F32)

    for i in range(3):
        loads[i].wait()
    q = (dot(x, vq[...]) + vector(qb, lane_w)).astype(BF)
    k = dot(x, vk[...]).astype(BF)
    v = (dot(x, vv[...]) + vector(vb, lane_w)).astype(BF)
    masks = head_masks()
    mixed = []
    for pair in range(2):
        l = slice(pair * 128, pair * 128 + 128)
        both = None
        for h in range(2):
            scores = jnp.where(allowed, dot_nt(q[:, l] * masks[h], k[:, l]) * 0.125, -1e30)
            weight = jnp.exp(scores - jnp.max(scores, axis=-1, keepdims=True))
            share = (weight * (1.0 / jnp.sum(weight, axis=-1, keepdims=True))).astype(BF)
            p_s[2 * pair + h] = share
            part = dot(share, v[:, l] * masks[h])
            both = part if both is None else both + part
        mixed.append(both.astype(BF))
    loads[3].wait()
    ow = jnp.concatenate(mixed, axis=1)
    ow_o[...] = ow
    branch = total(0, dot(ow, vo[...]))
    xhat1, rstd1 = standard(xf + branch + vector(ob))
    hidden = xhat1 * vector(g1) + vector(c1)
    hb = hidden.astype(BF)
    rows_s[...] = hidden
    hw_o[...] = rows_s[:, lane_w].astype(BF)
    rows_s[...] = xf
    xw_o[...] = rows_s[:, lane_w].astype(BF)
    loads[4].wait()
    loads[5].wait()
    wide = pl.ds(pl.multiple_of(d * 768, 768), 768)
    e, gp = gelu_parts(dot(hb, vi[...]) + vector(ib, wide))
    e = e.astype(BF)
    e_o[...] = e
    outer = total(1, dot(e, v2[...]))
    xhat2, rstd2 = standard(hidden + outer + vector(b2))
    z = (xhat2 * vector(g2) + vector(c2)).astype(BF)
    own = lax.broadcasted_iota(jnp.int32, (8, 128), 0) + 4 * me == lax.broadcasted_iota(jnp.int32, (8, 128), 1)
    own = own.astype(BF)
    z_o[...] = dot(own, z)
    for j, i in enumerate(behind):
        remote(cots, cot_all.at[i], cot_send.at[j], cot_recv.at[j], (i // 8, i % 8)).wait_recv()
    for i in range(32):
        rows_s[4 * i : 4 * i + 4, :] = cot_all[i].astype(F32)
    dy = rows_s[...]
    vec_o[6:7, :] = row_sum(dy * xhat2)
    vec_o[7:8, :] = row_sum(dy)
    dr2 = standard_back(dy * vector(g2), xhat2, rstd2)
    df = dr2.astype(BF)
    df_o[...] = df
    vec_o[5:6, :] = row_sum(df.astype(F32))
    du = (dot_nt(df, v2[...]).astype(BF).astype(F32) * gp).astype(BF)
    du_s[d] = du
    dh = dr2 + total(2, dot_nt(du, vi[...]))
    for n, peer in enumerate(far):
        cp = remote(du_s.at[d], du_s.at[d], us_send.at[n], us_recv.at[n], (peer, s))
        cp.start()
        sent.append(cp)
    vec_o[3:4, :] = row_sum(dh * xhat1)
    vec_o[4:5, :] = row_sum(dh)
    dr1 = standard_back(dh * vector(g1), xhat1, rstd1)
    da = dr1.astype(BF)
    da_o[...] = da
    vec_o[2:3, :] = row_sum(da.astype(F32))
    do = dot_nt(da, vo[...]).astype(BF)
    dqs, dks, dvs = [], [], []
    for pair in range(2):
        l = slice(pair * 128, pair * 128 + 128)
        dqp = dkp = dvp = 0.0
        for h in range(2):
            share = p_s[2 * pair + h]
            pf = share.astype(F32)
            dom = do[:, l] * masks[h]
            dp = dot_nt(dom, v[:, l]).astype(BF).astype(F32)
            ds = (pf * (dp - jnp.sum(pf * dp, axis=-1, keepdims=True))).astype(BF)
            dqp += dot(ds, k[:, l] * masks[h])
            dkp += dot_tn(ds, q[:, l] * masks[h])
            dvp += dot_tn(share, dom)
        dqs.append((dqp * 0.125).astype(BF))
        dks.append((dkp * 0.125).astype(BF))
        dvs.append(dvp.astype(BF))
    dq, dk, dv = (jnp.concatenate(t, axis=1) for t in (dqs, dks, dvs))
    dqkv_s[d, :, 0:256] = dq
    dqkv_s[d, :, 256:512] = dk
    dqkv_s[d, :, 512:768] = dv
    dx = dr1 + total(3, dot_nt(dq, vq[...]) + dot_nt(dk, vk[...]) + dot_nt(dv, vv[...]))
    for n, peer in enumerate(far):
        cp = remote(dqkv_s.at[d], dqkv_s.at[d], qs_send.at[n], qs_recv.at[n], (peer, s))
        cp.start()
        sent.append(cp)
    dcl = dx.astype(BF)
    dcl_o[...] = dot(own, dcl)
    back = dcl.astype(F32)
    emb_o[...] = back[0:32] + back[32:64] + back[64:96] + back[96:128]
    for n, peer in enumerate(far):
        remote(du_s.at[peer], du_s.at[peer], us_send.at[n], us_recv.at[n], (peer, s)).wait_recv()
        remote(dqkv_s.at[peer], dqkv_s.at[peer], qs_send.at[n], qs_recv.at[n], (peer, s)).wait_recv()
    outs = [pltpu.make_async_copy(du_s, du_o, o_sem.at[0]), pltpu.make_async_copy(dqkv_s, dqkv_o, o_sem.at[1])]
    for cp in outs:
        cp.start()
    for cp in sent:
        cp.wait_send()
    for cp in outs:
        cp.wait()


def cross(cls, emb, cot, docs, wq, wk, wv, wi, out_w, outer_w, vectors, collective_id):
    S = jax.ShapeDtypeStruct
    V = pl.BlockSpec(memory_space=pltpu.VMEM)
    VM, dma = pltpu.VMEM, pltpu.SemaphoreType.DMA
    low, win, four = S((128, 768), BF), S((128, 256), BF), S((4, 128, 768), BF)
    return pl.pallas_call(
        cross_kernel,
        out_shape=[
            S((8, 768), F32), S((8, 768), F32), win, win, win, low, four, four, low, low,
            S((8, 768), F32), S((32, 768), F32),
        ],
        in_specs=[V] * 3 + [ANY] * 7 + [V] * 9,
        out_specs=[V] * 6 + [ANY] * 2 + [V] * 4,
        scratch_shapes=[
            VM((768, 256), BF), VM((768, 256), BF), VM((768, 256), BF), VM((768, 768), BF), VM((256, 768), BF), VM((768, 768), BF),
            VM((4, 768), BF), VM((32, 4, 768), BF), VM((128, 768), F32), VM((4, 128, 128), BF),
            VM((4, 128, 768), BF), VM((4, 128, 768), BF),
            VM((4, 128, 768), BF), VM((4, 128, 768), BF), VM((4, 128, 768), BF), VM((4, 128, 768), BF),
            dma((6,)), dma((31,)), dma((31,)),
            VM((4, 8, 768), BF), VM((4, 768), BF), VM((32, 4, 768), BF), dma((4,)), dma((31,)), dma((31,)),
            dma((4,)), dma((4,)), dma((4,)), dma((4,)), dma((3,)), dma((3,)), dma((3,)), dma((3,)), dma((2,)),
        ],
        compiler_params=pltpu.CompilerParams(collective_id=collective_id, has_side_effects=True, vmem_limit_bytes=67043328),
        name="cross_block",
    )(cls, emb, docs, cot, wq, wk, wv, wi, out_w, outer_w, *vectors)


def finish_kernel(dx, y, outer, inner, mats, vec, emb, xw, hw, ow, e, dqkv, du, da, df, vec1,
                  y_o, dx_o, gq, gqb, gk, gv, gvb, go, gob, gg1, gc1, gi, gib, g2_, gb2, gg2, gc2, gemb,
                  vec_s, pass_s, pass_in, pass_out):
    moves = [pltpu.make_async_copy(src, pass_s.at[i], pass_in.at[i]) for i, src in enumerate((y, dx))]
    for cp in moves:
        cp.start()
    leaves = []
    for i, dst in enumerate((y_o, dx_o)):
        moves[i].wait()
        cp = pltpu.make_async_copy(pass_s.at[i], dst, pass_out.at[i])
        cp.start()
        leaves.append(cp)
    d = lax.axis_index("dp")
    odd = d % 2 == 1
    start, _ = window(d)

    def own(w):
        return jnp.where(odd, w[:, 64:256], w[:, 0:192])

    def whole(at):
        parts = [dqkv[i, :, at * 256 : at * 256 + 256] for i in range(4)]
        return jnp.concatenate(
            [
                parts[0][:, :128], parts[0][:, 128:] + parts[1][:, :128], parts[1][:, 128:],
                parts[2][:, :128], parts[2][:, 128:] + parts[3][:, :128], parts[3][:, 128:],
            ],
            axis=1,
        )

    x, h, o = own(xw[...].astype(F32)).astype(BF), own(hw[...].astype(F32)).astype(BF), own(ow[...].astype(F32)).astype(BF)
    dq, dk, dv = whole(0), whole(1), whole(2)
    for at, (out, left, right) in enumerate(((gq, x, dq), (gk, x, dk), (gv, x, dv), (go, o, da[...]))):
        out[0] = mats[at].astype(F32)
        out[1] = dot_tn(left, right)
    for j in range(4):
        l = slice(j * 768, j * 768 + 768)
        gi[0, :, l] = inner[:, l].astype(F32)
        gi[1, :, l] = dot_tn(h, du[j])
    g2_[0] = outer[...].astype(F32)
    g2_[1] = dot_tn(e[...], df[...])
    lanes = pl.ds(start, 256)
    mine = own(vec[:, lanes])
    vec_s[...] = vec1[...]
    vec_s[0:1, :] = row_sum(dq.astype(F32))
    vec_s[1:2, :] = row_sum(dv.astype(F32))
    cross = own(vec_s[:, lanes])
    for r, out in enumerate((gqb, gvb, gob, gg1, gc1, gb2, gg2, gc2)):
        out[0:1, :] = mine[r : r + 1]
        out[1:2, :] = cross[r : r + 1]
    gib[0:1, :] = vec[pl.ds(8 + d, 1), :]
    gib[1:2, :] = row_sum(du[d].astype(F32))
    gemb[...] = own(emb[:, lanes])
    for cp in leaves:
        cp.wait()


def finish(summed, crossed):
    (_, _, xw, hw, ow, e, dqkv, du, da, df, vec1, emb) = crossed
    S = jax.ShapeDtypeStruct
    V = pl.BlockSpec(memory_space=pltpu.VMEM)
    square, line = S((2, 192, 768), F32), S((2, 192), F32)
    dx, y, outer, inner, mats, vec = summed
    return pl.pallas_call(
        finish_kernel,
        out_shape=[
            S(y.shape, BF), S(dx.shape, BF),
            square, line, square, square, line, square, line, line, line,
            S((2, 192, 3072), F32), S((2, 768), F32), S((2, 768, 768), F32), line, line, line, S((32, 192), F32),
        ],
        in_specs=[ANY] * 2 + [V] * 14,
        out_specs=[ANY] * 2 + [V] * 16,
        scratch_shapes=[pltpu.VMEM((8, 768), F32), pltpu.VMEM((2,) + y.shape, BF), pltpu.SemaphoreType.DMA((2,)), pltpu.SemaphoreType.DMA((2,))],
        compiler_params=pltpu.CompilerParams(vmem_limit_bytes=67043328),
        name="finish_grads",
    )(dx, y, outer, inner, mats, vec, emb, xw, hw, ow, e, dqkv, du, da, df, vec1)


def fast_shards(
    inputs,
    doc_ids,
    cotangent,
    query_weight,
    query_bias,
    key_weight,
    value_weight,
    value_bias,
    out_weight,
    out_bias,
    first_gain,
    first_shift,
    inner_weight,
    inner_bias,
    outer_weight,
    outer_bias,
    second_gain,
    second_shift,
    segment_embed,
):
    weights = (query_weight, key_weight, value_weight, out_weight, inner_weight, outer_weight)
    vectors = (query_bias, value_bias, out_bias, first_gain, first_shift, inner_bias, outer_bias, second_gain, second_shift)
    full, windows, docs, saved, y, cls = start(inputs[0], weights, doc_ids, vectors, 1)
    windows = [w.reshape(-1, w.shape[-1]) for w in windows]
    crossed = cross(cls, segment_embed, cotangent, docs, *windows, out_weight, outer_weight, vectors, 2)
    summed = backward(
        inputs[0], cotangent[0], crossed[1], saved, y, crossed[0], full, first_gain, second_gain, 3
    )
    output, grad, *gradients = finish(summed, crossed)
    return (output[None], grad[None], *gradients)


def solution(mesh):
    placed = (
        P("dp", "seg", None),
        P("dp", None),
        P("dp", "seg", None),
        P(None, "dp", None),
        P(),
        P(None, "dp", None),
        P(None, "dp", None),
        P(),
        P(None, "dp", None),
        P(),
        P(),
        P(),
        P(None, "dp", None),
        P(),
        P(None, "dp", None),
        P(),
        P(),
        P(),
        P(),
    )
    square = mesh.shape["dp"] == 4 and mesh.shape["seg"] == 8
    return jax.shard_map(
        fast_shards if square else shards,
        mesh=mesh,
        in_specs=placed,
        out_specs=(
            P("dp", "seg", None),
            P("dp", "seg", None),
            P(None, "dp", None),
            P(None, "dp"),
            P(None, "dp", None),
            P(None, "dp", None),
            P(None, "dp"),
            P(None, "dp", None),
            P(None, "dp"),
            P(None, "dp"),
            P(None, "dp"),
            P(None, "dp", None),
            P(None, "dp"),
            P(None, "dp", None),
            P(None, "dp"),
            P(None, "dp"),
            P(None, "dp"),
            P(None, "dp"),
        ),
        check_vma=False,
    )
```

```python
import functools

import jax
import jax.numpy as jnp
from jax import lax
from jax.experimental import pallas as pl
from jax.experimental.pallas import tpu as pltpu
from jax.sharding import PartitionSpec as P

HEADS = 12
HEAD_DIM = 64
SEG_LEN = 128


epsilon = 1e-05


def normalize(values, gain, shift):
    centred = values - jnp.mean(values, axis=-1, keepdims=True)
    spread = jnp.mean(centred * centred, axis=-1, keepdims=True)
    return centred * lax.rsqrt(spread + epsilon) * gain + shift


def gelu_exact(values):
    return jax.nn.gelu(values, approximate=False)


def project(values, weight):
    return jnp.einsum("gnd,de->gne", values, weight, preferred_element_type=jnp.float32)


def back_project(values, weight):
    return jnp.einsum("gne,de->gnd", values, weight, preferred_element_type=jnp.float32)


def weight_grad(source, grads):
    return jnp.einsum("gnd,gne->de", source, grads, preferred_element_type=jnp.float32)


def row_total(values):
    return jnp.sum(values.astype(jnp.float32), axis=(0, 1))


def keep_pair(first_part, second_part):
    return (first_part, second_part)


def forward_layer(params, source, allowed, spread_keys):
    (
        query_weight,
        query_bias,
        key_weight,
        value_weight,
        value_bias,
        out_weight,
        out_bias,
        first_gain,
        first_shift,
        inner_weight,
        inner_bias,
        outer_weight,
        outer_bias,
        second_gain,
        second_shift,
    ) = params
    groups, length, width = source.shape
    queries = (project(source, query_weight) + query_bias.astype(jnp.float32)).astype(jnp.bfloat16)
    key_rows = project(source, key_weight).astype(jnp.bfloat16)
    value_rows = (project(source, value_weight) + value_bias.astype(jnp.float32)).astype(
        jnp.bfloat16
    )
    key_all, value_all = spread_keys(key_rows, value_rows)
    key_length = key_all.shape[1]
    query_heads = queries.reshape(groups, length, HEADS, HEAD_DIM)
    key_heads = key_all.reshape(groups, key_length, HEADS, HEAD_DIM)
    value_heads = value_all.reshape(groups, key_length, HEADS, HEAD_DIM)
    scores = (
        jnp.einsum("gqhe,gkhe->ghqk", query_heads, key_heads, preferred_element_type=jnp.float32)
        * 0.125
    )
    if allowed is not None:
        scores = jnp.where(allowed[:, None], scores, -1e30)
    attend = jax.nn.softmax(scores, axis=-1)
    attend_low = attend.astype(jnp.bfloat16)
    mixed = jnp.einsum(
        "ghqk,gkhe->gqhe", attend_low, value_heads, preferred_element_type=jnp.float32
    )
    mixed = mixed.astype(jnp.bfloat16).reshape(groups, length, width)
    branch = project(mixed, out_weight) + out_bias.astype(jnp.float32)
    hidden, first_pull = jax.vjp(
        normalize,
        source.astype(jnp.float32) + branch,
        first_gain.astype(jnp.float32),
        first_shift.astype(jnp.float32),
    )
    hidden_low = hidden.astype(jnp.bfloat16)
    inner = project(hidden_low, inner_weight) + inner_bias.astype(jnp.float32)
    active, gelu_pull = jax.vjp(gelu_exact, inner)
    active_low = active.astype(jnp.bfloat16)
    outer = project(active_low, outer_weight) + outer_bias.astype(jnp.float32)
    result, second_pull = jax.vjp(
        normalize, hidden + outer, second_gain.astype(jnp.float32), second_shift.astype(jnp.float32)
    )
    stored = (
        source,
        query_heads,
        key_heads,
        value_heads,
        attend,
        attend_low,
        mixed,
        first_pull,
        hidden_low,
        gelu_pull,
        active_low,
        second_pull,
    )
    return (result, stored)


def backward_layer(params, stored, grad_result, collect_keys):
    (
        query_weight,
        query_bias,
        key_weight,
        value_weight,
        value_bias,
        out_weight,
        out_bias,
        first_gain,
        first_shift,
        inner_weight,
        inner_bias,
        outer_weight,
        outer_bias,
        second_gain,
        second_shift,
    ) = params
    (
        source,
        query_heads,
        key_heads,
        value_heads,
        attend,
        attend_low,
        mixed,
        first_pull,
        hidden_low,
        gelu_pull,
        active_low,
        second_pull,
    ) = stored
    groups, length, width = source.shape
    key_length = key_heads.shape[1]
    grad_second_sum, grad_second_gain, grad_second_shift = second_pull(grad_result)
    grad_outer = grad_second_sum.astype(jnp.bfloat16)
    grad_outer_bias = row_total(grad_outer)
    grad_outer_weight = weight_grad(active_low, grad_outer)
    grad_active = back_project(grad_outer, outer_weight).astype(jnp.bfloat16)
    (grad_inner,) = gelu_pull(grad_active.astype(jnp.float32))
    grad_inner_low = grad_inner.astype(jnp.bfloat16)
    grad_inner_bias = row_total(grad_inner_low)
    grad_inner_weight = weight_grad(hidden_low, grad_inner_low)
    grad_hidden = grad_second_sum + back_project(grad_inner_low, inner_weight)
    grad_first_sum, grad_first_gain, grad_first_shift = first_pull(grad_hidden)
    grad_branch = grad_first_sum.astype(jnp.bfloat16)
    grad_out_bias = row_total(grad_branch)
    grad_out_weight = weight_grad(mixed, grad_branch)
    grad_mixed = back_project(grad_branch, out_weight).astype(jnp.bfloat16)
    grad_mixed = grad_mixed.reshape(groups, length, HEADS, HEAD_DIM)
    grad_attend = jnp.einsum(
        "gqhe,gkhe->ghqk", grad_mixed, value_heads, preferred_element_type=jnp.float32
    )
    grad_attend = grad_attend.astype(jnp.bfloat16).astype(jnp.float32)
    grad_value = jnp.einsum(
        "ghqk,gqhe->gkhe", attend_low, grad_mixed, preferred_element_type=jnp.float32
    )
    grad_value = grad_value.reshape(groups, key_length, width)
    grad_scores = attend * (grad_attend - jnp.sum(attend * grad_attend, axis=-1, keepdims=True))
    grad_scores = grad_scores.astype(jnp.bfloat16)
    grad_query = (
        jnp.einsum("ghqk,gkhe->gqhe", grad_scores, key_heads, preferred_element_type=jnp.float32)
        * 0.125
    )
    grad_query = grad_query.astype(jnp.bfloat16).reshape(groups, length, width)
    grad_key = (
        jnp.einsum("ghqk,gqhe->gkhe", grad_scores, query_heads, preferred_element_type=jnp.float32)
        * 0.125
    )
    grad_key = grad_key.reshape(groups, key_length, width)
    grad_key, grad_value = collect_keys(grad_key, grad_value)
    grad_key = grad_key.astype(jnp.bfloat16)
    grad_value = grad_value.astype(jnp.bfloat16)
    grad_source = (
        grad_first_sum
        + back_project(grad_query, query_weight)
        + back_project(grad_key, key_weight)
        + back_project(grad_value, value_weight)
    )
    gradients = (
        weight_grad(source, grad_query),
        row_total(grad_query),
        weight_grad(source, grad_key),
        weight_grad(source, grad_value),
        row_total(grad_value),
        grad_out_weight,
        grad_out_bias,
        grad_first_gain,
        grad_first_shift,
        grad_inner_weight,
        grad_inner_bias,
        grad_outer_weight,
        grad_outer_bias,
        grad_second_gain,
        grad_second_shift,
    )
    return (grad_source, gradients)


def shards(
    inputs,
    doc_ids,
    cotangent,
    query_weight,
    query_bias,
    key_weight,
    value_weight,
    value_bias,
    out_weight,
    out_bias,
    first_gain,
    first_shift,
    inner_weight,
    inner_bias,
    outer_weight,
    outer_bias,
    second_gain,
    second_shift,
    segment_embed,
):
    seg_count = lax.axis_size("seg")
    seg_index = lax.axis_index("seg")
    group_rows, local_length, width = inputs.shape
    seg_local = local_length // SEG_LEN
    query_full, key_full, value_full, out_full, inner_full, outer_full = (
        lax.all_gather(query_weight, "dp", axis=1, tiled=True),
        lax.all_gather(key_weight, "dp", axis=1, tiled=True),
        lax.all_gather(value_weight, "dp", axis=1, tiled=True),
        lax.all_gather(out_weight, "dp", axis=1, tiled=True),
        lax.all_gather(inner_weight, "dp", axis=1, tiled=True),
        lax.all_gather(outer_weight, "dp", axis=1, tiled=True),
    )
    stacked = (
        query_full,
        query_bias,
        key_full,
        value_full,
        value_bias,
        out_full,
        out_bias,
        first_gain,
        first_shift,
        inner_full,
        inner_bias,
        outer_full,
        outer_bias,
        second_gain,
        second_shift,
    )
    first_params = tuple((weight[0] for weight in stacked))
    cross_params = tuple((weight[1] for weight in stacked))
    pieces = inputs.reshape(group_rows * seg_local, SEG_LEN, width)
    segment_out, segment_stored = forward_layer(first_params, pieces, None, keep_pair)
    segment_grid = segment_out.reshape(group_rows, seg_local, SEG_LEN, width)
    position = lax.dynamic_slice_in_dim(segment_embed, seg_index * seg_local, seg_local, 0).astype(
        jnp.float32
    )
    heads_in = (segment_grid[:, :, 0, :] + position).astype(jnp.bfloat16)
    row_input = lax.all_gather(heads_in, "seg", axis=1, tiled=True)
    allowed = doc_ids[:, :, None] == doc_ids[:, None, :]
    cross_out, cross_stored = forward_layer(cross_params, row_input, allowed, keep_pair)
    returned = lax.dynamic_slice_in_dim(cross_out, seg_index * seg_local, seg_local, 1).astype(
        jnp.bfloat16
    )
    output = jnp.concatenate(
        [returned[:, :, None, :], segment_grid[:, :, 1:, :].astype(jnp.bfloat16)], axis=2
    )
    output = output.reshape(group_rows, local_length, width)
    cot_grid = cotangent.reshape(group_rows, seg_local, SEG_LEN, width)
    cot_heads = cot_grid[:, :, 0, :]
    grad_cross = lax.all_gather(cot_heads, "seg", axis=1, tiled=True)
    grad_row_input, cross_grads = backward_layer(
        cross_params, cross_stored, grad_cross.astype(jnp.float32), keep_pair
    )
    grad_row_low = grad_row_input.astype(jnp.bfloat16)
    factor = 1.0 / seg_count
    embed_grad = jnp.sum(grad_row_low.astype(jnp.float32), axis=0) * factor
    cross_grads = tuple((part * factor for part in cross_grads))
    grad_heads = lax.dynamic_slice_in_dim(grad_row_low, seg_index * seg_local, seg_local, 1)
    grad_grid = jnp.concatenate(
        [grad_heads[:, :, None, :].astype(jnp.float32), cot_grid[:, :, 1:, :].astype(jnp.float32)],
        axis=2,
    )
    grad_grid = grad_grid.reshape(group_rows * seg_local, SEG_LEN, width)
    grad_pieces, segment_grads = backward_layer(first_params, segment_stored, grad_grid, keep_pair)
    input_grad = grad_pieces.astype(jnp.bfloat16).reshape(group_rows, local_length, width)
    shares = (
        lax.psum_scatter(segment_grads[0], "dp", scatter_dimension=0, tiled=True),
        lax.psum_scatter(segment_grads[1], "dp", scatter_dimension=0, tiled=True),
        lax.psum_scatter(segment_grads[2], "dp", scatter_dimension=0, tiled=True),
        lax.psum_scatter(segment_grads[3], "dp", scatter_dimension=0, tiled=True),
        lax.psum_scatter(segment_grads[4], "dp", scatter_dimension=0, tiled=True),
        lax.psum_scatter(segment_grads[5], "dp", scatter_dimension=0, tiled=True),
        lax.psum_scatter(segment_grads[6], "dp", scatter_dimension=0, tiled=True),
        lax.psum_scatter(segment_grads[7], "dp", scatter_dimension=0, tiled=True),
        lax.psum_scatter(segment_grads[8], "dp", scatter_dimension=0, tiled=True),
        lax.psum_scatter(segment_grads[9], "dp", scatter_dimension=0, tiled=True),
        lax.psum_scatter(segment_grads[10], "dp", scatter_dimension=0, tiled=True),
        lax.psum_scatter(segment_grads[11], "dp", scatter_dimension=0, tiled=True),
        lax.psum_scatter(segment_grads[12], "dp", scatter_dimension=0, tiled=True),
        lax.psum_scatter(segment_grads[13], "dp", scatter_dimension=0, tiled=True),
        lax.psum_scatter(segment_grads[14], "dp", scatter_dimension=0, tiled=True),
        lax.psum_scatter(cross_grads[0], "dp", scatter_dimension=0, tiled=True),
        lax.psum_scatter(cross_grads[1], "dp", scatter_dimension=0, tiled=True),
        lax.psum_scatter(cross_grads[2], "dp", scatter_dimension=0, tiled=True),
        lax.psum_scatter(cross_grads[3], "dp", scatter_dimension=0, tiled=True),
        lax.psum_scatter(cross_grads[4], "dp", scatter_dimension=0, tiled=True),
        lax.psum_scatter(cross_grads[5], "dp", scatter_dimension=0, tiled=True),
        lax.psum_scatter(cross_grads[6], "dp", scatter_dimension=0, tiled=True),
        lax.psum_scatter(cross_grads[7], "dp", scatter_dimension=0, tiled=True),
        lax.psum_scatter(cross_grads[8], "dp", scatter_dimension=0, tiled=True),
        lax.psum_scatter(cross_grads[9], "dp", scatter_dimension=0, tiled=True),
        lax.psum_scatter(cross_grads[10], "dp", scatter_dimension=0, tiled=True),
        lax.psum_scatter(cross_grads[11], "dp", scatter_dimension=0, tiled=True),
        lax.psum_scatter(cross_grads[12], "dp", scatter_dimension=0, tiled=True),
        lax.psum_scatter(cross_grads[13], "dp", scatter_dimension=0, tiled=True),
        lax.psum_scatter(cross_grads[14], "dp", scatter_dimension=0, tiled=True),
        lax.psum_scatter(embed_grad, "dp", scatter_dimension=1, tiled=True),
    )
    summed = lax.psum(
        (
            shares[0],
            shares[1],
            shares[2],
            shares[3],
            shares[4],
            shares[5],
            shares[6],
            shares[7],
            shares[8],
            shares[9],
            shares[10],
            shares[11],
            shares[12],
            shares[13],
            shares[14],
            shares[15],
            shares[16],
            shares[17],
            shares[18],
            shares[19],
            shares[20],
            shares[21],
            shares[22],
            shares[23],
            shares[24],
            shares[25],
            shares[26],
            shares[27],
            shares[28],
            shares[29],
            shares[30],
        ),
        "seg",
    )
    totals = tuple((jnp.stack([summed[index], summed[index + 15]]) for index in range(15)))
    totals = totals + (summed[30],)
    return (output, input_grad) + tuple(totals)


MESH = pl.DeviceIdType.MESH
ANY = pl.BlockSpec(memory_space=pl.ANY)
BF = jnp.bfloat16
F32 = jnp.float32


def place():
    d = lax.axis_index("dp")
    s = lax.axis_index("seg")
    return d, s


def greet(peers):
    barrier = pltpu.get_barrier_semaphore()
    for peer in peers:
        pl.semaphore_signal(barrier, inc=1, device_id=peer, device_id_type=MESH)
    pl.semaphore_wait(barrier, len(peers))


def remote(src, dst, send, recv, peer):
    return pltpu.make_async_remote_copy(
        src_ref=src, dst_ref=dst, send_sem=send, recv_sem=recv, device_id=peer, device_id_type=MESH
    )


def plane_peers(d, s):
    c = s % 2
    x, y = d % 2, d // 2
    dx = 2 * y + 1 - x
    dy = 2 * (1 - y) + x
    first = dx * (1 - c) + dy * c
    second = dy * (1 - c) + dx * c
    return c, first, second, s + 1 - 2 * c


def window(d):
    return pl.multiple_of((3 * d) // 2 * 128, 128), d % 2 * 64


def everyone(d, s):
    me = d * 8 + s
    ahead = [lax.rem(me + j, 32) for j in range(1, 32)]
    behind = [lax.rem(me + 32 - j, 32) for j in range(1, 32)]
    return me, ahead, behind


AHEAD, LAG2, LAG4 = 3, 2, 4


def start_kernel(pieces, *refs):
    x, (qb, vb, ob, g1, c1, ib, b2, g2, c2), refs = refs[0], refs[1:10], refs[10:]
    shards, docs, refs = refs[:6], refs[6], refs[7:]
    fulls, wins, docs_all, refs = refs[:6], refs[6:10], refs[10], refs[11:]
    saved_o, y_o, cls_o, refs = refs[:12], refs[12], refs[13], refs[14:]
    full, wbounce, ids, refs = refs[:6], refs[6:10], refs[10], refs[11:]
    (q_s, k_s, v_s, p_s, o_s, h_s, e_s, gp_s, x1, r1, x2, r2), y_s, refs = refs[:12], refs[12], refs[13:]
    load_sem, link_send, link_recv, core_send, core_recv, wload_sem, store_sem, refs = *refs[:7], refs[7:]
    win_send, win_recv, wcore_send, wcore_recv, ids_send, ids_recv, full_sem, out_sem = refs
    vq, vk, vv, vo, vi, v2 = full
    d, s = place()
    c = s % 2
    z = s // 2
    xx, yy = d % 2, d // 2
    dx, dy, dd = 2 * yy + 1 - xx, 2 * (1 - yy) + xx, 3 - d
    other = s + 1 - 2 * c
    even = 1 - z % 2
    xpeer, ypeer, zpeer = (dx, s), (dy, s), (d, s + 4 * even - 2)

    def either(a, b):
        return a * even + b * (1 - even)

    segs = x.shape[0] // 128
    count = len(pieces)
    loads = [
        pltpu.make_async_copy(shards[i].at[0], full[i].at[pl.ds(pl.multiple_of(d * shards[i].shape[1], 64), shards[i].shape[1])], load_sem.at[i])
        for i in range(6)
    ]
    for cp in loads:
        cp.start()
    ids_load = pltpu.make_async_copy(docs, ids, load_sem.at[6])
    ids_load.start()
    origins = (shards[0], shards[1], shards[2], shards[4])
    wloads = []
    for w in range(4):
        width = wins[w].shape[-1]
        at = window(d)[0] if w < 3 else d * width
        cp = pltpu.make_async_copy(origins[w].at[1, :, pl.ds(pl.multiple_of(at, 128), width)], wbounce[w], wload_sem.at[w])
        cp.start()
        wloads.append(cp)
    greet([xpeer, ypeer, (dd, s), zpeer, (d, other)])

    def cols(ref):
        half = ref.shape[-1] // 2
        return pl.ds(pl.multiple_of(c * half, half), half)

    def mine(p, h):
        i, r0, rn = pieces[p]
        n = rn // 4
        return shards[i].at[0, pl.ds(pl.multiple_of(r0 + (2 * h + c) * n, 16), n)]

    def slot(p, src, h):
        i, r0, rn = pieces[p]
        n = rn // 4
        return full[i].at[pl.ds(pl.multiple_of(src * shards[i].shape[1] + r0 + (2 * h + c) * n, 16), n)]

    started, shared, stores = [], [], []

    def link(kind, p, src, dst, peer):
        return remote(src, dst, link_send.at[kind, p], link_recv.at[kind, p], peer)

    def go(cp):
        cp.start()
        started.append(cp)

    def arrived(kind, p, ref):
        link(kind, p, ref, ref, zpeer).wait_recv()
        cp = remote(ref, ref, core_send.at[kind, p], core_recv.at[kind, p], (d, other))
        cp.start()
        shared.append((pieces[p][0], cp))
        started.append(cp)

    def own(p):
        if p < count:
            go(link(0, p, mine(p, 1), slot(p, d, 1), xpeer))
            go(link(1, p, mine(p, 0), slot(p, d, 0), ypeer))

    loaded = set()

    far = (dd, dx, dy)

    def columns(w, dev, core):
        wide = wins[w].shape[-1]
        begin = window(dev)[0] if w < 3 else dev * wide
        return pl.ds(pl.multiple_of(begin + core * (wide // 2), 128), wide // 2)

    def cross_needs():
        ids_load.wait()
        for k, peer in enumerate(far):
            for w in range(4):
                go(remote(
                    origins[w].at[1, :, columns(w, peer, c)], wins[w].at[d, :, cols(wins[w])],
                    win_send.at[k, w], win_recv.at[k, w], (peer, s),
                ))
            go(remote(ids, docs_all.at[d], ids_send.at[k], ids_recv.at[k], (peer, s)))

    def step(p):
        own(p + AHEAD)
        if p < count:
            i = pieces[p][0]
            if i not in loaded:
                loads[i].wait()
                loaded.add(i)
            arrived(0, p, slot(p, dx, 1))
            arrived(1, p, slot(p, dy, 0))
            ref = slot(p, either(d, dy), 0)
            go(link(2, p, ref, ref, xpeer))
            ref = slot(p, either(d, dx), 1)
            go(link(3, p, ref, ref, ypeer))
            if p == count - 1:
                cross_needs()
        n = p - LAG2
        if 0 <= n < count:
            for kind, src, h in ((2, either(dx, dd), 0), (3, either(dy, dd), 1)):
                ref = slot(n, src, h)
                arrived(kind, n, ref)
                go(link(kind + 2, n, ref, ref, zpeer))
        n = p - LAG4
        if 0 <= n < count:
            arrived(4, n, slot(n, either(dd, dx), 0))
            arrived(5, n, slot(n, either(dd, dy), 1))

    ready = set()

    def whole(i):
        for j, cp in shared:
            if j == i:
                cp.wait_recv()
        assert i not in ready
        ready.add(i)
        cp = pltpu.make_async_copy(full[i], fulls[i], full_sem.at[i])
        cp.start()
        stores.append(cp)

    def save(n, ref):
        cp = pltpu.make_async_copy(ref, y_o if n == 12 else saved_o[n], out_sem.at[n])
        cp.start()
        stores.append(cp)

    rows, width = x.shape
    nt = width // TILE
    for p in range(AHEAD):
        own(p)
    at = 0

    def advance(upto):
        nonlocal at
        while at < min(upto, count + LAG4):
            step(at)
            at += 1

    last = {i: max(p for p in range(count) if pieces[p][0] == i) for i in range(6)}
    advance(last[2] + LAG4 + 1)
    for i in range(3):
        whole(i)

    for t in range(nt):
        lanes = slice(t * TILE, t * TILE + TILE)
        q_s[:, lanes] = (dot(x[...], vq[:, lanes]) + qb[0:1, lanes].astype(F32)).astype(BF)
        k_s[:, lanes] = dot(x[...], vk[:, lanes]).astype(BF)
        v_s[:, lanes] = (dot(x[...], vv[:, lanes]) + vb[0:1, lanes].astype(F32)).astype(BF)
    for n, ref in enumerate((q_s, k_s, v_s)):
        save(n, ref)
    advance(last[2] + LAG4 + 2)
    masks = head_masks()

    def attend(hp, carry):
        lanes = tiles(hp, 128)
        for s in range(segs):
            here = slice(s * 128, s * 128 + 128)
            qs, ks, vs = q_s[here, lanes], k_s[here, lanes], v_s[here, lanes]
            mixed = None
            for h in range(2):
                scores = dot_nt(qs * masks[h], ks)
                top = jnp.max(scores, axis=-1, keepdims=True)
                weight = jnp.exp((scores - top) * 0.125)
                share = (weight * (1.0 / jnp.sum(weight, axis=-1, keepdims=True))).astype(BF)
                p_s[hp, s, h] = share
                part = dot(share, vs * masks[h])
                mixed = part if mixed is None else mixed + part
            o_s[here, lanes] = mixed.astype(BF)
        return carry

    pairs = width // 128
    for g in range(pairs // 2):
        lax.fori_loop(2 * g, 2 * g + 2, attend, 0)
        advance(last[2] + LAG4 + 3 + g)
    save(3, p_s)
    save(4, o_s)
    advance(last[3] + LAG4 + 1)
    whole(3)

    def out(t, carry):
        lanes = tiles(t)
        x1[:, lanes] = dot(o_s[...], vo[:, lanes]) + ob[0:1, lanes].astype(F32) + x[:, lanes].astype(F32)
        return carry

    lax.fori_loop(0, nt, out, 0)

    def first(i, carry):
        r = tiles(i, 64)
        xhat, rstd = standard(x1[r, :])
        x1[r, :] = xhat
        r1[r, :] = jnp.broadcast_to(rstd, (64, 128))
        hidden = xhat * g1[0:1, :].astype(F32) + c1[0:1, :].astype(F32)
        h_s[r, :] = hidden.astype(BF)
        x2[r, :] = hidden + b2[0:1, :].astype(F32)
        return carry

    lax.fori_loop(0, rows // 64, first, 0)
    for n, ref in ((5, h_s), (8, x1), (9, r1)):
        save(n, ref)
    advance(last[4] + LAG4 + 1)
    whole(4)

    def ffn(t, carry):
        lanes = tiles(t)
        u = dot(h_s[...], vi[:, lanes]) + ib[0:1, lanes].astype(F32)
        e, gp = gelu_parts(u)
        e_s[:, lanes] = e.astype(BF)
        gp_s[:, lanes] = gp.astype(BF)
        return carry

    groups = vi.shape[1] // TILE // 2
    for g in range(groups):
        lax.fori_loop(2 * g, 2 * g + 2, ffn, 0)
        advance(last[4] + LAG4 + 2 + g)
    advance(count + LAG4)
    for w in range(4):
        wloads[w].wait()
        cp = pltpu.make_async_copy(wbounce[w], wins[w].at[d], store_sem.at[w])
        cp.start()
        stores.append(cp)
    for src, dst, i in ((ids, docs_all.at[d], 4),):
        cp = pltpu.make_async_copy(src, dst, store_sem.at[i])
        cp.start()
        stores.append(cp)
    save(6, e_s)
    save(7, gp_s)
    whole(5)

    def outer(t, carry):
        lanes = tiles(t)
        x2[:, lanes] += dot(e_s[...], v2[:, lanes])
        return carry

    lax.fori_loop(0, nt, outer, 0)

    def second(i, carry):
        r = tiles(i, 64)
        xhat, rstd = standard(x2[r, :])
        x2[r, :] = xhat
        r2[r, :] = jnp.broadcast_to(rstd, (64, 128))
        y_s[r, :] = (xhat * g2[0:1, :].astype(F32) + c2[0:1, :].astype(F32)).astype(BF)
        return carry

    lax.fori_loop(0, rows // 64, second, 0)
    for n, ref in ((10, x2), (11, r2), (12, y_s)):
        save(n, ref)
    for s_ in range(segs):
        cls_o[s_ : s_ + 1, :] = x2[s_ * 128 : s_ * 128 + 1, :] * g2[0:1, :].astype(F32) + c2[0:1, :].astype(F32)
    wcores = []
    for k, peer in enumerate(far):
        for w in range(4):
            got = wins[w].at[peer, :, cols(wins[w])]
            remote(got, got, win_send.at[k, w], win_recv.at[k, w], (peer, s)).wait_recv()
            cp = remote(got, got, wcore_send.at[k, w], wcore_recv.at[k, w], (d, other))
            cp.start()
            wcores.append(cp)
        remote(ids, docs_all.at[peer], ids_send.at[k], ids_recv.at[k], (peer, s)).wait_recv()
    for cp in started:
        cp.wait_send()
    for cp in wcores:
        cp.wait()
    for cp in stores:
        cp.wait()


def start(x, shards, docs, vectors, collective_id):
    cuts = (1, 1, 1, 1, 3, 4)
    pieces = []
    for i, w in enumerate(shards):
        n = w.shape[1] // cuts[i]
        pieces += [(i, p * n, n) for p in range(cuts[i])]
    count = len(pieces)
    S, VM, dma = jax.ShapeDtypeStruct, pltpu.VMEM, pltpu.SemaphoreType.DMA
    V = pl.BlockSpec(memory_space=pltpu.VMEM)
    part, width = shards[0].shape[1:]
    rows = x.shape[0]
    ff = shards[4].shape[2]
    segs = rows // 128
    wins = [(part, 256)] * 3 + [(part, ff // 4)]
    low, full, wide, col = ((rows, width), BF), ((rows, width), F32), ((rows, ff), BF), ((rows, 128), F32)
    saved = [low, low, low, ((width // 128, segs, 2, 128, 128), BF), low, low, wide, wide, full, col, full, col, low]
    outs = pl.pallas_call(
        functools.partial(start_kernel, pieces),
        out_shape=[S((4 * w.shape[1], w.shape[2]), w.dtype) for w in shards]
        + [S((4,) + w, BF) for w in wins]
        + [S((4,) + docs.shape, docs.dtype)]
        + [S(*t) for t in saved]
        + [S((segs, width), F32)],
        in_specs=[V] * 10 + [ANY] * 7,
        out_specs=[ANY] * 24 + [V],
        scratch_shapes=[VM((4 * w.shape[1], w.shape[2]), w.dtype) for w in shards]
        + [VM(w, BF) for w in wins]
        + [VM(docs.shape, docs.dtype)]
        + [VM(*t) for t in saved]
        + [dma((7,)), dma((6, count)), dma((6, count)), dma((6, count)), dma((6, count)), dma((4,)), dma((5,))]
        + [dma((3, 4)), dma((3, 4)), dma((3, 4)), dma((3, 4)), dma((3,)), dma((3,)), dma((6,)), dma((13,))],
        compiler_params=pltpu.CompilerParams(collective_id=collective_id, has_side_effects=True, vmem_limit_bytes=67043328),
        name="gather_forward",
    )(x, *vectors, *shards, docs)
    return outs[:6], outs[6:10], outs[10], outs[11:23], outs[23], outs[24]


def add_into(dst, a, b, rows):
    step = 48 if rows % 48 == 0 else 32

    def body(i, carry):
        r = pl.ds(pl.multiple_of(i * step, 16), step)
        dst[r, :] = (a[r, :].astype(F32) + b[r, :].astype(F32)).astype(dst.dtype)
        return carry

    lax.fori_loop(0, rows // step, body, 0)


TILE = 256


def dot(a, b):
    return lax.dot_general(a, b, (((1,), (0,)), ((), ())), preferred_element_type=F32)


def dot_nt(a, b):
    return lax.dot_general(a, b, (((1,), (1,)), ((), ())), preferred_element_type=F32)


def dot_tn(a, b):
    return lax.dot_general(a, b, (((0,), (0,)), ((), ())), preferred_element_type=F32)


def tiles(i, size=TILE):
    return pl.ds(pl.multiple_of(i * size, size), size)


def standard(r):
    centred = r - jnp.mean(r, axis=-1, keepdims=True)
    rstd = lax.rsqrt(jnp.mean(centred * centred, axis=-1, keepdims=True) + epsilon)
    return centred * rstd, rstd


def standard_back(grad, xhat, rstd):
    return rstd * (
        grad
        - jnp.mean(grad, axis=-1, keepdims=True)
        - xhat * jnp.mean(grad * xhat, axis=-1, keepdims=True)
    )


def gelu_parts(u):
    phi = 0.5 * (1.0 + lax.erf(u * 0.7071067811865476))
    return u * phi, phi + u * (0.3989422804014327 * jnp.exp(-0.5 * u * u))


def head_masks():
    lane = lax.broadcasted_iota(jnp.int32, (1, 128), 1)
    low = (lane < 64).astype(F32)
    return (low.astype(BF), (1.0 - low).astype(BF))


def row_sum(v):
    return jnp.sum(v, axis=0, keepdims=True)


LAGS = (0, 2, 3, 4, 5, 6, 7, 8)
CHUNKS = [("rows", 0), ("cols", 0), ("rows", 1), ("cols", 1), ("rows", 2), ("cols", 2), ("mats", 3), ("mats", 0), ("mats", 1), ("mats", 2)]


def backward_kernel(dcl, z, g1, g2, du_own, dqkv_own, x, cot, q, k, v, p, o, hb, e, gp, x1, r1, x2, r2, y, wq, wk, wv, wo, wi, w2, *refs):
    (dx_o, y_o, outer_o, inner_o, mats_o, du_all, dqkv_all, vec_o), refs = refs[:8], refs[8:]
    (xs, ds_, qs_, ks_, vs_, p_s, os_, hs, e_s, gp_s, x1s, r1s, acc, r2s, ys), refs = refs[:15], refs[15:]
    (vi, v2, df, ht, vecs, g_rows, g_cols, g_mats), refs = refs[:8], refs[8:]
    bufs, refs = refs[:18], refs[18:]
    in_sem, w_sem, res_sem, out_sem, vsum, vgot, vsend, vrcv, send, recv, kept, kept_sem, far_send, far_recv, near_send, near_recv = refs
    dev, s = place()
    c, first, second, other = plane_peers(dev, s)
    px, py = dev % 2, dev // 2
    a = px * (1 - c) + py * c
    b = py * (1 - c) + px * c
    z_at = s // 2
    z0, z1 = z_at % 2, z_at // 2
    znear = (z_at + 1 - 2 * z0) * 2 + c
    zfar = (z_at + 2 - 4 * z1) * 2 + c
    order = [(cot, ds_), (y, ys), (x2, acc), (r2, r2s), (hb, hs), (w2, v2), (e, e_s), (gp, gp_s), (wi, vi),
             (x1, x1s), (r1, r1s), (o, os_), (p, p_s), (q, qs_), (k, ks_), (v, vs_), (x, xs)]
    loads = [pltpu.make_async_copy(src, dst, in_sem.at[i]) for i, (src, dst) in enumerate(order)]
    for cp in loads:
        cp.start()
    greet([(first, s), (second, s), (3 - dev, s), (dev, other), (dev, znear), (dev, zfar)])
    rows, width = xs.shape
    segs, nt = rows // 128, width // TILE
    share = width // 4
    started, outs, results = [], [], []

    def go(cp):
        cp.start()
        started.append(cp)

    def arrived(ref, sem):
        pltpu.make_async_copy(ref, ref, sem).wait()

    crossing = ((du_own, du_all), (dqkv_own, dqkv_all))
    far = (3 - dev, first, second)
    half_rows = pl.ds(pl.multiple_of(c * 64, 64), 64)
    keeps, shared = [], []
    for m, (src, dst) in enumerate(crossing):
        for n, peer in enumerate(far):
            go(remote(src.at[half_rows], dst.at[dev, half_rows], far_send.at[m, n], far_recv.at[m, n], (peer, s)))
        cp = pltpu.make_async_copy(src, kept.at[m], kept_sem.at[0, m])
        cp.start()
        keeps.append(cp)

    def cross_share():
        for m, (src, dst) in enumerate(crossing):
            for n, peer in enumerate(far):
                got = dst.at[peer, half_rows]
                remote(got, got, far_send.at[m, n], far_recv.at[m, n], (peer, s)).wait_recv()
                cp = remote(got, got, near_send.at[m, n], near_recv.at[m, n], (dev, other))
                cp.start()
                shared.append(cp)
            keeps[m].wait()
            cp = pltpu.make_async_copy(kept.at[m], dst.at[dev], kept_sem.at[1, m])
            cp.start()
            outs.append(cp)

    families = {"rows": 0, "cols": 1, "mats": 2}

    def part(n, core, quarters):
        kind, i = CHUNKS[n]
        if kind == "rows":
            return g_rows.at[quarters, pl.ds(pl.multiple_of(i * 256 + core * 128, 128), 128), :]
        ref = g_cols if kind == "cols" else g_mats
        half = ref.shape[-1] // 2
        return ref.at[i, quarters, :, pl.ds(pl.multiple_of(core * half, 128), half)]

    def buf(n, j):
        kind, i = CHUNKS[n]
        ref = bufs[families[kind] * 6 + j]
        return ref.at[i] if j < 5 else ref.at[:, i]

    def size(n):
        return 128 if CHUNKS[n][0] == "rows" else 192

    def own(n, quarter):
        return part(n, c, quarter)

    def fin(n, core, at=0, count=None):
        kind, i = CHUNKS[n]
        count = size(n) if count is None else count
        return bufs[families[kind] * 6 + 5].at[core, i, pl.ds(pl.multiple_of(at, 16), count), :]

    def quarter(aa, bb):
        return aa * (1 + c) + bb * (2 - c)

    def offer(n):
        go(remote(part(n, 1 - c, slice(None)), buf(n, 0), send.at[0, n], recv.at[0, n], (dev, other)))

    def write(n, core, i):
        kind, at = CHUNKS[n]
        src = bufs[families[kind] * 6 + 5].at[core, at]
        if kind == "rows":
            pairs_ = [(src, outer_o.at[pl.ds(pl.multiple_of(at * 256 + core * 128, 128), 128), :])]
        elif kind == "mats":
            pairs_ = [(src, mats_o.at[at, :, pl.ds(pl.multiple_of(core * 384, 128), 384)])]
        else:
            pairs_ = [
                (src.at[:, j * 256 : j * 256 + 256], inner_o.at[:, pl.ds(pl.multiple_of((2 * core + j) * 768 + at * 256, 128), 256)])
                for j in range(2)
            ]
        for j, (left, right) in enumerate(pairs_):
            cp = pltpu.make_async_copy(left, right, out_sem.at[i, j, n])
            cp.start()
            outs.append(cp)

    def stage(t, n):
        r = size(n)
        h, f = r // 2, r // 4
        if t == 1:
            got = buf(n, 0)
            arrived(got, recv.at[0, n])
            for bb in range(2):
                away = quarter(1 - a, bb)
                add_into(own(n, away), own(n, away), got.at[away], r)
                go(remote(own(n, away), buf(n, 1).at[bb], send.at[1 + bb, n], recv.at[1 + bb, n], (first, s)))
            for bb in range(2):
                keep = quarter(a, bb)
                add_into(own(n, keep), own(n, keep), got.at[keep], r)
        elif t == 2:
            got = buf(n, 1)
            for bb in range(2):
                arrived(got.at[bb], recv.at[1 + bb, n])
            away, keep = quarter(a, 1 - b), quarter(a, b)
            add_into(own(n, away), own(n, away), got.at[1 - b], r)
            go(remote(own(n, away), buf(n, 2), send.at[3, n], recv.at[3, n], (second, s)))
            add_into(own(n, keep), own(n, keep), got.at[b], r)
        elif t == 3:
            got = buf(n, 2)
            arrived(got, recv.at[3, n])
            keep = own(n, quarter(a, b))
            away = pl.ds(pl.multiple_of((1 - z0) * h, 16), h)
            mine = pl.ds(pl.multiple_of(z0 * h, 16), h)
            add_into(keep.at[away], keep.at[away], got.at[away], h)
            go(remote(keep.at[away], buf(n, 3), send.at[4, n], recv.at[4, n], (dev, znear)))
            add_into(keep.at[mine], keep.at[mine], got.at[mine], h)
        elif t == 4:
            got = buf(n, 3)
            arrived(got, recv.at[4, n])
            keep = own(n, quarter(a, b))
            away = pl.ds(pl.multiple_of(z0 * h + (1 - z1) * f, 16), f)
            mine = pl.ds(pl.multiple_of(z0 * h + z1 * f, 16), f)
            add_into(keep.at[away], keep.at[away], got.at[pl.ds(pl.multiple_of((1 - z1) * f, 16), f)], f)
            go(remote(keep.at[away], buf(n, 4), send.at[5, n], recv.at[5, n], (dev, zfar)))
            add_into(keep.at[mine], keep.at[mine], got.at[pl.ds(pl.multiple_of(z1 * f, 16), f)], f)
        elif t == 5:
            got = buf(n, 4)
            arrived(got, recv.at[5, n])
            mine = own(n, quarter(a, b)).at[pl.ds(pl.multiple_of(z0 * h + z1 * f, 16), f)]
            done = fin(n, c, z0 * h + z1 * f, f)
            add_into(done, mine, got, f)
            go(remote(done, done, send.at[6, n], recv.at[6, n], (dev, zfar)))
        elif t == 6:
            arrived(fin(n, c, z0 * h + (1 - z1) * f, f), recv.at[6, n])
            half = fin(n, c, z0 * h, h)
            go(remote(half, half, send.at[7, n], recv.at[7, n], (dev, znear)))
        elif t == 7:
            arrived(fin(n, c, (1 - z0) * h, h), recv.at[7, n])
            go(remote(fin(n, c), fin(n, c), send.at[8, n], recv.at[8, n], (dev, other)))
            write(n, c, 0)
        elif t == 8:
            arrived(fin(n, 1 - c), recv.at[8, n])
            write(n, 1 - c, 1)

    nc = len(CHUNKS)

    def slot(i):
        for t in range(8, 0, -1):
            n = i - LAGS[t - 1]
            if 0 <= n < nc:
                stage(t, n)

    vecs[...] = jnp.zeros_like(vecs)
    for i in range(4):
        loads[i].wait()

    def norm2(i, carry):
        gain_sum, shift_sum, bias_sum = carry
        r = tiles(i, 64)
        dy, out = ds_[r, :].astype(F32), ys[r, :].astype(F32)
        at = lax.broadcasted_iota(jnp.int32, (64, 1), 0) + i * 64
        for j in range(segs):
            dy = jnp.where(at == j * 128, dcl[j : j + 1, :], dy)
            out = jnp.where(at == j * 128, z[j : j + 1, :], out)
        ys[r, :] = out.astype(BF)
        xhat = acc[r, :]
        back = standard_back(dy * g2[0:1, :].astype(F32), xhat, r2s[r, 0:1])
        acc[r, :] = back
        low = back.astype(BF)
        df[r, :] = low
        return (gain_sum + row_sum(dy * xhat), shift_sum + row_sum(dy), bias_sum + row_sum(low.astype(F32)))

    zero = jnp.zeros((1, width), F32)
    sums = lax.fori_loop(0, rows // 64, norm2, (zero, zero, zero))
    vecs[6:7, :], vecs[7:8, :], vecs[5:6, :] = sums
    results.append(pltpu.make_async_copy(ys, y_o, res_sem.at[0]))
    results[0].start()
    loads[4].wait()
    ht[...] = hs[...].T
    for i in range(5, 9):
        loads[i].wait()

    def ffn(j):
        def body(block, carry):
            wide = tiles(block * nt + j)
            lanes = slice(j * TILE, j * TILE + TILE)
            de = dot_nt(df[...], v2[wide, :]).astype(BF).astype(F32)
            du = (de * gp_s[:, wide].astype(F32)).astype(BF)
            vecs[pl.ds(8 + block, 1), lanes] = row_sum(du.astype(F32))
            g_rows[block, lanes, :] = dot_tn(e_s[:, wide], df[...]).astype(BF)
            inner = dot(ht[...], du).astype(BF)
            for i in range(4):
                g_cols[j, i, :, tiles(block)] = inner[i * share : i * share + share]
            acc[...] += dot_nt(du, vi[:, wide])
            return carry

        return body

    lax.fori_loop(0, 4, ffn(0), 0)
    offer(0)
    offer(1)
    cross_share()
    lax.fori_loop(0, 2, ffn(1), 0)
    slot(0)
    lax.fori_loop(2, 4, ffn(1), 0)
    offer(2)
    offer(3)
    slot(1)
    lax.fori_loop(0, 2, ffn(2), 0)
    slot(2)
    lax.fori_loop(2, 4, ffn(2), 0)
    offer(4)
    offer(5)
    wloads = [
        pltpu.make_async_copy(src, v2.at[i * width : i * width + width], w_sem.at[i])
        for i, src in enumerate((wo, wq, wk, wv))
    ]
    for cp in wloads:
        cp.start()
    slot(3)
    for i in range(9, 17):
        loads[i].wait()

    def norm1(i, carry):
        gain_sum, shift_sum, bias_sum = carry
        r = tiles(i, 64)
        dh = acc[r, :]
        xhat = x1s[r, :]
        back = standard_back(dh * g1[0:1, :].astype(F32), xhat, r1s[r, 0:1])
        acc[r, :] = back
        low = back.astype(BF)
        df[r, :] = low
        return (gain_sum + row_sum(dh * xhat), shift_sum + row_sum(dh), bias_sum + row_sum(low.astype(F32)))

    sums = lax.fori_loop(0, rows // 64, norm1, (zero, zero, zero))
    vecs[3:4, :], vecs[4:5, :], vecs[2:3, :] = sums
    ht[...] = os_[...].T

    def weights(at, rhs):
        def body(t, carry):
            lanes = tiles(t)
            back = dot(ht[...], rhs[:, lanes]).astype(BF)
            for i in range(4):
                g_mats[at, i, :, lanes] = back[i * share : i * share + share]
            return carry

        lax.fori_loop(0, nt, body, 0)

    weights(3, df)
    offer(6)
    slot(4)
    wloads[0].wait()

    def mixed(t, carry):
        lanes = tiles(t)
        ds_[:, lanes] = dot_nt(df[...], v2[lanes, :]).astype(BF)
        return carry

    lax.fori_loop(0, nt, mixed, 0)
    masks = head_masks()

    def attend(hp, carry):
        lanes = tiles(hp, 128)
        for j in range(segs):
            here = slice(j * 128, j * 128 + 128)
            qs, ks, vs, dos = qs_[here, lanes], ks_[here, lanes], vs_[here, lanes], ds_[here, lanes]
            dqs = dks = dvs = 0.0
            for h in range(2):
                pl_ = p_s[hp, j, h]
                pf = pl_.astype(F32)
                dom = dos * masks[h]
                dp = dot_nt(dom, vs).astype(BF).astype(F32)
                ds = (pf * (dp - jnp.sum(pf * dp, axis=-1, keepdims=True))).astype(BF)
                dqs += dot(ds, ks * masks[h])
                dks += dot_tn(ds, qs * masks[h])
                dvs += dot_tn(pl_, dom)
            qs_[here, lanes] = (dqs * 0.125).astype(BF)
            ks_[here, lanes] = (dks * 0.125).astype(BF)
            vs_[here, lanes] = dvs.astype(BF)
        return carry

    lax.fori_loop(0, 3, attend, 0)
    slot(5)
    lax.fori_loop(3, width // 128, attend, 0)
    vecs[0:1, :] = row_sum(qs_[...].astype(F32))
    vecs[1:2, :] = row_sum(vs_[...].astype(F32))
    ht[...] = xs[...].T
    weights(0, qs_)
    offer(7)
    slot(6)
    weights(1, ks_)
    offer(8)
    weights(2, vs_)
    offer(9)
    hops = [(dev, other), (first, s), (second, s), (dev, znear), (dev, zfar)]
    vsum[0] = vecs[...]

    def vector_hop(j):
        if j > 0:
            arrived(vgot.at[j - 1], vrcv.at[j - 1])
            vsum[j] = vsum[j - 1] + vgot[j - 1]
        if j < 5:
            go(remote(vsum.at[j], vgot.at[j], vsend.at[j], vrcv.at[j], hops[j]))

    slot(7)
    vector_hop(0)
    for i in range(1, 4):
        wloads[i].wait()

    def source(t, carry):
        r = tiles(t)
        dx = acc[:, r]
        for i, g in enumerate((qs_, ks_, vs_)):
            dx += dot_nt(g[...], v2[pl.ds(pl.multiple_of((i + 1) * width + t * TILE, TILE), TILE), :])
        xs[:, r] = dx.astype(BF)
        return carry

    lax.fori_loop(0, nt, source, 0)
    results.append(pltpu.make_async_copy(xs, dx_o, res_sem.at[1]))
    results[1].start()
    for i in range(8, nc + LAGS[7]):
        slot(i)
        if i < 13:
            vector_hop(i - 7)
    vec_o[...] = vsum[5]
    for cp in started:
        cp.wait_send()
    for cp in outs + results + shared:
        cp.wait()


def backward(x, cot, crossed, saved, y, weights, g1, g2, collective_id):
    q, k, v, p, o, hb, e, gp, x1, r1, x2, r2 = saved
    rows, width = x.shape
    ff = weights[4].shape[1]
    share, nc = width // 4, len(CHUNKS)
    S, VM, dma = jax.ShapeDtypeStruct, pltpu.VMEM, pltpu.SemaphoreType.DMA
    V = pl.BlockSpec(memory_space=pltpu.VMEM)
    z, dcl, dqkv, du = crossed[0], crossed[1], crossed[6], crossed[7]
    four = S((4,) + du.shape, BF)
    arrays = (x, cot, q, k, v, p, o, hb, e, gp, x1, r1, x2, r2, y)

    def chunk(n, r, w):
        return [VM(t, BF) for t in ((n, 4, r, w), (n, 2, r, w), (n, r, w), (n, r // 2, w), (n, r // 4, w), (2, n, r, w))]

    return pl.pallas_call(
        backward_kernel,
        out_shape=[
            S((rows, width), BF), S((rows, width), BF), S((ff // 4, width), BF), S((share, ff), BF), S((4, share, width), BF),
            four, four, S((16, width), F32),
        ],
        in_specs=[V] * 4 + [ANY] * 23,
        out_specs=[ANY] * 7 + [V],
        scratch_shapes=[VM(t.shape, t.dtype) for t in arrays]
        + [
            VM((width, ff), BF), VM((ff, width), BF), VM((rows, width), BF), VM((width, rows), BF), VM((16, width), F32),
            VM((4, ff // 4, width), BF), VM((3, 4, share, ff // 3), BF), VM((4, 4, share, width), BF),
        ]
        + chunk(3, 128, width) + chunk(3, share, ff // 6) + chunk(4, share, width // 2)
        + [
            dma((17,)), dma((4,)), dma((2,)), dma((2, 2, nc)),
            VM((6, 16, width), F32), VM((5, 16, width), F32), dma((5,)), dma((5,)), dma((9, nc)), dma((9, nc)),
            VM((2,) + du.shape, BF), dma((2, 2)), dma((2, 3)), dma((2, 3)), dma((2, 3)), dma((2, 3)),
        ],
        compiler_params=pltpu.CompilerParams(collective_id=collective_id, has_side_effects=True, vmem_limit_bytes=67043328),
        name="backward_reduce",
    )(dcl, z, g1, g2, du, dqkv, *arrays, *weights)


def cross_kernel(cls, emb, docs, cot, wq, wk, wv, wi, out_w, outer_w,
                 qb, vb, ob, g1, c1, ib, b2, g2, c2,
                 z_o, dcl_o, xw_o, hw_o, ow_o, e_o, dqkv_o, du_o, da_o, df_o, vec_o, emb_o,
                 vq, vk, vv, vi, vo, v2, heads, xall, rows_s, p_s, part_s, total_s, send1, got1, send2, got2,
                 in_sem, all_send, all_recv, first_rows, cots, cot_all, row_sem, cot_send, cot_recv, s1, r1, s2, r2, s3, r3):
    d, s = place()
    c, first, second, other = plane_peers(d, s)
    start, off = window(d)
    me, ahead, behind = everyone(d, s)
    lane_w = pl.ds(start, 256)
    loads = [
        pltpu.make_async_copy(src, dst, in_sem.at[i])
        for i, (src, dst) in enumerate(
            (
                (wq, vq), (wk, vk), (wv, vv),
                (out_w.at[1], vo.at[pl.ds(pl.multiple_of(off, 64), 192)]),
                (wi, vi), (outer_w.at[1], v2),
            )
        )
    ]
    for cp in loads:
        cp.start()
    row_loads = [pltpu.make_async_copy(cot.at[0, pl.ds(i * 128, 8)], first_rows.at[i], row_sem.at[i]) for i in range(4)]
    for cp in row_loads:
        cp.start()
    vo[pl.ds(pl.multiple_of(192 * (1 - d % 2), 64), 64), :] = jnp.zeros((64, 768), BF)
    pick = lax.broadcasted_iota(jnp.int32, (8, 32), 0) + 4 * s == lax.broadcasted_iota(jnp.int32, (8, 32), 1)
    position = dot(pick.astype(BF), emb[...])
    heads[...] = (cls[...] + position[0:4]).astype(BF)
    greet([(i // 8, i % 8) for i in ahead])
    sent = []
    for j, i in enumerate(ahead):
        cp = remote(heads, xall.at[me], all_send.at[j], all_recv.at[j], (i // 8, i % 8))
        cp.start()
        sent.append(cp)
    xall[me] = heads[...]
    for cp in row_loads:
        cp.wait()
    cots[...] = jnp.concatenate([first_rows[i].astype(F32)[0:1] for i in range(4)], axis=0).astype(BF)
    cot_all[me] = cots[...]
    ids = lax.broadcasted_iota(jnp.int32, (8, 128), 1) // 32 * 1024
    ids = ids.astype(F32)
    lane = lax.broadcasted_iota(jnp.int32, (32, 128), 1)
    key = lax.broadcasted_iota(jnp.int32, (32, 128), 0)
    for r in range(4):
        numbers = jnp.broadcast_to(docs[r], (8, 32)).astype(F32).astype(BF)
        ids = ids + dot(numbers, (lane == key + 32 * r).astype(BF))
    across = jnp.broadcast_to(ids[0:1], (128, 128))
    allowed = across == across.T
    for j, i in enumerate(behind):
        remote(heads, xall.at[i], all_send.at[j], all_recv.at[j], (i // 8, i % 8)).wait_recv()
    for j, i in enumerate(ahead):
        cp = remote(cots, cot_all.at[me], cot_send.at[j], cot_recv.at[j], (i // 8, i % 8))
        cp.start()
        sent.append(cp)
    for i in range(32):
        rows_s[4 * i : 4 * i + 4, :] = xall[i].astype(F32)
    xf = rows_s[...]
    x = xf.astype(BF)

    def total(n, partial):
        half = pl.ds(pl.multiple_of(c * 64, 64), 64)
        part_s[...] = partial
        send1[n] = part_s[half, :].astype(BF)
        one = remote(send1.at[n], got1.at[n], s1.at[n], r1.at[n], (first, s))
        one.start()
        one.wait_recv()
        both = send1[n].astype(F32) + got1[n].astype(F32)
        send2[n] = both.astype(BF)
        two = remote(send2.at[n], got2.at[n], s2.at[n], r2.at[n], (second, s))
        two.start()
        two.wait_recv()
        total_s[n, half, :] = send2[n].astype(F32) + got2[n].astype(F32)
        three = remote(total_s.at[n, half], total_s.at[n, half], s3.at[n], r3.at[n], (d, other))
        three.start()
        three.wait_recv()
        sent.extend((one, two, three))
        return total_s[n]

    def vector(ref, lanes=slice(None)):
        return ref[1:2, lanes].astype(F32)

    for i in range(3):
        loads[i].wait()
    q = (dot(x, vq[...]) + vector(qb, lane_w)).astype(BF)
    k = dot(x, vk[...]).astype(BF)
    v = (dot(x, vv[...]) + vector(vb, lane_w)).astype(BF)
    masks = head_masks()
    mixed = []
    for pair in range(2):
        l = slice(pair * 128, pair * 128 + 128)
        both = None
        for h in range(2):
            scores = jnp.where(allowed, dot_nt(q[:, l] * masks[h], k[:, l]) * 0.125, -1e30)
            weight = jnp.exp(scores - jnp.max(scores, axis=-1, keepdims=True))
            share = (weight * (1.0 / jnp.sum(weight, axis=-1, keepdims=True))).astype(BF)
            p_s[2 * pair + h] = share
            part = dot(share, v[:, l] * masks[h])
            both = part if both is None else both + part
        mixed.append(both.astype(BF))
    loads[3].wait()
    ow = jnp.concatenate(mixed, axis=1)
    ow_o[...] = ow
    branch = total(0, dot(ow, vo[...]))
    xhat1, rstd1 = standard(xf + branch + vector(ob))
    hidden = xhat1 * vector(g1) + vector(c1)
    hb = hidden.astype(BF)
    rows_s[...] = hidden
    hw_o[...] = rows_s[:, lane_w].astype(BF)
    rows_s[...] = xf
    xw_o[...] = rows_s[:, lane_w].astype(BF)
    loads[4].wait()
    loads[5].wait()
    wide = pl.ds(pl.multiple_of(d * 768, 768), 768)
    e, gp = gelu_parts(dot(hb, vi[...]) + vector(ib, wide))
    e = e.astype(BF)
    e_o[...] = e
    outer = total(1, dot(e, v2[...]))
    xhat2, rstd2 = standard(hidden + outer + vector(b2))
    z = (xhat2 * vector(g2) + vector(c2)).astype(BF)
    own = lax.broadcasted_iota(jnp.int32, (8, 128), 0) + 4 * me == lax.broadcasted_iota(jnp.int32, (8, 128), 1)
    own = own.astype(BF)
    z_o[...] = dot(own, z)
    for j, i in enumerate(behind):
        remote(cots, cot_all.at[i], cot_send.at[j], cot_recv.at[j], (i // 8, i % 8)).wait_recv()
    for i in range(32):
        rows_s[4 * i : 4 * i + 4, :] = cot_all[i].astype(F32)
    dy = rows_s[...]
    vec_o[6:7, :] = row_sum(dy * xhat2)
    vec_o[7:8, :] = row_sum(dy)
    dr2 = standard_back(dy * vector(g2), xhat2, rstd2)
    df = dr2.astype(BF)
    df_o[...] = df
    vec_o[5:6, :] = row_sum(df.astype(F32))
    du = (dot_nt(df, v2[...]).astype(BF).astype(F32) * gp).astype(BF)
    du_o[...] = du
    dh = dr2 + total(2, dot_nt(du, vi[...]))
    vec_o[3:4, :] = row_sum(dh * xhat1)
    vec_o[4:5, :] = row_sum(dh)
    dr1 = standard_back(dh * vector(g1), xhat1, rstd1)
    da = dr1.astype(BF)
    da_o[...] = da
    vec_o[2:3, :] = row_sum(da.astype(F32))
    do = dot_nt(da, vo[...]).astype(BF)
    dqs, dks, dvs = [], [], []
    for pair in range(2):
        l = slice(pair * 128, pair * 128 + 128)
        dqp = dkp = dvp = 0.0
        for h in range(2):
            share = p_s[2 * pair + h]
            pf = share.astype(F32)
            dom = do[:, l] * masks[h]
            dp = dot_nt(dom, v[:, l]).astype(BF).astype(F32)
            ds = (pf * (dp - jnp.sum(pf * dp, axis=-1, keepdims=True))).astype(BF)
            dqp += dot(ds, k[:, l] * masks[h])
            dkp += dot_tn(ds, q[:, l] * masks[h])
            dvp += dot_tn(share, dom)
        dqs.append((dqp * 0.125).astype(BF))
        dks.append((dkp * 0.125).astype(BF))
        dvs.append(dvp.astype(BF))
    dq, dk, dv = (jnp.concatenate(t, axis=1) for t in (dqs, dks, dvs))
    dqkv_o[:, 0:256] = dq
    dqkv_o[:, 256:512] = dk
    dqkv_o[:, 512:768] = dv
    dx = dr1 + total(3, dot_nt(dq, vq[...]) + dot_nt(dk, vk[...]) + dot_nt(dv, vv[...]))
    dcl = dx.astype(BF)
    dcl_o[...] = dot(own, dcl)
    back = dcl.astype(F32)
    emb_o[...] = back[0:32] + back[32:64] + back[64:96] + back[96:128]
    for cp in sent:
        cp.wait_send()


def cross(cls, emb, cot, docs, wq, wk, wv, wi, out_w, outer_w, vectors, collective_id):
    S = jax.ShapeDtypeStruct
    V = pl.BlockSpec(memory_space=pltpu.VMEM)
    VM, dma = pltpu.VMEM, pltpu.SemaphoreType.DMA
    low, win = S((128, 768), BF), S((128, 256), BF)
    return pl.pallas_call(
        cross_kernel,
        out_shape=[
            S((8, 768), F32), S((8, 768), F32), win, win, win, low, low, low, low, low,
            S((8, 768), F32), S((32, 768), F32),
        ],
        in_specs=[V] * 3 + [ANY] * 7 + [V] * 9,
        out_specs=[V] * 12,
        scratch_shapes=[
            VM((768, 256), BF), VM((768, 256), BF), VM((768, 256), BF), VM((768, 768), BF), VM((256, 768), BF), VM((768, 768), BF),
            VM((4, 768), BF), VM((32, 4, 768), BF), VM((128, 768), F32), VM((4, 128, 128), BF),
            VM((128, 768), F32), VM((4, 128, 768), F32),
            VM((4, 64, 768), BF), VM((4, 64, 768), BF), VM((4, 64, 768), BF), VM((4, 64, 768), BF),
            dma((6,)), dma((31,)), dma((31,)),
            VM((4, 8, 768), BF), VM((4, 768), BF), VM((32, 4, 768), BF), dma((4,)), dma((31,)), dma((31,)),
            dma((4,)), dma((4,)), dma((4,)), dma((4,)), dma((4,)), dma((4,)),
        ],
        compiler_params=pltpu.CompilerParams(collective_id=collective_id, has_side_effects=True, vmem_limit_bytes=67043328),
        name="cross_block",
    )(cls, emb, docs, cot, wq, wk, wv, wi, out_w, outer_w, *vectors)


def finish_kernel(dx, y, outer, inner, mats, vec, emb, xw, hw, ow, e, dqkv, du, da, df, vec1,
                  y_o, dx_o, gq_o, gqb, gk_o, gv_o, gvb, go_o, gob, gg1, gc1, gi_o, gib, g2_o, gb2, gg2, gc2, gemb,
                  vec_s, pass_s, gq, gk, gv, go, gi, g2_, pass_in, pass_out, big_out):
    moves = [pltpu.make_async_copy(src, pass_s.at[i], pass_in.at[i]) for i, src in enumerate((y, dx))]
    for cp in moves:
        cp.start()
    leaves = []
    for i, dst in enumerate((y_o, dx_o)):
        moves[i].wait()
        cp = pltpu.make_async_copy(pass_s.at[i], dst, pass_out.at[i])
        cp.start()
        leaves.append(cp)
    d = lax.axis_index("dp")
    odd = d % 2 == 1
    start, _ = window(d)

    def own(w):
        return jnp.where(odd, w[:, 64:256], w[:, 0:192])

    def whole(at):
        parts = [dqkv[i, :, at * 256 : at * 256 + 256] for i in range(4)]
        return jnp.concatenate(
            [
                parts[0][:, :128], parts[0][:, 128:] + parts[1][:, :128], parts[1][:, 128:],
                parts[2][:, :128], parts[2][:, 128:] + parts[3][:, :128], parts[3][:, 128:],
            ],
            axis=1,
        )

    x, h, o = own(xw[...].astype(F32)).astype(BF), own(hw[...].astype(F32)).astype(BF), own(ow[...].astype(F32)).astype(BF)
    dq, dk, dv = whole(0), whole(1), whole(2)
    def leave(src, dst, n):
        cp = pltpu.make_async_copy(src, dst, big_out.at[n])
        cp.start()
        leaves.append(cp)

    for at, (out, dst, left, right) in enumerate(((gq, gq_o, x, dq), (gk, gk_o, x, dk), (gv, gv_o, x, dv), (go, go_o, o, da[...]))):
        out[0] = mats[at].astype(F32)
        out[1] = dot_tn(left, right)
        leave(out, dst, at)
    for j in range(4):
        l = slice(j * 768, j * 768 + 768)
        gi[0, :, l] = inner[:, l].astype(F32)
        gi[1, :, l] = dot_tn(h, du[j])
        leave(gi.at[:, :, l], gi_o.at[:, :, l], 4 + j)
    g2_[0] = outer[...].astype(F32)
    g2_[1] = dot_tn(e[...], df[...])
    leave(g2_, g2_o, 8)
    lanes = pl.ds(start, 256)
    mine = own(vec[:, lanes])
    vec_s[...] = vec1[...]
    vec_s[0:1, :] = row_sum(dq.astype(F32))
    vec_s[1:2, :] = row_sum(dv.astype(F32))
    cross = own(vec_s[:, lanes])
    for r, out in enumerate((gqb, gvb, gob, gg1, gc1, gb2, gg2, gc2)):
        out[0:1, :] = mine[r : r + 1]
        out[1:2, :] = cross[r : r + 1]
    gib[0:1, :] = vec[pl.ds(8 + d, 1), :]
    gib[1:2, :] = row_sum(du[d].astype(F32))
    gemb[...] = own(emb[:, lanes])
    for cp in leaves:
        cp.wait()


def finish(summed, crossed):
    (_, _, xw, hw, ow, e, _, _, da, df, vec1, emb) = crossed
    S = jax.ShapeDtypeStruct
    V = pl.BlockSpec(memory_space=pltpu.VMEM)
    square, line = S((2, 192, 768), F32), S((2, 192), F32)
    dx, y, outer, inner, mats, du, dqkv, vec = summed
    return pl.pallas_call(
        finish_kernel,
        out_shape=[
            S(y.shape, BF), S(dx.shape, BF),
            square, line, square, square, line, square, line, line, line,
            S((2, 192, 3072), F32), S((2, 768), F32), S((2, 768, 768), F32), line, line, line, S((32, 192), F32),
        ],
        in_specs=[ANY] * 2 + [V] * 14,
        out_specs=[ANY, ANY, ANY, V, ANY, ANY, V, ANY, V, V, V, ANY, V, ANY, V, V, V, V],
        scratch_shapes=[pltpu.VMEM((8, 768), F32), pltpu.VMEM((2,) + y.shape, BF)]
        + [pltpu.VMEM(t.shape, F32) for t in (square, square, square, square, S((2, 192, 3072), F32), S((2, 768, 768), F32))]
        + [pltpu.SemaphoreType.DMA((2,)), pltpu.SemaphoreType.DMA((2,)), pltpu.SemaphoreType.DMA((9,))],
        compiler_params=pltpu.CompilerParams(vmem_limit_bytes=67043328),
        name="finish_grads",
    )(dx, y, outer, inner, mats, vec, emb, xw, hw, ow, e, dqkv, du, da, df, vec1)


def fast_shards(
    inputs,
    doc_ids,
    cotangent,
    query_weight,
    query_bias,
    key_weight,
    value_weight,
    value_bias,
    out_weight,
    out_bias,
    first_gain,
    first_shift,
    inner_weight,
    inner_bias,
    outer_weight,
    outer_bias,
    second_gain,
    second_shift,
    segment_embed,
):
    weights = (query_weight, key_weight, value_weight, out_weight, inner_weight, outer_weight)
    vectors = (query_bias, value_bias, out_bias, first_gain, first_shift, inner_bias, outer_bias, second_gain, second_shift)
    full, windows, docs, saved, y, cls = start(inputs[0], weights, doc_ids, vectors, 1)
    windows = [w.reshape(-1, w.shape[-1]) for w in windows]
    crossed = cross(cls, segment_embed, cotangent, docs, *windows, out_weight, outer_weight, vectors, 2)
    summed = backward(
        inputs[0], cotangent[0], crossed, saved, y, full, first_gain, second_gain, 3
    )
    output, grad, *gradients = finish(summed, crossed)
    return (output[None], grad[None], *gradients)


def solution(mesh):
    placed = (
        P("dp", "seg", None),
        P("dp", None),
        P("dp", "seg", None),
        P(None, "dp", None),
        P(),
        P(None, "dp", None),
        P(None, "dp", None),
        P(),
        P(None, "dp", None),
        P(),
        P(),
        P(),
        P(None, "dp", None),
        P(),
        P(None, "dp", None),
        P(),
        P(),
        P(),
        P(),
    )
    square = mesh.shape["dp"] == 4 and mesh.shape["seg"] == 8
    return jax.shard_map(
        fast_shards if square else shards,
        mesh=mesh,
        in_specs=placed,
        out_specs=(
            P("dp", "seg", None),
            P("dp", "seg", None),
            P(None, "dp", None),
            P(None, "dp"),
            P(None, "dp", None),
            P(None, "dp", None),
            P(None, "dp"),
            P(None, "dp", None),
            P(None, "dp"),
            P(None, "dp"),
            P(None, "dp"),
            P(None, "dp", None),
            P(None, "dp"),
            P(None, "dp", None),
            P(None, "dp"),
            P(None, "dp"),
            P(None, "dp"),
            P(None, "dp"),
        ),
        check_vma=False,
    )
```

```python
import functools

import jax
import jax.numpy as jnp
from jax import lax
from jax.experimental import pallas as pl
from jax.experimental.pallas import tpu as pltpu
from jax.sharding import PartitionSpec as P

HEADS = 12
HEAD_DIM = 64
SEG_LEN = 128


epsilon = 1e-05


def normalize(values, gain, shift):
    centred = values - jnp.mean(values, axis=-1, keepdims=True)
    spread = jnp.mean(centred * centred, axis=-1, keepdims=True)
    return centred * lax.rsqrt(spread + epsilon) * gain + shift


def gelu_exact(values):
    return jax.nn.gelu(values, approximate=False)


def project(values, weight):
    return jnp.einsum("gnd,de->gne", values, weight, preferred_element_type=jnp.float32)


def back_project(values, weight):
    return jnp.einsum("gne,de->gnd", values, weight, preferred_element_type=jnp.float32)


def weight_grad(source, grads):
    return jnp.einsum("gnd,gne->de", source, grads, preferred_element_type=jnp.float32)


def row_total(values):
    return jnp.sum(values.astype(jnp.float32), axis=(0, 1))


def keep_pair(first_part, second_part):
    return (first_part, second_part)


def forward_layer(params, source, allowed, spread_keys):
    (
        query_weight,
        query_bias,
        key_weight,
        value_weight,
        value_bias,
        out_weight,
        out_bias,
        first_gain,
        first_shift,
        inner_weight,
        inner_bias,
        outer_weight,
        outer_bias,
        second_gain,
        second_shift,
    ) = params
    groups, length, width = source.shape
    queries = (project(source, query_weight) + query_bias.astype(jnp.float32)).astype(jnp.bfloat16)
    key_rows = project(source, key_weight).astype(jnp.bfloat16)
    value_rows = (project(source, value_weight) + value_bias.astype(jnp.float32)).astype(
        jnp.bfloat16
    )
    key_all, value_all = spread_keys(key_rows, value_rows)
    key_length = key_all.shape[1]
    query_heads = queries.reshape(groups, length, HEADS, HEAD_DIM)
    key_heads = key_all.reshape(groups, key_length, HEADS, HEAD_DIM)
    value_heads = value_all.reshape(groups, key_length, HEADS, HEAD_DIM)
    scores = (
        jnp.einsum("gqhe,gkhe->ghqk", query_heads, key_heads, preferred_element_type=jnp.float32)
        * 0.125
    )
    if allowed is not None:
        scores = jnp.where(allowed[:, None], scores, -1e30)
    attend = jax.nn.softmax(scores, axis=-1)
    attend_low = attend.astype(jnp.bfloat16)
    mixed = jnp.einsum(
        "ghqk,gkhe->gqhe", attend_low, value_heads, preferred_element_type=jnp.float32
    )
    mixed = mixed.astype(jnp.bfloat16).reshape(groups, length, width)
    branch = project(mixed, out_weight) + out_bias.astype(jnp.float32)
    hidden, first_pull = jax.vjp(
        normalize,
        source.astype(jnp.float32) + branch,
        first_gain.astype(jnp.float32),
        first_shift.astype(jnp.float32),
    )
    hidden_low = hidden.astype(jnp.bfloat16)
    inner = project(hidden_low, inner_weight) + inner_bias.astype(jnp.float32)
    active, gelu_pull = jax.vjp(gelu_exact, inner)
    active_low = active.astype(jnp.bfloat16)
    outer = project(active_low, outer_weight) + outer_bias.astype(jnp.float32)
    result, second_pull = jax.vjp(
        normalize, hidden + outer, second_gain.astype(jnp.float32), second_shift.astype(jnp.float32)
    )
    stored = (
        source,
        query_heads,
        key_heads,
        value_heads,
        attend,
        attend_low,
        mixed,
        first_pull,
        hidden_low,
        gelu_pull,
        active_low,
        second_pull,
    )
    return (result, stored)


def backward_layer(params, stored, grad_result, collect_keys):
    (
        query_weight,
        query_bias,
        key_weight,
        value_weight,
        value_bias,
        out_weight,
        out_bias,
        first_gain,
        first_shift,
        inner_weight,
        inner_bias,
        outer_weight,
        outer_bias,
        second_gain,
        second_shift,
    ) = params
    (
        source,
        query_heads,
        key_heads,
        value_heads,
        attend,
        attend_low,
        mixed,
        first_pull,
        hidden_low,
        gelu_pull,
        active_low,
        second_pull,
    ) = stored
    groups, length, width = source.shape
    key_length = key_heads.shape[1]
    grad_second_sum, grad_second_gain, grad_second_shift = second_pull(grad_result)
    grad_outer = grad_second_sum.astype(jnp.bfloat16)
    grad_outer_bias = row_total(grad_outer)
    grad_outer_weight = weight_grad(active_low, grad_outer)
    grad_active = back_project(grad_outer, outer_weight).astype(jnp.bfloat16)
    (grad_inner,) = gelu_pull(grad_active.astype(jnp.float32))
    grad_inner_low = grad_inner.astype(jnp.bfloat16)
    grad_inner_bias = row_total(grad_inner_low)
    grad_inner_weight = weight_grad(hidden_low, grad_inner_low)
    grad_hidden = grad_second_sum + back_project(grad_inner_low, inner_weight)
    grad_first_sum, grad_first_gain, grad_first_shift = first_pull(grad_hidden)
    grad_branch = grad_first_sum.astype(jnp.bfloat16)
    grad_out_bias = row_total(grad_branch)
    grad_out_weight = weight_grad(mixed, grad_branch)
    grad_mixed = back_project(grad_branch, out_weight).astype(jnp.bfloat16)
    grad_mixed = grad_mixed.reshape(groups, length, HEADS, HEAD_DIM)
    grad_attend = jnp.einsum(
        "gqhe,gkhe->ghqk", grad_mixed, value_heads, preferred_element_type=jnp.float32
    )
    grad_attend = grad_attend.astype(jnp.bfloat16).astype(jnp.float32)
    grad_value = jnp.einsum(
        "ghqk,gqhe->gkhe", attend_low, grad_mixed, preferred_element_type=jnp.float32
    )
    grad_value = grad_value.reshape(groups, key_length, width)
    grad_scores = attend * (grad_attend - jnp.sum(attend * grad_attend, axis=-1, keepdims=True))
    grad_scores = grad_scores.astype(jnp.bfloat16)
    grad_query = (
        jnp.einsum("ghqk,gkhe->gqhe", grad_scores, key_heads, preferred_element_type=jnp.float32)
        * 0.125
    )
    grad_query = grad_query.astype(jnp.bfloat16).reshape(groups, length, width)
    grad_key = (
        jnp.einsum("ghqk,gqhe->gkhe", grad_scores, query_heads, preferred_element_type=jnp.float32)
        * 0.125
    )
    grad_key = grad_key.reshape(groups, key_length, width)
    grad_key, grad_value = collect_keys(grad_key, grad_value)
    grad_key = grad_key.astype(jnp.bfloat16)
    grad_value = grad_value.astype(jnp.bfloat16)
    grad_source = (
        grad_first_sum
        + back_project(grad_query, query_weight)
        + back_project(grad_key, key_weight)
        + back_project(grad_value, value_weight)
    )
    gradients = (
        weight_grad(source, grad_query),
        row_total(grad_query),
        weight_grad(source, grad_key),
        weight_grad(source, grad_value),
        row_total(grad_value),
        grad_out_weight,
        grad_out_bias,
        grad_first_gain,
        grad_first_shift,
        grad_inner_weight,
        grad_inner_bias,
        grad_outer_weight,
        grad_outer_bias,
        grad_second_gain,
        grad_second_shift,
    )
    return (grad_source, gradients)


def shards(
    inputs,
    doc_ids,
    cotangent,
    query_weight,
    query_bias,
    key_weight,
    value_weight,
    value_bias,
    out_weight,
    out_bias,
    first_gain,
    first_shift,
    inner_weight,
    inner_bias,
    outer_weight,
    outer_bias,
    second_gain,
    second_shift,
    segment_embed,
):
    seg_count = lax.axis_size("seg")
    seg_index = lax.axis_index("seg")
    group_rows, local_length, width = inputs.shape
    seg_local = local_length // SEG_LEN
    query_full, key_full, value_full, out_full, inner_full, outer_full = (
        lax.all_gather(query_weight, "dp", axis=1, tiled=True),
        lax.all_gather(key_weight, "dp", axis=1, tiled=True),
        lax.all_gather(value_weight, "dp", axis=1, tiled=True),
        lax.all_gather(out_weight, "dp", axis=1, tiled=True),
        lax.all_gather(inner_weight, "dp", axis=1, tiled=True),
        lax.all_gather(outer_weight, "dp", axis=1, tiled=True),
    )
    stacked = (
        query_full,
        query_bias,
        key_full,
        value_full,
        value_bias,
        out_full,
        out_bias,
        first_gain,
        first_shift,
        inner_full,
        inner_bias,
        outer_full,
        outer_bias,
        second_gain,
        second_shift,
    )
    first_params = tuple((weight[0] for weight in stacked))
    cross_params = tuple((weight[1] for weight in stacked))
    pieces = inputs.reshape(group_rows * seg_local, SEG_LEN, width)
    segment_out, segment_stored = forward_layer(first_params, pieces, None, keep_pair)
    segment_grid = segment_out.reshape(group_rows, seg_local, SEG_LEN, width)
    position = lax.dynamic_slice_in_dim(segment_embed, seg_index * seg_local, seg_local, 0).astype(
        jnp.float32
    )
    heads_in = (segment_grid[:, :, 0, :] + position).astype(jnp.bfloat16)
    row_input = lax.all_gather(heads_in, "seg", axis=1, tiled=True)
    allowed = doc_ids[:, :, None] == doc_ids[:, None, :]
    cross_out, cross_stored = forward_layer(cross_params, row_input, allowed, keep_pair)
    returned = lax.dynamic_slice_in_dim(cross_out, seg_index * seg_local, seg_local, 1).astype(
        jnp.bfloat16
    )
    output = jnp.concatenate(
        [returned[:, :, None, :], segment_grid[:, :, 1:, :].astype(jnp.bfloat16)], axis=2
    )
    output = output.reshape(group_rows, local_length, width)
    cot_grid = cotangent.reshape(group_rows, seg_local, SEG_LEN, width)
    cot_heads = cot_grid[:, :, 0, :]
    grad_cross = lax.all_gather(cot_heads, "seg", axis=1, tiled=True)
    grad_row_input, cross_grads = backward_layer(
        cross_params, cross_stored, grad_cross.astype(jnp.float32), keep_pair
    )
    grad_row_low = grad_row_input.astype(jnp.bfloat16)
    factor = 1.0 / seg_count
    embed_grad = jnp.sum(grad_row_low.astype(jnp.float32), axis=0) * factor
    cross_grads = tuple((part * factor for part in cross_grads))
    grad_heads = lax.dynamic_slice_in_dim(grad_row_low, seg_index * seg_local, seg_local, 1)
    grad_grid = jnp.concatenate(
        [grad_heads[:, :, None, :].astype(jnp.float32), cot_grid[:, :, 1:, :].astype(jnp.float32)],
        axis=2,
    )
    grad_grid = grad_grid.reshape(group_rows * seg_local, SEG_LEN, width)
    grad_pieces, segment_grads = backward_layer(first_params, segment_stored, grad_grid, keep_pair)
    input_grad = grad_pieces.astype(jnp.bfloat16).reshape(group_rows, local_length, width)
    shares = (
        lax.psum_scatter(segment_grads[0], "dp", scatter_dimension=0, tiled=True),
        lax.psum_scatter(segment_grads[1], "dp", scatter_dimension=0, tiled=True),
        lax.psum_scatter(segment_grads[2], "dp", scatter_dimension=0, tiled=True),
        lax.psum_scatter(segment_grads[3], "dp", scatter_dimension=0, tiled=True),
        lax.psum_scatter(segment_grads[4], "dp", scatter_dimension=0, tiled=True),
        lax.psum_scatter(segment_grads[5], "dp", scatter_dimension=0, tiled=True),
        lax.psum_scatter(segment_grads[6], "dp", scatter_dimension=0, tiled=True),
        lax.psum_scatter(segment_grads[7], "dp", scatter_dimension=0, tiled=True),
        lax.psum_scatter(segment_grads[8], "dp", scatter_dimension=0, tiled=True),
        lax.psum_scatter(segment_grads[9], "dp", scatter_dimension=0, tiled=True),
        lax.psum_scatter(segment_grads[10], "dp", scatter_dimension=0, tiled=True),
        lax.psum_scatter(segment_grads[11], "dp", scatter_dimension=0, tiled=True),
        lax.psum_scatter(segment_grads[12], "dp", scatter_dimension=0, tiled=True),
        lax.psum_scatter(segment_grads[13], "dp", scatter_dimension=0, tiled=True),
        lax.psum_scatter(segment_grads[14], "dp", scatter_dimension=0, tiled=True),
        lax.psum_scatter(cross_grads[0], "dp", scatter_dimension=0, tiled=True),
        lax.psum_scatter(cross_grads[1], "dp", scatter_dimension=0, tiled=True),
        lax.psum_scatter(cross_grads[2], "dp", scatter_dimension=0, tiled=True),
        lax.psum_scatter(cross_grads[3], "dp", scatter_dimension=0, tiled=True),
        lax.psum_scatter(cross_grads[4], "dp", scatter_dimension=0, tiled=True),
        lax.psum_scatter(cross_grads[5], "dp", scatter_dimension=0, tiled=True),
        lax.psum_scatter(cross_grads[6], "dp", scatter_dimension=0, tiled=True),
        lax.psum_scatter(cross_grads[7], "dp", scatter_dimension=0, tiled=True),
        lax.psum_scatter(cross_grads[8], "dp", scatter_dimension=0, tiled=True),
        lax.psum_scatter(cross_grads[9], "dp", scatter_dimension=0, tiled=True),
        lax.psum_scatter(cross_grads[10], "dp", scatter_dimension=0, tiled=True),
        lax.psum_scatter(cross_grads[11], "dp", scatter_dimension=0, tiled=True),
        lax.psum_scatter(cross_grads[12], "dp", scatter_dimension=0, tiled=True),
        lax.psum_scatter(cross_grads[13], "dp", scatter_dimension=0, tiled=True),
        lax.psum_scatter(cross_grads[14], "dp", scatter_dimension=0, tiled=True),
        lax.psum_scatter(embed_grad, "dp", scatter_dimension=1, tiled=True),
    )
    summed = lax.psum(
        (
            shares[0],
            shares[1],
            shares[2],
            shares[3],
            shares[4],
            shares[5],
            shares[6],
            shares[7],
            shares[8],
            shares[9],
            shares[10],
            shares[11],
            shares[12],
            shares[13],
            shares[14],
            shares[15],
            shares[16],
            shares[17],
            shares[18],
            shares[19],
            shares[20],
            shares[21],
            shares[22],
            shares[23],
            shares[24],
            shares[25],
            shares[26],
            shares[27],
            shares[28],
            shares[29],
            shares[30],
        ),
        "seg",
    )
    totals = tuple((jnp.stack([summed[index], summed[index + 15]]) for index in range(15)))
    totals = totals + (summed[30],)
    return (output, input_grad) + tuple(totals)


MESH = pl.DeviceIdType.MESH
ANY = pl.BlockSpec(memory_space=pl.ANY)
BF = jnp.bfloat16
F32 = jnp.float32


def place():
    d = lax.axis_index("dp")
    s = lax.axis_index("seg")
    return d, s


def greet(peers):
    barrier = pltpu.get_barrier_semaphore()
    for peer in peers:
        pl.semaphore_signal(barrier, inc=1, device_id=peer, device_id_type=MESH)
    pl.semaphore_wait(barrier, len(peers))


def remote(src, dst, send, recv, peer):
    return pltpu.make_async_remote_copy(
        src_ref=src, dst_ref=dst, send_sem=send, recv_sem=recv, device_id=peer, device_id_type=MESH
    )


def plane_peers(d, s):
    c = s % 2
    x, y = d % 2, d // 2
    dx = 2 * y + 1 - x
    dy = 2 * (1 - y) + x
    first = dx * (1 - c) + dy * c
    second = dy * (1 - c) + dx * c
    return c, first, second, s + 1 - 2 * c


def window(d):
    return pl.multiple_of((3 * d) // 2 * 128, 128), d % 2 * 64


def everyone(d, s):
    me = d * 8 + s
    ahead = [lax.rem(me + j, 32) for j in range(1, 32)]
    behind = [lax.rem(me + 32 - j, 32) for j in range(1, 32)]
    return me, ahead, behind


AHEAD, LAG2, LAG4 = 3, 2, 4


def start_kernel(pieces, *refs):
    x, (qb, vb, ob, g1, c1, ib, b2, g2, c2), refs = refs[0], refs[1:10], refs[10:]
    shards, docs, refs = refs[:6], refs[6], refs[7:]
    fulls, wins, docs_all, refs = refs[:6], refs[6:10], refs[10], refs[11:]
    saved_o, y_o, cls_o, refs = refs[:12], refs[12], refs[13], refs[14:]
    full, wbounce, ids, refs = refs[:6], refs[6:10], refs[10], refs[11:]
    (q_s, k_s, v_s, p_s, o_s, h_s, e_s, gp_s, x1, r1, x2, r2), y_s, refs = refs[:12], refs[12], refs[13:]
    load_sem, link_send, link_recv, core_send, core_recv, wload_sem, store_sem, refs = *refs[:7], refs[7:]
    win_send, win_recv, wcore_send, wcore_recv, ids_send, ids_recv, full_sem, out_sem = refs
    vq, vk, vv, vo, vi, v2 = full
    d, s = place()
    c = s % 2
    z = s // 2
    xx, yy = d % 2, d // 2
    dx, dy, dd = 2 * yy + 1 - xx, 2 * (1 - yy) + xx, 3 - d
    other = s + 1 - 2 * c
    even = 1 - z % 2
    xpeer, ypeer, zpeer = (dx, s), (dy, s), (d, s + 4 * even - 2)

    def either(a, b):
        return a * even + b * (1 - even)

    segs = x.shape[0] // 128
    count = len(pieces)
    loads = [
        pltpu.make_async_copy(shards[i].at[0], full[i].at[pl.ds(pl.multiple_of(d * shards[i].shape[1], 64), shards[i].shape[1])], load_sem.at[i])
        for i in range(6)
    ]
    for cp in loads:
        cp.start()
    ids_load = pltpu.make_async_copy(docs, ids, load_sem.at[6])
    ids_load.start()
    origins = (shards[0], shards[1], shards[2], shards[4])
    wloads = []
    for w in range(4):
        width = wins[w].shape[-1]
        at = window(d)[0] if w < 3 else d * width
        cp = pltpu.make_async_copy(origins[w].at[1, :, pl.ds(pl.multiple_of(at, 128), width)], wbounce[w], wload_sem.at[w])
        cp.start()
        wloads.append(cp)
    greet([xpeer, ypeer, (dd, s), zpeer, (d, other)])

    def cols(ref):
        half = ref.shape[-1] // 2
        return pl.ds(pl.multiple_of(c * half, half), half)

    def mine(p, h):
        i, r0, rn = pieces[p]
        n = rn // 4
        return shards[i].at[0, pl.ds(pl.multiple_of(r0 + (2 * h + c) * n, 16), n)]

    def slot(p, src, h):
        i, r0, rn = pieces[p]
        n = rn // 4
        return full[i].at[pl.ds(pl.multiple_of(src * shards[i].shape[1] + r0 + (2 * h + c) * n, 16), n)]

    started, shared, stores = [], [], []

    def link(kind, p, src, dst, peer):
        return remote(src, dst, link_send.at[kind, p], link_recv.at[kind, p], peer)

    def go(cp):
        cp.start()
        started.append(cp)

    def arrived(kind, p, ref):
        link(kind, p, ref, ref, zpeer).wait_recv()
        cp = remote(ref, ref, core_send.at[kind, p], core_recv.at[kind, p], (d, other))
        cp.start()
        shared.append((pieces[p][0], cp))
        started.append(cp)

    def own(p):
        if p < count:
            go(link(0, p, mine(p, 1), slot(p, d, 1), xpeer))
            go(link(1, p, mine(p, 0), slot(p, d, 0), ypeer))

    loaded = set()

    far = (dd, dx, dy)

    def columns(w, dev, core):
        wide = wins[w].shape[-1]
        begin = window(dev)[0] if w < 3 else dev * wide
        return pl.ds(pl.multiple_of(begin + core * (wide // 2), 128), wide // 2)

    def cross_needs():
        ids_load.wait()
        for k, peer in enumerate(far):
            for w in range(4):
                go(remote(
                    origins[w].at[1, :, columns(w, peer, c)], wins[w].at[d, :, cols(wins[w])],
                    win_send.at[k, w], win_recv.at[k, w], (peer, s),
                ))
            go(remote(ids, docs_all.at[d], ids_send.at[k], ids_recv.at[k], (peer, s)))

    def step(p):
        own(p + AHEAD)
        if p < count:
            i = pieces[p][0]
            if i not in loaded:
                loads[i].wait()
                loaded.add(i)
            arrived(0, p, slot(p, dx, 1))
            arrived(1, p, slot(p, dy, 0))
            ref = slot(p, either(d, dy), 0)
            go(link(2, p, ref, ref, xpeer))
            ref = slot(p, either(d, dx), 1)
            go(link(3, p, ref, ref, ypeer))
            if p == count - 1:
                cross_needs()
        n = p - LAG2
        if 0 <= n < count:
            for kind, src, h in ((2, either(dx, dd), 0), (3, either(dy, dd), 1)):
                ref = slot(n, src, h)
                arrived(kind, n, ref)
                go(link(kind + 2, n, ref, ref, zpeer))
        n = p - LAG4
        if 0 <= n < count:
            arrived(4, n, slot(n, either(dd, dx), 0))
            arrived(5, n, slot(n, either(dd, dy), 1))

    ready = set()

    def whole(i):
        for j, cp in shared:
            if j == i:
                cp.wait_recv()
        assert i not in ready
        ready.add(i)
        cp = pltpu.make_async_copy(full[i], fulls[i], full_sem.at[i])
        cp.start()
        stores.append(cp)

    def save(n, ref):
        cp = pltpu.make_async_copy(ref, y_o if n == 12 else saved_o[n], out_sem.at[n])
        cp.start()
        stores.append(cp)

    rows, width = x.shape
    nt = width // TILE
    for p in range(AHEAD):
        own(p)
    at = 0

    def advance(upto):
        nonlocal at
        while at < min(upto, count + LAG4):
            step(at)
            at += 1

    last = {i: max(p for p in range(count) if pieces[p][0] == i) for i in range(6)}
    advance(last[2] + LAG4 + 1)
    for i in range(3):
        whole(i)

    for t in range(nt):
        lanes = slice(t * TILE, t * TILE + TILE)
        q_s[:, lanes] = (dot(x[...], vq[:, lanes]) + qb[0:1, lanes].astype(F32)).astype(BF)
        k_s[:, lanes] = dot(x[...], vk[:, lanes]).astype(BF)
        v_s[:, lanes] = (dot(x[...], vv[:, lanes]) + vb[0:1, lanes].astype(F32)).astype(BF)
    for n, ref in enumerate((q_s, k_s, v_s)):
        save(n, ref)
    advance(last[2] + LAG4 + 2)
    masks = head_masks()

    def attend(hp, carry):
        lanes = tiles(hp, 128)
        for s in range(segs):
            here = slice(s * 128, s * 128 + 128)
            qs, ks, vs = q_s[here, lanes], k_s[here, lanes], v_s[here, lanes]
            mixed = None
            for h in range(2):
                scores = dot_nt(qs * masks[h], ks)
                top = jnp.max(scores, axis=-1, keepdims=True)
                weight = jnp.exp((scores - top) * 0.125)
                share = (weight * (1.0 / jnp.sum(weight, axis=-1, keepdims=True))).astype(BF)
                p_s[hp, s, h] = share
                part = dot(share, vs * masks[h])
                mixed = part if mixed is None else mixed + part
            o_s[here, lanes] = mixed.astype(BF)
        return carry

    pairs = width // 128
    for g in range(pairs // 2):
        lax.fori_loop(2 * g, 2 * g + 2, attend, 0)
        advance(last[2] + LAG4 + 3 + g)
    save(3, p_s)
    save(4, o_s)
    advance(last[3] + LAG4 + 1)
    whole(3)

    def out(t, carry):
        lanes = tiles(t)
        x1[:, lanes] = dot(o_s[...], vo[:, lanes]) + ob[0:1, lanes].astype(F32) + x[:, lanes].astype(F32)
        return carry

    lax.fori_loop(0, nt, out, 0)

    def first(i, carry):
        r = tiles(i, 64)
        xhat, rstd = standard(x1[r, :])
        x1[r, :] = xhat
        r1[r, :] = jnp.broadcast_to(rstd, (64, 128))
        hidden = xhat * g1[0:1, :].astype(F32) + c1[0:1, :].astype(F32)
        h_s[r, :] = hidden.astype(BF)
        x2[r, :] = hidden + b2[0:1, :].astype(F32)
        return carry

    lax.fori_loop(0, rows // 64, first, 0)
    for n, ref in ((5, h_s), (8, x1), (9, r1)):
        save(n, ref)
    advance(last[4] + LAG4 + 1)
    whole(4)

    def ffn(t, carry):
        lanes = tiles(t)
        u = dot(h_s[...], vi[:, lanes]) + ib[0:1, lanes].astype(F32)
        e, gp = gelu_parts(u)
        e_s[:, lanes] = e.astype(BF)
        gp_s[:, lanes] = gp.astype(BF)
        return carry

    groups = vi.shape[1] // TILE // 2
    for g in range(groups):
        lax.fori_loop(2 * g, 2 * g + 2, ffn, 0)
        advance(last[4] + LAG4 + 2 + g)
    advance(count + LAG4)
    for w in range(4):
        wloads[w].wait()
        cp = pltpu.make_async_copy(wbounce[w], wins[w].at[d], store_sem.at[w])
        cp.start()
        stores.append(cp)
    for src, dst, i in ((ids, docs_all.at[d], 4),):
        cp = pltpu.make_async_copy(src, dst, store_sem.at[i])
        cp.start()
        stores.append(cp)
    save(6, e_s)
    save(7, gp_s)
    whole(5)

    def outer(t, carry):
        lanes = tiles(t)
        x2[:, lanes] += dot(e_s[...], v2[:, lanes])
        return carry

    lax.fori_loop(0, nt, outer, 0)

    def second(i, carry):
        r = tiles(i, 64)
        xhat, rstd = standard(x2[r, :])
        x2[r, :] = xhat
        r2[r, :] = jnp.broadcast_to(rstd, (64, 128))
        y_s[r, :] = (xhat * g2[0:1, :].astype(F32) + c2[0:1, :].astype(F32)).astype(BF)
        return carry

    lax.fori_loop(0, rows // 64, second, 0)
    for n, ref in ((10, x2), (11, r2), (12, y_s)):
        save(n, ref)
    for s_ in range(segs):
        cls_o[s_ : s_ + 1, :] = x2[s_ * 128 : s_ * 128 + 1, :] * g2[0:1, :].astype(F32) + c2[0:1, :].astype(F32)
    wcores = []
    for k, peer in enumerate(far):
        for w in range(4):
            got = wins[w].at[peer, :, cols(wins[w])]
            remote(got, got, win_send.at[k, w], win_recv.at[k, w], (peer, s)).wait_recv()
            cp = remote(got, got, wcore_send.at[k, w], wcore_recv.at[k, w], (d, other))
            cp.start()
            wcores.append(cp)
        remote(ids, docs_all.at[peer], ids_send.at[k], ids_recv.at[k], (peer, s)).wait_recv()
    for cp in started:
        cp.wait_send()
    for cp in wcores:
        cp.wait()
    for cp in stores:
        cp.wait()


def start(x, shards, docs, vectors, collective_id):
    cuts = (1, 1, 1, 1, 3, 4)
    pieces = []
    for i, w in enumerate(shards):
        n = w.shape[1] // cuts[i]
        pieces += [(i, p * n, n) for p in range(cuts[i])]
    count = len(pieces)
    S, VM, dma = jax.ShapeDtypeStruct, pltpu.VMEM, pltpu.SemaphoreType.DMA
    V = pl.BlockSpec(memory_space=pltpu.VMEM)
    part, width = shards[0].shape[1:]
    rows = x.shape[0]
    ff = shards[4].shape[2]
    segs = rows // 128
    wins = [(part, 256)] * 3 + [(part, ff // 4)]
    low, full, wide, col = ((rows, width), BF), ((rows, width), F32), ((rows, ff), BF), ((rows, 128), F32)
    saved = [low, low, low, ((width // 128, segs, 2, 128, 128), BF), low, low, wide, wide, full, col, full, col, low]
    outs = pl.pallas_call(
        functools.partial(start_kernel, pieces),
        out_shape=[S((4 * w.shape[1], w.shape[2]), w.dtype) for w in shards]
        + [S((4,) + w, BF) for w in wins]
        + [S((4,) + docs.shape, docs.dtype)]
        + [S(*t) for t in saved]
        + [S((segs, width), F32)],
        in_specs=[V] * 10 + [ANY] * 7,
        out_specs=[ANY] * 24 + [V],
        scratch_shapes=[VM((4 * w.shape[1], w.shape[2]), w.dtype) for w in shards]
        + [VM(w, BF) for w in wins]
        + [VM(docs.shape, docs.dtype)]
        + [VM(*t) for t in saved]
        + [dma((7,)), dma((6, count)), dma((6, count)), dma((6, count)), dma((6, count)), dma((4,)), dma((5,))]
        + [dma((3, 4)), dma((3, 4)), dma((3, 4)), dma((3, 4)), dma((3,)), dma((3,)), dma((6,)), dma((13,))],
        compiler_params=pltpu.CompilerParams(collective_id=collective_id, has_side_effects=True, vmem_limit_bytes=67043328),
        name="gather_forward",
    )(x, *vectors, *shards, docs)
    return outs[:6], outs[6:10], outs[10], outs[11:23], outs[23], outs[24]


def add_into(dst, a, b, rows):
    step = 48 if rows % 48 == 0 else 32

    def body(i, carry):
        r = pl.ds(pl.multiple_of(i * step, 16), step)
        dst[r, :] = (a[r, :].astype(F32) + b[r, :].astype(F32)).astype(dst.dtype)
        return carry

    lax.fori_loop(0, rows // step, body, 0)


TILE = 256


def dot(a, b):
    return lax.dot_general(a, b, (((1,), (0,)), ((), ())), preferred_element_type=F32)


def dot_nt(a, b):
    return lax.dot_general(a, b, (((1,), (1,)), ((), ())), preferred_element_type=F32)


def dot_tn(a, b):
    return lax.dot_general(a, b, (((0,), (0,)), ((), ())), preferred_element_type=F32)


def tiles(i, size=TILE):
    return pl.ds(pl.multiple_of(i * size, size), size)


def standard(r):
    centred = r - jnp.mean(r, axis=-1, keepdims=True)
    rstd = lax.rsqrt(jnp.mean(centred * centred, axis=-1, keepdims=True) + epsilon)
    return centred * rstd, rstd


def standard_back(grad, xhat, rstd):
    return rstd * (
        grad
        - jnp.mean(grad, axis=-1, keepdims=True)
        - xhat * jnp.mean(grad * xhat, axis=-1, keepdims=True)
    )


def gelu_parts(u):
    phi = 0.5 * (1.0 + lax.erf(u * 0.7071067811865476))
    return u * phi, phi + u * (0.3989422804014327 * jnp.exp(-0.5 * u * u))


def head_masks():
    lane = lax.broadcasted_iota(jnp.int32, (1, 128), 1)
    low = (lane < 64).astype(F32)
    return (low.astype(BF), (1.0 - low).astype(BF))


def row_sum(v):
    return jnp.sum(v, axis=0, keepdims=True)


LAGS = (0, 2, 3, 4, 5, 6, 7, 8)
CHUNKS = [("rows", 0), ("rows", 1), ("rows", 2), ("cols", 0), ("cols", 1), ("cols", 2), ("mats", 3), ("mats", 0), ("mats", 1), ("mats", 2)]


def backward_kernel(dcl, z, g1, g2, du_own, dqkv_own, x, cot, q, k, v, p, o, hb, e, gp, x1, r1, x2, r2, y, wq, wk, wv, wo, wi, w2, *refs):
    (dx_o, y_o, outer_o, inner_o, mats_o, du_all, dqkv_all, vec_o), refs = refs[:8], refs[8:]
    (xs, ds_, qs_, ks_, vs_, p_s, os_, hs, e_s, gp_s, x1s, r1s, acc, r2s, ys), refs = refs[:15], refs[15:]
    (vi, v2, df, ht, vecs, g_rows, g_cols, g_mats), refs = refs[:8], refs[8:]
    bufs, refs = refs[:18], refs[18:]
    in_sem, w_sem, res_sem, out_sem, vsum, vgot, vsend, vrcv, send, recv, kept, kept_sem, far_send, far_recv, near_send, near_recv = refs
    dev, s = place()
    c, first, second, other = plane_peers(dev, s)
    px, py = dev % 2, dev // 2
    a = px * (1 - c) + py * c
    b = py * (1 - c) + px * c
    z_at = s // 2
    z0, z1 = z_at % 2, z_at // 2
    znear = (z_at + 1 - 2 * z0) * 2 + c
    zfar = (z_at + 2 - 4 * z1) * 2 + c
    order = [(cot, ds_), (y, ys), (x2, acc), (r2, r2s), (e, e_s), (hb, hs), (w2, v2), (gp, gp_s), (wi, vi),
             (x1, x1s), (r1, r1s), (o, os_), (p, p_s), (q, qs_), (k, ks_), (v, vs_), (x, xs)]
    loads = [pltpu.make_async_copy(src, dst, in_sem.at[i]) for i, (src, dst) in enumerate(order)]
    for cp in loads:
        cp.start()
    greet([(first, s), (second, s), (3 - dev, s), (dev, other), (dev, znear), (dev, zfar)])
    rows, width = xs.shape
    segs, nt = rows // 128, width // TILE
    share = width // 4
    started, outs, results = [], [], []

    def go(cp):
        cp.start()
        started.append(cp)

    def arrived(ref, sem):
        pltpu.make_async_copy(ref, ref, sem).wait()

    crossing = ((du_own, du_all), (dqkv_own, dqkv_all))
    far = (3 - dev, first, second)
    half_rows = pl.ds(pl.multiple_of(c * 64, 64), 64)
    keeps, shared = [], []

    def cross_send():
        for m, (src, dst) in enumerate(crossing):
            for n, peer in enumerate(far):
                go(remote(src.at[half_rows], dst.at[dev, half_rows], far_send.at[m, n], far_recv.at[m, n], (peer, s)))

    for m, (src, dst) in enumerate(crossing):
        cp = pltpu.make_async_copy(src, kept.at[m], kept_sem.at[0, m])
        cp.start()
        keeps.append(cp)

    def cross_share():
        for m, (src, dst) in enumerate(crossing):
            for n, peer in enumerate(far):
                got = dst.at[peer, half_rows]
                remote(got, got, far_send.at[m, n], far_recv.at[m, n], (peer, s)).wait_recv()
                cp = remote(got, got, near_send.at[m, n], near_recv.at[m, n], (dev, other))
                cp.start()
                shared.append(cp)
            keeps[m].wait()
            cp = pltpu.make_async_copy(kept.at[m], dst.at[dev], kept_sem.at[1, m])
            cp.start()
            outs.append(cp)

    families = {"rows": 0, "cols": 1, "mats": 2}

    def part(n, core, quarters):
        kind, i = CHUNKS[n]
        if kind == "rows":
            return g_rows.at[quarters, pl.ds(pl.multiple_of(i * 256 + core * 128, 128), 128), :]
        ref = g_cols if kind == "cols" else g_mats
        half = ref.shape[-1] // 2
        return ref.at[i, quarters, :, pl.ds(pl.multiple_of(core * half, 128), half)]

    def buf(n, j):
        kind, i = CHUNKS[n]
        ref = bufs[families[kind] * 6 + j]
        return ref.at[i] if j < 5 else ref.at[:, i]

    def size(n):
        return 128 if CHUNKS[n][0] == "rows" else 192

    def own(n, quarter):
        return part(n, c, quarter)

    def fin(n, core, at=0, count=None):
        kind, i = CHUNKS[n]
        count = size(n) if count is None else count
        return bufs[families[kind] * 6 + 5].at[core, i, pl.ds(pl.multiple_of(at, 16), count), :]

    def quarter(aa, bb):
        return aa * (1 + c) + bb * (2 - c)

    def offer(n):
        go(remote(part(n, 1 - c, slice(None)), buf(n, 0), send.at[0, n], recv.at[0, n], (dev, other)))

    def write(n, core, i):
        kind, at = CHUNKS[n]
        src = bufs[families[kind] * 6 + 5].at[core, at]
        if kind == "rows":
            pairs_ = [(src, outer_o.at[pl.ds(pl.multiple_of(at * 256 + core * 128, 128), 128), :])]
        elif kind == "mats":
            pairs_ = [(src, mats_o.at[at, :, pl.ds(pl.multiple_of(core * 384, 128), 384)])]
        else:
            pairs_ = [
                (src.at[:, j * 256 : j * 256 + 256], inner_o.at[:, pl.ds(pl.multiple_of((2 * core + j) * 768 + at * 256, 128), 256)])
                for j in range(2)
            ]
        for j, (left, right) in enumerate(pairs_):
            cp = pltpu.make_async_copy(left, right, out_sem.at[i, j, n])
            cp.start()
            outs.append(cp)

    def stage(t, n):
        r = size(n)
        h, f = r // 2, r // 4
        if t == 1:
            got = buf(n, 0)
            arrived(got, recv.at[0, n])
            for bb in range(2):
                away = quarter(1 - a, bb)
                add_into(own(n, away), own(n, away), got.at[away], r)
                go(remote(own(n, away), buf(n, 1).at[bb], send.at[1 + bb, n], recv.at[1 + bb, n], (first, s)))
            for bb in range(2):
                keep = quarter(a, bb)
                add_into(own(n, keep), own(n, keep), got.at[keep], r)
        elif t == 2:
            got = buf(n, 1)
            for bb in range(2):
                arrived(got.at[bb], recv.at[1 + bb, n])
            away, keep = quarter(a, 1 - b), quarter(a, b)
            add_into(own(n, away), own(n, away), got.at[1 - b], r)
            go(remote(own(n, away), buf(n, 2), send.at[3, n], recv.at[3, n], (second, s)))
            add_into(own(n, keep), own(n, keep), got.at[b], r)
        elif t == 3:
            got = buf(n, 2)
            arrived(got, recv.at[3, n])
            keep = own(n, quarter(a, b))
            away = pl.ds(pl.multiple_of((1 - z0) * h, 16), h)
            mine = pl.ds(pl.multiple_of(z0 * h, 16), h)
            add_into(keep.at[away], keep.at[away], got.at[away], h)
            go(remote(keep.at[away], buf(n, 3), send.at[4, n], recv.at[4, n], (dev, znear)))
            add_into(keep.at[mine], keep.at[mine], got.at[mine], h)
        elif t == 4:
            got = buf(n, 3)
            arrived(got, recv.at[4, n])
            keep = own(n, quarter(a, b))
            away = pl.ds(pl.multiple_of(z0 * h + (1 - z1) * f, 16), f)
            mine = pl.ds(pl.multiple_of(z0 * h + z1 * f, 16), f)
            add_into(keep.at[away], keep.at[away], got.at[pl.ds(pl.multiple_of((1 - z1) * f, 16), f)], f)
            go(remote(keep.at[away], buf(n, 4), send.at[5, n], recv.at[5, n], (dev, zfar)))
            add_into(keep.at[mine], keep.at[mine], got.at[pl.ds(pl.multiple_of(z1 * f, 16), f)], f)
        elif t == 5:
            got = buf(n, 4)
            arrived(got, recv.at[5, n])
            mine = own(n, quarter(a, b)).at[pl.ds(pl.multiple_of(z0 * h + z1 * f, 16), f)]
            done = fin(n, c, z0 * h + z1 * f, f)
            add_into(done, mine, got, f)
            go(remote(done, done, send.at[6, n], recv.at[6, n], (dev, zfar)))
        elif t == 6:
            arrived(fin(n, c, z0 * h + (1 - z1) * f, f), recv.at[6, n])
            half = fin(n, c, z0 * h, h)
            go(remote(half, half, send.at[7, n], recv.at[7, n], (dev, znear)))
        elif t == 7:
            arrived(fin(n, c, (1 - z0) * h, h), recv.at[7, n])
            go(remote(fin(n, c), fin(n, c), send.at[8, n], recv.at[8, n], (dev, other)))
            write(n, c, 0)
        elif t == 8:
            arrived(fin(n, 1 - c), recv.at[8, n])
            write(n, 1 - c, 1)

    nc = len(CHUNKS)

    def slot(i):
        for t in (1, 2, 3, 4, 5, 6, 7, 8):
            n = i - LAGS[t - 1]
            if 0 <= n < nc:
                stage(t, n)

    vecs[...] = jnp.zeros_like(vecs)
    for i in range(4):
        loads[i].wait()

    def norm2(i, carry):
        gain_sum, shift_sum, bias_sum = carry
        r = tiles(i, 64)
        dy, out = ds_[r, :].astype(F32), ys[r, :].astype(F32)
        at = lax.broadcasted_iota(jnp.int32, (64, 1), 0) + i * 64
        for j in range(segs):
            dy = jnp.where(at == j * 128, dcl[j : j + 1, :], dy)
            out = jnp.where(at == j * 128, z[j : j + 1, :], out)
        ys[r, :] = out.astype(BF)
        xhat = acc[r, :]
        back = standard_back(dy * g2[0:1, :].astype(F32), xhat, r2s[r, 0:1])
        acc[r, :] = back
        low = back.astype(BF)
        df[r, :] = low
        return (gain_sum + row_sum(dy * xhat), shift_sum + row_sum(dy), bias_sum + row_sum(low.astype(F32)))

    zero = jnp.zeros((1, width), F32)
    sums = lax.fori_loop(0, rows // 64, norm2, (zero, zero, zero))
    vecs[6:7, :], vecs[7:8, :], vecs[5:6, :] = sums
    results.append(pltpu.make_async_copy(ys, y_o, res_sem.at[0]))
    results[0].start()
    loads[4].wait()

    def outer(j):
        def body(block, carry):
            g_rows[block, j * TILE : j * TILE + TILE, :] = dot_tn(e_s[:, tiles(block * nt + j)], df[...]).astype(BF)
            return carry

        return body

    lax.fori_loop(0, 4, outer(0), 0)
    offer(0)
    lax.fori_loop(0, 4, outer(1), 0)
    offer(1)
    slot(0)
    lax.fori_loop(0, 4, outer(2), 0)
    offer(2)
    slot(1)
    loads[5].wait()
    ht[...] = hs[...].T
    for i in range(6, 9):
        loads[i].wait()

    def ffn(j):
        def body(block, carry):
            wide = tiles(block * nt + j)
            lanes = slice(j * TILE, j * TILE + TILE)
            de = dot_nt(df[...], v2[wide, :]).astype(BF).astype(F32)
            du = (de * gp_s[:, wide].astype(F32)).astype(BF)
            vecs[pl.ds(8 + block, 1), lanes] = row_sum(du.astype(F32))
            inner = dot(ht[...], du).astype(BF)
            for i in range(4):
                g_cols[j, i, :, tiles(block)] = inner[i * share : i * share + share]
            acc[...] += dot_nt(du, vi[:, wide])
            return carry

        return body

    lax.fori_loop(0, 4, ffn(0), 0)
    offer(3)
    slot(2)
    lax.fori_loop(0, 2, ffn(1), 0)
    slot(3)
    lax.fori_loop(2, 4, ffn(1), 0)
    offer(4)
    lax.fori_loop(0, 4, ffn(2), 0)
    offer(5)
    wloads = [
        pltpu.make_async_copy(src, v2.at[i * width : i * width + width], w_sem.at[i])
        for i, src in enumerate((wo, wq, wk, wv))
    ]
    for cp in wloads:
        cp.start()
    slot(4)
    for i in range(9, 17):
        loads[i].wait()

    def norm1(i, carry):
        gain_sum, shift_sum, bias_sum = carry
        r = tiles(i, 64)
        dh = acc[r, :]
        xhat = x1s[r, :]
        back = standard_back(dh * g1[0:1, :].astype(F32), xhat, r1s[r, 0:1])
        acc[r, :] = back
        low = back.astype(BF)
        df[r, :] = low
        return (gain_sum + row_sum(dh * xhat), shift_sum + row_sum(dh), bias_sum + row_sum(low.astype(F32)))

    sums = lax.fori_loop(0, rows // 64, norm1, (zero, zero, zero))
    vecs[3:4, :], vecs[4:5, :], vecs[2:3, :] = sums
    ht[...] = os_[...].T

    def weights(at, rhs):
        def body(t, carry):
            lanes = tiles(t)
            back = dot(ht[...], rhs[:, lanes]).astype(BF)
            for i in range(4):
                g_mats[at, i, :, lanes] = back[i * share : i * share + share]
            return carry

        lax.fori_loop(0, nt, body, 0)

    weights(3, df)
    offer(6)
    slot(5)
    wloads[0].wait()

    def mixed(t, carry):
        lanes = tiles(t)
        ds_[:, lanes] = dot_nt(df[...], v2[lanes, :]).astype(BF)
        return carry

    lax.fori_loop(0, nt, mixed, 0)
    masks = head_masks()

    def attend(hp, carry):
        lanes = tiles(hp, 128)
        for j in range(segs):
            here = slice(j * 128, j * 128 + 128)
            qs, ks, vs, dos = qs_[here, lanes], ks_[here, lanes], vs_[here, lanes], ds_[here, lanes]
            dqs = dks = dvs = 0.0
            for h in range(2):
                pl_ = p_s[hp, j, h]
                pf = pl_.astype(F32)
                dom = dos * masks[h]
                dp = dot_nt(dom, vs).astype(BF).astype(F32)
                ds = (pf * (dp - jnp.sum(pf * dp, axis=-1, keepdims=True))).astype(BF)
                dqs += dot(ds, ks * masks[h])
                dks += dot_tn(ds, qs * masks[h])
                dvs += dot_tn(pl_, dom)
            qs_[here, lanes] = (dqs * 0.125).astype(BF)
            ks_[here, lanes] = (dks * 0.125).astype(BF)
            vs_[here, lanes] = dvs.astype(BF)
        return carry

    lax.fori_loop(0, 3, attend, 0)
    slot(6)
    lax.fori_loop(3, width // 128, attend, 0)
    vecs[0:1, :] = row_sum(qs_[...].astype(F32))
    vecs[1:2, :] = row_sum(vs_[...].astype(F32))
    ht[...] = xs[...].T
    weights(0, qs_)
    offer(7)
    slot(7)
    weights(1, ks_)
    offer(8)
    weights(2, vs_)
    offer(9)
    hops = [(dev, other), (first, s), (second, s), (dev, znear), (dev, zfar)]
    vsum[0] = vecs[...]

    def vector_hop(j):
        if j > 0:
            arrived(vgot.at[j - 1], vrcv.at[j - 1])
            vsum[j] = vsum[j - 1] + vgot[j - 1]
        if j < 5:
            go(remote(vsum.at[j], vgot.at[j], vsend.at[j], vrcv.at[j], hops[j]))

    slot(8)
    vector_hop(0)
    for i in range(1, 4):
        wloads[i].wait()

    def source(t, carry):
        r = tiles(t)
        dx = acc[:, r]
        for i, g in enumerate((qs_, ks_, vs_)):
            dx += dot_nt(g[...], v2[pl.ds(pl.multiple_of((i + 1) * width + t * TILE, TILE), TILE), :])
        xs[:, r] = dx.astype(BF)
        return carry

    lax.fori_loop(0, nt, source, 0)
    results.append(pltpu.make_async_copy(xs, dx_o, res_sem.at[1]))
    results[1].start()
    for i in range(9, nc + LAGS[7]):
        slot(i)
        if i < 14:
            vector_hop(i - 8)
        if i == nc + 1:
            cross_send()
    cross_share()
    vec_o[...] = vsum[5]
    for cp in started:
        cp.wait_send()
    for cp in outs + results + shared:
        cp.wait()


def backward(x, cot, crossed, saved, y, weights, g1, g2, collective_id):
    q, k, v, p, o, hb, e, gp, x1, r1, x2, r2 = saved
    rows, width = x.shape
    ff = weights[4].shape[1]
    share, nc = width // 4, len(CHUNKS)
    S, VM, dma = jax.ShapeDtypeStruct, pltpu.VMEM, pltpu.SemaphoreType.DMA
    V = pl.BlockSpec(memory_space=pltpu.VMEM)
    z, dcl, dqkv, du = crossed[0], crossed[1], crossed[6], crossed[7]
    four = S((4,) + du.shape, BF)
    arrays = (x, cot, q, k, v, p, o, hb, e, gp, x1, r1, x2, r2, y)

    def chunk(n, r, w):
        return [VM(t, BF) for t in ((n, 4, r, w), (n, 2, r, w), (n, r, w), (n, r // 2, w), (n, r // 4, w), (2, n, r, w))]

    return pl.pallas_call(
        backward_kernel,
        out_shape=[
            S((rows, width), BF), S((rows, width), BF), S((ff // 4, width), BF), S((share, ff), BF), S((4, share, width), BF),
            four, four, S((16, width), F32),
        ],
        in_specs=[V] * 4 + [ANY] * 23,
        out_specs=[ANY] * 7 + [V],
        scratch_shapes=[VM(t.shape, t.dtype) for t in arrays]
        + [
            VM((width, ff), BF), VM((ff, width), BF), VM((rows, width), BF), VM((width, rows), BF), VM((16, width), F32),
            VM((4, ff // 4, width), BF), VM((3, 4, share, ff // 3), BF), VM((4, 4, share, width), BF),
        ]
        + chunk(3, 128, width) + chunk(3, share, ff // 6) + chunk(4, share, width // 2)
        + [
            dma((17,)), dma((4,)), dma((2,)), dma((2, 2, nc)),
            VM((6, 16, width), F32), VM((5, 16, width), F32), dma((5,)), dma((5,)), dma((9, nc)), dma((9, nc)),
            VM((2,) + du.shape, BF), dma((2, 2)), dma((2, 3)), dma((2, 3)), dma((2, 3)), dma((2, 3)),
        ],
        compiler_params=pltpu.CompilerParams(collective_id=collective_id, has_side_effects=True, vmem_limit_bytes=67043328),
        name="backward_reduce",
    )(dcl, z, g1, g2, du, dqkv, *arrays, *weights)


def cross_kernel(cls, emb, docs, cot, wq, wk, wv, wi, out_w, outer_w,
                 qb, vb, ob, g1, c1, ib, b2, g2, c2,
                 z_o, dcl_o, xw_o, hw_o, ow_o, e_o, dqkv_o, du_o, da_o, df_o, vec_o, emb_o,
                 vq, vk, vv, vi, vo, v2, heads, xall, rows_s, p_s, part_s, total_s, send1, got1, send2, got2,
                 in_sem, all_send, all_recv, first_rows, cots, cot_all, row_sem, cot_send, cot_recv, s1, r1, s2, r2, s3, r3):
    d, s = place()
    c, first, second, other = plane_peers(d, s)
    start, off = window(d)
    me, ahead, behind = everyone(d, s)
    lane_w = pl.ds(start, 256)
    loads = [
        pltpu.make_async_copy(src, dst, in_sem.at[i])
        for i, (src, dst) in enumerate(
            (
                (wq, vq), (wk, vk), (wv, vv),
                (out_w.at[1], vo.at[pl.ds(pl.multiple_of(off, 64), 192)]),
                (wi, vi), (outer_w.at[1], v2),
            )
        )
    ]
    for cp in loads:
        cp.start()
    row_loads = [pltpu.make_async_copy(cot.at[0, pl.ds(i * 128, 8)], first_rows.at[i], row_sem.at[i]) for i in range(4)]
    for cp in row_loads:
        cp.start()
    vo[pl.ds(pl.multiple_of(192 * (1 - d % 2), 64), 64), :] = jnp.zeros((64, 768), BF)
    pick = lax.broadcasted_iota(jnp.int32, (8, 32), 0) + 4 * s == lax.broadcasted_iota(jnp.int32, (8, 32), 1)
    position = dot(pick.astype(BF), emb[...])
    heads[...] = (cls[...] + position[0:4]).astype(BF)
    greet([(i // 8, i % 8) for i in ahead])
    sent = []
    for j, i in enumerate(ahead):
        cp = remote(heads, xall.at[me], all_send.at[j], all_recv.at[j], (i // 8, i % 8))
        cp.start()
        sent.append(cp)
    xall[me] = heads[...]
    for cp in row_loads:
        cp.wait()
    cots[...] = jnp.concatenate([first_rows[i].astype(F32)[0:1] for i in range(4)], axis=0).astype(BF)
    cot_all[me] = cots[...]
    ids = lax.broadcasted_iota(jnp.int32, (8, 128), 1) // 32 * 1024
    ids = ids.astype(F32)
    lane = lax.broadcasted_iota(jnp.int32, (32, 128), 1)
    key = lax.broadcasted_iota(jnp.int32, (32, 128), 0)
    for r in range(4):
        numbers = jnp.broadcast_to(docs[r], (8, 32)).astype(F32).astype(BF)
        ids = ids + dot(numbers, (lane == key + 32 * r).astype(BF))
    across = jnp.broadcast_to(ids[0:1], (128, 128))
    allowed = across == across.T
    for j, i in enumerate(behind):
        remote(heads, xall.at[i], all_send.at[j], all_recv.at[j], (i // 8, i % 8)).wait_recv()
    for j, i in enumerate(ahead):
        cp = remote(cots, cot_all.at[me], cot_send.at[j], cot_recv.at[j], (i // 8, i % 8))
        cp.start()
        sent.append(cp)
    for i in range(32):
        rows_s[4 * i : 4 * i + 4, :] = xall[i].astype(F32)
    xf = rows_s[...]
    x = xf.astype(BF)

    def total(n, partial):
        half = pl.ds(pl.multiple_of(c * 64, 64), 64)
        part_s[...] = partial
        send1[n] = part_s[half, :].astype(BF)
        one = remote(send1.at[n], got1.at[n], s1.at[n], r1.at[n], (first, s))
        one.start()
        one.wait_recv()
        both = send1[n].astype(F32) + got1[n].astype(F32)
        send2[n] = both.astype(BF)
        two = remote(send2.at[n], got2.at[n], s2.at[n], r2.at[n], (second, s))
        two.start()
        two.wait_recv()
        total_s[n, half, :] = send2[n].astype(F32) + got2[n].astype(F32)
        three = remote(total_s.at[n, half], total_s.at[n, half], s3.at[n], r3.at[n], (d, other))
        three.start()
        three.wait_recv()
        sent.extend((one, two, three))
        return total_s[n]

    def vector(ref, lanes=slice(None)):
        return ref[1:2, lanes].astype(F32)

    for i in range(3):
        loads[i].wait()
    q = (dot(x, vq[...]) + vector(qb, lane_w)).astype(BF)
    k = dot(x, vk[...]).astype(BF)
    v = (dot(x, vv[...]) + vector(vb, lane_w)).astype(BF)
    masks = head_masks()
    mixed = []
    for pair in range(2):
        l = slice(pair * 128, pair * 128 + 128)
        both = None
        for h in range(2):
            scores = jnp.where(allowed, dot_nt(q[:, l] * masks[h], k[:, l]) * 0.125, -1e30)
            weight = jnp.exp(scores - jnp.max(scores, axis=-1, keepdims=True))
            share = (weight * (1.0 / jnp.sum(weight, axis=-1, keepdims=True))).astype(BF)
            p_s[2 * pair + h] = share
            part = dot(share, v[:, l] * masks[h])
            both = part if both is None else both + part
        mixed.append(both.astype(BF))
    loads[3].wait()
    ow = jnp.concatenate(mixed, axis=1)
    ow_o[...] = ow
    branch = total(0, dot(ow, vo[...]))
    xhat1, rstd1 = standard(xf + branch + vector(ob))
    hidden = xhat1 * vector(g1) + vector(c1)
    hb = hidden.astype(BF)
    rows_s[...] = hidden
    hw_o[...] = rows_s[:, lane_w].astype(BF)
    rows_s[...] = xf
    xw_o[...] = rows_s[:, lane_w].astype(BF)
    loads[4].wait()
    loads[5].wait()
    wide = pl.ds(pl.multiple_of(d * 768, 768), 768)
    e, gp = gelu_parts(dot(hb, vi[...]) + vector(ib, wide))
    e = e.astype(BF)
    e_o[...] = e
    outer = total(1, dot(e, v2[...]))
    xhat2, rstd2 = standard(hidden + outer + vector(b2))
    z = (xhat2 * vector(g2) + vector(c2)).astype(BF)
    own = lax.broadcasted_iota(jnp.int32, (8, 128), 0) + 4 * me == lax.broadcasted_iota(jnp.int32, (8, 128), 1)
    own = own.astype(BF)
    z_o[...] = dot(own, z)
    for j, i in enumerate(behind):
        remote(cots, cot_all.at[i], cot_send.at[j], cot_recv.at[j], (i // 8, i % 8)).wait_recv()
    for i in range(32):
        rows_s[4 * i : 4 * i + 4, :] = cot_all[i].astype(F32)
    dy = rows_s[...]
    vec_o[6:7, :] = row_sum(dy * xhat2)
    vec_o[7:8, :] = row_sum(dy)
    dr2 = standard_back(dy * vector(g2), xhat2, rstd2)
    df = dr2.astype(BF)
    df_o[...] = df
    vec_o[5:6, :] = row_sum(df.astype(F32))
    du = (dot_nt(df, v2[...]).astype(BF).astype(F32) * gp).astype(BF)
    du_o[...] = du
    dh = dr2 + total(2, dot_nt(du, vi[...]))
    vec_o[3:4, :] = row_sum(dh * xhat1)
    vec_o[4:5, :] = row_sum(dh)
    dr1 = standard_back(dh * vector(g1), xhat1, rstd1)
    da = dr1.astype(BF)
    da_o[...] = da
    vec_o[2:3, :] = row_sum(da.astype(F32))
    do = dot_nt(da, vo[...]).astype(BF)
    dqs, dks, dvs = [], [], []
    for pair in range(2):
        l = slice(pair * 128, pair * 128 + 128)
        dqp = dkp = dvp = 0.0
        for h in range(2):
            share = p_s[2 * pair + h]
            pf = share.astype(F32)
            dom = do[:, l] * masks[h]
            dp = dot_nt(dom, v[:, l]).astype(BF).astype(F32)
            ds = (pf * (dp - jnp.sum(pf * dp, axis=-1, keepdims=True))).astype(BF)
            dqp += dot(ds, k[:, l] * masks[h])
            dkp += dot_tn(ds, q[:, l] * masks[h])
            dvp += dot_tn(share, dom)
        dqs.append((dqp * 0.125).astype(BF))
        dks.append((dkp * 0.125).astype(BF))
        dvs.append(dvp.astype(BF))
    dq, dk, dv = (jnp.concatenate(t, axis=1) for t in (dqs, dks, dvs))
    dqkv_o[:, 0:256] = dq
    dqkv_o[:, 256:512] = dk
    dqkv_o[:, 512:768] = dv
    dx = dr1 + total(3, dot_nt(dq, vq[...]) + dot_nt(dk, vk[...]) + dot_nt(dv, vv[...]))
    dcl = dx.astype(BF)
    dcl_o[...] = dot(own, dcl)
    back = dcl.astype(F32)
    emb_o[...] = back[0:32] + back[32:64] + back[64:96] + back[96:128]
    for cp in sent:
        cp.wait_send()


def cross(cls, emb, cot, docs, wq, wk, wv, wi, out_w, outer_w, vectors, collective_id):
    S = jax.ShapeDtypeStruct
    V = pl.BlockSpec(memory_space=pltpu.VMEM)
    VM, dma = pltpu.VMEM, pltpu.SemaphoreType.DMA
    low, win = S((128, 768), BF), S((128, 256), BF)
    return pl.pallas_call(
        cross_kernel,
        out_shape=[
            S((8, 768), F32), S((8, 768), F32), win, win, win, low, low, low, low, low,
            S((8, 768), F32), S((32, 768), F32),
        ],
        in_specs=[V] * 3 + [ANY] * 7 + [V] * 9,
        out_specs=[V] * 12,
        scratch_shapes=[
            VM((768, 256), BF), VM((768, 256), BF), VM((768, 256), BF), VM((768, 768), BF), VM((256, 768), BF), VM((768, 768), BF),
            VM((4, 768), BF), VM((32, 4, 768), BF), VM((128, 768), F32), VM((4, 128, 128), BF),
            VM((128, 768), F32), VM((4, 128, 768), F32),
            VM((4, 64, 768), BF), VM((4, 64, 768), BF), VM((4, 64, 768), BF), VM((4, 64, 768), BF),
            dma((6,)), dma((31,)), dma((31,)),
            VM((4, 8, 768), BF), VM((4, 768), BF), VM((32, 4, 768), BF), dma((4,)), dma((31,)), dma((31,)),
            dma((4,)), dma((4,)), dma((4,)), dma((4,)), dma((4,)), dma((4,)),
        ],
        compiler_params=pltpu.CompilerParams(collective_id=collective_id, has_side_effects=True, vmem_limit_bytes=67043328),
        name="cross_block",
    )(cls, emb, docs, cot, wq, wk, wv, wi, out_w, outer_w, *vectors)


def finish_kernel(dx, y, outer, inner, mats, vec, emb, xw, hw, ow, e, dqkv, du, da, df, vec1,
                  y_o, dx_o, gq_o, gqb, gk_o, gv_o, gvb, go_o, gob, gg1, gc1, gi_o, gib, g2_o, gb2, gg2, gc2, gemb,
                  vec_s, pass_s, gq, gk, gv, go, gi, g2_, pass_in, pass_out, big_out):
    moves = [pltpu.make_async_copy(src, pass_s.at[i], pass_in.at[i]) for i, src in enumerate((y, dx))]
    for cp in moves:
        cp.start()
    leaves = []
    for i, dst in enumerate((y_o, dx_o)):
        moves[i].wait()
        cp = pltpu.make_async_copy(pass_s.at[i], dst, pass_out.at[i])
        cp.start()
        leaves.append(cp)
    d = lax.axis_index("dp")
    odd = d % 2 == 1
    start, _ = window(d)

    def own(w):
        return jnp.where(odd, w[:, 64:256], w[:, 0:192])

    def whole(at):
        parts = [dqkv[i, :, at * 256 : at * 256 + 256] for i in range(4)]
        return jnp.concatenate(
            [
                parts[0][:, :128], parts[0][:, 128:] + parts[1][:, :128], parts[1][:, 128:],
                parts[2][:, :128], parts[2][:, 128:] + parts[3][:, :128], parts[3][:, 128:],
            ],
            axis=1,
        )

    x, h, o = own(xw[...].astype(F32)).astype(BF), own(hw[...].astype(F32)).astype(BF), own(ow[...].astype(F32)).astype(BF)
    dq, dk, dv = whole(0), whole(1), whole(2)
    def leave(src, dst, n):
        cp = pltpu.make_async_copy(src, dst, big_out.at[n])
        cp.start()
        leaves.append(cp)

    for at, (out, dst, left, right) in enumerate(((gq, gq_o, x, dq), (gk, gk_o, x, dk), (gv, gv_o, x, dv), (go, go_o, o, da[...]))):
        out[0] = mats[at].astype(F32)
        out[1] = dot_tn(left, right)
        leave(out, dst, at)
    for j in range(4):
        l = slice(j * 768, j * 768 + 768)
        gi[0, :, l] = inner[:, l].astype(F32)
        gi[1, :, l] = dot_tn(h, du[j])
        leave(gi.at[:, :, l], gi_o.at[:, :, l], 4 + j)
    g2_[0] = outer[...].astype(F32)
    g2_[1] = dot_tn(e[...], df[...])
    leave(g2_, g2_o, 8)
    lanes = pl.ds(start, 256)
    mine = own(vec[:, lanes])
    vec_s[...] = vec1[...]
    vec_s[0:1, :] = row_sum(dq.astype(F32))
    vec_s[1:2, :] = row_sum(dv.astype(F32))
    cross = own(vec_s[:, lanes])
    for r, out in enumerate((gqb, gvb, gob, gg1, gc1, gb2, gg2, gc2)):
        out[0:1, :] = mine[r : r + 1]
        out[1:2, :] = cross[r : r + 1]
    gib[0:1, :] = vec[pl.ds(8 + d, 1), :]
    gib[1:2, :] = row_sum(du[d].astype(F32))
    gemb[...] = own(emb[:, lanes])
    for cp in leaves:
        cp.wait()


def finish(summed, crossed):
    (_, _, xw, hw, ow, e, _, _, da, df, vec1, emb) = crossed
    S = jax.ShapeDtypeStruct
    V = pl.BlockSpec(memory_space=pltpu.VMEM)
    square, line = S((2, 192, 768), F32), S((2, 192), F32)
    dx, y, outer, inner, mats, du, dqkv, vec = summed
    return pl.pallas_call(
        finish_kernel,
        out_shape=[
            S(y.shape, BF), S(dx.shape, BF),
            square, line, square, square, line, square, line, line, line,
            S((2, 192, 3072), F32), S((2, 768), F32), S((2, 768, 768), F32), line, line, line, S((32, 192), F32),
        ],
        in_specs=[ANY] * 2 + [V] * 14,
        out_specs=[ANY, ANY, ANY, V, ANY, ANY, V, ANY, V, V, V, ANY, V, ANY, V, V, V, V],
        scratch_shapes=[pltpu.VMEM((8, 768), F32), pltpu.VMEM((2,) + y.shape, BF)]
        + [pltpu.VMEM(t.shape, F32) for t in (square, square, square, square, S((2, 192, 3072), F32), S((2, 768, 768), F32))]
        + [pltpu.SemaphoreType.DMA((2,)), pltpu.SemaphoreType.DMA((2,)), pltpu.SemaphoreType.DMA((9,))],
        compiler_params=pltpu.CompilerParams(vmem_limit_bytes=67043328),
        name="finish_grads",
    )(dx, y, outer, inner, mats, vec, emb, xw, hw, ow, e, dqkv, du, da, df, vec1)


def fast_shards(
    inputs,
    doc_ids,
    cotangent,
    query_weight,
    query_bias,
    key_weight,
    value_weight,
    value_bias,
    out_weight,
    out_bias,
    first_gain,
    first_shift,
    inner_weight,
    inner_bias,
    outer_weight,
    outer_bias,
    second_gain,
    second_shift,
    segment_embed,
):
    weights = (query_weight, key_weight, value_weight, out_weight, inner_weight, outer_weight)
    vectors = (query_bias, value_bias, out_bias, first_gain, first_shift, inner_bias, outer_bias, second_gain, second_shift)
    full, windows, docs, saved, y, cls = start(inputs[0], weights, doc_ids, vectors, 1)
    windows = [w.reshape(-1, w.shape[-1]) for w in windows]
    crossed = cross(cls, segment_embed, cotangent, docs, *windows, out_weight, outer_weight, vectors, 2)
    summed = backward(
        inputs[0], cotangent[0], crossed, saved, y, full, first_gain, second_gain, 3
    )
    output, grad, *gradients = finish(summed, crossed)
    return (output[None], grad[None], *gradients)


def solution(mesh):
    placed = (
        P("dp", "seg", None),
        P("dp", None),
        P("dp", "seg", None),
        P(None, "dp", None),
        P(),
        P(None, "dp", None),
        P(None, "dp", None),
        P(),
        P(None, "dp", None),
        P(),
        P(),
        P(),
        P(None, "dp", None),
        P(),
        P(None, "dp", None),
        P(),
        P(),
        P(),
        P(),
    )
    square = mesh.shape["dp"] == 4 and mesh.shape["seg"] == 8
    return jax.shard_map(
        fast_shards if square else shards,
        mesh=mesh,
        in_specs=placed,
        out_specs=(
            P("dp", "seg", None),
            P("dp", "seg", None),
            P(None, "dp", None),
            P(None, "dp"),
            P(None, "dp", None),
            P(None, "dp", None),
            P(None, "dp"),
            P(None, "dp", None),
            P(None, "dp"),
            P(None, "dp"),
            P(None, "dp"),
            P(None, "dp", None),
            P(None, "dp"),
            P(None, "dp", None),
            P(None, "dp"),
            P(None, "dp"),
            P(None, "dp"),
            P(None, "dp"),
        ),
        check_vma=False,
    )
```

```python
import functools

import jax
import jax.numpy as jnp
from jax import lax
from jax.experimental import pallas as pl
from jax.experimental.pallas import tpu as pltpu
from jax.sharding import PartitionSpec as P

HEADS = 12
HEAD_DIM = 64
SEG_LEN = 128


epsilon = 1e-05


def normalize(values, gain, shift):
    centred = values - jnp.mean(values, axis=-1, keepdims=True)
    spread = jnp.mean(centred * centred, axis=-1, keepdims=True)
    return centred * lax.rsqrt(spread + epsilon) * gain + shift


def gelu_exact(values):
    return jax.nn.gelu(values, approximate=False)


def project(values, weight):
    return jnp.einsum("gnd,de->gne", values, weight, preferred_element_type=jnp.float32)


def back_project(values, weight):
    return jnp.einsum("gne,de->gnd", values, weight, preferred_element_type=jnp.float32)


def weight_grad(source, grads):
    return jnp.einsum("gnd,gne->de", source, grads, preferred_element_type=jnp.float32)


def row_total(values):
    return jnp.sum(values.astype(jnp.float32), axis=(0, 1))


def keep_pair(first_part, second_part):
    return (first_part, second_part)


def forward_layer(params, source, allowed, spread_keys):
    (
        query_weight,
        query_bias,
        key_weight,
        value_weight,
        value_bias,
        out_weight,
        out_bias,
        first_gain,
        first_shift,
        inner_weight,
        inner_bias,
        outer_weight,
        outer_bias,
        second_gain,
        second_shift,
    ) = params
    groups, length, width = source.shape
    queries = (project(source, query_weight) + query_bias.astype(jnp.float32)).astype(jnp.bfloat16)
    key_rows = project(source, key_weight).astype(jnp.bfloat16)
    value_rows = (project(source, value_weight) + value_bias.astype(jnp.float32)).astype(
        jnp.bfloat16
    )
    key_all, value_all = spread_keys(key_rows, value_rows)
    key_length = key_all.shape[1]
    query_heads = queries.reshape(groups, length, HEADS, HEAD_DIM)
    key_heads = key_all.reshape(groups, key_length, HEADS, HEAD_DIM)
    value_heads = value_all.reshape(groups, key_length, HEADS, HEAD_DIM)
    scores = (
        jnp.einsum("gqhe,gkhe->ghqk", query_heads, key_heads, preferred_element_type=jnp.float32)
        * 0.125
    )
    if allowed is not None:
        scores = jnp.where(allowed[:, None], scores, -1e30)
    attend = jax.nn.softmax(scores, axis=-1)
    attend_low = attend.astype(jnp.bfloat16)
    mixed = jnp.einsum(
        "ghqk,gkhe->gqhe", attend_low, value_heads, preferred_element_type=jnp.float32
    )
    mixed = mixed.astype(jnp.bfloat16).reshape(groups, length, width)
    branch = project(mixed, out_weight) + out_bias.astype(jnp.float32)
    hidden, first_pull = jax.vjp(
        normalize,
        source.astype(jnp.float32) + branch,
        first_gain.astype(jnp.float32),
        first_shift.astype(jnp.float32),
    )
    hidden_low = hidden.astype(jnp.bfloat16)
    inner = project(hidden_low, inner_weight) + inner_bias.astype(jnp.float32)
    active, gelu_pull = jax.vjp(gelu_exact, inner)
    active_low = active.astype(jnp.bfloat16)
    outer = project(active_low, outer_weight) + outer_bias.astype(jnp.float32)
    result, second_pull = jax.vjp(
        normalize, hidden + outer, second_gain.astype(jnp.float32), second_shift.astype(jnp.float32)
    )
    stored = (
        source,
        query_heads,
        key_heads,
        value_heads,
        attend,
        attend_low,
        mixed,
        first_pull,
        hidden_low,
        gelu_pull,
        active_low,
        second_pull,
    )
    return (result, stored)


def backward_layer(params, stored, grad_result, collect_keys):
    (
        query_weight,
        query_bias,
        key_weight,
        value_weight,
        value_bias,
        out_weight,
        out_bias,
        first_gain,
        first_shift,
        inner_weight,
        inner_bias,
        outer_weight,
        outer_bias,
        second_gain,
        second_shift,
    ) = params
    (
        source,
        query_heads,
        key_heads,
        value_heads,
        attend,
        attend_low,
        mixed,
        first_pull,
        hidden_low,
        gelu_pull,
        active_low,
        second_pull,
    ) = stored
    groups, length, width = source.shape
    key_length = key_heads.shape[1]
    grad_second_sum, grad_second_gain, grad_second_shift = second_pull(grad_result)
    grad_outer = grad_second_sum.astype(jnp.bfloat16)
    grad_outer_bias = row_total(grad_outer)
    grad_outer_weight = weight_grad(active_low, grad_outer)
    grad_active = back_project(grad_outer, outer_weight).astype(jnp.bfloat16)
    (grad_inner,) = gelu_pull(grad_active.astype(jnp.float32))
    grad_inner_low = grad_inner.astype(jnp.bfloat16)
    grad_inner_bias = row_total(grad_inner_low)
    grad_inner_weight = weight_grad(hidden_low, grad_inner_low)
    grad_hidden = grad_second_sum + back_project(grad_inner_low, inner_weight)
    grad_first_sum, grad_first_gain, grad_first_shift = first_pull(grad_hidden)
    grad_branch = grad_first_sum.astype(jnp.bfloat16)
    grad_out_bias = row_total(grad_branch)
    grad_out_weight = weight_grad(mixed, grad_branch)
    grad_mixed = back_project(grad_branch, out_weight).astype(jnp.bfloat16)
    grad_mixed = grad_mixed.reshape(groups, length, HEADS, HEAD_DIM)
    grad_attend = jnp.einsum(
        "gqhe,gkhe->ghqk", grad_mixed, value_heads, preferred_element_type=jnp.float32
    )
    grad_attend = grad_attend.astype(jnp.bfloat16).astype(jnp.float32)
    grad_value = jnp.einsum(
        "ghqk,gqhe->gkhe", attend_low, grad_mixed, preferred_element_type=jnp.float32
    )
    grad_value = grad_value.reshape(groups, key_length, width)
    grad_scores = attend * (grad_attend - jnp.sum(attend * grad_attend, axis=-1, keepdims=True))
    grad_scores = grad_scores.astype(jnp.bfloat16)
    grad_query = (
        jnp.einsum("ghqk,gkhe->gqhe", grad_scores, key_heads, preferred_element_type=jnp.float32)
        * 0.125
    )
    grad_query = grad_query.astype(jnp.bfloat16).reshape(groups, length, width)
    grad_key = (
        jnp.einsum("ghqk,gqhe->gkhe", grad_scores, query_heads, preferred_element_type=jnp.float32)
        * 0.125
    )
    grad_key = grad_key.reshape(groups, key_length, width)
    grad_key, grad_value = collect_keys(grad_key, grad_value)
    grad_key = grad_key.astype(jnp.bfloat16)
    grad_value = grad_value.astype(jnp.bfloat16)
    grad_source = (
        grad_first_sum
        + back_project(grad_query, query_weight)
        + back_project(grad_key, key_weight)
        + back_project(grad_value, value_weight)
    )
    gradients = (
        weight_grad(source, grad_query),
        row_total(grad_query),
        weight_grad(source, grad_key),
        weight_grad(source, grad_value),
        row_total(grad_value),
        grad_out_weight,
        grad_out_bias,
        grad_first_gain,
        grad_first_shift,
        grad_inner_weight,
        grad_inner_bias,
        grad_outer_weight,
        grad_outer_bias,
        grad_second_gain,
        grad_second_shift,
    )
    return (grad_source, gradients)


def shards(
    inputs,
    doc_ids,
    cotangent,
    query_weight,
    query_bias,
    key_weight,
    value_weight,
    value_bias,
    out_weight,
    out_bias,
    first_gain,
    first_shift,
    inner_weight,
    inner_bias,
    outer_weight,
    outer_bias,
    second_gain,
    second_shift,
    segment_embed,
):
    seg_count = lax.axis_size("seg")
    seg_index = lax.axis_index("seg")
    group_rows, local_length, width = inputs.shape
    seg_local = local_length // SEG_LEN
    query_full, key_full, value_full, out_full, inner_full, outer_full = (
        lax.all_gather(query_weight, "dp", axis=1, tiled=True),
        lax.all_gather(key_weight, "dp", axis=1, tiled=True),
        lax.all_gather(value_weight, "dp", axis=1, tiled=True),
        lax.all_gather(out_weight, "dp", axis=1, tiled=True),
        lax.all_gather(inner_weight, "dp", axis=1, tiled=True),
        lax.all_gather(outer_weight, "dp", axis=1, tiled=True),
    )
    stacked = (
        query_full,
        query_bias,
        key_full,
        value_full,
        value_bias,
        out_full,
        out_bias,
        first_gain,
        first_shift,
        inner_full,
        inner_bias,
        outer_full,
        outer_bias,
        second_gain,
        second_shift,
    )
    first_params = tuple((weight[0] for weight in stacked))
    cross_params = tuple((weight[1] for weight in stacked))
    pieces = inputs.reshape(group_rows * seg_local, SEG_LEN, width)
    segment_out, segment_stored = forward_layer(first_params, pieces, None, keep_pair)
    segment_grid = segment_out.reshape(group_rows, seg_local, SEG_LEN, width)
    position = lax.dynamic_slice_in_dim(segment_embed, seg_index * seg_local, seg_local, 0).astype(
        jnp.float32
    )
    heads_in = (segment_grid[:, :, 0, :] + position).astype(jnp.bfloat16)
    row_input = lax.all_gather(heads_in, "seg", axis=1, tiled=True)
    allowed = doc_ids[:, :, None] == doc_ids[:, None, :]
    cross_out, cross_stored = forward_layer(cross_params, row_input, allowed, keep_pair)
    returned = lax.dynamic_slice_in_dim(cross_out, seg_index * seg_local, seg_local, 1).astype(
        jnp.bfloat16
    )
    output = jnp.concatenate(
        [returned[:, :, None, :], segment_grid[:, :, 1:, :].astype(jnp.bfloat16)], axis=2
    )
    output = output.reshape(group_rows, local_length, width)
    cot_grid = cotangent.reshape(group_rows, seg_local, SEG_LEN, width)
    cot_heads = cot_grid[:, :, 0, :]
    grad_cross = lax.all_gather(cot_heads, "seg", axis=1, tiled=True)
    grad_row_input, cross_grads = backward_layer(
        cross_params, cross_stored, grad_cross.astype(jnp.float32), keep_pair
    )
    grad_row_low = grad_row_input.astype(jnp.bfloat16)
    factor = 1.0 / seg_count
    embed_grad = jnp.sum(grad_row_low.astype(jnp.float32), axis=0) * factor
    cross_grads = tuple((part * factor for part in cross_grads))
    grad_heads = lax.dynamic_slice_in_dim(grad_row_low, seg_index * seg_local, seg_local, 1)
    grad_grid = jnp.concatenate(
        [grad_heads[:, :, None, :].astype(jnp.float32), cot_grid[:, :, 1:, :].astype(jnp.float32)],
        axis=2,
    )
    grad_grid = grad_grid.reshape(group_rows * seg_local, SEG_LEN, width)
    grad_pieces, segment_grads = backward_layer(first_params, segment_stored, grad_grid, keep_pair)
    input_grad = grad_pieces.astype(jnp.bfloat16).reshape(group_rows, local_length, width)
    shares = (
        lax.psum_scatter(segment_grads[0], "dp", scatter_dimension=0, tiled=True),
        lax.psum_scatter(segment_grads[1], "dp", scatter_dimension=0, tiled=True),
        lax.psum_scatter(segment_grads[2], "dp", scatter_dimension=0, tiled=True),
        lax.psum_scatter(segment_grads[3], "dp", scatter_dimension=0, tiled=True),
        lax.psum_scatter(segment_grads[4], "dp", scatter_dimension=0, tiled=True),
        lax.psum_scatter(segment_grads[5], "dp", scatter_dimension=0, tiled=True),
        lax.psum_scatter(segment_grads[6], "dp", scatter_dimension=0, tiled=True),
        lax.psum_scatter(segment_grads[7], "dp", scatter_dimension=0, tiled=True),
        lax.psum_scatter(segment_grads[8], "dp", scatter_dimension=0, tiled=True),
        lax.psum_scatter(segment_grads[9], "dp", scatter_dimension=0, tiled=True),
        lax.psum_scatter(segment_grads[10], "dp", scatter_dimension=0, tiled=True),
        lax.psum_scatter(segment_grads[11], "dp", scatter_dimension=0, tiled=True),
        lax.psum_scatter(segment_grads[12], "dp", scatter_dimension=0, tiled=True),
        lax.psum_scatter(segment_grads[13], "dp", scatter_dimension=0, tiled=True),
        lax.psum_scatter(segment_grads[14], "dp", scatter_dimension=0, tiled=True),
        lax.psum_scatter(cross_grads[0], "dp", scatter_dimension=0, tiled=True),
        lax.psum_scatter(cross_grads[1], "dp", scatter_dimension=0, tiled=True),
        lax.psum_scatter(cross_grads[2], "dp", scatter_dimension=0, tiled=True),
        lax.psum_scatter(cross_grads[3], "dp", scatter_dimension=0, tiled=True),
        lax.psum_scatter(cross_grads[4], "dp", scatter_dimension=0, tiled=True),
        lax.psum_scatter(cross_grads[5], "dp", scatter_dimension=0, tiled=True),
        lax.psum_scatter(cross_grads[6], "dp", scatter_dimension=0, tiled=True),
        lax.psum_scatter(cross_grads[7], "dp", scatter_dimension=0, tiled=True),
        lax.psum_scatter(cross_grads[8], "dp", scatter_dimension=0, tiled=True),
        lax.psum_scatter(cross_grads[9], "dp", scatter_dimension=0, tiled=True),
        lax.psum_scatter(cross_grads[10], "dp", scatter_dimension=0, tiled=True),
        lax.psum_scatter(cross_grads[11], "dp", scatter_dimension=0, tiled=True),
        lax.psum_scatter(cross_grads[12], "dp", scatter_dimension=0, tiled=True),
        lax.psum_scatter(cross_grads[13], "dp", scatter_dimension=0, tiled=True),
        lax.psum_scatter(cross_grads[14], "dp", scatter_dimension=0, tiled=True),
        lax.psum_scatter(embed_grad, "dp", scatter_dimension=1, tiled=True),
    )
    summed = lax.psum(
        (
            shares[0],
            shares[1],
            shares[2],
            shares[3],
            shares[4],
            shares[5],
            shares[6],
            shares[7],
            shares[8],
            shares[9],
            shares[10],
            shares[11],
            shares[12],
            shares[13],
            shares[14],
            shares[15],
            shares[16],
            shares[17],
            shares[18],
            shares[19],
            shares[20],
            shares[21],
            shares[22],
            shares[23],
            shares[24],
            shares[25],
            shares[26],
            shares[27],
            shares[28],
            shares[29],
            shares[30],
        ),
        "seg",
    )
    totals = tuple((jnp.stack([summed[index], summed[index + 15]]) for index in range(15)))
    totals = totals + (summed[30],)
    return (output, input_grad) + tuple(totals)


MESH = pl.DeviceIdType.MESH
ANY = pl.BlockSpec(memory_space=pl.ANY)
BF = jnp.bfloat16
F32 = jnp.float32


def place():
    d = lax.axis_index("dp")
    s = lax.axis_index("seg")
    return d, s


def greet(peers):
    barrier = pltpu.get_barrier_semaphore()
    for peer in peers:
        pl.semaphore_signal(barrier, inc=1, device_id=peer, device_id_type=MESH)
    pl.semaphore_wait(barrier, len(peers))


def remote(src, dst, send, recv, peer):
    return pltpu.make_async_remote_copy(
        src_ref=src, dst_ref=dst, send_sem=send, recv_sem=recv, device_id=peer, device_id_type=MESH
    )


def plane_peers(d, s):
    c = s % 2
    x, y = d % 2, d // 2
    dx = 2 * y + 1 - x
    dy = 2 * (1 - y) + x
    first = dx * (1 - c) + dy * c
    second = dy * (1 - c) + dx * c
    return c, first, second, s + 1 - 2 * c


def window(d):
    return pl.multiple_of((3 * d) // 2 * 128, 128), d % 2 * 64


def everyone(d, s):
    me = d * 8 + s
    ahead = [lax.rem(me + j, 32) for j in range(1, 32)]
    behind = [lax.rem(me + 32 - j, 32) for j in range(1, 32)]
    return me, ahead, behind


AHEAD, LAG2, LAG4 = 3, 2, 4


def start_kernel(pieces, *refs):
    x, (qb, vb, ob, g1, c1, ib, b2, g2, c2), refs = refs[0], refs[1:10], refs[10:]
    shards, docs, refs = refs[:6], refs[6], refs[7:]
    fulls, wins, docs_all, refs = refs[:6], refs[6:10], refs[10], refs[11:]
    saved_o, y_o, cls_o, refs = refs[:12], refs[12], refs[13], refs[14:]
    full, wbounce, ids, refs = refs[:6], refs[6:10], refs[10], refs[11:]
    (q_s, k_s, v_s, p_s, o_s, h_s, e_s, gp_s, x1, r1, x2, r2), y_s, refs = refs[:12], refs[12], refs[13:]
    load_sem, link_send, link_recv, core_send, core_recv, wload_sem, store_sem, refs = *refs[:7], refs[7:]
    win_send, win_recv, wcore_send, wcore_recv, ids_send, ids_recv, full_sem, out_sem = refs
    vq, vk, vv, vo, vi, v2 = full
    d, s = place()
    c = s % 2
    z = s // 2
    xx, yy = d % 2, d // 2
    dx, dy, dd = 2 * yy + 1 - xx, 2 * (1 - yy) + xx, 3 - d
    other = s + 1 - 2 * c
    even = 1 - z % 2
    xpeer, ypeer, zpeer = (dx, s), (dy, s), (d, s + 4 * even - 2)

    def either(a, b):
        return a * even + b * (1 - even)

    segs = x.shape[0] // 128
    count = len(pieces)
    loads = [
        pltpu.make_async_copy(shards[i].at[0], full[i].at[pl.ds(pl.multiple_of(d * shards[i].shape[1], 64), shards[i].shape[1])], load_sem.at[i])
        for i in range(6)
    ]
    for cp in loads:
        cp.start()
    ids_load = pltpu.make_async_copy(docs, ids, load_sem.at[6])
    ids_load.start()
    origins = (shards[0], shards[1], shards[2], shards[4])
    wloads = []
    for w in range(4):
        width = wins[w].shape[-1]
        at = window(d)[0] if w < 3 else d * width
        cp = pltpu.make_async_copy(origins[w].at[1, :, pl.ds(pl.multiple_of(at, 128), width)], wbounce[w], wload_sem.at[w])
        cp.start()
        wloads.append(cp)
    greet([xpeer, ypeer, (dd, s), zpeer, (d, other)])

    def cols(ref):
        half = ref.shape[-1] // 2
        return pl.ds(pl.multiple_of(c * half, half), half)

    def mine(p, h):
        i, r0, rn = pieces[p]
        n = rn // 4
        return shards[i].at[0, pl.ds(pl.multiple_of(r0 + (2 * h + c) * n, 16), n)]

    def slot(p, src, h):
        i, r0, rn = pieces[p]
        n = rn // 4
        return full[i].at[pl.ds(pl.multiple_of(src * shards[i].shape[1] + r0 + (2 * h + c) * n, 16), n)]

    started, shared, stores = [], [], []

    def link(kind, p, src, dst, peer):
        return remote(src, dst, link_send.at[kind, p], link_recv.at[kind, p], peer)

    def go(cp):
        cp.start()
        started.append(cp)

    def arrived(kind, p, ref):
        link(kind, p, ref, ref, zpeer).wait_recv()
        cp = remote(ref, ref, core_send.at[kind, p], core_recv.at[kind, p], (d, other))
        cp.start()
        shared.append((pieces[p][0], cp))
        started.append(cp)

    def own(p):
        if p < count:
            go(link(0, p, mine(p, 1), slot(p, d, 1), xpeer))
            go(link(1, p, mine(p, 0), slot(p, d, 0), ypeer))

    loaded = set()

    far = (dd, dx, dy)

    def columns(w, dev, core):
        wide = wins[w].shape[-1]
        begin = window(dev)[0] if w < 3 else dev * wide
        return pl.ds(pl.multiple_of(begin + core * (wide // 2), 128), wide // 2)

    def cross_needs():
        ids_load.wait()
        for k, peer in enumerate(far):
            for w in range(4):
                go(remote(
                    origins[w].at[1, :, columns(w, peer, c)], wins[w].at[d, :, cols(wins[w])],
                    win_send.at[k, w], win_recv.at[k, w], (peer, s),
                ))
            go(remote(ids, docs_all.at[d], ids_send.at[k], ids_recv.at[k], (peer, s)))

    def step(p):
        own(p + AHEAD)
        if p < count:
            i = pieces[p][0]
            if i not in loaded:
                loads[i].wait()
                loaded.add(i)
            arrived(0, p, slot(p, dx, 1))
            arrived(1, p, slot(p, dy, 0))
            ref = slot(p, either(d, dy), 0)
            go(link(2, p, ref, ref, xpeer))
            ref = slot(p, either(d, dx), 1)
            go(link(3, p, ref, ref, ypeer))
            if p == count - 1:
                cross_needs()
        n = p - LAG2
        if 0 <= n < count:
            for kind, src, h in ((2, either(dx, dd), 0), (3, either(dy, dd), 1)):
                ref = slot(n, src, h)
                arrived(kind, n, ref)
                go(link(kind + 2, n, ref, ref, zpeer))
        n = p - LAG4
        if 0 <= n < count:
            arrived(4, n, slot(n, either(dd, dx), 0))
            arrived(5, n, slot(n, either(dd, dy), 1))

    ready = set()

    def whole(i):
        for j, cp in shared:
            if j == i:
                cp.wait_recv()
        assert i not in ready
        ready.add(i)
        cp = pltpu.make_async_copy(full[i], fulls[i], full_sem.at[i])
        cp.start()
        stores.append(cp)

    def save(n, ref):
        cp = pltpu.make_async_copy(ref, y_o if n == 12 else saved_o[n], out_sem.at[n])
        cp.start()
        stores.append(cp)

    rows, width = x.shape
    nt = width // TILE
    for p in range(AHEAD):
        own(p)
    at = 0

    def advance(upto):
        nonlocal at
        while at < min(upto, count + LAG4):
            step(at)
            at += 1

    last = {i: max(p for p in range(count) if pieces[p][0] == i) for i in range(6)}
    advance(last[2] + LAG4 + 1)
    for i in range(3):
        whole(i)

    for t in range(nt):
        lanes = slice(t * TILE, t * TILE + TILE)
        q_s[:, lanes] = (dot(x[...], vq[:, lanes]) + qb[0:1, lanes].astype(F32)).astype(BF)
        k_s[:, lanes] = dot(x[...], vk[:, lanes]).astype(BF)
        v_s[:, lanes] = (dot(x[...], vv[:, lanes]) + vb[0:1, lanes].astype(F32)).astype(BF)
    for n, ref in enumerate((q_s, k_s, v_s)):
        save(n, ref)
    advance(last[2] + LAG4 + 2)
    masks = head_masks()

    def attend(hp, carry):
        lanes = tiles(hp, 128)
        for s in range(segs):
            here = slice(s * 128, s * 128 + 128)
            qs, ks, vs = q_s[here, lanes], k_s[here, lanes], v_s[here, lanes]
            mixed = None
            for h in range(2):
                scores = dot_nt(qs * masks[h], ks)
                top = jnp.max(scores, axis=-1, keepdims=True)
                weight = jnp.exp((scores - top) * 0.125)
                share = (weight * (1.0 / jnp.sum(weight, axis=-1, keepdims=True))).astype(BF)
                p_s[hp, s, h] = share
                part = dot(share, vs * masks[h])
                mixed = part if mixed is None else mixed + part
            o_s[here, lanes] = mixed.astype(BF)
        return carry

    pairs = width // 128
    for g in range(pairs // 2):
        lax.fori_loop(2 * g, 2 * g + 2, attend, 0)
        advance(last[2] + LAG4 + 3 + g)
    save(3, p_s)
    save(4, o_s)
    advance(last[3] + LAG4 + 1)
    whole(3)

    def out(t, carry):
        lanes = tiles(t)
        x1[:, lanes] = dot(o_s[...], vo[:, lanes]) + ob[0:1, lanes].astype(F32) + x[:, lanes].astype(F32)
        return carry

    lax.fori_loop(0, nt, out, 0)

    def first(i, carry):
        r = tiles(i, 64)
        xhat, rstd = standard(x1[r, :])
        x1[r, :] = xhat
        r1[r, :] = jnp.broadcast_to(rstd, (64, 128))
        hidden = xhat * g1[0:1, :].astype(F32) + c1[0:1, :].astype(F32)
        h_s[r, :] = hidden.astype(BF)
        x2[r, :] = hidden + b2[0:1, :].astype(F32)
        return carry

    lax.fori_loop(0, rows // 64, first, 0)
    for n, ref in ((5, h_s), (8, x1), (9, r1)):
        save(n, ref)
    advance(last[4] + LAG4 + 1)
    whole(4)

    def ffn(t, carry):
        lanes = tiles(t)
        u = dot(h_s[...], vi[:, lanes]) + ib[0:1, lanes].astype(F32)
        e, gp = gelu_parts(u)
        e_s[:, lanes] = e.astype(BF)
        gp_s[:, lanes] = gp.astype(BF)
        return carry

    groups = vi.shape[1] // TILE // 2
    for g in range(groups):
        lax.fori_loop(2 * g, 2 * g + 2, ffn, 0)
        advance(last[4] + LAG4 + 2 + g)
    advance(count + LAG4)
    for w in range(4):
        wloads[w].wait()
        cp = pltpu.make_async_copy(wbounce[w], wins[w].at[d], store_sem.at[w])
        cp.start()
        stores.append(cp)
    for src, dst, i in ((ids, docs_all.at[d], 4),):
        cp = pltpu.make_async_copy(src, dst, store_sem.at[i])
        cp.start()
        stores.append(cp)
    save(6, e_s)
    save(7, gp_s)
    whole(5)

    def outer(t, carry):
        lanes = tiles(t)
        x2[:, lanes] += dot(e_s[...], v2[:, lanes])
        return carry

    lax.fori_loop(0, nt, outer, 0)

    def second(i, carry):
        r = tiles(i, 64)
        xhat, rstd = standard(x2[r, :])
        x2[r, :] = xhat
        r2[r, :] = jnp.broadcast_to(rstd, (64, 128))
        y_s[r, :] = (xhat * g2[0:1, :].astype(F32) + c2[0:1, :].astype(F32)).astype(BF)
        return carry

    lax.fori_loop(0, rows // 64, second, 0)
    for n, ref in ((10, x2), (11, r2), (12, y_s)):
        save(n, ref)
    for s_ in range(segs):
        cls_o[s_ : s_ + 1, :] = x2[s_ * 128 : s_ * 128 + 1, :] * g2[0:1, :].astype(F32) + c2[0:1, :].astype(F32)
    wcores = []
    for k, peer in enumerate(far):
        for w in range(4):
            got = wins[w].at[peer, :, cols(wins[w])]
            remote(got, got, win_send.at[k, w], win_recv.at[k, w], (peer, s)).wait_recv()
            cp = remote(got, got, wcore_send.at[k, w], wcore_recv.at[k, w], (d, other))
            cp.start()
            wcores.append(cp)
        remote(ids, docs_all.at[peer], ids_send.at[k], ids_recv.at[k], (peer, s)).wait_recv()
    for cp in started:
        cp.wait_send()
    for cp in wcores:
        cp.wait()
    for cp in stores:
        cp.wait()


def start(x, shards, docs, vectors, collective_id):
    cuts = (1, 1, 1, 1, 3, 4)
    pieces = []
    for i, w in enumerate(shards):
        n = w.shape[1] // cuts[i]
        pieces += [(i, p * n, n) for p in range(cuts[i])]
    count = len(pieces)
    S, VM, dma = jax.ShapeDtypeStruct, pltpu.VMEM, pltpu.SemaphoreType.DMA
    V = pl.BlockSpec(memory_space=pltpu.VMEM)
    part, width = shards[0].shape[1:]
    rows = x.shape[0]
    ff = shards[4].shape[2]
    segs = rows // 128
    wins = [(part, 256)] * 3 + [(part, ff // 4)]
    low, full, wide, col = ((rows, width), BF), ((rows, width), F32), ((rows, ff), BF), ((rows, 128), F32)
    saved = [low, low, low, ((width // 128, segs, 2, 128, 128), BF), low, low, wide, wide, full, col, full, col, low]
    outs = pl.pallas_call(
        functools.partial(start_kernel, pieces),
        out_shape=[S((4 * w.shape[1], w.shape[2]), w.dtype) for w in shards]
        + [S((4,) + w, BF) for w in wins]
        + [S((4,) + docs.shape, docs.dtype)]
        + [S(*t) for t in saved]
        + [S((segs, width), F32)],
        in_specs=[V] * 10 + [ANY] * 7,
        out_specs=[ANY] * 24 + [V],
        scratch_shapes=[VM((4 * w.shape[1], w.shape[2]), w.dtype) for w in shards]
        + [VM(w, BF) for w in wins]
        + [VM(docs.shape, docs.dtype)]
        + [VM(*t) for t in saved]
        + [dma((7,)), dma((6, count)), dma((6, count)), dma((6, count)), dma((6, count)), dma((4,)), dma((5,))]
        + [dma((3, 4)), dma((3, 4)), dma((3, 4)), dma((3, 4)), dma((3,)), dma((3,)), dma((6,)), dma((13,))],
        compiler_params=pltpu.CompilerParams(collective_id=collective_id, has_side_effects=True, vmem_limit_bytes=67043328),
        name="gather_forward",
    )(x, *vectors, *shards, docs)
    return outs[:6], outs[6:10], outs[10], outs[11:23], outs[23], outs[24]


def add_into(dst, a, b, rows):
    step = 48 if rows % 48 == 0 else 32

    def body(i, carry):
        r = pl.ds(pl.multiple_of(i * step, 16), step)
        dst[r, :] = (a[r, :].astype(F32) + b[r, :].astype(F32)).astype(dst.dtype)
        return carry

    lax.fori_loop(0, rows // step, body, 0)


TILE = 256


def dot(a, b):
    return lax.dot_general(a, b, (((1,), (0,)), ((), ())), preferred_element_type=F32)


def dot_nt(a, b):
    return lax.dot_general(a, b, (((1,), (1,)), ((), ())), preferred_element_type=F32)


def dot_tn(a, b):
    return lax.dot_general(a, b, (((0,), (0,)), ((), ())), preferred_element_type=F32)


def tiles(i, size=TILE):
    return pl.ds(pl.multiple_of(i * size, size), size)


def standard(r):
    centred = r - jnp.mean(r, axis=-1, keepdims=True)
    rstd = lax.rsqrt(jnp.mean(centred * centred, axis=-1, keepdims=True) + epsilon)
    return centred * rstd, rstd


def standard_back(grad, xhat, rstd):
    return rstd * (
        grad
        - jnp.mean(grad, axis=-1, keepdims=True)
        - xhat * jnp.mean(grad * xhat, axis=-1, keepdims=True)
    )


def gelu_parts(u):
    phi = 0.5 * (1.0 + lax.erf(u * 0.7071067811865476))
    return u * phi, phi + u * (0.3989422804014327 * jnp.exp(-0.5 * u * u))


def head_masks():
    lane = lax.broadcasted_iota(jnp.int32, (1, 128), 1)
    low = (lane < 64).astype(F32)
    return (low.astype(BF), (1.0 - low).astype(BF))


def row_sum(v):
    return jnp.sum(v, axis=0, keepdims=True)


LAGS = (0, 2, 3, 4, 5, 6, 7, 8)
CHUNKS = [("rows", 0), ("rows", 1), ("rows", 2), ("cols", 0), ("cols", 1), ("cols", 2), ("mats", 3), ("mats", 0), ("mats", 1), ("mats", 2)]


def backward_kernel(dcl, z, g1, g2, du_own, dqkv_own, x, cot, q, k, v, p, o, hb, e, gp, x1, r1, x2, r2, y, wq, wk, wv, wo, wi, w2, *refs):
    (dx_o, y_o, outer_o, inner_o, mats_o, du_all, dqkv_all, vec_o), refs = refs[:8], refs[8:]
    (xs, ds_, qs_, ks_, vs_, p_s, os_, hs, e_s, gp_s, x1s, r1s, acc, r2s, ys), refs = refs[:15], refs[15:]
    (vi, v2, df, ht, vecs, g_rows, g_cols, g_mats), refs = refs[:8], refs[8:]
    bufs, refs = refs[:18], refs[18:]
    in_sem, w_sem, res_sem, out_sem, vsum, vgot, vsend, vrcv, send, recv, kept, kept_sem, far_send, far_recv, near_send, near_recv = refs
    dev, s = place()
    c, first, second, other = plane_peers(dev, s)
    px, py = dev % 2, dev // 2
    a = px * (1 - c) + py * c
    b = py * (1 - c) + px * c
    z_at = s // 2
    z0, z1 = z_at % 2, z_at // 2
    znear = (z_at + 1 - 2 * z0) * 2 + c
    zfar = (z_at + 2 - 4 * z1) * 2 + c
    order = [(cot, ds_), (y, ys), (x2, acc), (r2, r2s), (e, e_s), (hb, hs), (w2, v2), (gp, gp_s), (wi, vi),
             (x1, x1s), (r1, r1s), (o, os_), (p, p_s), (q, qs_), (k, ks_), (v, vs_), (x, xs)]
    loads = [pltpu.make_async_copy(src, dst, in_sem.at[i]) for i, (src, dst) in enumerate(order)]
    for cp in loads:
        cp.start()
    greet([(first, s), (second, s), (3 - dev, s), (dev, other), (dev, znear), (dev, zfar)])
    rows, width = xs.shape
    segs, nt = rows // 128, width // TILE
    share = width // 4
    started, outs, results = [], [], []

    def go(cp):
        cp.start()
        started.append(cp)

    def arrived(ref, sem):
        pltpu.make_async_copy(ref, ref, sem).wait()

    crossing = ((du_own, du_all), (dqkv_own, dqkv_all))
    far = (3 - dev, first, second)
    half_rows = pl.ds(pl.multiple_of(c * 64, 64), 64)
    keeps, shared = [], []

    def cross_send():
        for m, (src, dst) in enumerate(crossing):
            for n, peer in enumerate(far):
                go(remote(src.at[half_rows], dst.at[dev, half_rows], far_send.at[m, n], far_recv.at[m, n], (peer, s)))

    for m, (src, dst) in enumerate(crossing):
        cp = pltpu.make_async_copy(src, kept.at[m], kept_sem.at[0, m])
        cp.start()
        keeps.append(cp)

    def cross_share():
        for m, (src, dst) in enumerate(crossing):
            for n, peer in enumerate(far):
                got = dst.at[peer, half_rows]
                remote(got, got, far_send.at[m, n], far_recv.at[m, n], (peer, s)).wait_recv()
                cp = remote(got, got, near_send.at[m, n], near_recv.at[m, n], (dev, other))
                cp.start()
                shared.append(cp)
            keeps[m].wait()
            cp = pltpu.make_async_copy(kept.at[m], dst.at[dev], kept_sem.at[1, m])
            cp.start()
            outs.append(cp)

    families = {"rows": 0, "cols": 1, "mats": 2}

    def part(n, core, quarters):
        kind, i = CHUNKS[n]
        if kind == "rows":
            return g_rows.at[quarters, pl.ds(pl.multiple_of(i * 256 + core * 128, 128), 128), :]
        ref = g_cols if kind == "cols" else g_mats
        half = ref.shape[-1] // 2
        return ref.at[i, quarters, :, pl.ds(pl.multiple_of(core * half, 128), half)]

    def buf(n, j):
        kind, i = CHUNKS[n]
        ref = bufs[families[kind] * 6 + j]
        return ref.at[i] if j < 5 else ref.at[:, i]

    def size(n):
        return 128 if CHUNKS[n][0] == "rows" else 192

    def own(n, quarter):
        return part(n, c, quarter)

    def fin(n, core, at=0, count=None):
        kind, i = CHUNKS[n]
        count = size(n) if count is None else count
        return bufs[families[kind] * 6 + 5].at[core, i, pl.ds(pl.multiple_of(at, 16), count), :]

    def quarter(aa, bb):
        return aa * (1 + c) + bb * (2 - c)

    def offer(n):
        go(remote(part(n, 1 - c, slice(None)), buf(n, 0), send.at[0, n], recv.at[0, n], (dev, other)))

    def write(n, core, i):
        kind, at = CHUNKS[n]
        src = bufs[families[kind] * 6 + 5].at[core, at]
        if kind == "rows":
            pairs_ = [(src, outer_o.at[pl.ds(pl.multiple_of(at * 256 + core * 128, 128), 128), :])]
        elif kind == "mats":
            pairs_ = [(src, mats_o.at[at, :, pl.ds(pl.multiple_of(core * 384, 128), 384)])]
        else:
            pairs_ = [
                (src.at[:, j * 256 : j * 256 + 256], inner_o.at[:, pl.ds(pl.multiple_of((2 * core + j) * 768 + at * 256, 128), 256)])
                for j in range(2)
            ]
        for j, (left, right) in enumerate(pairs_):
            cp = pltpu.make_async_copy(left, right, out_sem.at[i, j, n])
            cp.start()
            outs.append(cp)

    def stage(t, n):
        r = size(n)
        h, f = r // 2, r // 4
        if t == 1:
            got = buf(n, 0)
            arrived(got, recv.at[0, n])
            for bb in range(2):
                away = quarter(1 - a, bb)
                add_into(own(n, away), own(n, away), got.at[away], r)
                go(remote(own(n, away), buf(n, 1).at[bb], send.at[1 + bb, n], recv.at[1 + bb, n], (first, s)))
            for bb in range(2):
                keep = quarter(a, bb)
                add_into(own(n, keep), own(n, keep), got.at[keep], r)
        elif t == 2:
            got = buf(n, 1)
            for bb in range(2):
                arrived(got.at[bb], recv.at[1 + bb, n])
            away, keep = quarter(a, 1 - b), quarter(a, b)
            add_into(own(n, away), own(n, away), got.at[1 - b], r)
            go(remote(own(n, away), buf(n, 2), send.at[3, n], recv.at[3, n], (second, s)))
            add_into(own(n, keep), own(n, keep), got.at[b], r)
        elif t == 3:
            got = buf(n, 2)
            arrived(got, recv.at[3, n])
            keep = own(n, quarter(a, b))
            away = pl.ds(pl.multiple_of((1 - z0) * h, 16), h)
            mine = pl.ds(pl.multiple_of(z0 * h, 16), h)
            add_into(keep.at[away], keep.at[away], got.at[away], h)
            go(remote(keep.at[away], buf(n, 3), send.at[4, n], recv.at[4, n], (dev, znear)))
            add_into(keep.at[mine], keep.at[mine], got.at[mine], h)
        elif t == 4:
            got = buf(n, 3)
            arrived(got, recv.at[4, n])
            keep = own(n, quarter(a, b))
            away = pl.ds(pl.multiple_of(z0 * h + (1 - z1) * f, 16), f)
            mine = pl.ds(pl.multiple_of(z0 * h + z1 * f, 16), f)
            add_into(keep.at[away], keep.at[away], got.at[pl.ds(pl.multiple_of((1 - z1) * f, 16), f)], f)
            go(remote(keep.at[away], buf(n, 4), send.at[5, n], recv.at[5, n], (dev, zfar)))
            add_into(keep.at[mine], keep.at[mine], got.at[pl.ds(pl.multiple_of(z1 * f, 16), f)], f)
        elif t == 5:
            got = buf(n, 4)
            arrived(got, recv.at[5, n])
            mine = own(n, quarter(a, b)).at[pl.ds(pl.multiple_of(z0 * h + z1 * f, 16), f)]
            done = fin(n, c, z0 * h + z1 * f, f)
            add_into(done, mine, got, f)
            go(remote(done, done, send.at[6, n], recv.at[6, n], (dev, zfar)))
        elif t == 6:
            arrived(fin(n, c, z0 * h + (1 - z1) * f, f), recv.at[6, n])
            half = fin(n, c, z0 * h, h)
            go(remote(half, half, send.at[7, n], recv.at[7, n], (dev, znear)))
        elif t == 7:
            arrived(fin(n, c, (1 - z0) * h, h), recv.at[7, n])
            go(remote(fin(n, c), fin(n, c), send.at[8, n], recv.at[8, n], (dev, other)))
            write(n, c, 0)
        elif t == 8:
            arrived(fin(n, 1 - c), recv.at[8, n])
            write(n, 1 - c, 1)

    nc = len(CHUNKS)

    def slot(i):
        for t in (1, 2, 3, 4, 5, 6, 7, 8):
            n = i - LAGS[t - 1]
            if 0 <= n < nc:
                stage(t, n)

    vecs[...] = jnp.zeros_like(vecs)
    for i in range(4):
        loads[i].wait()

    def norm2(i, carry):
        gain_sum, shift_sum, bias_sum = carry
        r = tiles(i, 64)
        dy, out = ds_[r, :].astype(F32), ys[r, :].astype(F32)
        at = lax.broadcasted_iota(jnp.int32, (64, 1), 0) + i * 64
        for j in range(segs):
            dy = jnp.where(at == j * 128, dcl[j : j + 1, :], dy)
            out = jnp.where(at == j * 128, z[j : j + 1, :], out)
        ys[r, :] = out.astype(BF)
        xhat = acc[r, :]
        back = standard_back(dy * g2[0:1, :].astype(F32), xhat, r2s[r, 0:1])
        acc[r, :] = back
        low = back.astype(BF)
        df[r, :] = low
        return (gain_sum + row_sum(dy * xhat), shift_sum + row_sum(dy), bias_sum + row_sum(low.astype(F32)))

    zero = jnp.zeros((1, width), F32)
    sums = lax.fori_loop(0, rows // 64, norm2, (zero, zero, zero))
    vecs[6:7, :], vecs[7:8, :], vecs[5:6, :] = sums
    results.append(pltpu.make_async_copy(ys, y_o, res_sem.at[0]))
    results[0].start()
    loads[4].wait()

    def outer(j):
        def body(block, carry):
            g_rows[block, j * TILE : j * TILE + TILE, :] = dot_tn(e_s[:, tiles(block * nt + j)], df[...]).astype(BF)
            return carry

        return body

    lax.fori_loop(0, 4, outer(0), 0)
    offer(0)
    lax.fori_loop(0, 4, outer(1), 0)
    offer(1)
    slot(0)
    lax.fori_loop(0, 4, outer(2), 0)
    offer(2)
    slot(1)
    loads[5].wait()
    ht[...] = hs[...].T
    for i in range(6, 9):
        loads[i].wait()

    def ffn(j):
        def body(block, carry):
            wide = tiles(block * nt + j)
            lanes = slice(j * TILE, j * TILE + TILE)
            de = dot_nt(df[...], v2[wide, :]).astype(BF).astype(F32)
            du = (de * gp_s[:, wide].astype(F32)).astype(BF)
            vecs[pl.ds(8 + block, 1), lanes] = row_sum(du.astype(F32))
            inner = dot(ht[...], du).astype(BF)
            for i in range(4):
                g_cols[j, i, :, tiles(block)] = inner[i * share : i * share + share]
            acc[...] += dot_nt(du, vi[:, wide])
            return carry

        return body

    lax.fori_loop(0, 4, ffn(0), 0)
    offer(3)
    slot(2)
    lax.fori_loop(0, 2, ffn(1), 0)
    slot(3)
    lax.fori_loop(2, 4, ffn(1), 0)
    offer(4)
    lax.fori_loop(0, 4, ffn(2), 0)
    offer(5)
    wloads = [
        pltpu.make_async_copy(src, v2.at[i * width : i * width + width], w_sem.at[i])
        for i, src in enumerate((wo, wq, wk, wv))
    ]
    for cp in wloads:
        cp.start()
    slot(4)
    for i in range(9, 17):
        loads[i].wait()

    def norm1(i, carry):
        gain_sum, shift_sum, bias_sum = carry
        r = tiles(i, 64)
        dh = acc[r, :]
        xhat = x1s[r, :]
        back = standard_back(dh * g1[0:1, :].astype(F32), xhat, r1s[r, 0:1])
        acc[r, :] = back
        low = back.astype(BF)
        df[r, :] = low
        return (gain_sum + row_sum(dh * xhat), shift_sum + row_sum(dh), bias_sum + row_sum(low.astype(F32)))

    sums = lax.fori_loop(0, rows // 64, norm1, (zero, zero, zero))
    vecs[3:4, :], vecs[4:5, :], vecs[2:3, :] = sums
    ht[...] = os_[...].T

    def weights(at, rhs):
        def body(t, carry):
            lanes = tiles(t)
            back = dot(ht[...], rhs[:, lanes]).astype(BF)
            for i in range(4):
                g_mats[at, i, :, lanes] = back[i * share : i * share + share]
            return carry

        lax.fori_loop(0, nt, body, 0)

    weights(3, df)
    offer(6)
    slot(5)
    wloads[0].wait()

    def mixed(t, carry):
        lanes = tiles(t)
        ds_[:, lanes] = dot_nt(df[...], v2[lanes, :]).astype(BF)
        return carry

    lax.fori_loop(0, nt, mixed, 0)
    masks = head_masks()

    def attend(hp, carry):
        lanes = tiles(hp, 128)
        for j in range(segs):
            here = slice(j * 128, j * 128 + 128)
            qs, ks, vs, dos = qs_[here, lanes], ks_[here, lanes], vs_[here, lanes], ds_[here, lanes]
            dqs = dks = dvs = 0.0
            for h in range(2):
                pl_ = p_s[hp, j, h]
                pf = pl_.astype(F32)
                dom = dos * masks[h]
                dp = dot_nt(dom, vs).astype(BF).astype(F32)
                ds = (pf * (dp - jnp.sum(pf * dp, axis=-1, keepdims=True))).astype(BF)
                dqs += dot(ds, ks * masks[h])
                dks += dot_tn(ds, qs * masks[h])
                dvs += dot_tn(pl_, dom)
            qs_[here, lanes] = (dqs * 0.125).astype(BF)
            ks_[here, lanes] = (dks * 0.125).astype(BF)
            vs_[here, lanes] = dvs.astype(BF)
        return carry

    lax.fori_loop(0, 3, attend, 0)
    slot(6)
    lax.fori_loop(3, width // 128, attend, 0)
    vecs[0:1, :] = row_sum(qs_[...].astype(F32))
    vecs[1:2, :] = row_sum(vs_[...].astype(F32))
    ht[...] = xs[...].T
    weights(0, qs_)
    offer(7)
    slot(7)
    weights(1, ks_)
    offer(8)
    weights(2, vs_)
    offer(9)
    hops = [(dev, other), (first, s), (second, s), (dev, znear), (dev, zfar)]
    vsum[0] = vecs[...]

    def vector_hop(j):
        if j > 0:
            arrived(vgot.at[j - 1], vrcv.at[j - 1])
            vsum[j] = vsum[j - 1] + vgot[j - 1]
        if j < 5:
            go(remote(vsum.at[j], vgot.at[j], vsend.at[j], vrcv.at[j], hops[j]))

    slot(8)
    vector_hop(0)
    for i in range(1, 4):
        wloads[i].wait()

    def source(t, carry):
        r = tiles(t)
        dx = acc[:, r]
        for i, g in enumerate((qs_, ks_, vs_)):
            dx += dot_nt(g[...], v2[pl.ds(pl.multiple_of((i + 1) * width + t * TILE, TILE), TILE), :])
        xs[:, r] = dx.astype(BF)
        return carry

    lax.fori_loop(0, nt, source, 0)
    results.append(pltpu.make_async_copy(xs, dx_o, res_sem.at[1]))
    results[1].start()
    for i in range(9, nc + LAGS[7]):
        slot(i)
        if i < 14:
            vector_hop(i - 8)
        if i == nc + 1:
            cross_send()
    cross_share()
    vec_o[...] = vsum[5]
    for cp in started:
        cp.wait_send()
    for cp in outs + results + shared:
        cp.wait()


def backward(x, cot, crossed, saved, y, weights, g1, g2, collective_id):
    q, k, v, p, o, hb, e, gp, x1, r1, x2, r2 = saved
    rows, width = x.shape
    ff = weights[4].shape[1]
    share, nc = width // 4, len(CHUNKS)
    S, VM, dma = jax.ShapeDtypeStruct, pltpu.VMEM, pltpu.SemaphoreType.DMA
    V = pl.BlockSpec(memory_space=pltpu.VMEM)
    z, dcl, dqkv, du = crossed[0], crossed[1], crossed[6], crossed[7]
    four = S((4,) + du.shape, BF)
    arrays = (x, cot, q, k, v, p, o, hb, e, gp, x1, r1, x2, r2, y)

    def chunk(n, r, w):
        return [VM(t, BF) for t in ((n, 4, r, w), (n, 2, r, w), (n, r, w), (n, r // 2, w), (n, r // 4, w), (2, n, r, w))]

    return pl.pallas_call(
        backward_kernel,
        out_shape=[
            S((rows, width), BF), S((rows, width), BF), S((ff // 4, width), BF), S((share, ff), BF), S((4, share, width), BF),
            four, four, S((16, width), F32),
        ],
        in_specs=[V] * 4 + [ANY] * 23,
        out_specs=[ANY] * 7 + [V],
        scratch_shapes=[VM(t.shape, t.dtype) for t in arrays]
        + [
            VM((width, ff), BF), VM((ff, width), BF), VM((rows, width), BF), VM((width, rows), BF), VM((16, width), F32),
            VM((4, ff // 4, width), BF), VM((3, 4, share, ff // 3), BF), VM((4, 4, share, width), BF),
        ]
        + chunk(3, 128, width) + chunk(3, share, ff // 6) + chunk(4, share, width // 2)
        + [
            dma((17,)), dma((4,)), dma((2,)), dma((2, 2, nc)),
            VM((6, 16, width), F32), VM((5, 16, width), F32), dma((5,)), dma((5,)), dma((9, nc)), dma((9, nc)),
            VM((2,) + du.shape, BF), dma((2, 2)), dma((2, 3)), dma((2, 3)), dma((2, 3)), dma((2, 3)),
        ],
        compiler_params=pltpu.CompilerParams(collective_id=collective_id, has_side_effects=True, vmem_limit_bytes=67043328),
        name="backward_reduce",
    )(dcl, z, g1, g2, du, dqkv, *arrays, *weights)


def cross_kernel(cls, emb, docs, cot, wq, wk, wv, wi, out_w, outer_w,
                 qb, vb, ob, g1, c1, ib, b2, g2, c2,
                 z_o, dcl_o, xw_o, hw_o, ow_o, e_o, dqkv_o, du_o, da_o, df_o, vec_o, emb_o,
                 vq, vk, vv, vi, vo, v2, heads, xall, rows_s, p_s, part_s, total_s, send1, got1, send2, got2,
                 in_sem, all_send, all_recv, first_rows, cots, cot_all, row_sem, cot_send, cot_recv, s1, r1, s2, r2, s3, r3):
    d, s = place()
    c, first, second, other = plane_peers(d, s)
    start, off = window(d)
    me, ahead, behind = everyone(d, s)
    lane_w = pl.ds(start, 256)
    loads = [
        pltpu.make_async_copy(src, dst, in_sem.at[i])
        for i, (src, dst) in enumerate(
            (
                (wq, vq), (wk, vk), (wv, vv),
                (out_w.at[1], vo.at[pl.ds(pl.multiple_of(off, 64), 192)]),
                (wi, vi), (outer_w.at[1], v2),
            )
        )
    ]
    for cp in loads:
        cp.start()
    row_loads = [pltpu.make_async_copy(cot.at[0, pl.ds(i * 128, 8)], first_rows.at[i], row_sem.at[i]) for i in range(4)]
    for cp in row_loads:
        cp.start()
    vo[pl.ds(pl.multiple_of(192 * (1 - d % 2), 64), 64), :] = jnp.zeros((64, 768), BF)
    pick = lax.broadcasted_iota(jnp.int32, (8, 32), 0) + 4 * s == lax.broadcasted_iota(jnp.int32, (8, 32), 1)
    position = dot(pick.astype(BF), emb[...])
    heads[...] = (cls[...] + position[0:4]).astype(BF)
    greet([(i // 8, i % 8) for i in ahead])
    sent = []
    for j, i in enumerate(ahead):
        cp = remote(heads, xall.at[me], all_send.at[j], all_recv.at[j], (i // 8, i % 8))
        cp.start()
        sent.append(cp)
    xall[me] = heads[...]
    for cp in row_loads:
        cp.wait()
    cots[...] = jnp.concatenate([first_rows[i].astype(F32)[0:1] for i in range(4)], axis=0).astype(BF)
    cot_all[me] = cots[...]
    ids = lax.broadcasted_iota(jnp.int32, (8, 128), 1) // 32 * 1024
    ids = ids.astype(F32)
    lane = lax.broadcasted_iota(jnp.int32, (32, 128), 1)
    key = lax.broadcasted_iota(jnp.int32, (32, 128), 0)
    for r in range(4):
        numbers = jnp.broadcast_to(docs[r], (8, 32)).astype(F32).astype(BF)
        ids = ids + dot(numbers, (lane == key + 32 * r).astype(BF))
    across = jnp.broadcast_to(ids[0:1], (128, 128))
    allowed = across == across.T
    for j, i in enumerate(behind):
        remote(heads, xall.at[i], all_send.at[j], all_recv.at[j], (i // 8, i % 8)).wait_recv()
    for j, i in enumerate(ahead):
        cp = remote(cots, cot_all.at[me], cot_send.at[j], cot_recv.at[j], (i // 8, i % 8))
        cp.start()
        sent.append(cp)
    for i in range(32):
        rows_s[4 * i : 4 * i + 4, :] = xall[i].astype(F32)
    xf = rows_s[...]
    x = xf.astype(BF)

    def total(n, partial):
        half = pl.ds(pl.multiple_of(c * 64, 64), 64)
        part_s[...] = partial
        send1[n] = part_s[half, :].astype(BF)
        one = remote(send1.at[n], got1.at[n], s1.at[n], r1.at[n], (first, s))
        one.start()
        one.wait_recv()
        both = send1[n].astype(F32) + got1[n].astype(F32)
        send2[n] = both.astype(BF)
        two = remote(send2.at[n], got2.at[n], s2.at[n], r2.at[n], (second, s))
        two.start()
        two.wait_recv()
        total_s[n, half, :] = send2[n].astype(F32) + got2[n].astype(F32)
        three = remote(total_s.at[n, half], total_s.at[n, half], s3.at[n], r3.at[n], (d, other))
        three.start()
        three.wait_recv()
        sent.extend((one, two, three))
        return total_s[n]

    def vector(ref, lanes=slice(None)):
        return ref[1:2, lanes].astype(F32)

    for i in range(3):
        loads[i].wait()
    q = (dot(x, vq[...]) + vector(qb, lane_w)).astype(BF)
    k = dot(x, vk[...]).astype(BF)
    v = (dot(x, vv[...]) + vector(vb, lane_w)).astype(BF)
    masks = head_masks()
    mixed = []
    for pair in range(2):
        l = slice(pair * 128, pair * 128 + 128)
        both = None
        for h in range(2):
            scores = jnp.where(allowed, dot_nt(q[:, l] * masks[h], k[:, l]) * 0.125, -1e30)
            weight = jnp.exp(scores - jnp.max(scores, axis=-1, keepdims=True))
            share = (weight * (1.0 / jnp.sum(weight, axis=-1, keepdims=True))).astype(BF)
            p_s[2 * pair + h] = share
            part = dot(share, v[:, l] * masks[h])
            both = part if both is None else both + part
        mixed.append(both.astype(BF))
    loads[3].wait()
    ow = jnp.concatenate(mixed, axis=1)
    ow_o[...] = ow
    branch = total(0, dot(ow, vo[...]))
    xhat1, rstd1 = standard(xf + branch + vector(ob))
    hidden = xhat1 * vector(g1) + vector(c1)
    hb = hidden.astype(BF)
    rows_s[...] = hidden
    hw_o[...] = rows_s[:, lane_w].astype(BF)
    rows_s[...] = xf
    xw_o[...] = rows_s[:, lane_w].astype(BF)
    loads[4].wait()
    loads[5].wait()
    wide = pl.ds(pl.multiple_of(d * 768, 768), 768)
    e, gp = gelu_parts(dot(hb, vi[...]) + vector(ib, wide))
    e = e.astype(BF)
    e_o[...] = e
    outer = total(1, dot(e, v2[...]))
    xhat2, rstd2 = standard(hidden + outer + vector(b2))
    z = (xhat2 * vector(g2) + vector(c2)).astype(BF)
    own = lax.broadcasted_iota(jnp.int32, (8, 128), 0) + 4 * me == lax.broadcasted_iota(jnp.int32, (8, 128), 1)
    own = own.astype(BF)
    z_o[...] = dot(own, z)
    for j, i in enumerate(behind):
        remote(cots, cot_all.at[i], cot_send.at[j], cot_recv.at[j], (i // 8, i % 8)).wait_recv()
    for i in range(32):
        rows_s[4 * i : 4 * i + 4, :] = cot_all[i].astype(F32)
    dy = rows_s[...]
    vec_o[6:7, :] = row_sum(dy * xhat2)
    vec_o[7:8, :] = row_sum(dy)
    dr2 = standard_back(dy * vector(g2), xhat2, rstd2)
    df = dr2.astype(BF)
    df_o[...] = df
    vec_o[5:6, :] = row_sum(df.astype(F32))
    du = (dot_nt(df, v2[...]).astype(BF).astype(F32) * gp).astype(BF)
    du_o[...] = du
    dh = dr2 + total(2, dot_nt(du, vi[...]))
    vec_o[3:4, :] = row_sum(dh * xhat1)
    vec_o[4:5, :] = row_sum(dh)
    dr1 = standard_back(dh * vector(g1), xhat1, rstd1)
    da = dr1.astype(BF)
    da_o[...] = da
    vec_o[2:3, :] = row_sum(da.astype(F32))
    do = dot_nt(da, vo[...]).astype(BF)
    dqs, dks, dvs = [], [], []
    for pair in range(2):
        l = slice(pair * 128, pair * 128 + 128)
        dqp = dkp = dvp = 0.0
        for h in range(2):
            share = p_s[2 * pair + h]
            pf = share.astype(F32)
            dom = do[:, l] * masks[h]
            dp = dot_nt(dom, v[:, l]).astype(BF).astype(F32)
            ds = (pf * (dp - jnp.sum(pf * dp, axis=-1, keepdims=True))).astype(BF)
            dqp += dot(ds, k[:, l] * masks[h])
            dkp += dot_tn(ds, q[:, l] * masks[h])
            dvp += dot_tn(share, dom)
        dqs.append((dqp * 0.125).astype(BF))
        dks.append((dkp * 0.125).astype(BF))
        dvs.append(dvp.astype(BF))
    dq, dk, dv = (jnp.concatenate(t, axis=1) for t in (dqs, dks, dvs))
    dqkv_o[:, 0:256] = dq
    dqkv_o[:, 256:512] = dk
    dqkv_o[:, 512:768] = dv
    dx = dr1 + total(3, dot_nt(dq, vq[...]) + dot_nt(dk, vk[...]) + dot_nt(dv, vv[...]))
    dcl = dx.astype(BF)
    dcl_o[...] = dot(own, dcl)
    back = dcl.astype(F32)
    emb_o[...] = back[0:32] + back[32:64] + back[64:96] + back[96:128]
    for cp in sent:
        cp.wait_send()


def cross(cls, emb, cot, docs, wq, wk, wv, wi, out_w, outer_w, vectors, collective_id):
    S = jax.ShapeDtypeStruct
    V = pl.BlockSpec(memory_space=pltpu.VMEM)
    VM, dma = pltpu.VMEM, pltpu.SemaphoreType.DMA
    low, win = S((128, 768), BF), S((128, 256), BF)
    return pl.pallas_call(
        cross_kernel,
        out_shape=[
            S((8, 768), F32), S((8, 768), F32), win, win, win, low, low, low, low, low,
            S((8, 768), F32), S((32, 768), F32),
        ],
        in_specs=[V] * 3 + [ANY] * 7 + [V] * 9,
        out_specs=[V] * 12,
        scratch_shapes=[
            VM((768, 256), BF), VM((768, 256), BF), VM((768, 256), BF), VM((768, 768), BF), VM((256, 768), BF), VM((768, 768), BF),
            VM((4, 768), BF), VM((32, 4, 768), BF), VM((128, 768), F32), VM((4, 128, 128), BF),
            VM((128, 768), F32), VM((4, 128, 768), F32),
            VM((4, 64, 768), BF), VM((4, 64, 768), BF), VM((4, 64, 768), BF), VM((4, 64, 768), BF),
            dma((6,)), dma((31,)), dma((31,)),
            VM((4, 8, 768), BF), VM((4, 768), BF), VM((32, 4, 768), BF), dma((4,)), dma((31,)), dma((31,)),
            dma((4,)), dma((4,)), dma((4,)), dma((4,)), dma((4,)), dma((4,)),
        ],
        compiler_params=pltpu.CompilerParams(collective_id=collective_id, has_side_effects=True, vmem_limit_bytes=67043328),
        name="cross_block",
    )(cls, emb, docs, cot, wq, wk, wv, wi, out_w, outer_w, *vectors)


def finish_kernel(dx, y, outer_h, inner_h, mats_h, vec, emb, xw, hw, ow, e, dqkv, du, da, df, vec1,
                  y_o, dx_o, gq_o, gqb, gk_o, gv_o, gvb, go_o, gob, gg1, gc1, gi_o, gib, g2_o, gb2, gg2, gc2, gemb,
                  vec_s, pass_s, gq, gk, gv, go, gi, g2_, outer, inner, mats, pass_in, pass_out, big_out, sum_in):
    sums = [pltpu.make_async_copy(src, dst, sum_in.at[i]) for i, (src, dst) in enumerate(((mats_h, mats), (inner_h, inner), (outer_h, outer)))]
    for cp in sums:
        cp.start()
    moves = [pltpu.make_async_copy(src, pass_s.at[i], pass_in.at[i]) for i, src in enumerate((y, dx))]
    for cp in moves:
        cp.start()
    leaves = []
    d = lax.axis_index("dp")
    odd = d % 2 == 1
    start, _ = window(d)

    def own(w):
        return jnp.where(odd, w[:, 64:256], w[:, 0:192])

    def whole(at):
        parts = [dqkv[i, :, at * 256 : at * 256 + 256] for i in range(4)]
        return jnp.concatenate(
            [
                parts[0][:, :128], parts[0][:, 128:] + parts[1][:, :128], parts[1][:, 128:],
                parts[2][:, :128], parts[2][:, 128:] + parts[3][:, :128], parts[3][:, 128:],
            ],
            axis=1,
        )

    x, h, o = own(xw[...].astype(F32)).astype(BF), own(hw[...].astype(F32)).astype(BF), own(ow[...].astype(F32)).astype(BF)
    dq, dk, dv = whole(0), whole(1), whole(2)
    def leave(src, dst, n):
        cp = pltpu.make_async_copy(src, dst, big_out.at[n])
        cp.start()
        leaves.append(cp)

    sums[0].wait()
    for at, (out, dst, left, right) in enumerate(((gq, gq_o, x, dq), (gk, gk_o, x, dk), (gv, gv_o, x, dv), (go, go_o, o, da[...]))):
        out[0] = mats[at].astype(F32)
        out[1] = dot_tn(left, right)
        leave(out, dst, at)
    for i, dst in enumerate((y_o, dx_o)):
        moves[i].wait()
        cp = pltpu.make_async_copy(pass_s.at[i], dst, pass_out.at[i])
        cp.start()
        leaves.append(cp)
    sums[1].wait()
    for j in range(4):
        l = slice(j * 768, j * 768 + 768)
        gi[0, :, l] = inner[:, l].astype(F32)
        gi[1, :, l] = dot_tn(h, du[j])
        leave(gi.at[:, :, l], gi_o.at[:, :, l], 4 + j)
    sums[2].wait()
    for j in range(3):
        r = slice(j * 256, j * 256 + 256)
        g2_[0, r] = outer[r, :].astype(F32)
        g2_[1, r] = dot_tn(e[:, r], df[...])
        leave(g2_.at[:, r], g2_o.at[:, r], 8 + j)
    lanes = pl.ds(start, 256)
    mine = own(vec[:, lanes])
    vec_s[...] = vec1[...]
    vec_s[0:1, :] = row_sum(dq.astype(F32))
    vec_s[1:2, :] = row_sum(dv.astype(F32))
    cross = own(vec_s[:, lanes])
    for r, out in enumerate((gqb, gvb, gob, gg1, gc1, gb2, gg2, gc2)):
        out[0:1, :] = mine[r : r + 1]
        out[1:2, :] = cross[r : r + 1]
    gib[0:1, :] = vec[pl.ds(8 + d, 1), :]
    gib[1:2, :] = row_sum(du[d].astype(F32))
    gemb[...] = own(emb[:, lanes])
    for cp in leaves:
        cp.wait()


def finish(summed, crossed):
    (_, _, xw, hw, ow, e, _, _, da, df, vec1, emb) = crossed
    S = jax.ShapeDtypeStruct
    V = pl.BlockSpec(memory_space=pltpu.VMEM)
    square, line = S((2, 192, 768), F32), S((2, 192), F32)
    dx, y, outer, inner, mats, du, dqkv, vec = summed
    return pl.pallas_call(
        finish_kernel,
        out_shape=[
            S(y.shape, BF), S(dx.shape, BF),
            square, line, square, square, line, square, line, line, line,
            S((2, 192, 3072), F32), S((2, 768), F32), S((2, 768, 768), F32), line, line, line, S((32, 192), F32),
        ],
        in_specs=[ANY] * 5 + [V] * 11,
        out_specs=[ANY, ANY, ANY, V, ANY, ANY, V, ANY, V, V, V, ANY, V, ANY, V, V, V, V],
        scratch_shapes=[pltpu.VMEM((8, 768), F32), pltpu.VMEM((2,) + y.shape, BF)]
        + [pltpu.VMEM(t.shape, F32) for t in (square, square, square, square, S((2, 192, 3072), F32), S((2, 768, 768), F32))]
        + [pltpu.VMEM(t.shape, BF) for t in (outer, inner, mats)]
        + [pltpu.SemaphoreType.DMA((2,)), pltpu.SemaphoreType.DMA((2,)), pltpu.SemaphoreType.DMA((11,)), pltpu.SemaphoreType.DMA((3,))],
        compiler_params=pltpu.CompilerParams(vmem_limit_bytes=67043328),
        name="finish_grads",
    )(dx, y, outer, inner, mats, vec, emb, xw, hw, ow, e, dqkv, du, da, df, vec1)


def fast_shards(
    inputs,
    doc_ids,
    cotangent,
    query_weight,
    query_bias,
    key_weight,
    value_weight,
    value_bias,
    out_weight,
    out_bias,
    first_gain,
    first_shift,
    inner_weight,
    inner_bias,
    outer_weight,
    outer_bias,
    second_gain,
    second_shift,
    segment_embed,
):
    weights = (query_weight, key_weight, value_weight, out_weight, inner_weight, outer_weight)
    vectors = (query_bias, value_bias, out_bias, first_gain, first_shift, inner_bias, outer_bias, second_gain, second_shift)
    full, windows, docs, saved, y, cls = start(inputs[0], weights, doc_ids, vectors, 1)
    windows = [w.reshape(-1, w.shape[-1]) for w in windows]
    crossed = cross(cls, segment_embed, cotangent, docs, *windows, out_weight, outer_weight, vectors, 2)
    summed = backward(
        inputs[0], cotangent[0], crossed, saved, y, full, first_gain, second_gain, 3
    )
    output, grad, *gradients = finish(summed, crossed)
    return (output[None], grad[None], *gradients)


def solution(mesh):
    placed = (
        P("dp", "seg", None),
        P("dp", None),
        P("dp", "seg", None),
        P(None, "dp", None),
        P(),
        P(None, "dp", None),
        P(None, "dp", None),
        P(),
        P(None, "dp", None),
        P(),
        P(),
        P(),
        P(None, "dp", None),
        P(),
        P(None, "dp", None),
        P(),
        P(),
        P(),
        P(),
    )
    square = mesh.shape["dp"] == 4 and mesh.shape["seg"] == 8
    return jax.shard_map(
        fast_shards if square else shards,
        mesh=mesh,
        in_specs=placed,
        out_specs=(
            P("dp", "seg", None),
            P("dp", "seg", None),
            P(None, "dp", None),
            P(None, "dp"),
            P(None, "dp", None),
            P(None, "dp", None),
            P(None, "dp"),
            P(None, "dp", None),
            P(None, "dp"),
            P(None, "dp"),
            P(None, "dp"),
            P(None, "dp", None),
            P(None, "dp"),
            P(None, "dp", None),
            P(None, "dp"),
            P(None, "dp"),
            P(None, "dp"),
            P(None, "dp"),
        ),
        check_vma=False,
    )
```
